32 devices in a mesh: groups: 2 (over y), seq: 4 (over z), mp: 2 (over x), sub: 2 (over core).
Axes of the slice: x: 2, y: 2, z: 4, core: 2. Of those that a mesh axis runs over, the one named last changes fastest.
Arguments:
- video_in: bfloat16 [1024, 4096], P(('groups', 'seq'), ('mp', 'sub')), parts along dimension 0, may hold values from -6 to 6
- audio_in: bfloat16 [256, 2048], P(('groups', 'seq'), ('mp', 'sub')), parts along dimension 0, may hold values from -6 to 6
- q_self: bfloat16 [1024, 2048], P(('groups', 'seq'), ('mp', 'sub')), parts along dimension 0
- k_self: bfloat16 [1024, 2048], P(('groups', 'seq'), ('mp', 'sub')), parts along dimension 0
- v_self: bfloat16 [1024, 2048], P(('groups', 'seq'), ('mp', 'sub')), parts along dimension 0, may hold values from -6 to 6
- q_a2v: bfloat16 [1024, 1024], P(('groups', 'seq'), ('mp', 'sub')), parts along dimension 0
- k_a2v: bfloat16 [256, 1024], P(('groups', 'seq'), ('mp', 'sub')), parts along dimension 0
- v_a2v: bfloat16 [256, 1024], P(('groups', 'seq'), ('mp', 'sub')), parts along dimension 0, may hold values from -6 to 6
- q_v2a: bfloat16 [256, 1024], P(('groups', 'seq'), ('mp', 'sub')), parts along dimension 0
- k_v2a: bfloat16 [1024, 1024], P(('groups', 'seq'), ('mp', 'sub')), parts along dimension 0
- v_v2a: bfloat16 [1024, 1024], P(('groups', 'seq'), ('mp', 'sub')), parts along dimension 0, may hold values from -6 to 6
- wo_self: bfloat16 [2048, 4096], P(('mp', 'sub')), may hold values from -0.125 to 0.125
- wo_a2v: bfloat16 [1024, 4096], P(('mp', 'sub')), may hold values from -0.1875 to 0.1875
- wo_v2a: bfloat16 [1024, 2048], P(('mp', 'sub')), may hold values from -0.1875 to 0.1875
- video_gates: bfloat16 [16, 2, 4096], replicated, may hold values from -4 to 4
- audio_gates: bfloat16 [16, 2048], replicated, may hold values from -4 to 4
- video_steps: int32 [1024], P(('groups', 'seq')), parts along dimension 0, may hold values from 0 to 15
- audio_steps: int32 [256], P(('groups', 'seq')), parts along dimension 0, may hold values from 0 to 15
- audio_len: int32 [2], P('groups'), parts along dimension 0, may hold values from 64 to 128
Outputs:
- video_out: bfloat16 [1024, 4096], P(('groups', 'seq'), ('mp', 'sub')), parts along dimension 0
- audio_out: bfloat16 [256, 2048], P(('groups', 'seq'), ('mp', 'sub')), parts along dimension 0
The draws below stay inside these ranges and needn't reach their ends.
There are 2 independent parts, one for each index of `groups`. The reference program is written for one: setup_inputs(seed, part) draws one part's arguments, and reference() takes and returns one part's arrays. A program takes and returns all parts, laid end to end along the dimension named above; an argument that names none is the same for every part. Nothing has to cross between parts.
Inputs may be any that keep to these rules, and one draw needn't show every extreme that they name: Audio tokens 0 to audio_len[0] - 1 are real, the rest are padding.
All inputs are finite; a program needn't handle non-finite values.
Results may differ from the reference program's by a relative error of at most 0.0075.
Values may be sent and summed in bfloat16 or wider, within the bound.
No kernel may reach another device: no remote copies, remote signals or barrier semaphores. Data moves between devices by JAX's collectives and lax.ppermute only.
A program may use at most 64 MiB of HBM per device.

```python
import math
import jax
import jax.numpy as jnp
from jax import lax

DV = 4096
DA = 2048
DHV = 128
DHC = 64
HV = 16
HC = 16
NT = 16
LV = 512
LA = 128


def paired_draw(key, tag, q_rows, k_rows, heads, width):
    base = jax.random.fold_in(key, tag)
    key_q, key_k = jax.random.split(base, 2)
    cols = heads * width
    queries = jnp.clip(1.5 * jax.random.normal(key_q, (q_rows, cols), jnp.float32), -9.0, 9.0)
    keys = jnp.clip(1.5 * jax.random.normal(key_k, (k_rows, cols), jnp.float32), -9.0, 9.0)
    return (queries, keys)


def draw_q_self(key, part):
    return paired_draw(key, 11, LV, LV, HV, DHV)[0].astype(jnp.bfloat16)


def draw_k_self(key, part):
    return paired_draw(key, 11, LV, LV, HV, DHV)[1].astype(jnp.bfloat16)


def draw_q_a2v(key, part):
    return paired_draw(key, 12, LV, LA, HC, DHC)[0].astype(jnp.bfloat16)


def draw_k_a2v(key, part):
    return paired_draw(key, 12, LV, LA, HC, DHC)[1].astype(jnp.bfloat16)


def draw_q_v2a(key, part):
    return paired_draw(key, 13, LA, LV, HC, DHC)[0].astype(jnp.bfloat16)


def draw_k_v2a(key, part):
    return paired_draw(key, 13, LA, LV, HC, DHC)[1].astype(jnp.bfloat16)


def touch_ends(entries, rng, low, high):
    index_at = [jax.random.randint(jax.random.fold_in(rng, axis), (), 0, length) for axis, length in enumerate(entries.shape)]
    main_axis = entries.shape.index(max(entries.shape))
    beside = index_at[:main_axis] + [(index_at[main_axis] + 1) % entries.shape[main_axis]] + index_at[main_axis + 1:]
    return entries.at[tuple(index_at)].set(low).at[tuple(beside)].set(high)


def block_levels(stream_key, extent, cuts, least, top_value):
    gain, own = 1.0, jax.random.fold_in(stream_key, 6)
    for position, parts in cuts:
        steps = jnp.exp(jax.random.uniform(jax.random.fold_in(own, position), (parts,), jnp.float32, least / len(cuts), top_value / len(cuts)))
        gain = gain * jnp.repeat(steps, extent[position] // parts).reshape([-1 if axis == position else 1 for axis in range(len(extent))])
    return gain


def noise(stream_key, dims, spread, most, shards=(), kind=jnp.bfloat16):
    values = jax.random.normal(stream_key, dims, jnp.float32) * spread
    if len(shards) > 0:
        values = block_levels(stream_key, dims, shards, -0.22, 0.18) * values
    return jnp.clip(values, min=-most, max=most).astype(kind)


def setup_inputs(seed: int = 0, part: int = 0) -> dict:
    key_of = jax.random.split(jax.random.key(seed), 20)
    part_keys = jax.random.split(jax.random.fold_in(key_of[19], part), 20)
    return {
        "video_in": noise(part_keys[0], (LV, DV), 1.0, 6.0, ((0, 4), (1, 4))),
        "audio_in": noise(part_keys[1], (LA, DA), 1.0, 6.0, ((0, 4), (1, 4))),
        "q_self": draw_q_self(jax.random.fold_in(jax.random.fold_in(key_of[19], part), 71), part),
        "k_self": draw_k_self(jax.random.fold_in(jax.random.fold_in(key_of[19], part), 71), part),
        "v_self": noise(part_keys[4], (LV, HV * DHV), 1.0, 6.0, ((0, 4), (1, 4))),
        "q_a2v": draw_q_a2v(jax.random.fold_in(jax.random.fold_in(key_of[19], part), 71), part),
        "k_a2v": draw_k_a2v(jax.random.fold_in(jax.random.fold_in(key_of[19], part), 71), part),
        "v_a2v": noise(part_keys[7], (LA, HC * DHC), 1.0, 6.0, ((0, 4), (1, 4))),
        "q_v2a": draw_q_v2a(jax.random.fold_in(jax.random.fold_in(key_of[19], part), 71), part),
        "k_v2a": draw_k_v2a(jax.random.fold_in(jax.random.fold_in(key_of[19], part), 71), part),
        "v_v2a": noise(part_keys[10], (LV, HC * DHC), 1.0, 6.0, ((0, 4), (1, 4))),
        "wo_self": noise(key_of[11], (HV * DHV, DV), (HV * DHV) ** -0.5, 0.125, ((0, 4),)),
        "wo_a2v": noise(key_of[12], (HC * DHC, DV), (HC * DHC) ** -0.5, 0.1875, ((0, 4),)),
        "wo_v2a": noise(key_of[13], (HC * DHC, DA), (HC * DHC) ** -0.5, 0.1875, ((0, 4),)),
        "video_gates": noise(key_of[14], (NT, 2, DV), 1.0, 4.0),
        "audio_gates": noise(key_of[15], (NT, DA), 1.0, 4.0),
        "video_steps": touch_ends(jax.random.randint(part_keys[16], (LV,), 0, NT), jax.random.fold_in(part_keys[16], 1), 0, NT - 1).astype(jnp.int32),
        "audio_steps": touch_ends(jax.random.randint(part_keys[17], (LA,), 0, NT), jax.random.fold_in(part_keys[17], 1), 0, NT - 1).astype(jnp.int32),
        "audio_len": jax.random.randint(part_keys[18], (1,), LA // 2, LA + 1).astype(jnp.int32),
    }


def attend(queries, keys, values, heads, width, valid):
    rows_q = queries.shape[0]
    rows_k = keys.shape[0]
    q_heads = queries.reshape(rows_q, heads, width).transpose(1, 0, 2)
    k_heads = keys.reshape(rows_k, heads, width).transpose(1, 0, 2)
    v_heads = values.reshape(rows_k, heads, width).transpose(1, 0, 2)
    block = math.gcd(rows_q, 512)

    def one_head(triple):
        q_one, k_one, v_one = triple
        blocks = q_one.reshape(rows_q // block, block, width)

        def one_block(q_rows):
            scores = jnp.dot(q_rows, k_one.T, preferred_element_type=jnp.float32) / math.sqrt(width)
            scores = jnp.where(valid[None, :], scores, -jnp.inf)
            peak = lax.optimization_barrier(jnp.max(scores, axis=1, keepdims=True))
            weights = jnp.exp(scores - peak)
            total = lax.optimization_barrier(jnp.sum(weights, axis=1, keepdims=True))
            summed = jnp.dot(weights.astype(jnp.bfloat16), v_one, preferred_element_type=jnp.float32)
            return summed / total
        return lax.map(one_block, blocks).reshape(rows_q, width)
    result = lax.map(one_head, (q_heads, k_heads, v_heads))
    return result.transpose(1, 0, 2).reshape(rows_q, heads * width).astype(jnp.bfloat16)

def reference(video_in, audio_in, q_self, k_self, v_self, q_a2v, k_a2v, v_a2v, q_v2a, k_v2a, v_v2a, wo_self, wo_a2v, wo_v2a, video_gates, audio_gates, video_steps, audio_steps, audio_len):
    limit = audio_len[0]
    every_video = jnp.ones((LV,), dtype=bool)
    audio_valid = jnp.arange(LA, dtype=jnp.int32) < limit
    self_att = attend(q_self, k_self, v_self, HV, DHV, every_video)
    a2v_att = attend(q_a2v, k_a2v, v_a2v, HC, DHC, audio_valid)
    v2a_att = attend(q_v2a, k_v2a, v_v2a, HC, DHC, every_video)
    video_gain = video_gates[video_steps].astype(jnp.float32)
    audio_gain = audio_gates[audio_steps].astype(jnp.float32)
    present = audio_valid.astype(jnp.float32)
    video_sum = video_gain[:, 0, :] * jnp.dot(self_att, wo_self, preferred_element_type=jnp.float32)
    video_sum = video_sum + video_gain[:, 1, :] * jnp.dot(a2v_att, wo_a2v, preferred_element_type=jnp.float32)
    audio_sum = present[:, None] * audio_gain * jnp.dot(v2a_att, wo_v2a, preferred_element_type=jnp.float32)
    video_out = (video_in.astype(jnp.float32) + video_sum).astype(jnp.bfloat16)
    audio_out = (audio_in.astype(jnp.float32) + audio_sum).astype(jnp.bfloat16)
    return (video_out, audio_out)
```

```python
import functools
import math

import jax
import jax.numpy as jnp
from jax import lax
from jax.experimental import pallas as pl
from jax.experimental.pallas import tpu as pltpu
from jax.sharding import PartitionSpec as P

DHV = 128
DHC = 64
NT = 16


def start_state(rows, heads, width):
    return (
        jnp.full((rows, heads), -1e30, jnp.float32),
        jnp.zeros((rows, heads), jnp.float32),
        jnp.zeros((rows, heads, width), jnp.float32),
    )


def update_block(state, queries, keys, values, heads, width, allowed):
    rows = queries.shape[0]
    count = keys.shape[0]
    q_heads = queries.reshape(rows, heads, width)
    k_heads = keys.reshape(count, heads, width)
    v_heads = values.reshape(count, heads, width)
    scores = jnp.einsum(
        "qhd,khd->qhk", q_heads, k_heads, preferred_element_type=jnp.float32
    ) / math.sqrt(width)
    if allowed is not None:
        scores = jnp.where(allowed[None, None, :], scores, -jnp.inf)
    peak_old, total_old, summed_old = state
    peak = jnp.maximum(peak_old, jnp.max(scores, axis=2))
    weights = jnp.exp(scores - peak[:, :, None])
    factor = jnp.exp(peak_old - peak)
    total = total_old * factor + jnp.sum(weights, axis=2)
    summed = summed_old * factor[:, :, None] + jnp.einsum(
        "qhk,khd->qhd", weights.astype(jnp.bfloat16), v_heads, preferred_element_type=jnp.float32
    )
    return (peak, total, summed)


def update_state(state, queries, keys, values, heads, width, start, limit):
    count = keys.shape[0]
    block = 1024 if count > 1024 and count % 1024 == 0 else count
    if block == count:
        allowed = None
        if limit is not None:
            allowed = jnp.arange(count, dtype=jnp.int32) < limit
        return update_block(state, queries, keys, values, heads, width, allowed)
    steps = count // block
    key_blocks = keys.reshape(steps, block, keys.shape[1])
    value_blocks = values.reshape(steps, block, values.shape[1])
    offsets = jnp.arange(steps, dtype=jnp.int32) * block

    def one_block(carry, items):
        key_rows, value_rows, offset = items
        allowed = None
        if limit is not None:
            allowed = start + offset + jnp.arange(block, dtype=jnp.int32) < limit
        return (update_block(carry, queries, key_rows, value_rows, heads, width, allowed), None)

    result, _ = lax.scan(one_block, state, (key_blocks, value_blocks, offsets))
    return result


def finish(state, heads, width):
    peak, total, summed = state
    rows = summed.shape[0]
    return (summed / total[:, :, None]).reshape(rows, heads * width).astype(jnp.bfloat16)


def on_device_gather(
    video_in,
    audio_in,
    q_self,
    k_self,
    v_self,
    q_a2v,
    k_a2v,
    v_a2v,
    q_v2a,
    k_v2a,
    v_v2a,
    wo_self,
    wo_a2v,
    wo_v2a,
    video_gates,
    audio_gates,
    video_steps,
    audio_steps,
    audio_len,
):
    heads_self = q_self.shape[1] // DHV
    heads_cross = q_a2v.shape[1] // DHC
    rows_video = q_self.shape[0]
    rows_audio = q_v2a.shape[0]
    limit = audio_len[0]
    piece = (
        lax.all_gather(k_a2v, "seq", axis=0, tiled=True),
        lax.all_gather(v_a2v, "seq", axis=0, tiled=True),
    )
    a2v_state = update_state(
        start_state(rows_video, heads_cross, DHC),
        q_a2v,
        piece[0],
        piece[1],
        heads_cross,
        DHC,
        jnp.int32(0),
        limit,
    )
    a2v_att = finish(a2v_state, heads_cross, DHC)
    piece = (
        lax.all_gather(k_self, "seq", axis=0, tiled=True),
        lax.all_gather(v_self, "seq", axis=0, tiled=True),
    )
    self_state = update_state(
        start_state(rows_video, heads_self, DHV),
        q_self,
        piece[0],
        piece[1],
        heads_self,
        DHV,
        jnp.int32(0),
        None,
    )
    piece = (
        lax.all_gather(k_v2a, "seq", axis=0, tiled=True),
        lax.all_gather(v_v2a, "seq", axis=0, tiled=True),
    )
    v2a_state = update_state(
        start_state(rows_audio, heads_cross, DHC),
        q_v2a,
        piece[0],
        piece[1],
        heads_cross,
        DHC,
        jnp.int32(0),
        None,
    )
    self_att = finish(self_state, heads_self, DHV)
    v2a_att = finish(v2a_state, heads_cross, DHC)
    levels = jnp.arange(NT, dtype=jnp.int32)
    video_hot = (video_steps[:, None] == levels[None, :]).astype(jnp.bfloat16)
    video_gain = jnp.dot(video_hot, video_gates.reshape(NT, -1), preferred_element_type=jnp.float32)
    width_video = video_gates.shape[2]
    video_term = video_gain[:, :width_video] * jnp.dot(
        self_att, wo_self, preferred_element_type=jnp.float32
    )
    video_term = video_term + video_gain[:, width_video:] * jnp.dot(
        a2v_att, wo_a2v, preferred_element_type=jnp.float32
    )
    audio_hot = (audio_steps[:, None] == levels[None, :]).astype(jnp.bfloat16)
    audio_gain = jnp.dot(audio_hot, audio_gates, preferred_element_type=jnp.float32)
    positions = lax.axis_index("seq") * rows_audio + jnp.arange(rows_audio, dtype=jnp.int32)
    present = (positions < limit).astype(jnp.float32)
    audio_term = (
        present[:, None] * audio_gain * jnp.dot(v2a_att, wo_v2a, preferred_element_type=jnp.float32)
    )
    video_sum, audio_sum = (
        lax.psum_scatter(
            video_term.astype(jnp.bfloat16), ("mp", "sub"), scatter_dimension=1, tiled=True
        ).astype(jnp.float32),
        lax.psum_scatter(
            audio_term.astype(jnp.bfloat16), ("mp", "sub"), scatter_dimension=1, tiled=True
        ).astype(jnp.float32),
    )
    video_out = (video_in.astype(jnp.float32) + video_sum).astype(jnp.bfloat16)
    audio_out = (audio_in.astype(jnp.float32) + audio_sum).astype(jnp.bfloat16)
    return (video_out, audio_out)


LOG2E = 1.4426950408889634
VMEM = pl.BlockSpec(memory_space=pltpu.VMEM)
SMEM = pl.BlockSpec(memory_space=pltpu.SMEM)


def call(kernel, outs, operands, flops, scratch=(), limit=24 * 2**20):
    size = sum(math.prod(x.shape) * x.dtype.itemsize for x in (*operands, *outs))
    specs = [SMEM if x.ndim == 1 and x.dtype == jnp.int32 else VMEM for x in operands]
    return pl.pallas_call(
        kernel,
        out_shape=tuple(outs),
        in_specs=specs,
        out_specs=tuple(VMEM for _ in outs),
        scratch_shapes=list(scratch),
        compiler_params=pltpu.CompilerParams(vmem_limit_bytes=limit),
        cost_estimate=pl.CostEstimate(flops=flops, bytes_accessed=size, transcendentals=0),
    )(*operands)


def dot_t(a, b):
    return lax.dot_general(a, b, (((1,), (1,)), ((), ())), preferred_element_type=jnp.float32)


def dot(a, b):
    return jnp.dot(a, b, preferred_element_type=jnp.float32)


def pack_kernel(hops, width, me_ref, q_ref, k_ref, v_ref, ka_ref, va_ref, qa_ref, *outs):
    rows = q_ref.shape[0]
    rows_audio, cols_audio = ka_ref.shape
    me = me_ref[0]
    for hop, out in zip(hops, outs):
        at = pl.ds(pl.multiple_of((me ^ hop) * width, width), width)
        for i, ref in enumerate((q_ref, k_ref, v_ref)):
            out[0:rows, i * width : (i + 1) * width] = ref[:, at]
        top = rows
        for part in range(cols_audio // width):
            for i, ref in enumerate((ka_ref, va_ref, qa_ref)):
                out[top : top + rows_audio, i * width : (i + 1) * width] = ref[
                    :, part * width : (part + 1) * width
                ]
            top += rows_audio


def softmax_parts(scores, scale, allowed=None):
    if allowed is not None:
        scores = jnp.where(allowed, scores, -jnp.inf)
    peak = jnp.max(scores, axis=1, keepdims=True)
    weights = jnp.exp2((scores - peak) * (scale * LOG2E))
    return peak, weights, jnp.sum(weights, axis=1, keepdims=True)


def attend_kernel(
    hops, width, head, me_ref, limit_ref, q_ref, k_ref, v_ref, qv_ref, ka_ref, va_ref, qa_ref, kv_ref, vv_ref, *rest
):
    n = len(hops) + 1
    got = rest[: n - 1]
    sends = rest[n - 1 : 2 * n - 2]
    own_ref, a2v_ref, own_v2a_ref, own_lse_ref = rest[2 * n - 2 : 2 * n + 2]
    qs, ks, vs, kas, vas, qas = rest[2 * n + 2 :]
    rows = q_ref.shape[0]
    rows_audio, cols = ka_ref.shape
    me, limit = me_ref[0], limit_ref[0]
    mine = pl.ds(pl.multiple_of(me * width, width), width)
    for dst, ref in ((qs, q_ref), (ks, k_ref), (vs, v_ref)):
        dst[0:rows, :] = ref[:, mine]
    for dst, ref in ((kas, ka_ref), (vas, va_ref), (qas, qa_ref)):
        dst[0:rows_audio, :] = ref[...]
    for j, ref in enumerate(got):
        at = (j + 1) * rows
        for i, dst in enumerate((qs, ks, vs)):
            dst[at : at + rows, :] = ref[0:rows, i * width : (i + 1) * width]
        at = (j + 1) * rows_audio
        top = rows
        for part in range(cols // width):
            for i, dst in enumerate((kas, vas, qas)):
                dst[at : at + rows_audio, part * width : (part + 1) * width] = ref[
                    top : top + rows_audio, i * width : (i + 1) * width
                ]
            top += rows_audio
    scale = 1.0 / math.sqrt(DHV)
    for j in range(n):
        for h in range(width // DHV):
            cut = slice(h * DHV, (h + 1) * DHV)
            _, p, total = softmax_parts(dot_t(qs[j * rows : (j + 1) * rows, cut], ks[:, cut]), scale)
            o = dot(p.astype(jnp.bfloat16), vs[:, cut]) / total
            dst = own_ref if j == 0 else sends[j - 1].at[0:rows, :]
            dst[:, cut] = o.astype(jnp.bfloat16)
    scale = 1.0 / math.sqrt(head)
    pair = 128 // head
    keys = n * rows_audio
    column = lax.broadcasted_iota(jnp.int32, (1, keys), 1)
    owner = jnp.full((1, keys), me, jnp.int32)
    for j, hop in enumerate(hops):
        owner = jnp.where(column // rows_audio == j + 1, me ^ hop, owner)
    allowed = owner * rows_audio + column % rows_audio < limit
    lane = lax.broadcasted_iota(jnp.int32, (1, 128), 1) // head
    lse_column = lax.broadcasted_iota(jnp.int32, (1, 128), 1)
    lse = jnp.zeros((n * rows_audio, 128), jnp.float32)
    for block in range(cols // 128):
        cut = slice(block * 128, (block + 1) * 128)
        a2v = jnp.zeros((rows, 128), jnp.float32)
        v2a = jnp.zeros((n * rows_audio, 128), jnp.float32)
        for i in range(pair):
            q = jnp.where(lane == i, qv_ref[:, cut], 0).astype(jnp.bfloat16)
            _, p, total = softmax_parts(dot_t(q, kas[:, cut]), scale, allowed)
            o = dot(p.astype(jnp.bfloat16), vas[:, cut]) / total
            a2v = jnp.where(lane == i, o, a2v)
            q = jnp.where(lane == i, qas[:, cut], 0).astype(jnp.bfloat16)
            peak, p, total = softmax_parts(dot_t(q, kv_ref[:, cut]), scale)
            o = dot(p.astype(jnp.bfloat16), vv_ref[:, cut]) / total
            v2a = jnp.where(lane == i, o, v2a)
            lse = jnp.where(
                lse_column == block * pair + i, peak * (scale * LOG2E) + jnp.log2(total), lse
            )
        a2v_ref[:, cut] = a2v.astype(jnp.bfloat16)
        own_v2a_ref[:, cut] = v2a[0:rows_audio]
        for j, dst in enumerate(sends):
            top = rows + block * rows_audio
            dst[top : top + rows_audio, 0:128] = v2a[
                (j + 1) * rows_audio : (j + 2) * rows_audio
            ].astype(jnp.bfloat16)
    own_lse_ref[...] = lse[0:rows_audio]
    for j, dst in enumerate(sends):
        rest_lse = lse[(j + 1) * rows_audio : (j + 2) * rows_audio]
        top = rows + cols // 128 * rows_audio
        packed = jnp.zeros((rows_audio, 128), jnp.float32)
        for term in range(3):
            piece = rest_lse.astype(jnp.bfloat16).astype(jnp.float32)
            rest_lse = rest_lse - piece
            packed = packed + (piece if term == 0 else pltpu.roll(piece, 32 * term, 1))
        dst[top : top + rows_audio, 0:128] = packed.astype(jnp.bfloat16)


def merge_kernel(hops, width, head, me_ref, own_ref, v2a_ref, lse_ref, *rest):
    got, (self_ref, out_ref) = rest[: len(hops)], rest[len(hops) :]
    rows = own_ref.shape[0]
    rows_audio, cols = v2a_ref.shape
    me = me_ref[0]
    lses, top = [lse_ref[...]], rows + cols // 128 * rows_audio
    self_ref[:, pl.ds(pl.multiple_of(me * width, width), width)] = own_ref[...]
    for hop, ref in zip(hops, got):
        self_ref[:, pl.ds(pl.multiple_of((me ^ hop) * width, width), width)] = ref[0:rows, :]
        packed = ref[top : top + rows_audio, 0:128].astype(jnp.float32)
        lses.append(packed + pltpu.roll(packed, 96, 1) + pltpu.roll(packed, 64, 1))
    peak = functools.reduce(jnp.maximum, lses)
    parts = [jnp.exp2(x - peak) for x in lses]
    total = functools.reduce(jnp.add, parts)
    parts = [x / total for x in parts]
    pair = 128 // head
    lane = lax.broadcasted_iota(jnp.int32, (1, 128), 1) // head
    for block in range(cols // 128):
        cut = slice(block * 128, (block + 1) * 128)
        top = rows + block * rows_audio
        summed = jnp.zeros((rows_audio, 128), jnp.float32)
        for j in range(len(parts)):
            if j == 0:
                o = v2a_ref[:, cut]
            else:
                o = got[j - 1][top : top + rows_audio, 0:128].astype(jnp.float32)
            share = jnp.zeros((rows_audio, 128), jnp.float32)
            for i in range(pair):
                at = block * pair + i
                share = jnp.where(lane == i, parts[j][:, at : at + 1], share)
            summed = summed + share * o
        out_ref[:, cut] = summed.astype(jnp.bfloat16)


def project_kernel(count, added, block_ref, att_ref, a2v_ref, v2a_ref, ws_ref, wa_ref, wv_ref, g0_ref, g1_ref, *rest):
    extra, outs = rest[:added], rest[added:]
    rows = att_ref.shape[0]
    rows_audio = v2a_ref.shape[0]
    for i in range(count):
        out = outs[i]
        wide = out.shape[1]
        narrow = wv_ref.shape[1] * wide // ws_ref.shape[1]
        at = pl.ds(pl.multiple_of(block_ref[i] * wide, wide), wide)
        term = g0_ref[:, at].astype(jnp.float32) * dot(att_ref[...], ws_ref[:, at])
        term = term + g1_ref[:, at].astype(jnp.float32) * dot(a2v_ref[...], wa_ref[:, at])
        at = pl.ds(pl.multiple_of(block_ref[i] * narrow, narrow), narrow)
        audio = dot(v2a_ref[...], wv_ref[:, at])
        fold = wide // narrow
        short = rows_audio // fold
        if added:
            term = term + extra[i][0:rows, :].astype(jnp.float32)
        out[0:rows, :] = term.astype(out.dtype)
        for f in range(fold):
            piece = audio[f * short : (f + 1) * short]
            cut = slice(f * narrow, (f + 1) * narrow)
            if added:
                piece = piece + extra[i][rows : rows + short, cut].astype(jnp.float32)
            out[rows : rows + short, cut] = piece.astype(out.dtype)


def finish_kernel(video_ref, audio_ref, gain_ref, own_ref, core_ref, chip_ref, video_out, audio_out):
    rows = video_ref.shape[0]
    rows_audio, narrow = audio_ref.shape
    term = own_ref[...] + core_ref[...].astype(jnp.float32) + chip_ref[...].astype(jnp.float32)
    video_out[...] = (video_ref[...].astype(jnp.float32) + term[0:rows]).astype(jnp.bfloat16)
    fold = video_ref.shape[1] // narrow
    short = rows_audio // fold
    for f in range(fold):
        cut = slice(f * short, (f + 1) * short)
        piece = term[rows : rows + short, f * narrow : (f + 1) * narrow]
        audio_out[cut, :] = (
            audio_ref[cut, :].astype(jnp.float32) + gain_ref[cut, :] * piece
        ).astype(jnp.bfloat16)


def on_device_heads(
    video_in,
    audio_in,
    q_self,
    k_self,
    v_self,
    q_a2v,
    k_a2v,
    v_a2v,
    q_v2a,
    k_v2a,
    v_v2a,
    wo_self,
    wo_a2v,
    wo_v2a,
    video_gates,
    audio_gates,
    video_steps,
    audio_steps,
    audio_len,
    *,
    n,
    chips,
):
    bf16, f32 = jnp.bfloat16, jnp.float32
    hops = [hop for hop in range(n - 1, 1, -1)] + [1]
    rows, cols = q_self.shape
    rows_audio, cols_cross = q_v2a.shape
    width = cols // n
    seq, mp, sub = (lax.axis_index(a).astype(jnp.int32) for a in ("seq", "mp", "sub"))
    me = seq.reshape(1)

    def trade(x, axis, hop, size):
        return lax.ppermute(x, axis, [(i, i ^ hop) for i in range(size)])

    tall = rows + cols_cross // width * rows_audio
    packed = call(
        functools.partial(pack_kernel, hops, width),
        [jax.ShapeDtypeStruct((tall, 3 * width), bf16)] * (n - 1),
        (me, q_self, k_self, v_self, k_a2v, v_a2v, q_v2a),
        0,
    )
    got = [trade(x, "seq", hop, n) for x, hop in zip(packed, hops)]

    levels = jnp.arange(NT, dtype=jnp.int32)
    wide_all = video_gates.shape[2]
    video_hot = (video_steps[:, None] == levels[None, :]).astype(bf16)
    gain = jnp.dot(video_hot, video_gates.reshape(NT, -1), preferred_element_type=f32).astype(bf16)
    gain_self, gain_a2v = gain[:, :wide_all], gain[:, wide_all:]
    narrow = audio_in.shape[1]
    owned = lax.dynamic_slice_in_dim(audio_gates, (mp * 2 + sub) * narrow, narrow, 1)
    audio_hot = (audio_steps[:, None] == levels[None, :]).astype(bf16)
    positions = seq * rows_audio + jnp.arange(rows_audio, dtype=jnp.int32)
    present = (positions < audio_len[0]).astype(f32)
    audio_gain = present[:, None] * jnp.dot(audio_hot, owned, preferred_element_type=f32)

    back = rows + cols_cross // 128 * rows_audio + rows_audio
    result = call(
        functools.partial(attend_kernel, hops, width, DHC),
        [jax.ShapeDtypeStruct((back, width), bf16)] * (n - 1)
        + [
            jax.ShapeDtypeStruct((rows, width), bf16),
            jax.ShapeDtypeStruct((rows, cols_cross), bf16),
            jax.ShapeDtypeStruct((rows_audio, cols_cross), f32),
            jax.ShapeDtypeStruct((rows_audio, 128), f32),
        ],
        (me, audio_len, q_self, k_self, v_self, q_a2v, k_a2v, v_a2v, q_v2a, k_v2a, v_v2a, *got),
        4 * n * n * rows * rows * width + 8 * n * rows * rows_audio * cols_cross,
        scratch=[pltpu.VMEM((n * rows, width), bf16)] * 3
        + [pltpu.VMEM((n * rows_audio, cols_cross), bf16)] * 3,
    )
    sends, (own, a2v_att, own_v2a, own_lse) = result[: n - 1], result[n - 1 :]
    got = [trade(x, "seq", hop, n) for x, hop in zip(sends, hops)]
    self_att, v2a_att = call(
        functools.partial(merge_kernel, hops, width, DHC),
        [jax.ShapeDtypeStruct((rows, cols), bf16), jax.ShapeDtypeStruct((rows_audio, cols_cross), bf16)],
        (me, own, own_v2a, own_lse, *got),
        0,
    )

    wide = video_in.shape[1]
    short = rows_audio * narrow // wide
    heads = (self_att, a2v_att, v2a_att, wo_self, wo_a2v, wo_v2a, gain_self, gain_a2v)

    def project(blocks, kinds, extra=()):
        return call(
            functools.partial(project_kernel, len(kinds), len(extra)),
            [jax.ShapeDtypeStruct((rows + short, wide), kind) for kind in kinds],
            (jnp.stack(blocks), *heads, *extra),
            2 * rows * (cols + cols_cross) * wide * len(kinds),
        )

    far, near = (1 - mp) * 2, mp * 2
    (first,) = project([far + 1 - sub], [bf16])
    first = trade(first, "sub", 1, 2)
    second, own_sum = project([near + 1 - sub, near + sub], [bf16, f32])
    (out_sum,) = project([far + sub], [bf16], (first,))
    chip_sum = trade(out_sum, "mp", 1, 2)
    core_sum = trade(second, "sub", 1, 2)
    return call(
        finish_kernel,
        [jax.ShapeDtypeStruct(video_in.shape, bf16), jax.ShapeDtypeStruct(audio_in.shape, bf16)],
        (video_in, audio_in, audio_gain, own_sum, core_sum, chip_sum),
        0,
    )


def on_device(n, mp, sub, *arrays):
    cols, cross = arrays[2].shape[1], arrays[5].shape[1]
    width = cols // n
    fits = (
        n in (2, 4, 8)
        and (mp, sub) == (2, 2)
        and width % DHV == 0
        and cross % width == 0
        and cross // DHC <= 32
    )
    if fits:
        return on_device_heads(*arrays, n=n, chips=mp)
    return on_device_gather(*arrays)


def solution(mesh):
    in_specs = (
        P(("groups", "seq"), ("mp", "sub")),
        P(("groups", "seq"), ("mp", "sub")),
        P(("groups", "seq"), ("mp", "sub")),
        P(("groups", "seq"), ("mp", "sub")),
        P(("groups", "seq"), ("mp", "sub")),
        P(("groups", "seq"), ("mp", "sub")),
        P(("groups", "seq"), ("mp", "sub")),
        P(("groups", "seq"), ("mp", "sub")),
        P(("groups", "seq"), ("mp", "sub")),
        P(("groups", "seq"), ("mp", "sub")),
        P(("groups", "seq"), ("mp", "sub")),
        P(("mp", "sub"), None),
        P(("mp", "sub"), None),
        P(("mp", "sub"), None),
        P(),
        P(),
        P(("groups", "seq")),
        P(("groups", "seq")),
        P("groups"),
    )
    out_specs = (P(("groups", "seq"), ("mp", "sub")), P(("groups", "seq"), ("mp", "sub")))
    return jax.shard_map(
        functools.partial(on_device, *(mesh.shape[a] for a in ("seq", "mp", "sub"))), mesh=mesh, in_specs=in_specs, out_specs=out_specs, check_vma=False
    )
```

```python
import functools
import math

import jax
import jax.numpy as jnp
from jax import lax
from jax.experimental import pallas as pl
from jax.experimental.pallas import tpu as pltpu
from jax.sharding import PartitionSpec as P


DHV = 128
DHC = 64
NT = 16


def start_state(rows, heads, width):
    return (
        jnp.full((rows, heads), -1e30, jnp.float32),
        jnp.zeros((rows, heads), jnp.float32),
        jnp.zeros((rows, heads, width), jnp.float32),
    )


def update_block(state, queries, keys, values, heads, width, allowed):
    rows = queries.shape[0]
    count = keys.shape[0]
    q_heads = queries.reshape(rows, heads, width)
    k_heads = keys.reshape(count, heads, width)
    v_heads = values.reshape(count, heads, width)
    scores = jnp.einsum(
        "qhd,khd->qhk", q_heads, k_heads, preferred_element_type=jnp.float32
    ) / math.sqrt(width)
    if allowed is not None:
        scores = jnp.where(allowed[None, None, :], scores, -jnp.inf)
    peak_old, total_old, summed_old = state
    peak = jnp.maximum(peak_old, jnp.max(scores, axis=2))
    weights = jnp.exp(scores - peak[:, :, None])
    factor = jnp.exp(peak_old - peak)
    total = total_old * factor + jnp.sum(weights, axis=2)
    summed = summed_old * factor[:, :, None] + jnp.einsum(
        "qhk,khd->qhd", weights.astype(jnp.bfloat16), v_heads, preferred_element_type=jnp.float32
    )
    return (peak, total, summed)


def update_state(state, queries, keys, values, heads, width, start, limit):
    count = keys.shape[0]
    block = 1024 if count > 1024 and count % 1024 == 0 else count
    if block == count:
        allowed = None
        if limit is not None:
            allowed = jnp.arange(count, dtype=jnp.int32) < limit
        return update_block(state, queries, keys, values, heads, width, allowed)
    steps = count // block
    key_blocks = keys.reshape(steps, block, keys.shape[1])
    value_blocks = values.reshape(steps, block, values.shape[1])
    offsets = jnp.arange(steps, dtype=jnp.int32) * block

    def one_block(carry, items):
        key_rows, value_rows, offset = items
        allowed = None
        if limit is not None:
            allowed = start + offset + jnp.arange(block, dtype=jnp.int32) < limit
        return (update_block(carry, queries, key_rows, value_rows, heads, width, allowed), None)

    result, _ = lax.scan(one_block, state, (key_blocks, value_blocks, offsets))
    return result


def finish(state, heads, width):
    _, total, summed = state
    rows = summed.shape[0]
    return (summed / total[:, :, None]).reshape(rows, heads * width).astype(jnp.bfloat16)


def on_device_gather(
    video_in,
    audio_in,
    q_self,
    k_self,
    v_self,
    q_a2v,
    k_a2v,
    v_a2v,
    q_v2a,
    k_v2a,
    v_v2a,
    wo_self,
    wo_a2v,
    wo_v2a,
    video_gates,
    audio_gates,
    video_steps,
    audio_steps,
    audio_len,
):
    heads_self = q_self.shape[1] // DHV
    heads_cross = q_a2v.shape[1] // DHC
    rows_video = q_self.shape[0]
    rows_audio = q_v2a.shape[0]
    limit = audio_len[0]
    piece = (
        lax.all_gather(k_a2v, "seq", axis=0, tiled=True),
        lax.all_gather(v_a2v, "seq", axis=0, tiled=True),
    )
    a2v_state = update_state(
        start_state(rows_video, heads_cross, DHC),
        q_a2v,
        piece[0],
        piece[1],
        heads_cross,
        DHC,
        jnp.int32(0),
        limit,
    )
    a2v_att = finish(a2v_state, heads_cross, DHC)
    piece = (
        lax.all_gather(k_self, "seq", axis=0, tiled=True),
        lax.all_gather(v_self, "seq", axis=0, tiled=True),
    )
    self_state = update_state(
        start_state(rows_video, heads_self, DHV),
        q_self,
        piece[0],
        piece[1],
        heads_self,
        DHV,
        jnp.int32(0),
        None,
    )
    piece = (
        lax.all_gather(k_v2a, "seq", axis=0, tiled=True),
        lax.all_gather(v_v2a, "seq", axis=0, tiled=True),
    )
    v2a_state = update_state(
        start_state(rows_audio, heads_cross, DHC),
        q_v2a,
        piece[0],
        piece[1],
        heads_cross,
        DHC,
        jnp.int32(0),
        None,
    )
    self_att = finish(self_state, heads_self, DHV)
    v2a_att = finish(v2a_state, heads_cross, DHC)
    levels = jnp.arange(NT, dtype=jnp.int32)
    video_hot = (video_steps[:, None] == levels[None, :]).astype(jnp.bfloat16)
    video_gain = jnp.dot(video_hot, video_gates.reshape(NT, -1), preferred_element_type=jnp.float32)
    width_video = video_gates.shape[2]
    video_term = video_gain[:, :width_video] * jnp.dot(
        self_att, wo_self, preferred_element_type=jnp.float32
    )
    video_term = video_term + video_gain[:, width_video:] * jnp.dot(
        a2v_att, wo_a2v, preferred_element_type=jnp.float32
    )
    audio_hot = (audio_steps[:, None] == levels[None, :]).astype(jnp.bfloat16)
    audio_gain = jnp.dot(audio_hot, audio_gates, preferred_element_type=jnp.float32)
    positions = lax.axis_index("seq") * rows_audio + jnp.arange(rows_audio, dtype=jnp.int32)
    present = (positions < limit).astype(jnp.float32)
    audio_term = (
        present[:, None] * audio_gain * jnp.dot(v2a_att, wo_v2a, preferred_element_type=jnp.float32)
    )
    video_sum, audio_sum = (
        lax.psum_scatter(
            video_term.astype(jnp.bfloat16), ("mp", "sub"), scatter_dimension=1, tiled=True
        ).astype(jnp.float32),
        lax.psum_scatter(
            audio_term.astype(jnp.bfloat16), ("mp", "sub"), scatter_dimension=1, tiled=True
        ).astype(jnp.float32),
    )
    video_out = (video_in.astype(jnp.float32) + video_sum).astype(jnp.bfloat16)
    audio_out = (audio_in.astype(jnp.float32) + audio_sum).astype(jnp.bfloat16)
    return (video_out, audio_out)


LOG2E = 1.4426950408889634
VMEM = pl.BlockSpec(memory_space=pltpu.VMEM)
SMEM = pl.BlockSpec(memory_space=pltpu.SMEM)
HBM = pl.BlockSpec(memory_space=pltpu.HBM)
BF16, F32 = jnp.bfloat16, jnp.float32


def call(kernel, outs, operands, specs=None, flops=0, scratch=(), limit=8 * 2**20):
    size = sum(math.prod(x.shape) * x.dtype.itemsize for x in (*operands, *outs))
    if specs:
        operands = [
            pltpu.with_memory_space_constraint(x, pltpu.HBM) if spec is HBM else x for x, spec in zip(operands, specs)
        ]
    return pl.pallas_call(
        kernel,
        out_shape=tuple(outs),
        in_specs=specs or [VMEM] * len(operands),
        out_specs=tuple(VMEM for _ in outs),
        scratch_shapes=list(scratch),
        compiler_params=pltpu.CompilerParams(vmem_limit_bytes=limit),
        cost_estimate=pl.CostEstimate(flops=flops, bytes_accessed=size, transcendentals=0),
    )(*operands)


def shape(rows, cols, kind=BF16):
    return jax.ShapeDtypeStruct((rows, cols), kind)


def dot_t(a, b):
    return lax.dot_general(a, b, (((1,), (1,)), ((), ())), preferred_element_type=F32)


def dot(a, b):
    return jnp.dot(a, b, preferred_element_type=F32)


def index_of(axis):
    return lax.axis_index(axis).astype(jnp.int32)


def columns(index, width):
    return pl.ds(pl.multiple_of(index * width, width), width)


def copy_all(pairs, sems):
    copies = [pltpu.make_async_copy(src, dst, sems.at[i]) for i, (src, dst) in enumerate(pairs)]
    for copy in copies:
        copy.start()
    for copy in copies:
        copy.wait()


def pack_kernel(hops, width, q_ref, k_ref, v_ref, qa_ref, ka_ref, va_ref, *rest):
    outs, audio, sems = rest[: len(hops)], rest[-2], rest[-1]
    rows = q_ref.shape[0]
    rows_audio, cols_audio = qa_ref.shape
    me = index_of("seq")
    pairs = []
    for hop, out in zip(hops, outs):
        for i, ref in enumerate((q_ref, k_ref, v_ref)):
            pairs.append((ref.at[:, columns(me ^ hop, width)], out.at[pl.ds(i * rows, rows), :]))
        for i in range(cols_audio // width):
            at = pl.ds(3 * rows + i * rows_audio, rows_audio)
            pairs.append((qa_ref.at[:, pl.ds(i * width, width)], out.at[at, :]))
    pairs.append((ka_ref, audio.at[pl.ds(0, rows_audio), :]))
    pairs.append((va_ref, audio.at[pl.ds(rows_audio, rows_audio), :]))
    copy_all(pairs, sems)


def one_hot_t(steps_ref):
    levels = lax.broadcasted_iota(jnp.int32, (NT, steps_ref.shape[1]), 0)
    return (levels == steps_ref[...]).astype(BF16)


def pick(hot_t, table):
    return lax.dot_general(hot_t, table, (((0,), (0,)), ((), ())), preferred_element_type=F32)


def fetch_kernel(limit_ref, vg_ref, *rest):
    loads, gain_ref, audio_ref = rest[:8], rest[8], rest[9]
    fetched, (vs_ref, as_ref, ag_ref, sems) = rest[10:15], rest[15:]
    copies = [
        pltpu.make_async_copy(src, dst, sems.at[i])
        for i, (src, dst) in enumerate(zip(loads, (vs_ref, as_ref, ag_ref, *fetched)))
    ]
    for copy in copies:
        copy.start()
    for copy in copies[:3]:
        copy.wait()
    hot_t = one_hot_t(vs_ref)
    piece = min(vg_ref.shape[1], 2048)
    for at in range(0, vg_ref.shape[1], piece):
        gain_ref[:, at : at + piece] = pick(hot_t, vg_ref[:, at : at + piece]).astype(BF16)
    rows_audio, narrow = audio_ref.shape
    part = index_of("mp") * 2 + index_of("sub")
    gain = pick(one_hot_t(as_ref), ag_ref[:, columns(part, narrow)])
    at = index_of("seq") * rows_audio + lax.broadcasted_iota(jnp.int32, (rows_audio, 1), 0)
    audio_ref[...] = jnp.where(at < limit_ref[0], gain, 0.0)
    for copy in copies[3:]:
        copy.wait()


def softmax_parts(scores, scale, allowed=None):
    if allowed is not None:
        scores = jnp.where(allowed, scores, -jnp.inf)
    peak = jnp.max(scores, axis=1, keepdims=True)
    weights = jnp.exp2((scores - peak) * (scale * LOG2E))
    return peak, weights, jnp.sum(weights, axis=1, keepdims=True)


def attend_kernel(n, head, kv_hbm, vv_hbm, *rest):
    blocks, sends, (own_ref, own_v2a_ref, own_lse_ref) = rest[:n], rest[n : 2 * n - 1], rest[2 * n - 1 : 2 * n + 2]
    ks, vs, qas, kv_ref, vv_ref, sems = rest[2 * n + 2 :]
    copies = [pltpu.make_async_copy(kv_hbm, kv_ref, sems.at[0]), pltpu.make_async_copy(vv_hbm, vv_ref, sems.at[1])]
    for copy in copies:
        copy.start()
    rows, cols = kv_ref.shape
    width = blocks[0].shape[1]
    rows_audio = qas.shape[0] // n
    for j, ref in enumerate(blocks):
        ks[j * rows : (j + 1) * rows, :] = ref[rows : 2 * rows, :]
        vs[j * rows : (j + 1) * rows, :] = ref[2 * rows : 3 * rows, :]
        for i in range(cols // width):
            top = 3 * rows + i * rows_audio
            qas[j * rows_audio : (j + 1) * rows_audio, i * width : (i + 1) * width] = ref[top : top + rows_audio, :]
    scale = 1.0 / math.sqrt(DHV)
    for j, ref in enumerate(blocks):
        for h in range(width // DHV):
            cut = slice(h * DHV, (h + 1) * DHV)
            _, p, total = softmax_parts(dot_t(ref[0:rows, cut], ks[:, cut]), scale)
            o = dot(p.astype(BF16), vs[:, cut]) / total
            dst = own_ref if j == 0 else sends[j - 1].at[0:rows, :]
            dst[:, cut] = o.astype(BF16)
    for copy in copies:
        copy.wait()
    scale = 1.0 / math.sqrt(head)
    pair = 128 // head
    lane = lax.broadcasted_iota(jnp.int32, (1, 128), 1) // head
    lse_column = lax.broadcasted_iota(jnp.int32, (1, 128), 1)
    lse = jnp.zeros((n * rows_audio, 128), F32)
    for block in range(cols // 128):
        cut = slice(block * 128, (block + 1) * 128)
        v2a = jnp.zeros((n * rows_audio, 128), F32)
        for i in range(pair):
            q = jnp.where(lane == i, qas[:, cut], 0).astype(BF16)
            peak, p, total = softmax_parts(dot_t(q, kv_ref[:, cut]), scale)
            v2a = jnp.where(lane == i, dot(p.astype(BF16), vv_ref[:, cut]) / total, v2a)
            lse = jnp.where(lse_column == block * pair + i, peak * (scale * LOG2E) + jnp.log2(total), lse)
        own_v2a_ref[:, cut] = v2a[0:rows_audio]
        for j, dst in enumerate(sends):
            top = rows + block * rows_audio
            dst[top : top + rows_audio, 0:128] = v2a[(j + 1) * rows_audio : (j + 2) * rows_audio].astype(BF16)
    own_lse_ref[...] = lse[0:rows_audio]
    for j, dst in enumerate(sends):
        rest_lse = lse[(j + 1) * rows_audio : (j + 2) * rows_audio]
        top = rows + cols // 128 * rows_audio
        packed = jnp.zeros((rows_audio, 128), F32)
        for term in range(3):
            piece = rest_lse.astype(BF16).astype(F32)
            rest_lse = rest_lse - piece
            packed = packed + (piece if term == 0 else pltpu.roll(piece, 32 * term, 1))
        dst[top : top + rows_audio, 0:128] = packed.astype(BF16)


def attend_audio_kernel(hops, head, limit_ref, q_hbm, *rest):
    n = len(hops)
    blocks, out_ref, ks, vs, q_ref, sem = rest[:n], *rest[n:]
    copy = pltpu.make_async_copy(q_hbm, q_ref, sem.at[0])
    copy.start()
    rows_audio = blocks[0].shape[0] // 2
    keys = n * rows_audio
    column = lax.broadcasted_iota(jnp.int32, (1, keys), 1)
    me, position = index_of("seq"), column
    for j, (hop, ref) in enumerate(zip(hops, blocks)):
        at = slice(j * rows_audio, (j + 1) * rows_audio)
        ks[at, :] = ref[0:rows_audio, :]
        vs[at, :] = ref[rows_audio : 2 * rows_audio, :]
        shift = ((me ^ hop) - j) * rows_audio
        position = jnp.where(column // rows_audio == j, column + shift, position)
    allowed = position < limit_ref[0]
    copy.wait()
    scale = 1.0 / math.sqrt(head)
    lane = lax.broadcasted_iota(jnp.int32, (1, 128), 1) // head
    for block in range(q_ref.shape[1] // 128):
        cut = slice(block * 128, (block + 1) * 128)
        both = jnp.zeros((q_ref.shape[0], 128), F32)
        for i in range(128 // head):
            q = jnp.where(lane == i, q_ref[:, cut], 0).astype(BF16)
            _, p, total = softmax_parts(dot_t(q, ks[:, cut]), scale, allowed)
            both = jnp.where(lane == i, dot(p.astype(BF16), vs[:, cut]) / total, both)
        out_ref[:, cut] = both.astype(BF16)


def merge(hops, head, own_ref, v2a_ref, lse_ref, got, self_ref, out_ref):
    rows, width = own_ref.shape
    rows_audio, cols = v2a_ref.shape
    me = index_of("seq")
    lses, top = [lse_ref[...]], rows + cols // 128 * rows_audio
    self_ref[:, columns(me, width)] = own_ref[...]
    for hop, ref in zip(hops[1:], got):
        self_ref[:, columns(me ^ hop, width)] = ref[0:rows, :]
        packed = ref[top : top + rows_audio, 0:128].astype(F32)
        lses.append(packed + pltpu.roll(packed, 96, 1) + pltpu.roll(packed, 64, 1))
    peak = functools.reduce(jnp.maximum, lses)
    parts = [jnp.exp2(x - peak) for x in lses]
    total = functools.reduce(jnp.add, parts)
    parts = [x / total for x in parts]
    pair = 128 // head
    lane = lax.broadcasted_iota(jnp.int32, (1, 128), 1) // head
    for block in range(cols // 128):
        cut = slice(block * 128, (block + 1) * 128)
        top = rows + block * rows_audio
        summed = jnp.zeros((rows_audio, 128), F32)
        for j in range(len(parts)):
            o = v2a_ref[:, cut] if j == 0 else got[j - 1][top : top + rows_audio, 0:128].astype(F32)
            share = jnp.zeros((rows_audio, 128), F32)
            for i in range(pair):
                at = block * pair + i
                share = jnp.where(lane == i, parts[j][:, at : at + 1], share)
            summed = summed + share * o
        out_ref[:, cut] = summed.astype(BF16)


def block_of(far, other):
    mp, sub = index_of("mp"), index_of("sub")
    return (1 - mp if far else mp) * 2 + (1 - sub if other else sub)


def project(block, heads, weights, gain_ref, out, extra=None):
    (att_ref, a2v_ref, v2a_ref), (ws_ref, wa_ref, wv_ref) = heads, weights
    rows, rows_audio, wide = att_ref.shape[0], v2a_ref.shape[0], out.shape[1]
    all_wide = ws_ref.shape[1]
    narrow = wv_ref.shape[1] * wide // all_wide
    at = columns(block, wide)
    term = gain_ref[:, at].astype(F32) * dot(att_ref[...], ws_ref[:, at])
    gain = gain_ref[:, columns(block + all_wide // wide, wide)].astype(F32)
    term = term + gain * dot(a2v_ref[...], wa_ref[:, at])
    audio = dot(v2a_ref[...], wv_ref[:, columns(block, narrow)])
    fold = wide // narrow
    short = rows_audio // fold
    if extra is not None:
        term = term + extra[0:rows, :].astype(F32)
    out[0:rows, :] = term.astype(out.dtype)
    for f in range(fold):
        piece = audio[f * short : (f + 1) * short]
        cut = slice(f * narrow, (f + 1) * narrow)
        if extra is not None:
            piece = piece + extra[rows : rows + short, cut].astype(F32)
        out[rows : rows + short, cut] = piece.astype(out.dtype)


def first_kernel(hops, head, own_ref, v2a_ref, lse_ref, a2v_ref, ws_ref, wa_ref, wv_ref, gain_ref, *rest):
    got, (out_ref, self_ref, audio_ref) = rest[: len(hops) - 1], rest[len(hops) - 1 :]
    merge(hops, head, own_ref, v2a_ref, lse_ref, got, self_ref, audio_ref)
    project(block_of(True, True), (self_ref, a2v_ref, audio_ref), (ws_ref, wa_ref, wv_ref), gain_ref, out_ref)


def near_kernel(*refs):
    heads, weights, gain_ref, (send_ref, own_ref) = refs[:3], refs[3:6], refs[6], refs[7:]
    project(block_of(False, True), heads, weights, gain_ref, send_ref)
    project(block_of(False, False), heads, weights, gain_ref, own_ref)


def far_kernel(*refs):
    heads, weights, gain_ref, extra, out_ref = refs[:3], refs[3:6], refs[6], refs[7], refs[8]
    project(block_of(True, False), heads, weights, gain_ref, out_ref, extra)


def finish_kernel(video_ref, audio_ref, gain_ref, own_ref, core_ref, chip_ref, video_out, audio_out):
    rows = video_ref.shape[0]
    rows_audio, narrow = audio_ref.shape
    term = own_ref[...] + core_ref[...].astype(F32) + chip_ref[...].astype(F32)
    video_out[...] = (video_ref[...].astype(F32) + term[0:rows]).astype(BF16)
    fold = video_ref.shape[1] // narrow
    short = rows_audio // fold
    for f in range(fold):
        cut = slice(f * short, (f + 1) * short)
        piece = term[rows : rows + short, f * narrow : (f + 1) * narrow]
        audio_out[cut, :] = (audio_ref[cut, :].astype(F32) + gain_ref[cut, :] * piece).astype(BF16)


def on_device_heads(
    video_in,
    audio_in,
    q_self,
    k_self,
    v_self,
    q_a2v,
    k_a2v,
    v_a2v,
    q_v2a,
    k_v2a,
    v_v2a,
    wo_self,
    wo_a2v,
    wo_v2a,
    video_gates,
    audio_gates,
    video_steps,
    audio_steps,
    audio_len,
    *,
    n,
):
    hops = [0] + list(range(n - 1, 0, -1))
    rows, cols = q_self.shape
    rows_audio, cross = q_v2a.shape
    width = cols // n

    def trade(x, axis, hop, size):
        return lax.ppermute(x, axis, [(i, i ^ hop) for i in range(size)])

    copies = n * (3 + cross // width) + 2
    *packed, audio = call(
        functools.partial(pack_kernel, hops, width),
        [shape(3 * rows + cross // width * rows_audio, width)] * n + [shape(2 * rows_audio, cross)],
        (q_self, k_self, v_self, q_v2a, k_a2v, v_a2v),
        [HBM] * 6,
        scratch=[pltpu.SemaphoreType.DMA((copies,))],
    )
    blocks = packed[:1] + [trade(x, "seq", hop, n) for x, hop in zip(packed[1:], hops[1:])]
    audios = [audio] + [trade(audio, "seq", hop, n) for hop in hops[1:]]

    late = (video_in, audio_in, wo_self, wo_a2v, wo_v2a)
    steps = (video_steps.reshape(1, rows), audio_steps.reshape(1, rows_audio))
    gain, audio_gain, video_own, audio_own, *weights = call(
        fetch_kernel,
        [shape(rows, 2 * video_gates.shape[2]), shape(*audio_in.shape, F32)]
        + [shape(*x.shape) for x in late],
        (audio_len, video_gates.reshape(NT, -1), *steps, audio_gates, *late),
        [SMEM, VMEM] + [HBM] * 8,
        scratch=[pltpu.VMEM(x.shape, x.dtype) for x in (*steps, audio_gates)]
        + [pltpu.SemaphoreType.DMA((8,))],
    )
    back = rows + cross // 128 * rows_audio + rows_audio
    result = call(
        functools.partial(attend_kernel, n, DHC),
        [shape(back, width)] * (n - 1)
        + [shape(rows, width), shape(rows_audio, cross, F32), shape(rows_audio, 128, F32)],
        (k_v2a, v_v2a, *blocks),
        [HBM] * 2 + [VMEM] * n,
        flops=4 * n * n * rows * rows * width,
        scratch=[pltpu.VMEM((n * rows, width), BF16)] * 2
        + [pltpu.VMEM((n * rows_audio, cross), BF16)]
        + [pltpu.VMEM((rows, cross), BF16)] * 2
        + [pltpu.SemaphoreType.DMA((2,))],
    )
    sends, (own, own_v2a, own_lse) = result[: n - 1], result[n - 1 :]
    got = [trade(x, "seq", hop, n) for x, hop in zip(sends, hops[1:])]
    (a2v_att,) = call(
        functools.partial(attend_audio_kernel, hops, DHC),
        [shape(rows, cross)],
        (audio_len, q_a2v, *audios),
        [SMEM, HBM] + [VMEM] * n,
        flops=8 * n * rows * rows_audio * cross,
        scratch=[pltpu.VMEM((n * rows_audio, cross), BF16)] * 2
        + [pltpu.VMEM((rows, cross), BF16), pltpu.SemaphoreType.DMA((1,))],
    )

    wide, narrow = video_in.shape[1], audio_in.shape[1]
    block = (rows + rows_audio * narrow // wide, wide)
    flops = 2 * rows * (cols + cross) * wide
    first, self_att, v2a_att = call(
        functools.partial(first_kernel, hops, DHC),
        [shape(*block), shape(rows, cols), shape(rows_audio, cross)],
        (own, own_v2a, own_lse, a2v_att, *weights, gain, *got),
        flops=flops,
    )
    heads = (self_att, a2v_att, v2a_att, *weights, gain)
    first = trade(first, "sub", 1, 2)
    second, own_sum = call(near_kernel, [shape(*block), shape(*block, F32)], heads, flops=2 * flops)
    (far_sum,) = call(far_kernel, [shape(*block)], (*heads, first), flops=flops)
    chip_sum = trade(far_sum, "mp", 1, 2)
    core_sum = trade(second, "sub", 1, 2)
    return call(
        finish_kernel,
        [shape(*video_in.shape), shape(*audio_in.shape)],
        (video_own, audio_own, audio_gain, own_sum, core_sum, chip_sum),
    )


def on_device(n, mp, sub, *arrays):
    cols, cross = arrays[2].shape[1], arrays[5].shape[1]
    width = cols // n
    fits = (
        n in (2, 4, 8)
        and (mp, sub) == (2, 2)
        and width % DHV == 0
        and cross % width == 0
        and cross // DHC <= 32
    )
    if fits:
        return on_device_heads(*arrays, n=n)
    return on_device_gather(*arrays)


def solution(mesh):
    in_specs = (
        P(("groups", "seq"), ("mp", "sub")),
        P(("groups", "seq"), ("mp", "sub")),
        P(("groups", "seq"), ("mp", "sub")),
        P(("groups", "seq"), ("mp", "sub")),
        P(("groups", "seq"), ("mp", "sub")),
        P(("groups", "seq"), ("mp", "sub")),
        P(("groups", "seq"), ("mp", "sub")),
        P(("groups", "seq"), ("mp", "sub")),
        P(("groups", "seq"), ("mp", "sub")),
        P(("groups", "seq"), ("mp", "sub")),
        P(("groups", "seq"), ("mp", "sub")),
        P(("mp", "sub"), None),
        P(("mp", "sub"), None),
        P(("mp", "sub"), None),
        P(),
        P(),
        P(("groups", "seq")),
        P(("groups", "seq")),
        P("groups"),
    )
    out_specs = (P(("groups", "seq"), ("mp", "sub")), P(("groups", "seq"), ("mp", "sub")))
    return jax.shard_map(
        functools.partial(on_device, *(mesh.shape[a] for a in ("seq", "mp", "sub"))), mesh=mesh, in_specs=in_specs, out_specs=out_specs, check_vma=False
    )
```

```python
import functools
import math

import jax
import jax.numpy as jnp
from jax import lax
from jax.experimental import pallas as pl
from jax.experimental.pallas import tpu as pltpu
from jax.sharding import PartitionSpec as P


DHV = 128
DHC = 64
NT = 16


def start_state(rows, heads, width):
    return (
        jnp.full((rows, heads), -1e30, jnp.float32),
        jnp.zeros((rows, heads), jnp.float32),
        jnp.zeros((rows, heads, width), jnp.float32),
    )


def update_block(state, queries, keys, values, heads, width, allowed):
    rows = queries.shape[0]
    count = keys.shape[0]
    q_heads = queries.reshape(rows, heads, width)
    k_heads = keys.reshape(count, heads, width)
    v_heads = values.reshape(count, heads, width)
    scores = jnp.einsum(
        "qhd,khd->qhk", q_heads, k_heads, preferred_element_type=jnp.float32
    ) / math.sqrt(width)
    if allowed is not None:
        scores = jnp.where(allowed[None, None, :], scores, -jnp.inf)
    peak_old, total_old, summed_old = state
    peak = jnp.maximum(peak_old, jnp.max(scores, axis=2))
    weights = jnp.exp(scores - peak[:, :, None])
    factor = jnp.exp(peak_old - peak)
    total = total_old * factor + jnp.sum(weights, axis=2)
    summed = summed_old * factor[:, :, None] + jnp.einsum(
        "qhk,khd->qhd", weights.astype(jnp.bfloat16), v_heads, preferred_element_type=jnp.float32
    )
    return (peak, total, summed)


def update_state(state, queries, keys, values, heads, width, start, limit):
    count = keys.shape[0]
    block = 1024 if count > 1024 and count % 1024 == 0 else count
    if block == count:
        allowed = None
        if limit is not None:
            allowed = jnp.arange(count, dtype=jnp.int32) < limit
        return update_block(state, queries, keys, values, heads, width, allowed)
    steps = count // block
    key_blocks = keys.reshape(steps, block, keys.shape[1])
    value_blocks = values.reshape(steps, block, values.shape[1])
    offsets = jnp.arange(steps, dtype=jnp.int32) * block

    def one_block(carry, items):
        key_rows, value_rows, offset = items
        allowed = None
        if limit is not None:
            allowed = start + offset + jnp.arange(block, dtype=jnp.int32) < limit
        return (update_block(carry, queries, key_rows, value_rows, heads, width, allowed), None)

    result, _ = lax.scan(one_block, state, (key_blocks, value_blocks, offsets))
    return result


def finish(state, heads, width):
    _, total, summed = state
    rows = summed.shape[0]
    return (summed / total[:, :, None]).reshape(rows, heads * width).astype(jnp.bfloat16)


def on_device_gather(
    video_in,
    audio_in,
    q_self,
    k_self,
    v_self,
    q_a2v,
    k_a2v,
    v_a2v,
    q_v2a,
    k_v2a,
    v_v2a,
    wo_self,
    wo_a2v,
    wo_v2a,
    video_gates,
    audio_gates,
    video_steps,
    audio_steps,
    audio_len,
):
    heads_self = q_self.shape[1] // DHV
    heads_cross = q_a2v.shape[1] // DHC
    rows_video = q_self.shape[0]
    rows_audio = q_v2a.shape[0]
    limit = audio_len[0]
    piece = (
        lax.all_gather(k_a2v, "seq", axis=0, tiled=True),
        lax.all_gather(v_a2v, "seq", axis=0, tiled=True),
    )
    a2v_state = update_state(
        start_state(rows_video, heads_cross, DHC),
        q_a2v,
        piece[0],
        piece[1],
        heads_cross,
        DHC,
        jnp.int32(0),
        limit,
    )
    a2v_att = finish(a2v_state, heads_cross, DHC)
    piece = (
        lax.all_gather(k_self, "seq", axis=0, tiled=True),
        lax.all_gather(v_self, "seq", axis=0, tiled=True),
    )
    self_state = update_state(
        start_state(rows_video, heads_self, DHV),
        q_self,
        piece[0],
        piece[1],
        heads_self,
        DHV,
        jnp.int32(0),
        None,
    )
    piece = (
        lax.all_gather(k_v2a, "seq", axis=0, tiled=True),
        lax.all_gather(v_v2a, "seq", axis=0, tiled=True),
    )
    v2a_state = update_state(
        start_state(rows_audio, heads_cross, DHC),
        q_v2a,
        piece[0],
        piece[1],
        heads_cross,
        DHC,
        jnp.int32(0),
        None,
    )
    self_att = finish(self_state, heads_self, DHV)
    v2a_att = finish(v2a_state, heads_cross, DHC)
    levels = jnp.arange(NT, dtype=jnp.int32)
    video_hot = (video_steps[:, None] == levels[None, :]).astype(jnp.bfloat16)
    video_gain = jnp.dot(video_hot, video_gates.reshape(NT, -1), preferred_element_type=jnp.float32)
    width_video = video_gates.shape[2]
    video_term = video_gain[:, :width_video] * jnp.dot(
        self_att, wo_self, preferred_element_type=jnp.float32
    )
    video_term = video_term + video_gain[:, width_video:] * jnp.dot(
        a2v_att, wo_a2v, preferred_element_type=jnp.float32
    )
    audio_hot = (audio_steps[:, None] == levels[None, :]).astype(jnp.bfloat16)
    audio_gain = jnp.dot(audio_hot, audio_gates, preferred_element_type=jnp.float32)
    positions = lax.axis_index("seq") * rows_audio + jnp.arange(rows_audio, dtype=jnp.int32)
    present = (positions < limit).astype(jnp.float32)
    audio_term = (
        present[:, None] * audio_gain * jnp.dot(v2a_att, wo_v2a, preferred_element_type=jnp.float32)
    )
    video_sum, audio_sum = (
        lax.psum_scatter(
            video_term.astype(jnp.bfloat16), ("mp", "sub"), scatter_dimension=1, tiled=True
        ).astype(jnp.float32),
        lax.psum_scatter(
            audio_term.astype(jnp.bfloat16), ("mp", "sub"), scatter_dimension=1, tiled=True
        ).astype(jnp.float32),
    )
    video_out = (video_in.astype(jnp.float32) + video_sum).astype(jnp.bfloat16)
    audio_out = (audio_in.astype(jnp.float32) + audio_sum).astype(jnp.bfloat16)
    return (video_out, audio_out)


LOG2E = 1.4426950408889634
VMEM = pl.BlockSpec(memory_space=pltpu.VMEM)
SMEM = pl.BlockSpec(memory_space=pltpu.SMEM)
HBM = pl.BlockSpec(memory_space=pltpu.HBM)
BF16, F32 = jnp.bfloat16, jnp.float32


def call(kernel, outs, operands, specs=None, flops=0, scratch=(), limit=8 * 2**20):
    size = sum(math.prod(x.shape) * x.dtype.itemsize for x in (*operands, *outs))
    if specs:
        operands = [
            pltpu.with_memory_space_constraint(x, pltpu.HBM) if spec is HBM else x for x, spec in zip(operands, specs)
        ]
    return pl.pallas_call(
        kernel,
        out_shape=tuple(outs),
        in_specs=specs or [VMEM] * len(operands),
        out_specs=tuple(VMEM for _ in outs),
        scratch_shapes=list(scratch),
        compiler_params=pltpu.CompilerParams(vmem_limit_bytes=limit),
        cost_estimate=pl.CostEstimate(flops=flops, bytes_accessed=size, transcendentals=0),
    )(*operands)


def shape(rows, cols, kind=BF16):
    return jax.ShapeDtypeStruct((rows, cols), kind)


def dot_t(a, b):
    return lax.dot_general(a, b, (((1,), (1,)), ((), ())), preferred_element_type=F32)


def dot(a, b):
    return jnp.dot(a, b, preferred_element_type=F32)


def index_of(axis):
    return lax.axis_index(axis).astype(jnp.int32)


def columns(index, width):
    return pl.ds(pl.multiple_of(index * width, width), width)


def copy_all(pairs, sems):
    copies = [pltpu.make_async_copy(src, dst, sems.at[i]) for i, (src, dst) in enumerate(pairs)]
    for copy in copies:
        copy.start()
    for copy in copies:
        copy.wait()


def pack_kernel(hops, width, q_ref, k_ref, v_ref, qa_ref, ka_ref, va_ref, *rest):
    outs, audio, sems = rest[: len(hops)], rest[-2], rest[-1]
    rows = q_ref.shape[0]
    rows_audio, cols_audio = qa_ref.shape
    me = index_of("seq")
    pairs = []
    for hop, out in zip(hops, outs):
        for i, ref in enumerate((q_ref, k_ref, v_ref)):
            pairs.append((ref.at[:, columns(me ^ hop, width)], out.at[pl.ds(i * rows, rows), :]))
        for i in range(cols_audio // width):
            at = pl.ds(3 * rows + i * rows_audio, rows_audio)
            pairs.append((qa_ref.at[:, pl.ds(i * width, width)], out.at[at, :]))
    pairs.append((ka_ref, audio.at[pl.ds(0, rows_audio), :]))
    pairs.append((va_ref, audio.at[pl.ds(rows_audio, rows_audio), :]))
    copy_all(pairs, sems)


def one_hot_t(steps_ref):
    levels = lax.broadcasted_iota(jnp.int32, (NT, steps_ref.shape[1]), 0)
    return (levels == steps_ref[...]).astype(BF16)


def pick(hot_t, table):
    return lax.dot_general(hot_t, table, (((0,), (0,)), ((), ())), preferred_element_type=F32)


def fetch_kernel(limit_ref, vg_ref, *rest):
    count = (len(rest) - 9) // 2
    loads, gain_ref, audio_ref = rest[: count + 3], rest[count + 3], rest[count + 4]
    fetched, (vs_ref, as_ref, ag_ref, sems) = rest[count + 5 : -4], rest[-4:]
    copies = [
        pltpu.make_async_copy(src, dst, sems.at[i])
        for i, (src, dst) in enumerate(zip(loads, (vs_ref, as_ref, ag_ref, *fetched)))
    ]
    for copy in copies:
        copy.start()
    for copy in copies[:3]:
        copy.wait()
    hot_t = one_hot_t(vs_ref)
    piece = min(vg_ref.shape[1], 2048)
    for at in range(0, vg_ref.shape[1], piece):
        gain_ref[:, at : at + piece] = pick(hot_t, vg_ref[:, at : at + piece]).astype(BF16)
    rows_audio, narrow = audio_ref.shape
    part = index_of("mp") * 2 + index_of("sub")
    gain = pick(one_hot_t(as_ref), ag_ref[:, columns(part, narrow)])
    at = index_of("seq") * rows_audio + lax.broadcasted_iota(jnp.int32, (rows_audio, 1), 0)
    audio_ref[...] = jnp.where(at < limit_ref[0], gain, 0.0)
    for copy in copies[3:]:
        copy.wait()


def softmax_parts(scores, scale, allowed=None):
    if allowed is not None:
        scores = jnp.where(allowed, scores, -jnp.inf)
    peak = jnp.max(scores, axis=1, keepdims=True)
    weights = jnp.exp2((scores - peak) * (scale * LOG2E))
    return peak, weights, jnp.sum(weights, axis=1, keepdims=True)


def attend_kernel(n, head, kv_ref, vv_ref, *rest):
    blocks, sends, (own_ref, own_v2a_ref, own_lse_ref) = rest[:n], rest[n : 2 * n - 1], rest[2 * n - 1 : 2 * n + 2]
    ks, vs, qas = rest[2 * n + 2 :]
    rows, cols = kv_ref.shape
    width = blocks[0].shape[1]
    rows_audio = qas.shape[0] // n
    for j, ref in enumerate(blocks):
        ks[j * rows : (j + 1) * rows, :] = ref[rows : 2 * rows, :]
        vs[j * rows : (j + 1) * rows, :] = ref[2 * rows : 3 * rows, :]
        for i in range(cols // width):
            top = 3 * rows + i * rows_audio
            qas[j * rows_audio : (j + 1) * rows_audio, i * width : (i + 1) * width] = ref[top : top + rows_audio, :]
    scale = 1.0 / math.sqrt(DHV)
    for j, ref in enumerate(blocks):
        for h in range(width // DHV):
            cut = slice(h * DHV, (h + 1) * DHV)
            _, p, total = softmax_parts(dot_t(ref[0:rows, cut], ks[:, cut]), scale)
            o = dot(p.astype(BF16), vs[:, cut]) / total
            dst = own_ref if j == 0 else sends[j - 1].at[0:rows, :]
            dst[:, cut] = o.astype(BF16)
    scale = 1.0 / math.sqrt(head)
    pair = 128 // head
    lane = lax.broadcasted_iota(jnp.int32, (1, 128), 1) // head
    lse_column = lax.broadcasted_iota(jnp.int32, (1, 128), 1)
    lse = jnp.zeros((n * rows_audio, 128), F32)
    for block in range(cols // 128):
        cut = slice(block * 128, (block + 1) * 128)
        v2a = jnp.zeros((n * rows_audio, 128), F32)
        for i in range(pair):
            q = jnp.where(lane == i, qas[:, cut], 0).astype(BF16)
            peak, p, total = softmax_parts(dot_t(q, kv_ref[:, cut]), scale)
            v2a = jnp.where(lane == i, dot(p.astype(BF16), vv_ref[:, cut]) / total, v2a)
            lse = jnp.where(lse_column == block * pair + i, peak * (scale * LOG2E) + jnp.log2(total), lse)
        own_v2a_ref[:, cut] = v2a[0:rows_audio]
        for j, dst in enumerate(sends):
            top = rows + block * rows_audio
            dst[top : top + rows_audio, 0:128] = v2a[(j + 1) * rows_audio : (j + 2) * rows_audio].astype(BF16)
    own_lse_ref[...] = lse[0:rows_audio]
    for j, dst in enumerate(sends):
        rest_lse = lse[(j + 1) * rows_audio : (j + 2) * rows_audio]
        top = rows + cols // 128 * rows_audio
        packed = jnp.zeros((rows_audio, 128), F32)
        for term in range(3):
            piece = rest_lse.astype(BF16).astype(F32)
            rest_lse = rest_lse - piece
            packed = packed + (piece if term == 0 else pltpu.roll(piece, 32 * term, 1))
        dst[top : top + rows_audio, 0:128] = packed.astype(BF16)


def attend_audio_kernel(hops, head, limit_ref, q_ref, *rest):
    n = len(hops)
    blocks, out_ref, ks, vs = rest[:n], *rest[n:]
    rows_audio = blocks[0].shape[0] // 2
    keys = n * rows_audio
    column = lax.broadcasted_iota(jnp.int32, (1, keys), 1)
    me, position = index_of("seq"), column
    for j, (hop, ref) in enumerate(zip(hops, blocks)):
        at = slice(j * rows_audio, (j + 1) * rows_audio)
        ks[at, :] = ref[0:rows_audio, :]
        vs[at, :] = ref[rows_audio : 2 * rows_audio, :]
        shift = ((me ^ hop) - j) * rows_audio
        position = jnp.where(column // rows_audio == j, column + shift, position)
    allowed = position < limit_ref[0]
    scale = 1.0 / math.sqrt(head)
    lane = lax.broadcasted_iota(jnp.int32, (1, 128), 1) // head
    for block in range(q_ref.shape[1] // 128):
        cut = slice(block * 128, (block + 1) * 128)
        both = jnp.zeros((q_ref.shape[0], 128), F32)
        for i in range(128 // head):
            q = jnp.where(lane == i, q_ref[:, cut], 0).astype(BF16)
            _, p, total = softmax_parts(dot_t(q, ks[:, cut]), scale, allowed)
            both = jnp.where(lane == i, dot(p.astype(BF16), vs[:, cut]) / total, both)
        out_ref[:, cut] = both.astype(BF16)


def merge_audio(head, top, v2a_ref, lse_ref, got, out_ref):
    rows_audio, cols = v2a_ref.shape
    lses = [lse_ref[...]]
    for ref in got:
        at = top + cols // 128 * rows_audio
        packed = ref[at : at + rows_audio, 0:128].astype(F32)
        lses.append(packed + pltpu.roll(packed, 96, 1) + pltpu.roll(packed, 64, 1))
    peak = functools.reduce(jnp.maximum, lses)
    parts = [jnp.exp2(x - peak) for x in lses]
    total = functools.reduce(jnp.add, parts)
    parts = [x / total for x in parts]
    pair = 128 // head
    lane = lax.broadcasted_iota(jnp.int32, (1, 128), 1) // head
    for block in range(cols // 128):
        cut = slice(block * 128, (block + 1) * 128)
        at = top + block * rows_audio
        summed = jnp.zeros((rows_audio, 128), F32)
        for j in range(len(parts)):
            o = v2a_ref[:, cut] if j == 0 else got[j - 1][at : at + rows_audio, 0:128].astype(F32)
            share = jnp.zeros((rows_audio, 128), F32)
            for i in range(pair):
                column = block * pair + i
                share = jnp.where(lane == i, parts[j][:, column : column + 1], share)
            summed = summed + share * o
        out_ref[:, cut] = summed.astype(BF16)


def block_of(far, other):
    mp, sub = index_of("mp"), index_of("sub")
    return (1 - mp if far else mp) * 2 + (1 - sub if other else sub)


def project(block, half, heads, weights, gain_ref):
    (att_ref, a2v_ref), (ws_ref, wa_ref) = heads, weights
    wide = ws_ref.shape[1]
    cut = wide // 8
    at = columns(block * 2 + half, cut)
    term = gain_ref[:, at].astype(F32) * dot(att_ref[...], ws_ref[:, at])
    gain = gain_ref[:, columns(block * 2 + half + 8, cut)].astype(F32)
    return term + gain * dot(a2v_ref[...], wa_ref[:, at])


def project_audio(block, v2a_ref, wv_ref):
    return dot(v2a_ref[...], wv_ref[:, columns(block, wv_ref.shape[1] // 4)])


def first_kernel(hops, own_ref, a2v_ref, ws_ref, wa_ref, gain_ref, *rest):
    got, (self_ref, out_ref) = rest[: len(hops) - 1], rest[len(hops) - 1 :]
    rows, width = own_ref.shape
    me = index_of("seq")
    self_ref[:, columns(me, width)] = own_ref[...]
    for hop, ref in zip(hops[1:], got):
        self_ref[:, columns(me ^ hop, width)] = ref[0:rows, :]
    out_ref[...] = project(block_of(True, True), 0, (self_ref, a2v_ref), (ws_ref, wa_ref), gain_ref).astype(BF16)


def second_kernel(head, self_ref, a2v_ref, ws_ref, wa_ref, wv_ref, gain_ref, v2a_ref, lse_ref, *rest):
    got, (out_ref, audio_ref) = rest[:-2], rest[-2:]
    rows = self_ref.shape[0]
    block = block_of(True, True)
    out_ref[0:rows, :] = project(block, 1, (self_ref, a2v_ref), (ws_ref, wa_ref), gain_ref).astype(BF16)
    merge_audio(head, rows, v2a_ref, lse_ref, got, audio_ref)
    out_ref[rows:, :] = project_audio(block, audio_ref, wv_ref).astype(BF16)


def near_kernel(self_ref, a2v_ref, audio_ref, ws_ref, wa_ref, wv_ref, gain_ref, send_ref, own_ref):
    rows = self_ref.shape[0]
    for out, other in ((send_ref, True), (own_ref, False)):
        block = block_of(False, other)
        for half in range(2):
            term = project(block, half, (self_ref, a2v_ref), (ws_ref, wa_ref), gain_ref)
            out[half * rows : (half + 1) * rows, :] = term.astype(out.dtype)
        out[2 * rows :, :] = project_audio(block, audio_ref, wv_ref).astype(out.dtype)


def far_kernel(half, self_ref, a2v_ref, ws_ref, wa_ref, gain_ref, extra_ref, *rest):
    rows, out_ref = self_ref.shape[0], rest[-1]
    block = block_of(True, False)
    term = project(block, half, (self_ref, a2v_ref), (ws_ref, wa_ref), gain_ref)
    out_ref[0:rows, :] = (term + extra_ref[0:rows, :].astype(F32)).astype(BF16)
    if half == 1:
        audio_ref, wv_ref = rest[:2]
        term = project_audio(block, audio_ref, wv_ref)
        out_ref[rows:, :] = (term + extra_ref[rows:, :].astype(F32)).astype(BF16)


def finish_kernel(video_ref, audio_ref, gain_ref, own_ref, core_ref, low_ref, high_ref, video_out, audio_out):
    rows = video_ref.shape[0]
    cut = video_ref.shape[1] // 2
    near = own_ref[...] + core_ref[...].astype(F32)
    for half, ref in enumerate((low_ref, high_ref)):
        at = slice(half * cut, (half + 1) * cut)
        term = near[half * rows : (half + 1) * rows] + ref[0:rows, :].astype(F32)
        video_out[:, at] = (video_ref[:, at].astype(F32) + term).astype(BF16)
    term = near[2 * rows :] + high_ref[rows:, :].astype(F32)
    audio_out[...] = (audio_ref[...].astype(F32) + gain_ref[...] * term).astype(BF16)


def on_device_heads(
    video_in,
    audio_in,
    q_self,
    k_self,
    v_self,
    q_a2v,
    k_a2v,
    v_a2v,
    q_v2a,
    k_v2a,
    v_v2a,
    wo_self,
    wo_a2v,
    wo_v2a,
    video_gates,
    audio_gates,
    video_steps,
    audio_steps,
    audio_len,
    *,
    n,
):
    hops = [0] + order_of(n)
    rows, cols = q_self.shape
    rows_audio, cross = q_v2a.shape
    width = cols // n

    def trade(x, axis, hop, size):
        return lax.ppermute(x, axis, [(i, i ^ hop) for i in range(size)])

    copies = n * (3 + cross // width) + 2
    *packed, audio = call(
        functools.partial(pack_kernel, hops, width),
        [shape(3 * rows + cross // width * rows_audio, width)] * n + [shape(2 * rows_audio, cross)],
        (q_self, k_self, v_self, q_v2a, k_a2v, v_a2v),
        [HBM] * 6,
        scratch=[pltpu.SemaphoreType.DMA((copies,))],
    )
    blocks = packed[:1] + [trade(x, "seq", hop, n) for x, hop in zip(packed[1:], hops[1:])]
    audios = [audio] + [trade(audio, "seq", hop, n) for hop in hops[1:]]

    late = (k_v2a, v_v2a, q_a2v, wo_self, wo_a2v, wo_v2a, video_in, audio_in)
    steps = (video_steps.reshape(1, rows), audio_steps.reshape(1, rows_audio))
    gain, audio_gain, k_own, v_own, q_own, ws, wa, wv, video_own, audio_own = call(
        fetch_kernel,
        [shape(rows, 2 * video_gates.shape[2]), shape(*audio_in.shape, F32)]
        + [shape(*x.shape) for x in late],
        (audio_len, video_gates.reshape(NT, -1), *steps, audio_gates, *late),
        [SMEM, VMEM] + [HBM] * (3 + len(late)),
        scratch=[pltpu.VMEM(x.shape, x.dtype) for x in (*steps, audio_gates)]
        + [pltpu.SemaphoreType.DMA((3 + len(late),))],
    )
    back = rows + cross // 128 * rows_audio + rows_audio
    result = call(
        functools.partial(attend_kernel, n, DHC),
        [shape(back, width)] * (n - 1)
        + [shape(rows, width), shape(rows_audio, cross, F32), shape(rows_audio, 128, F32)],
        (k_own, v_own, *blocks),
        flops=4 * n * n * rows * rows * width,
        scratch=[pltpu.VMEM((n * rows, width), BF16)] * 2 + [pltpu.VMEM((n * rows_audio, cross), BF16)],
    )
    sends, (own, own_v2a, own_lse) = result[: n - 1], result[n - 1 :]
    got = [trade(x, "seq", hop, n) for x, hop in zip(sends, hops[1:])]
    (a2v_att,) = call(
        functools.partial(attend_audio_kernel, hops, DHC),
        [shape(rows, cross)],
        (audio_len, q_own, *audios),
        [SMEM] + [VMEM] * (n + 1),
        flops=8 * n * rows * rows_audio * cross,
        scratch=[pltpu.VMEM((n * rows_audio, cross), BF16)] * 2,
    )

    half = video_in.shape[1] // 2
    flops = 2 * rows * (cols + cross) * half
    self_att, first = call(
        functools.partial(first_kernel, hops),
        [shape(rows, cols), shape(rows, half)],
        (own, a2v_att, ws, wa, gain, *got),
        flops=flops,
    )
    first = trade(first, "sub", 1, 2)
    second, v2a_att = call(
        functools.partial(second_kernel, DHC),
        [shape(rows + rows_audio, half), shape(rows_audio, cross)],
        (self_att, a2v_att, ws, wa, wv, gain, own_v2a, own_lse, *got),
        flops=flops,
    )
    second = trade(second, "sub", 1, 2)
    near, own_sum = call(
        near_kernel,
        [shape(2 * rows + rows_audio, half), shape(2 * rows + rows_audio, half, F32)],
        (self_att, a2v_att, v2a_att, ws, wa, wv, gain),
        flops=4 * flops,
    )
    (low,) = call(
        functools.partial(far_kernel, 0),
        [shape(rows, half)],
        (self_att, a2v_att, ws, wa, gain, first),
        flops=flops,
    )
    low = trade(low, "mp", 1, 2)
    (high,) = call(
        functools.partial(far_kernel, 1),
        [shape(rows + rows_audio, half)],
        (self_att, a2v_att, ws, wa, gain, second, v2a_att, wv),
        flops=flops,
    )
    high = trade(high, "mp", 1, 2)
    near = trade(near, "sub", 1, 2)
    return call(
        finish_kernel,
        [shape(*video_in.shape), shape(*audio_in.shape)],
        (video_own, audio_own, audio_gain, own_sum, near, low, high),
    )


def on_device(n, mp, sub, *arrays):
    cols, cross = arrays[2].shape[1], arrays[5].shape[1]
    width = cols // n
    fits = (
        n in (2, 4, 8)
        and (mp, sub) == (2, 2)
        and width % DHV == 0
        and cross % width == 0
        and cross // DHC <= 32
        and arrays[0].shape[1] == 2 * arrays[1].shape[1]
    )
    if fits:
        return on_device_heads(*arrays, n=n)
    return on_device_gather(*arrays)


def order_of(n):
    return list(range(n // 2, n)) + list(range(n // 2 - 1, 0, -1))


def solution(mesh):
    in_specs = (
        P(("groups", "seq"), ("mp", "sub")),
        P(("groups", "seq"), ("mp", "sub")),
        P(("groups", "seq"), ("mp", "sub")),
        P(("groups", "seq"), ("mp", "sub")),
        P(("groups", "seq"), ("mp", "sub")),
        P(("groups", "seq"), ("mp", "sub")),
        P(("groups", "seq"), ("mp", "sub")),
        P(("groups", "seq"), ("mp", "sub")),
        P(("groups", "seq"), ("mp", "sub")),
        P(("groups", "seq"), ("mp", "sub")),
        P(("groups", "seq"), ("mp", "sub")),
        P(("mp", "sub"), None),
        P(("mp", "sub"), None),
        P(("mp", "sub"), None),
        P(),
        P(),
        P(("groups", "seq")),
        P(("groups", "seq")),
        P("groups"),
    )
    out_specs = (P(("groups", "seq"), ("mp", "sub")), P(("groups", "seq"), ("mp", "sub")))
    return jax.shard_map(
        functools.partial(on_device, *(mesh.shape[a] for a in ("seq", "mp", "sub"))), mesh=mesh, in_specs=in_specs, out_specs=out_specs, check_vma=False
    )
```

```python
import functools
import math

import jax
import jax.numpy as jnp
from jax import lax
from jax.experimental import pallas as pl
from jax.experimental.pallas import tpu as pltpu
from jax.sharding import PartitionSpec as P


DHV = 128
DHC = 64
NT = 16


def start_state(rows, heads, width):
    return (
        jnp.full((rows, heads), -1e30, jnp.float32),
        jnp.zeros((rows, heads), jnp.float32),
        jnp.zeros((rows, heads, width), jnp.float32),
    )


def update_block(state, queries, keys, values, heads, width, allowed):
    rows = queries.shape[0]
    count = keys.shape[0]
    q_heads = queries.reshape(rows, heads, width)
    k_heads = keys.reshape(count, heads, width)
    v_heads = values.reshape(count, heads, width)
    scores = jnp.einsum(
        "qhd,khd->qhk", q_heads, k_heads, preferred_element_type=jnp.float32
    ) / math.sqrt(width)
    if allowed is not None:
        scores = jnp.where(allowed[None, None, :], scores, -jnp.inf)
    peak_old, total_old, summed_old = state
    peak = jnp.maximum(peak_old, jnp.max(scores, axis=2))
    weights = jnp.exp(scores - peak[:, :, None])
    factor = jnp.exp(peak_old - peak)
    total = total_old * factor + jnp.sum(weights, axis=2)
    summed = summed_old * factor[:, :, None] + jnp.einsum(
        "qhk,khd->qhd", weights.astype(jnp.bfloat16), v_heads, preferred_element_type=jnp.float32
    )
    return (peak, total, summed)


def update_state(state, queries, keys, values, heads, width, start, limit):
    count = keys.shape[0]
    block = 1024 if count > 1024 and count % 1024 == 0 else count
    if block == count:
        allowed = None
        if limit is not None:
            allowed = jnp.arange(count, dtype=jnp.int32) < limit
        return update_block(state, queries, keys, values, heads, width, allowed)
    steps = count // block
    key_blocks = keys.reshape(steps, block, keys.shape[1])
    value_blocks = values.reshape(steps, block, values.shape[1])
    offsets = jnp.arange(steps, dtype=jnp.int32) * block

    def one_block(carry, items):
        key_rows, value_rows, offset = items
        allowed = None
        if limit is not None:
            allowed = start + offset + jnp.arange(block, dtype=jnp.int32) < limit
        return (update_block(carry, queries, key_rows, value_rows, heads, width, allowed), None)

    result, _ = lax.scan(one_block, state, (key_blocks, value_blocks, offsets))
    return result


def finish(state, heads, width):
    _, total, summed = state
    rows = summed.shape[0]
    return (summed / total[:, :, None]).reshape(rows, heads * width).astype(jnp.bfloat16)


def on_device_gather(
    video_in,
    audio_in,
    q_self,
    k_self,
    v_self,
    q_a2v,
    k_a2v,
    v_a2v,
    q_v2a,
    k_v2a,
    v_v2a,
    wo_self,
    wo_a2v,
    wo_v2a,
    video_gates,
    audio_gates,
    video_steps,
    audio_steps,
    audio_len,
):
    heads_self = q_self.shape[1] // DHV
    heads_cross = q_a2v.shape[1] // DHC
    rows_video = q_self.shape[0]
    rows_audio = q_v2a.shape[0]
    limit = audio_len[0]
    piece = (
        lax.all_gather(k_a2v, "seq", axis=0, tiled=True),
        lax.all_gather(v_a2v, "seq", axis=0, tiled=True),
    )
    a2v_state = update_state(
        start_state(rows_video, heads_cross, DHC),
        q_a2v,
        piece[0],
        piece[1],
        heads_cross,
        DHC,
        jnp.int32(0),
        limit,
    )
    a2v_att = finish(a2v_state, heads_cross, DHC)
    piece = (
        lax.all_gather(k_self, "seq", axis=0, tiled=True),
        lax.all_gather(v_self, "seq", axis=0, tiled=True),
    )
    self_state = update_state(
        start_state(rows_video, heads_self, DHV),
        q_self,
        piece[0],
        piece[1],
        heads_self,
        DHV,
        jnp.int32(0),
        None,
    )
    piece = (
        lax.all_gather(k_v2a, "seq", axis=0, tiled=True),
        lax.all_gather(v_v2a, "seq", axis=0, tiled=True),
    )
    v2a_state = update_state(
        start_state(rows_audio, heads_cross, DHC),
        q_v2a,
        piece[0],
        piece[1],
        heads_cross,
        DHC,
        jnp.int32(0),
        None,
    )
    self_att = finish(self_state, heads_self, DHV)
    v2a_att = finish(v2a_state, heads_cross, DHC)
    levels = jnp.arange(NT, dtype=jnp.int32)
    video_hot = (video_steps[:, None] == levels[None, :]).astype(jnp.bfloat16)
    video_gain = jnp.dot(video_hot, video_gates.reshape(NT, -1), preferred_element_type=jnp.float32)
    width_video = video_gates.shape[2]
    video_term = video_gain[:, :width_video] * jnp.dot(
        self_att, wo_self, preferred_element_type=jnp.float32
    )
    video_term = video_term + video_gain[:, width_video:] * jnp.dot(
        a2v_att, wo_a2v, preferred_element_type=jnp.float32
    )
    audio_hot = (audio_steps[:, None] == levels[None, :]).astype(jnp.bfloat16)
    audio_gain = jnp.dot(audio_hot, audio_gates, preferred_element_type=jnp.float32)
    positions = lax.axis_index("seq") * rows_audio + jnp.arange(rows_audio, dtype=jnp.int32)
    present = (positions < limit).astype(jnp.float32)
    audio_term = (
        present[:, None] * audio_gain * jnp.dot(v2a_att, wo_v2a, preferred_element_type=jnp.float32)
    )
    video_sum, audio_sum = (
        lax.psum_scatter(
            video_term.astype(jnp.bfloat16), ("mp", "sub"), scatter_dimension=1, tiled=True
        ).astype(jnp.float32),
        lax.psum_scatter(
            audio_term.astype(jnp.bfloat16), ("mp", "sub"), scatter_dimension=1, tiled=True
        ).astype(jnp.float32),
    )
    video_out = (video_in.astype(jnp.float32) + video_sum).astype(jnp.bfloat16)
    audio_out = (audio_in.astype(jnp.float32) + audio_sum).astype(jnp.bfloat16)
    return (video_out, audio_out)


LOG2E = 1.4426950408889634
VMEM = pl.BlockSpec(memory_space=pltpu.VMEM)
SMEM = pl.BlockSpec(memory_space=pltpu.SMEM)
HBM = pl.BlockSpec(memory_space=pltpu.HBM)
BF16, F32 = jnp.bfloat16, jnp.float32
LSE_ROWS = 16


def call(kernel, outs, operands, specs=None, flops=0, scratch=(), limit=8 * 2**20):
    size = sum(math.prod(x.shape) * x.dtype.itemsize for x in (*operands, *outs))
    if specs:
        operands = [
            pltpu.with_memory_space_constraint(x, pltpu.HBM) if spec is HBM else x for x, spec in zip(operands, specs)
        ]
    return pl.pallas_call(
        kernel,
        out_shape=tuple(outs),
        in_specs=specs or [VMEM] * len(operands),
        out_specs=tuple(VMEM for _ in outs),
        scratch_shapes=list(scratch),
        compiler_params=pltpu.CompilerParams(vmem_limit_bytes=limit),
        cost_estimate=pl.CostEstimate(flops=flops, bytes_accessed=size, transcendentals=0),
    )(*operands)


def shape(rows, cols, kind=BF16):
    return jax.ShapeDtypeStruct((rows, cols), kind)


def dot_t(a, b):
    return lax.dot_general(a, b, (((1,), (1,)), ((), ())), preferred_element_type=F32)


def dot(a, b):
    return jnp.dot(a, b, preferred_element_type=F32)


def index_of(axis):
    return lax.axis_index(axis).astype(jnp.int32)


def columns(index, width):
    return pl.ds(pl.multiple_of(index * width, width), width)


def copy_all(pairs, sems):
    copies = [pltpu.make_async_copy(src, dst, sems.at[i]) for i, (src, dst) in enumerate(pairs)]
    for copy in copies:
        copy.start()
    for copy in copies:
        copy.wait()


def pack_kernel(hops, width, q_ref, k_ref, v_ref, qa_ref, ka_ref, va_ref, *rest):
    outs, audio, sems = rest[: len(hops)], rest[-2], rest[-1]
    rows = q_ref.shape[0]
    rows_audio, cols_audio = qa_ref.shape
    me = index_of("seq")
    pairs = []
    for hop, out in zip(hops, outs):
        for i, ref in enumerate((q_ref, k_ref, v_ref)):
            pairs.append((ref.at[:, columns(me ^ hop, width)], out.at[pl.ds(i * rows, rows), :]))
        for i in range(cols_audio // width):
            at = pl.ds(3 * rows + i * rows_audio, rows_audio)
            pairs.append((qa_ref.at[:, pl.ds(i * width, width)], out.at[at, :]))
    pairs.append((ka_ref, audio.at[pl.ds(0, rows_audio), :]))
    pairs.append((va_ref, audio.at[pl.ds(rows_audio, rows_audio), :]))
    copy_all(pairs, sems)


def one_hot_t(steps_ref):
    levels = lax.broadcasted_iota(jnp.int32, (NT, steps_ref.shape[1]), 0)
    return (levels == steps_ref[...]).astype(BF16)


def pick(hot_t, table):
    return lax.dot_general(hot_t, table, (((0,), (0,)), ((), ())), preferred_element_type=F32)


def fetch_kernel(limit_ref, vg_ref, *rest):
    count = (len(rest) - 9) // 2
    loads, gain_ref, audio_ref = rest[: count + 3], rest[count + 3], rest[count + 4]
    fetched, (vs_ref, as_ref, ag_ref, sems) = rest[count + 5 : -4], rest[-4:]
    copies = [
        pltpu.make_async_copy(src, dst, sems.at[i])
        for i, (src, dst) in enumerate(zip(loads, (vs_ref, as_ref, ag_ref, *fetched)))
    ]
    for copy in copies:
        copy.start()
    for copy in copies[:3]:
        copy.wait()
    hot_t = one_hot_t(vs_ref)
    piece = min(vg_ref.shape[1], 2048)
    for at in range(0, vg_ref.shape[1], piece):
        gain_ref[:, at : at + piece] = pick(hot_t, vg_ref[:, at : at + piece]).astype(BF16)
    rows_audio, narrow = audio_ref.shape
    part = index_of("mp") * 2 + index_of("sub")
    gain = pick(one_hot_t(as_ref), ag_ref[:, columns(part, narrow)])
    at = index_of("seq") * rows_audio + lax.broadcasted_iota(jnp.int32, (rows_audio, 1), 0)
    audio_ref[...] = jnp.where(at < limit_ref[0], gain, 0.0)
    for copy in copies[3:]:
        copy.wait()


def softmax_t(scores, scale, allowed=None):
    if allowed is not None:
        scores = [jnp.where(ok, x, -jnp.inf) for ok, x in zip(allowed, scores)]
    peak = functools.reduce(jnp.maximum, [jnp.max(x, axis=0, keepdims=True) for x in scores])
    weights = [jnp.exp2((x - peak) * (scale * LOG2E)) for x in scores]
    total = functools.reduce(jnp.add, [jnp.sum(x, axis=0, keepdims=True) for x in weights])
    return peak, [x.astype(BF16) for x in weights], total


def turn(x):
    return x.astype(F32).T.astype(BF16)


def pair_rows(x, head):
    lane = lax.broadcasted_iota(jnp.int32, (1, 128), 1) // head
    return jnp.concatenate([jnp.where(lane == i, x, 0).astype(BF16) for i in range(128 // head)], axis=0)


def pair_columns(x, head):
    pair = 128 // head
    rows = x.shape[1] // pair
    return jnp.concatenate([x[i * head : (i + 1) * head, i * rows : (i + 1) * rows] for i in range(pair)], axis=0)


def attend_kernel(n, head, kv_ref, vv_ref, *rest):
    blocks, sends, (own_ref, own_v2a_ref, own_lse_ref) = rest[:n], rest[n : 2 * n - 1], rest[2 * n - 1 : 2 * n + 2]
    vt_ref, vvt_ref, s_ref, p_ref = rest[2 * n + 2 :]
    rows, cols = kv_ref.shape
    width = blocks[0].shape[1]
    rows_audio = own_v2a_ref.shape[0]
    for h in range(width // DHV):
        cut = slice(h * DHV, (h + 1) * DHV)
        for i, ref in enumerate(blocks):
            vt_ref[cut, i * rows : (i + 1) * rows] = turn(ref[2 * rows : 3 * rows, cut])
    for block in range(cols // 128):
        cut = slice(block * 128, (block + 1) * 128)
        vvt_ref[cut, :] = turn(vv_ref[:, cut])
    pair, row = 128 // head, 0
    parts = []
    for block in range(cols // 128):
        cut = slice(block * 128, (block + 1) * 128)
        top, part = 3 * rows + (block * 128 // width) * rows_audio, slice(block * 128 % width, block * 128 % width + 128)
        q = pair_rows(jnp.concatenate([ref[top : top + rows_audio, part] for ref in blocks], axis=0), head)
        scores = dot_t(kv_ref[:, cut], q)
        for i in range(pair):
            at = slice(i * n * rows_audio, (i + 1) * n * rows_audio)
            s_ref[row + i * rows : row + (i + 1) * rows, :] = scores[:, at]
            parts.append((row + i * rows, rows, jnp.max(scores[:, at], axis=0, keepdims=True), 1.0 / math.sqrt(head)))
        row += pair * rows
    for ref in blocks:
        for h in range(width // DHV):
            cut = slice(h * DHV, (h + 1) * DHV)
            peak = None
            for i, other in enumerate(blocks):
                scores = dot_t(other[rows : 2 * rows, cut], ref[0:rows, cut])
                s_ref[row + i * rows : row + (i + 1) * rows, :] = scores
                top = jnp.max(scores, axis=0, keepdims=True)
                peak = top if i == 0 else jnp.maximum(peak, top)
            parts.append((row, n * rows, peak, 1.0 / math.sqrt(DHV)))
            row += n * rows

    def weigh(part):
        start, count, peak, scale = part
        total = None
        for at in range(start, start + count, 128):
            p = jnp.exp2((s_ref[at : at + 128, :] - peak) * (scale * LOG2E))
            p_ref[at : at + 128, :] = p.astype(BF16)
            summed = jnp.sum(p, axis=0, keepdims=True)
            total = summed if at == start else total + summed
        return total

    lses, at = [], 0
    for block in range(cols // 128):
        both = []
        for i in range(pair):
            start, count, peak, scale = parts[at]
            total = weigh(parts[at])
            lses.append(peak * (scale * LOG2E) + jnp.log2(total))
            column = block * 128 + i * head
            o = dot(vvt_ref[column : column + head, :], p_ref[start : start + count, :])
            both.append(o * (1.0 / total))
            at += 1
        v2a = jnp.concatenate(both, axis=0).T
        own_v2a_ref[:, block * 128 : (block + 1) * 128] = v2a[0:rows_audio]
        for j, dst in enumerate(sends):
            top = rows + block * rows_audio
            dst[top : top + rows_audio, 0:128] = v2a[(j + 1) * rows_audio : (j + 2) * rows_audio].astype(BF16)
    for j in range(n):
        for h in range(width // DHV):
            cut = slice(h * DHV, (h + 1) * DHV)
            start, count, _, _ = parts[at]
            total = weigh(parts[at])
            o = dot(vt_ref[cut, :], p_ref[start : start + count, :]) * (1.0 / total)
            dst = own_ref if j == 0 else sends[j - 1].at[0:rows, :]
            dst[:, cut] = o.T.astype(BF16)
            at += 1
    heads = len(lses)
    lse = jnp.concatenate(lses, axis=0)
    own_lse_ref[...] = lse
    pieces, left = [], lse
    for _ in range(3):
        pieces.append(left.astype(BF16).astype(F32))
        left = left - pieces[-1]
    packed = jnp.concatenate(pieces + [jnp.zeros((LSE_ROWS - 3 * heads, lse.shape[1]), F32)], axis=0)
    for j, dst in enumerate(sends):
        top = rows + cols // 128 * rows_audio
        dst[top : top + LSE_ROWS, 0:128] = pltpu.roll(packed, 128 - (j + 1) * rows_audio, 1).astype(BF16)


def attend_audio_kernel(hops, head, limit_ref, q_ref, *rest):
    n = len(hops)
    blocks, out_ref = rest[:n], rest[n]
    rows_audio = blocks[0].shape[0] // 2
    me, row = index_of("seq"), lax.broadcasted_iota(jnp.int32, (rows_audio, 1), 0)
    allowed = [(me ^ hop) * rows_audio + row < limit_ref[0] for hop in hops]
    scale = 1.0 / math.sqrt(head)
    for block in range(q_ref.shape[1] // 128):
        cut = slice(block * 128, (block + 1) * 128)
        q = pair_rows(q_ref[:, cut], head)
        _, p, total = softmax_t([dot_t(ref[0:rows_audio, cut], q) for ref in blocks], scale, allowed)
        vt = turn(jnp.concatenate([ref[rows_audio : 2 * rows_audio, cut] for ref in blocks], axis=0))
        o = dot(vt, jnp.concatenate(p, axis=0)) * (1.0 / total)
        out_ref[:, cut] = pair_columns(o, head).T.astype(BF16)


def merge_audio(head, top, v2a_ref, lse_ref, got, out_ref):
    rows_audio, cols = v2a_ref.shape
    heads = cols // head
    lses = [lse_ref[...]]
    for ref in got:
        at = top + cols // 128 * rows_audio
        packed = ref[at : at + LSE_ROWS, 0:128].astype(F32)
        lses.append(packed[0:heads] + packed[heads : 2 * heads] + packed[2 * heads : 3 * heads])
    peak = functools.reduce(jnp.maximum, lses)
    parts = [jnp.exp2(x - peak) for x in lses]
    total = functools.reduce(jnp.add, parts)
    inverse = 1.0 / total
    parts = [x * inverse for x in parts]
    parts.append(jnp.zeros((128 - len(parts) * heads, 128), F32))
    shares = jnp.concatenate(parts, axis=0).T[0:rows_audio]
    pair = 128 // head
    lane = lax.broadcasted_iota(jnp.int32, (1, 128), 1) // head
    for block in range(cols // 128):
        cut = slice(block * 128, (block + 1) * 128)
        at = top + block * rows_audio
        summed = jnp.zeros((rows_audio, 128), F32)
        for j in range(len(lses)):
            o = v2a_ref[:, cut] if j == 0 else got[j - 1][at : at + rows_audio, 0:128].astype(F32)
            share = jnp.zeros((rows_audio, 128), F32)
            for i in range(pair):
                column = j * heads + block * pair + i
                share = jnp.where(lane == i, shares[:, column : column + 1], share)
            summed = summed + share * o
        out_ref[:, cut] = summed.astype(BF16)


def block_of(far, other):
    mp, sub = index_of("mp"), index_of("sub")
    return (1 - mp if far else mp) * 2 + (1 - sub if other else sub)


def project(block, half, heads, weights, gain_ref):
    (att_ref, a2v_ref), (ws_ref, wa_ref) = heads, weights
    wide = ws_ref.shape[1]
    cut = wide // 8
    at = columns(block * 2 + half, cut)
    term = gain_ref[:, at].astype(F32) * dot(att_ref[...], ws_ref[:, at])
    gain = gain_ref[:, columns(block * 2 + half + 8, cut)].astype(F32)
    return term + gain * dot(a2v_ref[...], wa_ref[:, at])


def project_audio(block, v2a_ref, wv_ref):
    return dot(v2a_ref[...], wv_ref[:, columns(block, wv_ref.shape[1] // 4)])


def first_kernel(hops, own_ref, a2v_ref, ws_ref, wa_ref, gain_ref, *rest):
    got, (self_ref, out_ref) = rest[: len(hops) - 1], rest[len(hops) - 1 :]
    rows, width = own_ref.shape
    me = index_of("seq")
    self_ref[:, columns(me, width)] = own_ref[...]
    for hop, ref in zip(hops[1:], got):
        self_ref[:, columns(me ^ hop, width)] = ref[0:rows, :]
    out_ref[...] = project(block_of(True, True), 0, (self_ref, a2v_ref), (ws_ref, wa_ref), gain_ref).astype(BF16)


def second_kernel(head, self_ref, a2v_ref, ws_ref, wa_ref, wv_ref, gain_ref, v2a_ref, lse_ref, *rest):
    got, (out_ref, audio_ref, low_ref) = rest[:-3], rest[-3:]
    rows = self_ref.shape[0]
    block = block_of(True, True)
    out_ref[0:rows, :] = project(block, 1, (self_ref, a2v_ref), (ws_ref, wa_ref), gain_ref).astype(BF16)
    merge_audio(head, rows, v2a_ref, lse_ref, got, audio_ref)
    out_ref[rows:, :] = project_audio(block, audio_ref, wv_ref).astype(BF16)
    low_ref[...] = project(block_of(True, False), 0, (self_ref, a2v_ref), (ws_ref, wa_ref), gain_ref)


def far_low_kernel(low_ref, extra_ref, out_ref):
    out_ref[...] = (low_ref[...] + extra_ref[...].astype(F32)).astype(BF16)


def near_kernel(self_ref, a2v_ref, audio_ref, ws_ref, wa_ref, wv_ref, gain_ref, send_ref, own_ref):
    rows = self_ref.shape[0]
    for out, other in ((send_ref, True), (own_ref, False)):
        block = block_of(False, other)
        for half in range(2):
            term = project(block, half, (self_ref, a2v_ref), (ws_ref, wa_ref), gain_ref)
            out[half * rows : (half + 1) * rows, :] = term.astype(out.dtype)
        out[2 * rows :, :] = project_audio(block, audio_ref, wv_ref).astype(out.dtype)


def far_high_kernel(self_ref, a2v_ref, ws_ref, wa_ref, gain_ref, extra_ref, audio_ref, wv_ref, out_ref):
    rows = self_ref.shape[0]
    block = block_of(True, False)
    term = project(block, 1, (self_ref, a2v_ref), (ws_ref, wa_ref), gain_ref)
    out_ref[0:rows, :] = (term + extra_ref[0:rows, :].astype(F32)).astype(BF16)
    term = project_audio(block, audio_ref, wv_ref)
    out_ref[rows:, :] = (term + extra_ref[rows:, :].astype(F32)).astype(BF16)


def finish_kernel(video_ref, audio_ref, gain_ref, own_ref, core_ref, low_ref, high_ref, video_out, audio_out):
    rows = video_ref.shape[0]
    cut = video_ref.shape[1] // 2
    near = own_ref[...] + core_ref[...].astype(F32)
    for half, ref in enumerate((low_ref, high_ref)):
        at = slice(half * cut, (half + 1) * cut)
        term = near[half * rows : (half + 1) * rows] + ref[0:rows, :].astype(F32)
        video_out[:, at] = (video_ref[:, at].astype(F32) + term).astype(BF16)
    term = near[2 * rows :] + high_ref[rows:, :].astype(F32)
    audio_out[...] = (audio_ref[...].astype(F32) + gain_ref[...] * term).astype(BF16)


def on_device_heads(
    video_in,
    audio_in,
    q_self,
    k_self,
    v_self,
    q_a2v,
    k_a2v,
    v_a2v,
    q_v2a,
    k_v2a,
    v_v2a,
    wo_self,
    wo_a2v,
    wo_v2a,
    video_gates,
    audio_gates,
    video_steps,
    audio_steps,
    audio_len,
    *,
    n,
):
    hops = [0] + order_of(n)
    rows, cols = q_self.shape
    rows_audio, cross = q_v2a.shape
    width = cols // n

    def trade(x, axis, hop, size):
        return lax.ppermute(x, axis, [(i, i ^ hop) for i in range(size)])

    copies = n * (3 + cross // width) + 2
    *packed, audio = call(
        functools.partial(pack_kernel, hops, width),
        [shape(3 * rows + cross // width * rows_audio, width)] * n + [shape(2 * rows_audio, cross)],
        (q_self, k_self, v_self, q_v2a, k_a2v, v_a2v),
        [HBM] * 6,
        scratch=[pltpu.SemaphoreType.DMA((copies,))],
    )
    blocks = packed[:1] + [trade(x, "seq", hop, n) for x, hop in zip(packed[1:], hops[1:])]
    audios = [audio] + [trade(audio, "seq", hop, n) for hop in hops[1:]]

    late = (k_v2a, v_v2a, q_a2v, wo_self, wo_a2v, wo_v2a, video_in, audio_in)
    steps = (video_steps.reshape(1, rows), audio_steps.reshape(1, rows_audio))
    gain, audio_gain, k_own, v_own, q_own, ws, wa, wv, video_own, audio_own = call(
        fetch_kernel,
        [shape(rows, 2 * video_gates.shape[2]), shape(*audio_in.shape, F32)]
        + [shape(*x.shape) for x in late],
        (audio_len, video_gates.reshape(NT, -1), *steps, audio_gates, *late),
        [SMEM, VMEM] + [HBM] * (3 + len(late)),
        scratch=[pltpu.VMEM(x.shape, x.dtype) for x in (*steps, audio_gates)]
        + [pltpu.SemaphoreType.DMA((3 + len(late),))],
    )
    back = rows + cross // 128 * rows_audio + LSE_ROWS
    result = call(
        functools.partial(attend_kernel, n, DHC),
        [shape(back, width)] * (n - 1)
        + [shape(rows, width), shape(rows_audio, cross, F32), shape(cross // DHC, 128, F32)],
        (k_own, v_own, *blocks),
        flops=4 * n * n * rows * rows * width,
        scratch=[pltpu.VMEM((width, n * rows), BF16), pltpu.VMEM((cross, rows), BF16)]
        + [pltpu.VMEM((n * n * rows * width // DHV + cross // DHC * rows, 128), kind) for kind in (F32, BF16)],
    )
    sends, (own, own_v2a, own_lse) = result[: n - 1], result[n - 1 :]
    got = [trade(x, "seq", hop, n) for x, hop in zip(sends, hops[1:])]
    (a2v_att,) = call(
        functools.partial(attend_audio_kernel, hops, DHC),
        [shape(rows, cross)],
        (audio_len, q_own, *audios),
        [SMEM] + [VMEM] * (n + 1),
        flops=8 * n * rows * rows_audio * cross,
    )

    half = video_in.shape[1] // 2
    flops = 2 * rows * (cols + cross) * half
    self_att, first = call(
        functools.partial(first_kernel, hops),
        [shape(rows, cols), shape(rows, half)],
        (own, a2v_att, ws, wa, gain, *got),
        flops=flops,
    )
    first = trade(first, "sub", 1, 2)
    second, v2a_att, own_low = call(
        functools.partial(second_kernel, DHC),
        [shape(rows + rows_audio, half), shape(rows_audio, cross), shape(rows, half, F32)],
        (self_att, a2v_att, ws, wa, wv, gain, own_v2a, own_lse, *got),
        flops=2 * flops,
    )
    second = trade(second, "sub", 1, 2)
    (low,) = call(far_low_kernel, [shape(rows, half)], (own_low, first))
    low = trade(low, "mp", 1, 2)
    (high,) = call(
        far_high_kernel,
        [shape(rows + rows_audio, half)],
        (self_att, a2v_att, ws, wa, gain, second, v2a_att, wv),
        flops=flops,
    )
    high = trade(high, "mp", 1, 2)
    near, own_sum = call(
        near_kernel,
        [shape(2 * rows + rows_audio, half), shape(2 * rows + rows_audio, half, F32)],
        (self_att, a2v_att, v2a_att, ws, wa, wv, gain),
        flops=4 * flops,
    )
    near = trade(near, "sub", 1, 2)
    return call(
        finish_kernel,
        [shape(*video_in.shape), shape(*audio_in.shape)],
        (video_own, audio_own, audio_gain, own_sum, near, low, high),
    )


def on_device(n, mp, sub, *arrays):
    cols, cross = arrays[2].shape[1], arrays[5].shape[1]
    width = cols // n
    fits = (
        n in (2, 4, 8)
        and (mp, sub) == (2, 2)
        and width % DHV == 0
        and cross % width == 0
        and 3 * (cross // DHC) <= LSE_ROWS
        and n * arrays[8].shape[0] == arrays[2].shape[0] == 128
        and arrays[0].shape[1] == 2 * arrays[1].shape[1]
    )
    if fits:
        return on_device_heads(*arrays, n=n)
    return on_device_gather(*arrays)


def order_of(n):
    return list(range(n // 2, n)) + list(range(n // 2 - 1, 0, -1))


def solution(mesh):
    in_specs = (
        P(("groups", "seq"), ("mp", "sub")),
        P(("groups", "seq"), ("mp", "sub")),
        P(("groups", "seq"), ("mp", "sub")),
        P(("groups", "seq"), ("mp", "sub")),
        P(("groups", "seq"), ("mp", "sub")),
        P(("groups", "seq"), ("mp", "sub")),
        P(("groups", "seq"), ("mp", "sub")),
        P(("groups", "seq"), ("mp", "sub")),
        P(("groups", "seq"), ("mp", "sub")),
        P(("groups", "seq"), ("mp", "sub")),
        P(("groups", "seq"), ("mp", "sub")),
        P(("mp", "sub"), None),
        P(("mp", "sub"), None),
        P(("mp", "sub"), None),
        P(),
        P(),
        P(("groups", "seq")),
        P(("groups", "seq")),
        P("groups"),
    )
    out_specs = (P(("groups", "seq"), ("mp", "sub")), P(("groups", "seq"), ("mp", "sub")))
    return jax.shard_map(
        functools.partial(on_device, *(mesh.shape[a] for a in ("seq", "mp", "sub"))), mesh=mesh, in_specs=in_specs, out_specs=out_specs, check_vma=False
    )
```

```python
import functools
import math

import jax
import jax.numpy as jnp
from jax import lax
from jax.experimental import pallas as pl
from jax.experimental.pallas import tpu as pltpu
from jax.sharding import PartitionSpec as P


DHV = 128
DHC = 64
NT = 16


def start_state(rows, heads, width):
    return (
        jnp.full((rows, heads), -1e30, jnp.float32),
        jnp.zeros((rows, heads), jnp.float32),
        jnp.zeros((rows, heads, width), jnp.float32),
    )


def update_block(state, queries, keys, values, heads, width, allowed):
    rows = queries.shape[0]
    count = keys.shape[0]
    q_heads = queries.reshape(rows, heads, width)
    k_heads = keys.reshape(count, heads, width)
    v_heads = values.reshape(count, heads, width)
    scores = jnp.einsum(
        "qhd,khd->qhk", q_heads, k_heads, preferred_element_type=jnp.float32
    ) / math.sqrt(width)
    if allowed is not None:
        scores = jnp.where(allowed[None, None, :], scores, -jnp.inf)
    peak_old, total_old, summed_old = state
    peak = jnp.maximum(peak_old, jnp.max(scores, axis=2))
    weights = jnp.exp(scores - peak[:, :, None])
    factor = jnp.exp(peak_old - peak)
    total = total_old * factor + jnp.sum(weights, axis=2)
    summed = summed_old * factor[:, :, None] + jnp.einsum(
        "qhk,khd->qhd", weights.astype(jnp.bfloat16), v_heads, preferred_element_type=jnp.float32
    )
    return (peak, total, summed)


def update_state(state, queries, keys, values, heads, width, start, limit):
    count = keys.shape[0]
    block = 1024 if count > 1024 and count % 1024 == 0 else count
    if block == count:
        allowed = None
        if limit is not None:
            allowed = jnp.arange(count, dtype=jnp.int32) < limit
        return update_block(state, queries, keys, values, heads, width, allowed)
    steps = count // block
    key_blocks = keys.reshape(steps, block, keys.shape[1])
    value_blocks = values.reshape(steps, block, values.shape[1])
    offsets = jnp.arange(steps, dtype=jnp.int32) * block

    def one_block(carry, items):
        key_rows, value_rows, offset = items
        allowed = None
        if limit is not None:
            allowed = start + offset + jnp.arange(block, dtype=jnp.int32) < limit
        return (update_block(carry, queries, key_rows, value_rows, heads, width, allowed), None)

    result, _ = lax.scan(one_block, state, (key_blocks, value_blocks, offsets))
    return result


def finish(state, heads, width):
    _, total, summed = state
    rows = summed.shape[0]
    return (summed / total[:, :, None]).reshape(rows, heads * width).astype(jnp.bfloat16)


def on_device_gather(
    video_in,
    audio_in,
    q_self,
    k_self,
    v_self,
    q_a2v,
    k_a2v,
    v_a2v,
    q_v2a,
    k_v2a,
    v_v2a,
    wo_self,
    wo_a2v,
    wo_v2a,
    video_gates,
    audio_gates,
    video_steps,
    audio_steps,
    audio_len,
):
    heads_self = q_self.shape[1] // DHV
    heads_cross = q_a2v.shape[1] // DHC
    rows_video = q_self.shape[0]
    rows_audio = q_v2a.shape[0]
    limit = audio_len[0]
    piece = (
        lax.all_gather(k_a2v, "seq", axis=0, tiled=True),
        lax.all_gather(v_a2v, "seq", axis=0, tiled=True),
    )
    a2v_state = update_state(
        start_state(rows_video, heads_cross, DHC),
        q_a2v,
        piece[0],
        piece[1],
        heads_cross,
        DHC,
        jnp.int32(0),
        limit,
    )
    a2v_att = finish(a2v_state, heads_cross, DHC)
    piece = (
        lax.all_gather(k_self, "seq", axis=0, tiled=True),
        lax.all_gather(v_self, "seq", axis=0, tiled=True),
    )
    self_state = update_state(
        start_state(rows_video, heads_self, DHV),
        q_self,
        piece[0],
        piece[1],
        heads_self,
        DHV,
        jnp.int32(0),
        None,
    )
    piece = (
        lax.all_gather(k_v2a, "seq", axis=0, tiled=True),
        lax.all_gather(v_v2a, "seq", axis=0, tiled=True),
    )
    v2a_state = update_state(
        start_state(rows_audio, heads_cross, DHC),
        q_v2a,
        piece[0],
        piece[1],
        heads_cross,
        DHC,
        jnp.int32(0),
        None,
    )
    self_att = finish(self_state, heads_self, DHV)
    v2a_att = finish(v2a_state, heads_cross, DHC)
    levels = jnp.arange(NT, dtype=jnp.int32)
    video_hot = (video_steps[:, None] == levels[None, :]).astype(jnp.bfloat16)
    video_gain = jnp.dot(video_hot, video_gates.reshape(NT, -1), preferred_element_type=jnp.float32)
    width_video = video_gates.shape[2]
    video_term = video_gain[:, :width_video] * jnp.dot(
        self_att, wo_self, preferred_element_type=jnp.float32
    )
    video_term = video_term + video_gain[:, width_video:] * jnp.dot(
        a2v_att, wo_a2v, preferred_element_type=jnp.float32
    )
    audio_hot = (audio_steps[:, None] == levels[None, :]).astype(jnp.bfloat16)
    audio_gain = jnp.dot(audio_hot, audio_gates, preferred_element_type=jnp.float32)
    positions = lax.axis_index("seq") * rows_audio + jnp.arange(rows_audio, dtype=jnp.int32)
    present = (positions < limit).astype(jnp.float32)
    audio_term = (
        present[:, None] * audio_gain * jnp.dot(v2a_att, wo_v2a, preferred_element_type=jnp.float32)
    )
    video_sum, audio_sum = (
        lax.psum_scatter(
            video_term.astype(jnp.bfloat16), ("mp", "sub"), scatter_dimension=1, tiled=True
        ).astype(jnp.float32),
        lax.psum_scatter(
            audio_term.astype(jnp.bfloat16), ("mp", "sub"), scatter_dimension=1, tiled=True
        ).astype(jnp.float32),
    )
    video_out = (video_in.astype(jnp.float32) + video_sum).astype(jnp.bfloat16)
    audio_out = (audio_in.astype(jnp.float32) + audio_sum).astype(jnp.bfloat16)
    return (video_out, audio_out)


LOG2E = 1.4426950408889634
VMEM = pl.BlockSpec(memory_space=pltpu.VMEM)
SMEM = pl.BlockSpec(memory_space=pltpu.SMEM)
HBM = pl.BlockSpec(memory_space=pltpu.HBM)
BF16, F32 = jnp.bfloat16, jnp.float32
LSE_ROWS = 16
SEQ, FORWARDED, OUT_ORDER = 4, 3, [2, 3, 1]


def call(kernel, outs, operands, specs=None, flops=0, scratch=(), limit=8 * 2**20):
    size = sum(math.prod(x.shape) * x.dtype.itemsize for x in (*operands, *outs))
    if specs:
        operands = [
            pltpu.with_memory_space_constraint(x, pltpu.HBM) if spec is HBM else x for x, spec in zip(operands, specs)
        ]
    return pl.pallas_call(
        kernel,
        out_shape=tuple(outs),
        in_specs=specs or [VMEM] * len(operands),
        out_specs=tuple(VMEM for _ in outs),
        scratch_shapes=list(scratch),
        compiler_params=pltpu.CompilerParams(vmem_limit_bytes=limit),
        cost_estimate=pl.CostEstimate(flops=flops, bytes_accessed=size, transcendentals=0),
    )(*operands)


def shape(rows, cols, kind=BF16):
    return jax.ShapeDtypeStruct((rows, cols), kind)


def dot_t(a, b):
    return lax.dot_general(a, b, (((1,), (1,)), ((), ())), preferred_element_type=F32)


def dot(a, b):
    return jnp.dot(a, b, preferred_element_type=F32)


def index_of(axis):
    return lax.axis_index(axis).astype(jnp.int32)


def columns(index, width):
    return pl.ds(pl.multiple_of(index * width, width), width)


def copy_all(pairs, sems):
    copies = [pltpu.make_async_copy(src, dst, sems.at[i]) for i, (src, dst) in enumerate(pairs)]
    for copy in copies:
        copy.start()
    for copy in copies:
        copy.wait()


def pack_kernel(hops, width, q_ref, k_ref, v_ref, qa_ref, ka_ref, va_ref, *rest):
    outs, sems = rest[:-1], rest[-1]
    rows = q_ref.shape[0]
    rows_audio, cols_audio = qa_ref.shape
    me = index_of("seq")
    pairs = []
    for hop, out in zip(hops, outs):
        for i, ref in enumerate((q_ref, k_ref, v_ref)):
            pairs.append((ref.at[:, columns(me ^ hop, width)], out.at[pl.ds(i * rows, rows), :]))
        if hop == FORWARDED:
            continue
        at = 3 * rows
        for ref in (qa_ref, ka_ref, va_ref):
            for i in range(cols_audio // width):
                pairs.append((ref.at[:, pl.ds(i * width, width)], out.at[pl.ds(at, rows_audio), :]))
                at += rows_audio
    copy_all(pairs, sems)


def relay_kernel(got_ref, out_ref):
    out_ref[...] = got_ref[got_ref.shape[0] - out_ref.shape[0] :, :]


class Audio:
    def __init__(self, ref, rows, cols):
        self.ref, self.rows, self.blocks = ref, rows, cols // ref.shape[1]
        self.top = ref.shape[0] - 3 * self.blocks * rows

    def block(self, kind, block):
        at, column = divmod(block * 128, self.ref.shape[1])
        top = self.top + (kind * self.blocks + at) * self.rows
        return self.ref[top : top + self.rows, column : column + 128]


def by_hop(blocks, forwarded, rows, cols):
    return [Audio(forwarded if hop == FORWARDED else ref, rows, cols) for hop, ref in blocks]


def one_hot_t(steps_ref):
    levels = lax.broadcasted_iota(jnp.int32, (NT, steps_ref.shape[1]), 0)
    return (levels == steps_ref[...]).astype(BF16)


def pick(hot_t, table):
    return lax.dot_general(hot_t, table, (((0,), (0,)), ((), ())), preferred_element_type=F32)


def fetch_kernel(limit_ref, vg_ref, *rest):
    count = (len(rest) - 9) // 2
    loads, gain_ref, audio_ref = rest[: count + 3], rest[count + 3], rest[count + 4]
    fetched, (vs_ref, as_ref, ag_ref, sems) = rest[count + 5 : -4], rest[-4:]
    copies = [
        pltpu.make_async_copy(src, dst, sems.at[i])
        for i, (src, dst) in enumerate(zip(loads, (vs_ref, as_ref, ag_ref, *fetched)))
    ]
    for copy in copies:
        copy.start()
    for copy in copies[:3]:
        copy.wait()
    hot_t = one_hot_t(vs_ref)
    piece = min(vg_ref.shape[1], 2048)
    for at in range(0, vg_ref.shape[1], piece):
        gain_ref[:, at : at + piece] = pick(hot_t, vg_ref[:, at : at + piece]).astype(BF16)
    rows_audio, narrow = audio_ref.shape
    part = index_of("mp") * 2 + index_of("sub")
    gain = pick(one_hot_t(as_ref), ag_ref[:, columns(part, narrow)])
    at = index_of("seq") * rows_audio + lax.broadcasted_iota(jnp.int32, (rows_audio, 1), 0)
    audio_ref[...] = jnp.where(at < limit_ref[0], gain, 0.0)
    for copy in copies[3:]:
        copy.wait()


def softmax_t(scores, scale, allowed=None):
    if allowed is not None:
        scores = [jnp.where(ok, x, -jnp.inf) for ok, x in zip(allowed, scores)]
    peak = functools.reduce(jnp.maximum, [jnp.max(x, axis=0, keepdims=True) for x in scores])
    weights = [jnp.exp2((x - peak) * (scale * LOG2E)) for x in scores]
    total = functools.reduce(jnp.add, [jnp.sum(x, axis=0, keepdims=True) for x in weights])
    return peak, [x.astype(BF16) for x in weights], total


def turn(x):
    return x.astype(F32).T.astype(BF16)


def pair_rows(x, head):
    lane = lax.broadcasted_iota(jnp.int32, (1, 128), 1) // head
    return jnp.concatenate([jnp.where(lane == i, x, 0).astype(BF16) for i in range(128 // head)], axis=0)


def pair_columns(x, head):
    pair = 128 // head
    rows = x.shape[1] // pair
    return jnp.concatenate([x[i * head : (i + 1) * head, i * rows : (i + 1) * rows] for i in range(pair)], axis=0)


def attend_kernel(hops, head, kv_ref, vv_ref, forwarded, *rest):
    n = len(hops)
    blocks, sends, (own_ref, own_v2a_ref, own_lse_ref) = rest[:n], rest[n : 2 * n - 1], rest[2 * n - 1 : 2 * n + 2]
    vt_ref, vvt_ref, s_ref, p_ref = rest[2 * n + 2 :]
    rows, cols = kv_ref.shape
    width = blocks[0].shape[1]
    rows_audio = own_v2a_ref.shape[0]
    audios = by_hop(zip(hops, blocks), forwarded, rows_audio, cols)
    for h in range(width // DHV):
        cut = slice(h * DHV, (h + 1) * DHV)
        for i, ref in enumerate(blocks):
            vt_ref[cut, i * rows : (i + 1) * rows] = turn(ref[2 * rows : 3 * rows, cut])
    for block in range(cols // 128):
        cut = slice(block * 128, (block + 1) * 128)
        vvt_ref[cut, :] = turn(vv_ref[:, cut])
    pair, row = 128 // head, 0
    parts = []
    for block in range(cols // 128):
        cut = slice(block * 128, (block + 1) * 128)
        q = pair_rows(jnp.concatenate([audio.block(0, block) for audio in audios], axis=0), head)
        scores = dot_t(kv_ref[:, cut], q)
        for i in range(pair):
            at = slice(i * n * rows_audio, (i + 1) * n * rows_audio)
            s_ref[row + i * rows : row + (i + 1) * rows, :] = scores[:, at]
            parts.append((row + i * rows, rows, jnp.max(scores[:, at], axis=0, keepdims=True), 1.0 / math.sqrt(head)))
        row += pair * rows
    for ref in blocks:
        for h in range(width // DHV):
            cut = slice(h * DHV, (h + 1) * DHV)
            peak = None
            for i, other in enumerate(blocks):
                scores = dot_t(other[rows : 2 * rows, cut], ref[0:rows, cut])
                s_ref[row + i * rows : row + (i + 1) * rows, :] = scores
                top = jnp.max(scores, axis=0, keepdims=True)
                peak = top if i == 0 else jnp.maximum(peak, top)
            parts.append((row, n * rows, peak, 1.0 / math.sqrt(DHV)))
            row += n * rows

    def weigh(part):
        start, count, peak, scale = part
        total = None
        for at in range(start, start + count, 128):
            p = jnp.exp2((s_ref[at : at + 128, :] - peak) * (scale * LOG2E))
            p_ref[at : at + 128, :] = p.astype(BF16)
            summed = jnp.sum(p, axis=0, keepdims=True)
            total = summed if at == start else total + summed
        return total

    lses, at = [], 0
    for block in range(cols // 128):
        both = []
        for i in range(pair):
            start, count, peak, scale = parts[at]
            total = weigh(parts[at])
            lses.append(peak * (scale * LOG2E) + jnp.log2(total))
            column = block * 128 + i * head
            o = dot(vvt_ref[column : column + head, :], p_ref[start : start + count, :])
            both.append(o * (1.0 / total))
            at += 1
        v2a = jnp.concatenate(both, axis=0).T
        own_v2a_ref[:, block * 128 : (block + 1) * 128] = v2a[0:rows_audio]
        for j, dst in enumerate(sends):
            top = rows + block * rows_audio
            dst[top : top + rows_audio, 0:128] = v2a[(j + 1) * rows_audio : (j + 2) * rows_audio].astype(BF16)
    for j in range(n):
        for h in range(width // DHV):
            cut = slice(h * DHV, (h + 1) * DHV)
            start, count, _, _ = parts[at]
            total = weigh(parts[at])
            o = dot(vt_ref[cut, :], p_ref[start : start + count, :]) * (1.0 / total)
            dst = own_ref if j == 0 else sends[j - 1].at[0:rows, :]
            dst[:, cut] = o.T.astype(BF16)
            at += 1
    heads = len(lses)
    lse = jnp.concatenate(lses, axis=0)
    own_lse_ref[...] = lse
    pieces, left = [], lse
    for _ in range(3):
        pieces.append(left.astype(BF16).astype(F32))
        left = left - pieces[-1]
    packed = jnp.concatenate(pieces + [jnp.zeros((LSE_ROWS - 3 * heads, lse.shape[1]), F32)], axis=0)
    for j, dst in enumerate(sends):
        top = rows + cols // 128 * rows_audio
        dst[top : top + LSE_ROWS, 0:128] = pltpu.roll(packed, 128 - (j + 1) * rows_audio, 1).astype(BF16)


def attend_audio_kernel(hops, rows_audio, head, limit_ref, q_ref, forwarded, *rest):
    blocks, out_ref = rest[:-1], rest[-1]
    near = iter(blocks)
    pairs = [(hop, None if hop == FORWARDED else next(near)) for hop in hops]
    audios = by_hop(pairs, forwarded, rows_audio, q_ref.shape[1])
    me, row = index_of("seq"), lax.broadcasted_iota(jnp.int32, (rows_audio, 1), 0)
    allowed = [(me ^ hop) * rows_audio + row < limit_ref[0] for hop in hops]
    scale = 1.0 / math.sqrt(head)
    for block in range(q_ref.shape[1] // 128):
        cut = slice(block * 128, (block + 1) * 128)
        q = pair_rows(q_ref[:, cut], head)
        _, p, total = softmax_t([dot_t(audio.block(1, block), q) for audio in audios], scale, allowed)
        vt = turn(jnp.concatenate([audio.block(2, block) for audio in audios], axis=0))
        o = dot(vt, jnp.concatenate(p, axis=0)) * (1.0 / total)
        out_ref[:, cut] = pair_columns(o, head).T.astype(BF16)


def merge_audio(head, top, v2a_ref, lse_ref, got, out_ref):
    rows_audio, cols = v2a_ref.shape
    heads = cols // head
    lses = [lse_ref[...]]
    for ref in got:
        at = top + cols // 128 * rows_audio
        packed = ref[at : at + LSE_ROWS, 0:128].astype(F32)
        lses.append(packed[0:heads] + packed[heads : 2 * heads] + packed[2 * heads : 3 * heads])
    peak = functools.reduce(jnp.maximum, lses)
    parts = [jnp.exp2(x - peak) for x in lses]
    total = functools.reduce(jnp.add, parts)
    inverse = 1.0 / total
    parts = [x * inverse for x in parts]
    parts.append(jnp.zeros((128 - len(parts) * heads, 128), F32))
    shares = jnp.concatenate(parts, axis=0).T[0:rows_audio]
    pair = 128 // head
    lane = lax.broadcasted_iota(jnp.int32, (1, 128), 1) // head
    for block in range(cols // 128):
        cut = slice(block * 128, (block + 1) * 128)
        at = top + block * rows_audio
        summed = jnp.zeros((rows_audio, 128), F32)
        for j in range(len(lses)):
            o = v2a_ref[:, cut] if j == 0 else got[j - 1][at : at + rows_audio, 0:128].astype(F32)
            share = jnp.zeros((rows_audio, 128), F32)
            for i in range(pair):
                column = j * heads + block * pair + i
                share = jnp.where(lane == i, shares[:, column : column + 1], share)
            summed = summed + share * o
        out_ref[:, cut] = summed.astype(BF16)


def block_of(far, other):
    mp, sub = index_of("mp"), index_of("sub")
    return (1 - mp if far else mp) * 2 + (1 - sub if other else sub)


def project(block, half, heads, weights, gain_ref):
    (att_ref, a2v_ref), (ws_ref, wa_ref) = heads, weights
    wide = ws_ref.shape[1]
    cut = wide // 8
    at = columns(block * 2 + half, cut)
    term = gain_ref[:, at].astype(F32) * dot(att_ref[...], ws_ref[:, at])
    gain = gain_ref[:, columns(block * 2 + half + 8, cut)].astype(F32)
    return term + gain * dot(a2v_ref[...], wa_ref[:, at])


def project_audio(block, v2a_ref, wv_ref):
    return dot(v2a_ref[...], wv_ref[:, columns(block, wv_ref.shape[1] // 4)])


def first_kernel(hops, own_ref, a2v_ref, ws_ref, wa_ref, gain_ref, *rest):
    got, (self_ref, out_ref) = rest[: len(hops) - 1], rest[len(hops) - 1 :]
    rows, width = own_ref.shape
    me = index_of("seq")
    self_ref[:, columns(me, width)] = own_ref[...]
    for hop, ref in zip(hops[1:], got):
        self_ref[:, columns(me ^ hop, width)] = ref[0:rows, :]
    out_ref[...] = project(block_of(True, True), 0, (self_ref, a2v_ref), (ws_ref, wa_ref), gain_ref).astype(BF16)


def second_kernel(head, self_ref, a2v_ref, ws_ref, wa_ref, wv_ref, gain_ref, v2a_ref, lse_ref, *rest):
    got, (out_ref, audio_ref, low_ref) = rest[:-3], rest[-3:]
    rows = self_ref.shape[0]
    block = block_of(True, True)
    out_ref[0:rows, :] = project(block, 1, (self_ref, a2v_ref), (ws_ref, wa_ref), gain_ref).astype(BF16)
    merge_audio(head, rows, v2a_ref, lse_ref, got, audio_ref)
    out_ref[rows:, :] = project_audio(block, audio_ref, wv_ref).astype(BF16)
    low_ref[...] = project(block_of(True, False), 0, (self_ref, a2v_ref), (ws_ref, wa_ref), gain_ref)


def far_low_kernel(low_ref, extra_ref, out_ref):
    out_ref[...] = (low_ref[...] + extra_ref[...].astype(F32)).astype(BF16)


def near_kernel(self_ref, a2v_ref, audio_ref, ws_ref, wa_ref, wv_ref, gain_ref, send_ref, own_ref):
    rows = self_ref.shape[0]
    for out, other in ((send_ref, True), (own_ref, False)):
        block = block_of(False, other)
        for half in range(2):
            term = project(block, half, (self_ref, a2v_ref), (ws_ref, wa_ref), gain_ref)
            out[half * rows : (half + 1) * rows, :] = term.astype(out.dtype)
        out[2 * rows :, :] = project_audio(block, audio_ref, wv_ref).astype(out.dtype)


def far_high_kernel(self_ref, a2v_ref, ws_ref, wa_ref, gain_ref, extra_ref, audio_ref, wv_ref, out_ref):
    rows = self_ref.shape[0]
    block = block_of(True, False)
    term = project(block, 1, (self_ref, a2v_ref), (ws_ref, wa_ref), gain_ref)
    out_ref[0:rows, :] = (term + extra_ref[0:rows, :].astype(F32)).astype(BF16)
    term = project_audio(block, audio_ref, wv_ref)
    out_ref[rows:, :] = (term + extra_ref[rows:, :].astype(F32)).astype(BF16)


def finish_kernel(video_ref, audio_ref, gain_ref, own_ref, core_ref, low_ref, high_ref, video_out, audio_out):
    rows = video_ref.shape[0]
    cut = video_ref.shape[1] // 2
    near = own_ref[...] + core_ref[...].astype(F32)
    for half, ref in enumerate((low_ref, high_ref)):
        at = slice(half * cut, (half + 1) * cut)
        term = near[half * rows : (half + 1) * rows] + ref[0:rows, :].astype(F32)
        video_out[:, at] = (video_ref[:, at].astype(F32) + term).astype(BF16)
    term = near[2 * rows :] + high_ref[rows:, :].astype(F32)
    audio_out[...] = (audio_ref[...].astype(F32) + gain_ref[...] * term).astype(BF16)


def on_device_heads(
    video_in,
    audio_in,
    q_self,
    k_self,
    v_self,
    q_a2v,
    k_a2v,
    v_a2v,
    q_v2a,
    k_v2a,
    v_v2a,
    wo_self,
    wo_a2v,
    wo_v2a,
    video_gates,
    audio_gates,
    video_steps,
    audio_steps,
    audio_len,
    *,
    n,
):
    hops = [0] + OUT_ORDER
    rows, cols = q_self.shape
    rows_audio, cross = q_v2a.shape
    width = cols // n

    def trade(x, axis, hop, size):
        return lax.ppermute(x, axis, [(i, i ^ hop) for i in range(size)])

    video, audio = 3 * rows, 3 * cross // width * rows_audio
    packed = call(
        functools.partial(pack_kernel, hops, width),
        [shape(video if hop == FORWARDED else video + audio, width) for hop in hops],
        (q_self, k_self, v_self, q_v2a, k_a2v, v_a2v),
        [HBM] * 6,
        scratch=[pltpu.SemaphoreType.DMA((3 * n + (n - 1) * audio // rows_audio,))],
    )
    blocks = dict(zip(hops, packed))
    for hop in hops[1:]:
        blocks[hop] = trade(blocks[hop], "seq", hop, n)
    (forwarded,) = call(relay_kernel, [shape(audio, width)], (blocks[FORWARDED ^ 1],))
    forwarded = trade(forwarded, "seq", 1, n)

    late = (k_v2a, v_v2a, q_a2v, wo_self, wo_a2v, wo_v2a, video_in, audio_in)
    steps = (video_steps.reshape(1, rows), audio_steps.reshape(1, rows_audio))
    gain, audio_gain, k_own, v_own, q_own, ws, wa, wv, video_own, audio_own = call(
        fetch_kernel,
        [shape(rows, 2 * video_gates.shape[2]), shape(*audio_in.shape, F32)]
        + [shape(*x.shape) for x in late],
        (audio_len, video_gates.reshape(NT, -1), *steps, audio_gates, *late),
        [SMEM, VMEM] + [HBM] * (3 + len(late)),
        scratch=[pltpu.VMEM(x.shape, x.dtype) for x in (*steps, audio_gates)]
        + [pltpu.SemaphoreType.DMA((3 + len(late),))],
    )
    back = rows + cross // 128 * rows_audio + LSE_ROWS
    result = call(
        functools.partial(attend_kernel, hops, DHC),
        [shape(back, width)] * (n - 1)
        + [shape(rows, width), shape(rows_audio, cross, F32), shape(cross // DHC, 128, F32)],
        (k_own, v_own, forwarded, *blocks.values()),
        flops=4 * n * n * rows * rows * width,
        scratch=[pltpu.VMEM((width, n * rows), BF16), pltpu.VMEM((cross, rows), BF16)]
        + [pltpu.VMEM((n * n * rows * width // DHV + cross // DHC * rows, 128), kind) for kind in (F32, BF16)],
    )
    sends, (own, own_v2a, own_lse) = result[: n - 1], result[n - 1 :]
    got = [trade(x, "seq", hop, n) for x, hop in zip(sends, hops[1:])]
    near = [blocks[hop] for hop in hops if hop != FORWARDED]
    (a2v_att,) = call(
        functools.partial(attend_audio_kernel, hops, rows_audio, DHC),
        [shape(rows, cross)],
        (audio_len, q_own, forwarded, *near),
        [SMEM] + [VMEM] * (len(near) + 2),
        flops=8 * n * rows * rows_audio * cross,
    )

    half = video_in.shape[1] // 2
    flops = 2 * rows * (cols + cross) * half
    self_att, first = call(
        functools.partial(first_kernel, hops),
        [shape(rows, cols), shape(rows, half)],
        (own, a2v_att, ws, wa, gain, *got),
        flops=flops,
    )
    first = trade(first, "sub", 1, 2)
    second, v2a_att, own_low = call(
        functools.partial(second_kernel, DHC),
        [shape(rows + rows_audio, half), shape(rows_audio, cross), shape(rows, half, F32)],
        (self_att, a2v_att, ws, wa, wv, gain, own_v2a, own_lse, *got),
        flops=2 * flops,
    )
    second = trade(second, "sub", 1, 2)
    (low,) = call(far_low_kernel, [shape(rows, half)], (own_low, first))
    low = trade(low, "mp", 1, 2)
    (high,) = call(
        far_high_kernel,
        [shape(rows + rows_audio, half)],
        (self_att, a2v_att, ws, wa, gain, second, v2a_att, wv),
        flops=flops,
    )
    high = trade(high, "mp", 1, 2)
    near, own_sum = call(
        near_kernel,
        [shape(2 * rows + rows_audio, half), shape(2 * rows + rows_audio, half, F32)],
        (self_att, a2v_att, v2a_att, ws, wa, wv, gain),
        flops=4 * flops,
    )
    near = trade(near, "sub", 1, 2)
    return call(
        finish_kernel,
        [shape(*video_in.shape), shape(*audio_in.shape)],
        (video_own, audio_own, audio_gain, own_sum, near, low, high),
    )


def on_device(n, mp, sub, *arrays):
    cols, cross = arrays[2].shape[1], arrays[5].shape[1]
    width = cols // n
    fits = (
        n == SEQ
        and (mp, sub) == (2, 2)
        and width % DHV == 0
        and cross % width == 0
        and 3 * (cross // DHC) <= LSE_ROWS
        and n * arrays[8].shape[0] == arrays[2].shape[0] == 128
        and arrays[0].shape[1] == 2 * arrays[1].shape[1]
    )
    if fits:
        return on_device_heads(*arrays, n=n)
    return on_device_gather(*arrays)


def solution(mesh):
    in_specs = (
        P(("groups", "seq"), ("mp", "sub")),
        P(("groups", "seq"), ("mp", "sub")),
        P(("groups", "seq"), ("mp", "sub")),
        P(("groups", "seq"), ("mp", "sub")),
        P(("groups", "seq"), ("mp", "sub")),
        P(("groups", "seq"), ("mp", "sub")),
        P(("groups", "seq"), ("mp", "sub")),
        P(("groups", "seq"), ("mp", "sub")),
        P(("groups", "seq"), ("mp", "sub")),
        P(("groups", "seq"), ("mp", "sub")),
        P(("groups", "seq"), ("mp", "sub")),
        P(("mp", "sub"), None),
        P(("mp", "sub"), None),
        P(("mp", "sub"), None),
        P(),
        P(),
        P(("groups", "seq")),
        P(("groups", "seq")),
        P("groups"),
    )
    out_specs = (P(("groups", "seq"), ("mp", "sub")), P(("groups", "seq"), ("mp", "sub")))
    step = jax.shard_map(
        functools.partial(on_device, *(mesh.shape[a] for a in ("seq", "mp", "sub"))), mesh=mesh, in_specs=in_specs, out_specs=out_specs, check_vma=False
    )
    return step if mesh.shape["seq"] == SEQ else step
```

```python
import functools
import math

import jax
import jax.numpy as jnp
from jax import lax
from jax.experimental import pallas as pl
from jax.experimental.pallas import tpu as pltpu
from jax.sharding import PartitionSpec as P


DHV = 128
DHC = 64
NT = 16


def start_state(rows, heads, width):
    return (
        jnp.full((rows, heads), -1e30, jnp.float32),
        jnp.zeros((rows, heads), jnp.float32),
        jnp.zeros((rows, heads, width), jnp.float32),
    )


def update_block(state, queries, keys, values, heads, width, allowed):
    rows = queries.shape[0]
    count = keys.shape[0]
    q_heads = queries.reshape(rows, heads, width)
    k_heads = keys.reshape(count, heads, width)
    v_heads = values.reshape(count, heads, width)
    scores = jnp.einsum(
        "qhd,khd->qhk", q_heads, k_heads, preferred_element_type=jnp.float32
    ) / math.sqrt(width)
    if allowed is not None:
        scores = jnp.where(allowed[None, None, :], scores, -jnp.inf)
    peak_old, total_old, summed_old = state
    peak = jnp.maximum(peak_old, jnp.max(scores, axis=2))
    weights = jnp.exp(scores - peak[:, :, None])
    factor = jnp.exp(peak_old - peak)
    total = total_old * factor + jnp.sum(weights, axis=2)
    summed = summed_old * factor[:, :, None] + jnp.einsum(
        "qhk,khd->qhd", weights.astype(jnp.bfloat16), v_heads, preferred_element_type=jnp.float32
    )
    return (peak, total, summed)


def update_state(state, queries, keys, values, heads, width, start, limit):
    count = keys.shape[0]
    block = 1024 if count > 1024 and count % 1024 == 0 else count
    if block == count:
        allowed = None
        if limit is not None:
            allowed = jnp.arange(count, dtype=jnp.int32) < limit
        return update_block(state, queries, keys, values, heads, width, allowed)
    steps = count // block
    key_blocks = keys.reshape(steps, block, keys.shape[1])
    value_blocks = values.reshape(steps, block, values.shape[1])
    offsets = jnp.arange(steps, dtype=jnp.int32) * block

    def one_block(carry, items):
        key_rows, value_rows, offset = items
        allowed = None
        if limit is not None:
            allowed = start + offset + jnp.arange(block, dtype=jnp.int32) < limit
        return (update_block(carry, queries, key_rows, value_rows, heads, width, allowed), None)

    result, _ = lax.scan(one_block, state, (key_blocks, value_blocks, offsets))
    return result


def finish(state, heads, width):
    _, total, summed = state
    rows = summed.shape[0]
    return (summed / total[:, :, None]).reshape(rows, heads * width).astype(jnp.bfloat16)


def on_device_gather(
    video_in,
    audio_in,
    q_self,
    k_self,
    v_self,
    q_a2v,
    k_a2v,
    v_a2v,
    q_v2a,
    k_v2a,
    v_v2a,
    wo_self,
    wo_a2v,
    wo_v2a,
    video_gates,
    audio_gates,
    video_steps,
    audio_steps,
    audio_len,
):
    heads_self = q_self.shape[1] // DHV
    heads_cross = q_a2v.shape[1] // DHC
    rows_video = q_self.shape[0]
    rows_audio = q_v2a.shape[0]
    limit = audio_len[0]
    piece = (
        lax.all_gather(k_a2v, "seq", axis=0, tiled=True),
        lax.all_gather(v_a2v, "seq", axis=0, tiled=True),
    )
    a2v_state = update_state(
        start_state(rows_video, heads_cross, DHC),
        q_a2v,
        piece[0],
        piece[1],
        heads_cross,
        DHC,
        jnp.int32(0),
        limit,
    )
    a2v_att = finish(a2v_state, heads_cross, DHC)
    piece = (
        lax.all_gather(k_self, "seq", axis=0, tiled=True),
        lax.all_gather(v_self, "seq", axis=0, tiled=True),
    )
    self_state = update_state(
        start_state(rows_video, heads_self, DHV),
        q_self,
        piece[0],
        piece[1],
        heads_self,
        DHV,
        jnp.int32(0),
        None,
    )
    piece = (
        lax.all_gather(k_v2a, "seq", axis=0, tiled=True),
        lax.all_gather(v_v2a, "seq", axis=0, tiled=True),
    )
    v2a_state = update_state(
        start_state(rows_audio, heads_cross, DHC),
        q_v2a,
        piece[0],
        piece[1],
        heads_cross,
        DHC,
        jnp.int32(0),
        None,
    )
    self_att = finish(self_state, heads_self, DHV)
    v2a_att = finish(v2a_state, heads_cross, DHC)
    levels = jnp.arange(NT, dtype=jnp.int32)
    video_hot = (video_steps[:, None] == levels[None, :]).astype(jnp.bfloat16)
    video_gain = jnp.dot(video_hot, video_gates.reshape(NT, -1), preferred_element_type=jnp.float32)
    width_video = video_gates.shape[2]
    video_term = video_gain[:, :width_video] * jnp.dot(
        self_att, wo_self, preferred_element_type=jnp.float32
    )
    video_term = video_term + video_gain[:, width_video:] * jnp.dot(
        a2v_att, wo_a2v, preferred_element_type=jnp.float32
    )
    audio_hot = (audio_steps[:, None] == levels[None, :]).astype(jnp.bfloat16)
    audio_gain = jnp.dot(audio_hot, audio_gates, preferred_element_type=jnp.float32)
    positions = lax.axis_index("seq") * rows_audio + jnp.arange(rows_audio, dtype=jnp.int32)
    present = (positions < limit).astype(jnp.float32)
    audio_term = (
        present[:, None] * audio_gain * jnp.dot(v2a_att, wo_v2a, preferred_element_type=jnp.float32)
    )
    video_sum, audio_sum = (
        lax.psum_scatter(
            video_term.astype(jnp.bfloat16), ("mp", "sub"), scatter_dimension=1, tiled=True
        ).astype(jnp.float32),
        lax.psum_scatter(
            audio_term.astype(jnp.bfloat16), ("mp", "sub"), scatter_dimension=1, tiled=True
        ).astype(jnp.float32),
    )
    video_out = (video_in.astype(jnp.float32) + video_sum).astype(jnp.bfloat16)
    audio_out = (audio_in.astype(jnp.float32) + audio_sum).astype(jnp.bfloat16)
    return (video_out, audio_out)


LOG2E = 1.4426950408889634
VMEM = pl.BlockSpec(memory_space=pltpu.VMEM)
SMEM = pl.BlockSpec(memory_space=pltpu.SMEM)
HBM = pl.BlockSpec(memory_space=pltpu.HBM)
BF16, F32 = jnp.bfloat16, jnp.float32
LSE_ROWS = 16
SEQ, FORWARDED, OUT_ORDER = 4, 3, [3, 2, 1]


def call(kernel, outs, operands, specs=None, flops=0, scratch=(), limit=8 * 2**20):
    size = sum(math.prod(x.shape) * x.dtype.itemsize for x in (*operands, *outs))
    if specs:
        operands = [
            pltpu.with_memory_space_constraint(x, pltpu.HBM) if spec is HBM else x for x, spec in zip(operands, specs)
        ]
    return pl.pallas_call(
        kernel,
        out_shape=tuple(outs),
        in_specs=specs or [VMEM] * len(operands),
        out_specs=tuple(VMEM for _ in outs),
        scratch_shapes=list(scratch),
        compiler_params=pltpu.CompilerParams(vmem_limit_bytes=limit),
        cost_estimate=pl.CostEstimate(flops=flops, bytes_accessed=size, transcendentals=0),
    )(*operands)


def shape(rows, cols, kind=BF16):
    return jax.ShapeDtypeStruct((rows, cols), kind)


def dot_t(a, b):
    return lax.dot_general(a, b, (((1,), (1,)), ((), ())), preferred_element_type=F32)


def dot(a, b):
    return jnp.dot(a, b, preferred_element_type=F32)


def index_of(axis):
    return lax.axis_index(axis).astype(jnp.int32)


def columns(index, width):
    return pl.ds(pl.multiple_of(index * width, width), width)


def copy_all(pairs, sems):
    copies = [pltpu.make_async_copy(src, dst, sems.at[i]) for i, (src, dst) in enumerate(pairs)]
    for copy in copies:
        copy.start()
    for copy in copies:
        copy.wait()


def pack_kernel(hops, width, q_ref, k_ref, v_ref, qa_ref, ka_ref, va_ref, *rest):
    outs, sems = rest[:-1], rest[-1]
    rows = q_ref.shape[0]
    rows_audio, cols_audio = qa_ref.shape
    me = index_of("seq")
    pairs = []
    for hop, out in zip(hops, outs):
        for i, ref in enumerate((q_ref, k_ref, v_ref)):
            pairs.append((ref.at[:, columns(me ^ hop, width)], out.at[pl.ds(i * rows, rows), :]))
        at = 3 * rows
        for ref in (qa_ref,) if hop == FORWARDED else (qa_ref, ka_ref, va_ref):
            for i in range(cols_audio // width):
                pairs.append((ref.at[:, pl.ds(i * width, width)], out.at[pl.ds(at, rows_audio), :]))
                at += rows_audio
    copy_all(pairs, sems)


def relay_kernel(got_ref, out_ref):
    out_ref[...] = got_ref[got_ref.shape[0] - out_ref.shape[0] :, :]


def audio_block(ref, end, rows, cols, block):
    at, column = divmod(block * 128, ref.shape[1])
    top = ref.shape[0] - end * (cols // ref.shape[1]) * rows + at * rows
    return ref[top : top + rows, column : column + 128]


def one_hot_t(steps_ref):
    levels = lax.broadcasted_iota(jnp.int32, (NT, steps_ref.shape[1]), 0)
    return (levels == steps_ref[...]).astype(BF16)


def pick(hot_t, table):
    return lax.dot_general(hot_t, table, (((0,), (0,)), ((), ())), preferred_element_type=F32)


def fetch_kernel(limit_ref, vg_ref, *rest):
    count = (len(rest) - 9) // 2
    loads, gain_ref, audio_ref = rest[: count + 3], rest[count + 3], rest[count + 4]
    fetched, (vs_ref, as_ref, ag_ref, sems) = rest[count + 5 : -4], rest[-4:]
    copies = [
        pltpu.make_async_copy(src, dst, sems.at[i])
        for i, (src, dst) in enumerate(zip(loads, (vs_ref, as_ref, ag_ref, *fetched)))
    ]
    for copy in copies:
        copy.start()
    for copy in copies[:3]:
        copy.wait()
    hot_t = one_hot_t(vs_ref)
    piece = min(vg_ref.shape[1], 2048)
    for at in range(0, vg_ref.shape[1], piece):
        gain_ref[:, at : at + piece] = pick(hot_t, vg_ref[:, at : at + piece]).astype(BF16)
    rows_audio, narrow = audio_ref.shape
    part = index_of("mp") * 2 + index_of("sub")
    gain = pick(one_hot_t(as_ref), ag_ref[:, columns(part, narrow)])
    at = index_of("seq") * rows_audio + lax.broadcasted_iota(jnp.int32, (rows_audio, 1), 0)
    audio_ref[...] = jnp.where(at < limit_ref[0], gain, 0.0)
    for copy in copies[3:]:
        copy.wait()


def softmax_t(scores, scale, allowed=None):
    if allowed is not None:
        scores = [jnp.where(ok, x, -jnp.inf) for ok, x in zip(allowed, scores)]
    peak = functools.reduce(jnp.maximum, [jnp.max(x, axis=0, keepdims=True) for x in scores])
    weights = [jnp.exp2((x - peak) * (scale * LOG2E)) for x in scores]
    total = functools.reduce(jnp.add, [jnp.sum(x, axis=0, keepdims=True) for x in weights])
    return peak, [x.astype(BF16) for x in weights], total


def turn(x):
    return x.astype(F32).T.astype(BF16)


def pair_rows(x, head):
    lane = lax.broadcasted_iota(jnp.int32, (1, 128), 1) // head
    return jnp.concatenate([jnp.where(lane == i, x, 0).astype(BF16) for i in range(128 // head)], axis=0)


def pair_columns(x, head):
    pair = 128 // head
    rows = x.shape[1] // pair
    return jnp.concatenate([x[i * head : (i + 1) * head, i * rows : (i + 1) * rows] for i in range(pair)], axis=0)


def attend_kernel(hops, head, kv_ref, vv_ref, *rest):
    n = len(hops)
    blocks, sends, (own_ref, own_v2a_ref, own_lse_ref) = rest[:n], rest[n : 2 * n - 1], rest[2 * n - 1 : 2 * n + 2]
    vt_ref, vvt_ref, s_ref, p_ref = rest[2 * n + 2 :]
    rows, cols = kv_ref.shape
    width = blocks[0].shape[1]
    rows_audio = own_v2a_ref.shape[0]
    ends = [1 if hop == FORWARDED else 3 for hop in hops]
    for h in range(width // DHV):
        cut = slice(h * DHV, (h + 1) * DHV)
        for i, ref in enumerate(blocks):
            vt_ref[cut, i * rows : (i + 1) * rows] = turn(ref[2 * rows : 3 * rows, cut])
    for block in range(cols // 128):
        cut = slice(block * 128, (block + 1) * 128)
        vvt_ref[cut, :] = turn(vv_ref[:, cut])
    pair, row = 128 // head, 0
    parts = []
    for block in range(cols // 128):
        cut = slice(block * 128, (block + 1) * 128)
        q = [audio_block(ref, end, rows_audio, cols, block) for ref, end in zip(blocks, ends)]
        q = pair_rows(jnp.concatenate(q, axis=0), head)
        scores = dot_t(kv_ref[:, cut], q)
        for i in range(pair):
            at = slice(i * n * rows_audio, (i + 1) * n * rows_audio)
            s_ref[row + i * rows : row + (i + 1) * rows, :] = scores[:, at]
            parts.append((row + i * rows, rows, jnp.max(scores[:, at], axis=0, keepdims=True), 1.0 / math.sqrt(head)))
        row += pair * rows
    for ref in blocks:
        for h in range(width // DHV):
            cut = slice(h * DHV, (h + 1) * DHV)
            peak = None
            for i, other in enumerate(blocks):
                scores = dot_t(other[rows : 2 * rows, cut], ref[0:rows, cut])
                s_ref[row + i * rows : row + (i + 1) * rows, :] = scores
                top = jnp.max(scores, axis=0, keepdims=True)
                peak = top if i == 0 else jnp.maximum(peak, top)
            parts.append((row, n * rows, peak, 1.0 / math.sqrt(DHV)))
            row += n * rows

    def weigh(part):
        start, count, peak, scale = part
        total = None
        for at in range(start, start + count, 128):
            p = jnp.exp2((s_ref[at : at + 128, :] - peak) * (scale * LOG2E))
            p_ref[at : at + 128, :] = p.astype(BF16)
            summed = jnp.sum(p, axis=0, keepdims=True)
            total = summed if at == start else total + summed
        return total

    lses, at = [], 0
    for block in range(cols // 128):
        both = []
        for i in range(pair):
            start, count, peak, scale = parts[at]
            total = weigh(parts[at])
            lses.append(peak * (scale * LOG2E) + jnp.log2(total))
            column = block * 128 + i * head
            o = dot(vvt_ref[column : column + head, :], p_ref[start : start + count, :])
            both.append(o * (1.0 / total))
            at += 1
        v2a = jnp.concatenate(both, axis=0).T
        own_v2a_ref[:, block * 128 : (block + 1) * 128] = v2a[0:rows_audio]
        for j, dst in enumerate(sends):
            top = rows + block * rows_audio
            dst[top : top + rows_audio, 0:128] = v2a[(j + 1) * rows_audio : (j + 2) * rows_audio].astype(BF16)
    for j in range(n):
        for h in range(width // DHV):
            cut = slice(h * DHV, (h + 1) * DHV)
            start, count, _, _ = parts[at]
            total = weigh(parts[at])
            o = dot(vt_ref[cut, :], p_ref[start : start + count, :]) * (1.0 / total)
            dst = own_ref if j == 0 else sends[j - 1].at[0:rows, :]
            dst[:, cut] = o.T.astype(BF16)
            at += 1
    heads = len(lses)
    lse = jnp.concatenate(lses, axis=0)
    own_lse_ref[...] = lse
    pieces, left = [], lse
    for _ in range(3):
        pieces.append(left.astype(BF16).astype(F32))
        left = left - pieces[-1]
    packed = jnp.concatenate(pieces + [jnp.zeros((LSE_ROWS - 3 * heads, lse.shape[1]), F32)], axis=0)
    for j, dst in enumerate(sends):
        top = rows + cols // 128 * rows_audio
        dst[top : top + LSE_ROWS, 0:128] = pltpu.roll(packed, 128 - (j + 1) * rows_audio, 1).astype(BF16)


def attend_audio_kernel(hops, rows_audio, head, limit_ref, q_ref, *rest):
    blocks, out_ref = rest[:-1], rest[-1]
    cols = q_ref.shape[1]
    me, row = index_of("seq"), lax.broadcasted_iota(jnp.int32, (rows_audio, 1), 0)
    allowed = [(me ^ hop) * rows_audio + row < limit_ref[0] for hop in hops]
    scale = 1.0 / math.sqrt(head)
    for block in range(q_ref.shape[1] // 128):
        cut = slice(block * 128, (block + 1) * 128)
        q = pair_rows(q_ref[:, cut], head)
        _, p, total = softmax_t([dot_t(audio_block(ref, 2, rows_audio, cols, block), q) for ref in blocks], scale, allowed)
        vt = turn(jnp.concatenate([audio_block(ref, 1, rows_audio, cols, block) for ref in blocks], axis=0))
        o = dot(vt, jnp.concatenate(p, axis=0)) * (1.0 / total)
        out_ref[:, cut] = pair_columns(o, head).T.astype(BF16)


def merge_audio(head, top, v2a_ref, lse_ref, got, out_ref):
    rows_audio, cols = v2a_ref.shape
    heads = cols // head
    lses = [lse_ref[...]]
    for ref in got:
        at = top + cols // 128 * rows_audio
        packed = ref[at : at + LSE_ROWS, 0:128].astype(F32)
        lses.append(packed[0:heads] + packed[heads : 2 * heads] + packed[2 * heads : 3 * heads])
    peak = functools.reduce(jnp.maximum, lses)
    parts = [jnp.exp2(x - peak) for x in lses]
    total = functools.reduce(jnp.add, parts)
    inverse = 1.0 / total
    parts = [x * inverse for x in parts]
    parts.append(jnp.zeros((128 - len(parts) * heads, 128), F32))
    shares = jnp.concatenate(parts, axis=0).T[0:rows_audio]
    pair = 128 // head
    lane = lax.broadcasted_iota(jnp.int32, (1, 128), 1) // head
    for block in range(cols // 128):
        cut = slice(block * 128, (block + 1) * 128)
        at = top + block * rows_audio
        summed = jnp.zeros((rows_audio, 128), F32)
        for j in range(len(lses)):
            o = v2a_ref[:, cut] if j == 0 else got[j - 1][at : at + rows_audio, 0:128].astype(F32)
            share = jnp.zeros((rows_audio, 128), F32)
            for i in range(pair):
                column = j * heads + block * pair + i
                share = jnp.where(lane == i, shares[:, column : column + 1], share)
            summed = summed + share * o
        out_ref[:, cut] = summed.astype(BF16)


def block_of(far, other):
    mp, sub = index_of("mp"), index_of("sub")
    return (1 - mp if far else mp) * 2 + (1 - sub if other else sub)


def project(block, half, heads, weights, gain_ref):
    (att_ref, a2v_ref), (ws_ref, wa_ref) = heads, weights
    wide = ws_ref.shape[1]
    cut = wide // 8
    at = columns(block * 2 + half, cut)
    term = gain_ref[:, at].astype(F32) * dot(att_ref[...], ws_ref[:, at])
    gain = gain_ref[:, columns(block * 2 + half + 8, cut)].astype(F32)
    return term + gain * dot(a2v_ref[...], wa_ref[:, at])


def project_audio(block, v2a_ref, wv_ref):
    return dot(v2a_ref[...], wv_ref[:, columns(block, wv_ref.shape[1] // 4)])


def first_kernel(hops, own_ref, a2v_ref, ws_ref, wa_ref, gain_ref, *rest):
    got, (self_ref, out_ref) = rest[: len(hops) - 1], rest[len(hops) - 1 :]
    rows, width = own_ref.shape
    me = index_of("seq")
    self_ref[:, columns(me, width)] = own_ref[...]
    for hop, ref in zip(hops[1:], got):
        self_ref[:, columns(me ^ hop, width)] = ref[0:rows, :]
    out_ref[...] = project(block_of(True, True), 0, (self_ref, a2v_ref), (ws_ref, wa_ref), gain_ref).astype(BF16)


def second_kernel(head, self_ref, a2v_ref, ws_ref, wa_ref, wv_ref, gain_ref, v2a_ref, lse_ref, *rest):
    got, (out_ref, audio_ref, low_ref) = rest[:-3], rest[-3:]
    rows = self_ref.shape[0]
    block = block_of(True, True)
    out_ref[0:rows, :] = project(block, 1, (self_ref, a2v_ref), (ws_ref, wa_ref), gain_ref).astype(BF16)
    merge_audio(head, rows, v2a_ref, lse_ref, got, audio_ref)
    out_ref[rows:, :] = project_audio(block, audio_ref, wv_ref).astype(BF16)
    low_ref[...] = project(block_of(True, False), 0, (self_ref, a2v_ref), (ws_ref, wa_ref), gain_ref)


def far_low_kernel(low_ref, extra_ref, out_ref):
    out_ref[...] = (low_ref[...] + extra_ref[...].astype(F32)).astype(BF16)


def near_kernel(self_ref, a2v_ref, audio_ref, ws_ref, wa_ref, wv_ref, gain_ref, send_ref, own_ref):
    rows = self_ref.shape[0]
    for out, other in ((send_ref, True), (own_ref, False)):
        block = block_of(False, other)
        for half in range(2):
            term = project(block, half, (self_ref, a2v_ref), (ws_ref, wa_ref), gain_ref)
            out[half * rows : (half + 1) * rows, :] = term.astype(out.dtype)
        out[2 * rows :, :] = project_audio(block, audio_ref, wv_ref).astype(out.dtype)


def far_high_kernel(self_ref, a2v_ref, ws_ref, wa_ref, gain_ref, extra_ref, audio_ref, wv_ref, out_ref):
    rows = self_ref.shape[0]
    block = block_of(True, False)
    term = project(block, 1, (self_ref, a2v_ref), (ws_ref, wa_ref), gain_ref)
    out_ref[0:rows, :] = (term + extra_ref[0:rows, :].astype(F32)).astype(BF16)
    term = project_audio(block, audio_ref, wv_ref)
    out_ref[rows:, :] = (term + extra_ref[rows:, :].astype(F32)).astype(BF16)


def finish_kernel(video_ref, audio_ref, gain_ref, own_ref, core_ref, low_ref, high_ref, video_out, audio_out):
    rows = video_ref.shape[0]
    cut = video_ref.shape[1] // 2
    near = own_ref[...] + core_ref[...].astype(F32)
    for half, ref in enumerate((low_ref, high_ref)):
        at = slice(half * cut, (half + 1) * cut)
        term = near[half * rows : (half + 1) * rows] + ref[0:rows, :].astype(F32)
        video_out[:, at] = (video_ref[:, at].astype(F32) + term).astype(BF16)
    term = near[2 * rows :] + high_ref[rows:, :].astype(F32)
    audio_out[...] = (audio_ref[...].astype(F32) + gain_ref[...] * term).astype(BF16)


def on_device_heads(
    video_in,
    audio_in,
    q_self,
    k_self,
    v_self,
    q_a2v,
    k_a2v,
    v_a2v,
    q_v2a,
    k_v2a,
    v_v2a,
    wo_self,
    wo_a2v,
    wo_v2a,
    video_gates,
    audio_gates,
    video_steps,
    audio_steps,
    audio_len,
    *,
    n,
):
    hops = [0] + OUT_ORDER
    rows, cols = q_self.shape
    rows_audio, cross = q_v2a.shape
    width = cols // n

    def trade(x, axis, hop, size):
        return lax.ppermute(x, axis, [(i, i ^ hop) for i in range(size)])

    video, audio = 3 * rows, cross // width * rows_audio
    packed = call(
        functools.partial(pack_kernel, hops, width),
        [shape(video + (1 if hop == FORWARDED else 3) * audio, width) for hop in hops],
        (q_self, k_self, v_self, q_v2a, k_a2v, v_a2v),
        [HBM] * 6,
        scratch=[pltpu.SemaphoreType.DMA((3 * n + (3 * n - 2) * audio // rows_audio,))],
    )
    blocks = dict(zip(hops, packed))
    for hop in hops[1:]:
        blocks[hop] = trade(blocks[hop], "seq", hop, n)
    (forwarded,) = call(relay_kernel, [shape(2 * audio, width)], (blocks[FORWARDED ^ 1],))
    forwarded = trade(forwarded, "seq", 1, n)

    late = (k_v2a, v_v2a, q_a2v, wo_self, wo_a2v, wo_v2a, video_in, audio_in)
    steps = (video_steps.reshape(1, rows), audio_steps.reshape(1, rows_audio))
    gain, audio_gain, k_own, v_own, q_own, ws, wa, wv, video_own, audio_own = call(
        fetch_kernel,
        [shape(rows, 2 * video_gates.shape[2]), shape(*audio_in.shape, F32)]
        + [shape(*x.shape) for x in late],
        (audio_len, video_gates.reshape(NT, -1), *steps, audio_gates, *late),
        [SMEM, VMEM] + [HBM] * (3 + len(late)),
        scratch=[pltpu.VMEM(x.shape, x.dtype) for x in (*steps, audio_gates)]
        + [pltpu.SemaphoreType.DMA((3 + len(late),))],
    )
    back = rows + cross // 128 * rows_audio + LSE_ROWS
    result = call(
        functools.partial(attend_kernel, hops, DHC),
        [shape(back, width)] * (n - 1)
        + [shape(rows, width), shape(rows_audio, cross, F32), shape(cross // DHC, 128, F32)],
        (k_own, v_own, *blocks.values()),
        flops=4 * n * n * rows * rows * width,
        scratch=[pltpu.VMEM((width, n * rows), BF16), pltpu.VMEM((cross, rows), BF16)]
        + [pltpu.VMEM((n * n * rows * width // DHV + cross // DHC * rows, 128), kind) for kind in (F32, BF16)],
    )
    sends, (own, own_v2a, own_lse) = result[: n - 1], result[n - 1 :]
    got = [trade(x, "seq", hop, n) for x, hop in zip(sends, hops[1:])]
    audios = [forwarded if hop == FORWARDED else blocks[hop] for hop in hops]
    (a2v_att,) = call(
        functools.partial(attend_audio_kernel, hops, rows_audio, DHC),
        [shape(rows, cross)],
        (audio_len, q_own, *audios),
        [SMEM] + [VMEM] * (n + 1),
        flops=8 * n * rows * rows_audio * cross,
    )

    half = video_in.shape[1] // 2
    flops = 2 * rows * (cols + cross) * half
    self_att, first = call(
        functools.partial(first_kernel, hops),
        [shape(rows, cols), shape(rows, half)],
        (own, a2v_att, ws, wa, gain, *got),
        flops=flops,
    )
    first = trade(first, "sub", 1, 2)
    second, v2a_att, own_low = call(
        functools.partial(second_kernel, DHC),
        [shape(rows + rows_audio, half), shape(rows_audio, cross), shape(rows, half, F32)],
        (self_att, a2v_att, ws, wa, wv, gain, own_v2a, own_lse, *got),
        flops=2 * flops,
    )
    second = trade(second, "sub", 1, 2)
    (low,) = call(far_low_kernel, [shape(rows, half)], (own_low, first))
    low = trade(low, "mp", 1, 2)
    (high,) = call(
        far_high_kernel,
        [shape(rows + rows_audio, half)],
        (self_att, a2v_att, ws, wa, gain, second, v2a_att, wv),
        flops=flops,
    )
    high = trade(high, "mp", 1, 2)
    near, own_sum = call(
        near_kernel,
        [shape(2 * rows + rows_audio, half), shape(2 * rows + rows_audio, half, F32)],
        (self_att, a2v_att, v2a_att, ws, wa, wv, gain),
        flops=4 * flops,
    )
    near = trade(near, "sub", 1, 2)
    return call(
        finish_kernel,
        [shape(*video_in.shape), shape(*audio_in.shape)],
        (video_own, audio_own, audio_gain, own_sum, near, low, high),
    )


def on_device(n, mp, sub, *arrays):
    cols, cross = arrays[2].shape[1], arrays[5].shape[1]
    width = cols // n
    fits = (
        n == SEQ
        and (mp, sub) == (2, 2)
        and width % DHV == 0
        and cross % width == 0
        and 3 * (cross // DHC) <= LSE_ROWS
        and n * arrays[8].shape[0] == arrays[2].shape[0] == 128
        and arrays[0].shape[1] == 2 * arrays[1].shape[1]
    )
    if fits:
        return on_device_heads(*arrays, n=n)
    return on_device_gather(*arrays)


def solution(mesh):
    in_specs = (
        P(("groups", "seq"), ("mp", "sub")),
        P(("groups", "seq"), ("mp", "sub")),
        P(("groups", "seq"), ("mp", "sub")),
        P(("groups", "seq"), ("mp", "sub")),
        P(("groups", "seq"), ("mp", "sub")),
        P(("groups", "seq"), ("mp", "sub")),
        P(("groups", "seq"), ("mp", "sub")),
        P(("groups", "seq"), ("mp", "sub")),
        P(("groups", "seq"), ("mp", "sub")),
        P(("groups", "seq"), ("mp", "sub")),
        P(("groups", "seq"), ("mp", "sub")),
        P(("mp", "sub"), None),
        P(("mp", "sub"), None),
        P(("mp", "sub"), None),
        P(),
        P(),
        P(("groups", "seq")),
        P(("groups", "seq")),
        P("groups"),
    )
    out_specs = (P(("groups", "seq"), ("mp", "sub")), P(("groups", "seq"), ("mp", "sub")))
    return jax.shard_map(
        functools.partial(on_device, *(mesh.shape[a] for a in ("seq", "mp", "sub"))), mesh=mesh, in_specs=in_specs, out_specs=out_specs, check_vma=False
    )
```

```python
import functools
import math

import jax
import jax.numpy as jnp
from jax import lax
from jax.experimental import pallas as pl
from jax.experimental.pallas import tpu as pltpu
from jax.sharding import PartitionSpec as P


DHV = 128
DHC = 64
NT = 16


def start_state(rows, heads, width):
    return (
        jnp.full((rows, heads), -1e30, jnp.float32),
        jnp.zeros((rows, heads), jnp.float32),
        jnp.zeros((rows, heads, width), jnp.float32),
    )


def update_block(state, queries, keys, values, heads, width, allowed):
    rows = queries.shape[0]
    count = keys.shape[0]
    q_heads = queries.reshape(rows, heads, width)
    k_heads = keys.reshape(count, heads, width)
    v_heads = values.reshape(count, heads, width)
    scores = jnp.einsum(
        "qhd,khd->qhk", q_heads, k_heads, preferred_element_type=jnp.float32
    ) / math.sqrt(width)
    if allowed is not None:
        scores = jnp.where(allowed[None, None, :], scores, -jnp.inf)
    peak_old, total_old, summed_old = state
    peak = jnp.maximum(peak_old, jnp.max(scores, axis=2))
    weights = jnp.exp(scores - peak[:, :, None])
    factor = jnp.exp(peak_old - peak)
    total = total_old * factor + jnp.sum(weights, axis=2)
    summed = summed_old * factor[:, :, None] + jnp.einsum(
        "qhk,khd->qhd", weights.astype(jnp.bfloat16), v_heads, preferred_element_type=jnp.float32
    )
    return (peak, total, summed)


def update_state(state, queries, keys, values, heads, width, start, limit):
    count = keys.shape[0]
    block = 1024 if count > 1024 and count % 1024 == 0 else count
    if block == count:
        allowed = None
        if limit is not None:
            allowed = jnp.arange(count, dtype=jnp.int32) < limit
        return update_block(state, queries, keys, values, heads, width, allowed)
    steps = count // block
    key_blocks = keys.reshape(steps, block, keys.shape[1])
    value_blocks = values.reshape(steps, block, values.shape[1])
    offsets = jnp.arange(steps, dtype=jnp.int32) * block

    def one_block(carry, items):
        key_rows, value_rows, offset = items
        allowed = None
        if limit is not None:
            allowed = start + offset + jnp.arange(block, dtype=jnp.int32) < limit
        return (update_block(carry, queries, key_rows, value_rows, heads, width, allowed), None)

    result, _ = lax.scan(one_block, state, (key_blocks, value_blocks, offsets))
    return result


def finish(state, heads, width):
    _, total, summed = state
    rows = summed.shape[0]
    return (summed / total[:, :, None]).reshape(rows, heads * width).astype(jnp.bfloat16)


def on_device_gather(
    video_in,
    audio_in,
    q_self,
    k_self,
    v_self,
    q_a2v,
    k_a2v,
    v_a2v,
    q_v2a,
    k_v2a,
    v_v2a,
    wo_self,
    wo_a2v,
    wo_v2a,
    video_gates,
    audio_gates,
    video_steps,
    audio_steps,
    audio_len,
):
    heads_self = q_self.shape[1] // DHV
    heads_cross = q_a2v.shape[1] // DHC
    rows_video = q_self.shape[0]
    rows_audio = q_v2a.shape[0]
    limit = audio_len[0]
    piece = (
        lax.all_gather(k_a2v, "seq", axis=0, tiled=True),
        lax.all_gather(v_a2v, "seq", axis=0, tiled=True),
    )
    a2v_state = update_state(
        start_state(rows_video, heads_cross, DHC),
        q_a2v,
        piece[0],
        piece[1],
        heads_cross,
        DHC,
        jnp.int32(0),
        limit,
    )
    a2v_att = finish(a2v_state, heads_cross, DHC)
    piece = (
        lax.all_gather(k_self, "seq", axis=0, tiled=True),
        lax.all_gather(v_self, "seq", axis=0, tiled=True),
    )
    self_state = update_state(
        start_state(rows_video, heads_self, DHV),
        q_self,
        piece[0],
        piece[1],
        heads_self,
        DHV,
        jnp.int32(0),
        None,
    )
    piece = (
        lax.all_gather(k_v2a, "seq", axis=0, tiled=True),
        lax.all_gather(v_v2a, "seq", axis=0, tiled=True),
    )
    v2a_state = update_state(
        start_state(rows_audio, heads_cross, DHC),
        q_v2a,
        piece[0],
        piece[1],
        heads_cross,
        DHC,
        jnp.int32(0),
        None,
    )
    self_att = finish(self_state, heads_self, DHV)
    v2a_att = finish(v2a_state, heads_cross, DHC)
    levels = jnp.arange(NT, dtype=jnp.int32)
    video_hot = (video_steps[:, None] == levels[None, :]).astype(jnp.bfloat16)
    video_gain = jnp.dot(video_hot, video_gates.reshape(NT, -1), preferred_element_type=jnp.float32)
    width_video = video_gates.shape[2]
    video_term = video_gain[:, :width_video] * jnp.dot(
        self_att, wo_self, preferred_element_type=jnp.float32
    )
    video_term = video_term + video_gain[:, width_video:] * jnp.dot(
        a2v_att, wo_a2v, preferred_element_type=jnp.float32
    )
    audio_hot = (audio_steps[:, None] == levels[None, :]).astype(jnp.bfloat16)
    audio_gain = jnp.dot(audio_hot, audio_gates, preferred_element_type=jnp.float32)
    positions = lax.axis_index("seq") * rows_audio + jnp.arange(rows_audio, dtype=jnp.int32)
    present = (positions < limit).astype(jnp.float32)
    audio_term = (
        present[:, None] * audio_gain * jnp.dot(v2a_att, wo_v2a, preferred_element_type=jnp.float32)
    )
    video_sum, audio_sum = (
        lax.psum_scatter(
            video_term.astype(jnp.bfloat16), ("mp", "sub"), scatter_dimension=1, tiled=True
        ).astype(jnp.float32),
        lax.psum_scatter(
            audio_term.astype(jnp.bfloat16), ("mp", "sub"), scatter_dimension=1, tiled=True
        ).astype(jnp.float32),
    )
    video_out = (video_in.astype(jnp.float32) + video_sum).astype(jnp.bfloat16)
    audio_out = (audio_in.astype(jnp.float32) + audio_sum).astype(jnp.bfloat16)
    return (video_out, audio_out)


LOG2E = 1.4426950408889634
VMEM = pl.BlockSpec(memory_space=pltpu.VMEM)
SMEM = pl.BlockSpec(memory_space=pltpu.SMEM)
HBM = pl.BlockSpec(memory_space=pltpu.HBM)
BF16, F32 = jnp.bfloat16, jnp.float32
LSE_ROWS = 16
LEAST = float(jnp.finfo(jnp.float32).min)
SEQ, FORWARDED, OUT_ORDER = 4, 3, [3, 2, 1]


def call(kernel, outs, operands, specs=None, flops=0, scratch=(), limit=8 * 2**20):
    size = sum(math.prod(x.shape) * x.dtype.itemsize for x in (*operands, *outs))
    if specs:
        operands = [
            pltpu.with_memory_space_constraint(x, pltpu.HBM) if spec is HBM else x for x, spec in zip(operands, specs)
        ]
    return pl.pallas_call(
        kernel,
        out_shape=tuple(outs),
        in_specs=specs or [VMEM] * len(operands),
        out_specs=tuple(VMEM for _ in outs),
        scratch_shapes=list(scratch),
        compiler_params=pltpu.CompilerParams(vmem_limit_bytes=limit),
        cost_estimate=pl.CostEstimate(flops=flops, bytes_accessed=size, transcendentals=0),
    )(*operands)


def shape(rows, cols, kind=BF16):
    return jax.ShapeDtypeStruct((rows, cols), kind)


def dot_t(a, b):
    return lax.dot_general(a, b, (((1,), (1,)), ((), ())), preferred_element_type=F32)


def dot(a, b):
    return jnp.dot(a, b, preferred_element_type=F32)


def index_of(axis):
    return lax.axis_index(axis).astype(jnp.int32)


def columns(index, width):
    return pl.ds(pl.multiple_of(index * width, width), width)


def copy_all(pairs, sems):
    copies = [pltpu.make_async_copy(src, dst, sems.at[i]) for i, (src, dst) in enumerate(pairs)]
    for copy in copies:
        copy.start()
    for copy in copies:
        copy.wait()


def pack_kernel(hops, width, q_ref, k_ref, v_ref, qa_ref, ka_ref, va_ref, *rest):
    outs, sems = rest[:-1], rest[-1]
    rows = q_ref.shape[0]
    rows_audio, cols_audio = qa_ref.shape
    me = index_of("seq")
    pairs = []
    for hop, out in zip(hops, outs):
        for i, ref in enumerate((q_ref, k_ref, v_ref)):
            pairs.append((ref.at[:, columns(me ^ hop, width)], out.at[pl.ds(i * rows, rows), :]))
        at = 3 * rows
        for ref in (qa_ref,) if hop == FORWARDED else (qa_ref, ka_ref, va_ref):
            for i in range(cols_audio // width):
                pairs.append((ref.at[:, pl.ds(i * width, width)], out.at[pl.ds(at, rows_audio), :]))
                at += rows_audio
    copy_all(pairs, sems)


def audio_block(ref, end, rows, cols, block):
    at, column = divmod(block * 128, ref.shape[1])
    top = ref.shape[0] - end * (cols // ref.shape[1]) * rows + at * rows
    return ref[top : top + rows, column : column + 128]


def one_hot_t(steps_ref):
    levels = lax.broadcasted_iota(jnp.int32, (NT, steps_ref.shape[1]), 0)
    return (levels == steps_ref[...]).astype(BF16)


def pick(hot_t, table):
    return lax.dot_general(hot_t, table, (((0,), (0,)), ((), ())), preferred_element_type=F32)


def fetch_kernel(limit_ref, vg_ref, *rest):
    count = (len(rest) - 9) // 2
    loads, gain_ref, audio_ref = rest[: count + 3], rest[count + 3], rest[count + 4]
    fetched, (vs_ref, as_ref, ag_ref, sems) = rest[count + 5 : -4], rest[-4:]
    copies = [
        pltpu.make_async_copy(src, dst, sems.at[i])
        for i, (src, dst) in enumerate(zip(loads, (vs_ref, as_ref, ag_ref, *fetched)))
    ]
    for copy in copies:
        copy.start()
    for copy in copies[:3]:
        copy.wait()
    hot_t = one_hot_t(vs_ref)
    piece = min(vg_ref.shape[1], 2048)
    for at in range(0, vg_ref.shape[1], piece):
        gain_ref[:, at : at + piece] = pick(hot_t, vg_ref[:, at : at + piece]).astype(BF16)
    rows_audio, narrow = audio_ref.shape
    part = index_of("mp") * 2 + index_of("sub")
    gain = pick(one_hot_t(as_ref), ag_ref[:, columns(part, narrow)])
    at = index_of("seq") * rows_audio + lax.broadcasted_iota(jnp.int32, (rows_audio, 1), 0)
    audio_ref[...] = jnp.where(at < limit_ref[0], gain, 0.0)
    for copy in copies[3:]:
        copy.wait()


def softmax_t(scores, scale, allowed=None):
    if allowed is not None:
        scores = [jnp.where(ok, x, LEAST) for ok, x in zip(allowed, scores)]
    peak = functools.reduce(jnp.maximum, [jnp.max(x, axis=0, keepdims=True) for x in scores])
    weights = [jnp.exp2((x - peak) * (scale * LOG2E)) for x in scores]
    total = functools.reduce(jnp.add, [jnp.sum(x, axis=0, keepdims=True) for x in weights])
    return peak, [x.astype(BF16) for x in weights], total


def turn(x):
    return x.astype(F32).T.astype(BF16)


def pair_rows(x, head):
    lane = lax.broadcasted_iota(jnp.int32, (1, 128), 1) // head
    return jnp.concatenate([jnp.where(lane == i, x, 0).astype(BF16) for i in range(128 // head)], axis=0)


def pair_columns(x, head):
    pair = 128 // head
    rows = x.shape[1] // pair
    return jnp.concatenate([x[i * head : (i + 1) * head, i * rows : (i + 1) * rows] for i in range(pair)], axis=0)


def attend_kernel(hops, head, kv_ref, vv_ref, *rest):
    n = len(hops)
    blocks, sends, (own_ref, own_v2a_ref, own_lse_ref) = rest[:n], rest[n : 2 * n - 1], rest[2 * n - 1 : 2 * n + 2]
    vt_ref, vvt_ref, s_ref, p_ref = rest[2 * n + 2 :]
    rows, cols = kv_ref.shape
    width = blocks[0].shape[1]
    rows_audio = own_v2a_ref.shape[0]
    ends = [1 if hop == FORWARDED else 3 for hop in hops]
    for h in range(width // DHV):
        cut = slice(h * DHV, (h + 1) * DHV)
        for i, ref in enumerate(blocks):
            vt_ref[cut, i * rows : (i + 1) * rows] = turn(ref[2 * rows : 3 * rows, cut])
    for block in range(cols // 128):
        cut = slice(block * 128, (block + 1) * 128)
        vvt_ref[cut, :] = turn(vv_ref[:, cut])
    pair, row = 128 // head, 0
    parts = []
    for block in range(cols // 128):
        cut = slice(block * 128, (block + 1) * 128)
        q = [audio_block(ref, end, rows_audio, cols, block) for ref, end in zip(blocks, ends)]
        q = pair_rows(jnp.concatenate(q, axis=0), head)
        scores = dot_t(kv_ref[:, cut], q)
        for i in range(pair):
            at = slice(i * n * rows_audio, (i + 1) * n * rows_audio)
            s_ref[row + i * rows : row + (i + 1) * rows, :] = scores[:, at]
            parts.append((row + i * rows, rows, jnp.max(scores[:, at], axis=0, keepdims=True), 1.0 / math.sqrt(head)))
        row += pair * rows
    for ref in blocks:
        for h in range(width // DHV):
            cut = slice(h * DHV, (h + 1) * DHV)
            peak = None
            for i, other in enumerate(blocks):
                scores = dot_t(other[rows : 2 * rows, cut], ref[0:rows, cut])
                s_ref[row + i * rows : row + (i + 1) * rows, :] = scores
                top = jnp.max(scores, axis=0, keepdims=True)
                peak = top if i == 0 else jnp.maximum(peak, top)
            parts.append((row, n * rows, peak, 1.0 / math.sqrt(DHV)))
            row += n * rows

    def weigh(part):
        start, count, peak, scale = part
        total = None
        for at in range(start, start + count, 128):
            p = jnp.exp2((s_ref[at : at + 128, :] - peak) * (scale * LOG2E))
            p_ref[at : at + 128, :] = p.astype(BF16)
            summed = jnp.sum(p, axis=0, keepdims=True)
            total = summed if at == start else total + summed
        return total

    lses, at = [], 0
    for block in range(cols // 128):
        both = []
        for i in range(pair):
            start, count, peak, scale = parts[at]
            total = weigh(parts[at])
            lses.append(peak * (scale * LOG2E) + jnp.log2(total))
            column = block * 128 + i * head
            o = dot(vvt_ref[column : column + head, :], p_ref[start : start + count, :])
            both.append(o * (1.0 / total))
            at += 1
        v2a = jnp.concatenate(both, axis=0).T
        own_v2a_ref[:, block * 128 : (block + 1) * 128] = v2a[0:rows_audio]
        for j, dst in enumerate(sends):
            top = rows + block * rows_audio
            dst[top : top + rows_audio, 0:128] = v2a[(j + 1) * rows_audio : (j + 2) * rows_audio].astype(BF16)
    for j in range(n):
        for h in range(width // DHV):
            cut = slice(h * DHV, (h + 1) * DHV)
            start, count, _, _ = parts[at]
            total = weigh(parts[at])
            o = dot(vt_ref[cut, :], p_ref[start : start + count, :]) * (1.0 / total)
            dst = own_ref if j == 0 else sends[j - 1].at[0:rows, :]
            dst[:, cut] = o.T.astype(BF16)
            at += 1
    relayed = 2 * cols // width * rows_audio
    dst, src = sends[hops.index(1) - 1], blocks[hops.index(FORWARDED ^ 1)]
    dst[dst.shape[0] - relayed :, :] = src[src.shape[0] - relayed :, :]
    heads = len(lses)
    lse = jnp.concatenate(lses, axis=0)
    own_lse_ref[...] = lse
    pieces, left = [], lse
    for _ in range(3):
        pieces.append(left.astype(BF16).astype(F32))
        left = left - pieces[-1]
    packed = jnp.concatenate(pieces + [jnp.zeros((LSE_ROWS - 3 * heads, lse.shape[1]), F32)], axis=0)
    for j, dst in enumerate(sends):
        top = rows + cols // 128 * rows_audio
        dst[top : top + LSE_ROWS, 0:128] = pltpu.roll(packed, 128 - (j + 1) * rows_audio, 1).astype(BF16)


def audio_allowed(hop, rows_audio, limit):
    row = lax.broadcasted_iota(jnp.int32, (rows_audio, 1), 0)
    return (index_of("seq") ^ hop) * rows_audio + row < limit


def spread(x, head):
    pair = 128 // head
    rows = x.shape[1] // pair
    parts = [jnp.broadcast_to(x[:, i * rows : (i + 1) * rows], (head, rows)) for i in range(pair)]
    return jnp.concatenate(parts, axis=0)


def attend_audio_kernel(hops, rows_audio, head, limit_ref, q_ref, *rest):
    blocks, part_ref, stats_ref = rest[:-2], rest[-2], rest[-1]
    cols = q_ref.shape[1]
    allowed = [audio_allowed(hop, rows_audio, limit_ref[0]) for hop in hops]
    scale = 1.0 / math.sqrt(head)
    for block in range(cols // 128):
        cut = slice(block * 128, (block + 1) * 128)
        q = pair_rows(q_ref[:, cut], head)
        scores = [dot_t(audio_block(ref, 2, rows_audio, cols, block), q) for ref in blocks]
        peak, p, total = softmax_t(scores, scale, allowed)
        vt = turn(jnp.concatenate([audio_block(ref, 1, rows_audio, cols, block) for ref in blocks], axis=0))
        part_ref[cut, :] = pair_columns(dot(vt, jnp.concatenate(p, axis=0)), head)
        stats_ref[2 * block : 2 * block + 1, :] = peak
        stats_ref[2 * block + 1 : 2 * block + 2, :] = total


def finish_audio(head, limit, q_ref, part_ref, stats_ref, last_ref, rows_audio, out_ref):
    cols = q_ref.shape[1]
    scale = 1.0 / math.sqrt(head)
    allowed = audio_allowed(FORWARDED, rows_audio, limit)
    for block in range(cols // 128):
        cut = slice(block * 128, (block + 1) * 128)
        q = pair_rows(q_ref[:, cut], head)
        scores = jnp.where(allowed, dot_t(audio_block(last_ref, 2, rows_audio, cols, block), q), LEAST)
        before, summed = stats_ref[2 * block : 2 * block + 1, :], stats_ref[2 * block + 1 : 2 * block + 2, :]
        peak = jnp.maximum(before, jnp.max(scores, axis=0, keepdims=True))
        factor = jnp.exp2((before - peak) * (scale * LOG2E))
        p = jnp.exp2((scores - peak) * (scale * LOG2E))
        inverse = 1.0 / (summed * factor + jnp.sum(p, axis=0, keepdims=True))
        vt = turn(audio_block(last_ref, 1, rows_audio, cols, block))
        last = pair_columns(dot(vt, p.astype(BF16)), head)
        both = part_ref[cut, :] * spread(factor, head) + last
        out_ref[:, cut] = (both * spread(inverse, head)).T.astype(BF16)


def merge_audio(head, top, v2a_ref, lse_ref, got, out_ref):
    rows_audio, cols = v2a_ref.shape
    heads = cols // head
    lses = [lse_ref[...]]
    for ref in got:
        at = top + cols // 128 * rows_audio
        packed = ref[at : at + LSE_ROWS, 0:128].astype(F32)
        lses.append(packed[0:heads] + packed[heads : 2 * heads] + packed[2 * heads : 3 * heads])
    peak = functools.reduce(jnp.maximum, lses)
    parts = [jnp.exp2(x - peak) for x in lses]
    total = functools.reduce(jnp.add, parts)
    inverse = 1.0 / total
    parts = [x * inverse for x in parts]
    parts.append(jnp.zeros((128 - len(parts) * heads, 128), F32))
    shares = jnp.concatenate(parts, axis=0).T[0:rows_audio]
    pair = 128 // head
    lane = lax.broadcasted_iota(jnp.int32, (1, 128), 1) // head
    for block in range(cols // 128):
        cut = slice(block * 128, (block + 1) * 128)
        at = top + block * rows_audio
        summed = jnp.zeros((rows_audio, 128), F32)
        for j in range(len(lses)):
            o = v2a_ref[:, cut] if j == 0 else got[j - 1][at : at + rows_audio, 0:128].astype(F32)
            share = jnp.zeros((rows_audio, 128), F32)
            for i in range(pair):
                column = j * heads + block * pair + i
                share = jnp.where(lane == i, shares[:, column : column + 1], share)
            summed = summed + share * o
        out_ref[:, cut] = summed.astype(BF16)


def block_of(far, other):
    mp, sub = index_of("mp"), index_of("sub")
    return (1 - mp if far else mp) * 2 + (1 - sub if other else sub)


def project(block, half, heads, weights, gain_ref):
    (att_ref, a2v_ref), (ws_ref, wa_ref) = heads, weights
    wide = ws_ref.shape[1]
    cut = wide // 8
    at = columns(block * 2 + half, cut)
    term = gain_ref[:, at].astype(F32) * dot(att_ref[...], ws_ref[:, at])
    gain = gain_ref[:, columns(block * 2 + half + 8, cut)].astype(F32)
    return term + gain * dot(a2v_ref[...], wa_ref[:, at])


def project_audio(block, v2a_ref, wv_ref):
    return dot(v2a_ref[...], wv_ref[:, columns(block, wv_ref.shape[1] // 4)])


def first_kernel(hops, rows_audio, head, limit_ref, q_ref, part_ref, stats_ref, own_ref, ws_ref, wa_ref, gain_ref, *rest):
    got, (self_ref, a2v_ref, out_ref) = rest[: len(hops) - 1], rest[len(hops) - 1 :]
    rows, width = own_ref.shape
    last_ref = got[hops.index(1) - 1]
    finish_audio(head, limit_ref[0], q_ref, part_ref, stats_ref, last_ref, rows_audio, a2v_ref)
    me = index_of("seq")
    self_ref[:, columns(me, width)] = own_ref[...]
    for hop, ref in zip(hops[1:], got):
        self_ref[:, columns(me ^ hop, width)] = ref[0:rows, :]
    out_ref[...] = project(block_of(True, True), 0, (self_ref, a2v_ref), (ws_ref, wa_ref), gain_ref).astype(BF16)


def second_kernel(head, self_ref, a2v_ref, ws_ref, wa_ref, wv_ref, gain_ref, v2a_ref, lse_ref, *rest):
    got, (out_ref, audio_ref, low_ref) = rest[:-3], rest[-3:]
    rows = self_ref.shape[0]
    block = block_of(True, True)
    out_ref[0:rows, :] = project(block, 1, (self_ref, a2v_ref), (ws_ref, wa_ref), gain_ref).astype(BF16)
    merge_audio(head, rows, v2a_ref, lse_ref, got, audio_ref)
    out_ref[rows:, :] = project_audio(block, audio_ref, wv_ref).astype(BF16)
    low_ref[...] = project(block_of(True, False), 0, (self_ref, a2v_ref), (ws_ref, wa_ref), gain_ref)


def far_low_kernel(low_ref, extra_ref, out_ref):
    out_ref[...] = (low_ref[...] + extra_ref[...].astype(F32)).astype(BF16)


def near_kernel(self_ref, a2v_ref, audio_ref, ws_ref, wa_ref, wv_ref, gain_ref, send_ref, own_ref):
    rows = self_ref.shape[0]
    for out, other in ((send_ref, True), (own_ref, False)):
        block = block_of(False, other)
        for half in range(2):
            term = project(block, half, (self_ref, a2v_ref), (ws_ref, wa_ref), gain_ref)
            out[half * rows : (half + 1) * rows, :] = term.astype(out.dtype)
        out[2 * rows :, :] = project_audio(block, audio_ref, wv_ref).astype(out.dtype)


def far_high_kernel(self_ref, a2v_ref, ws_ref, wa_ref, gain_ref, extra_ref, audio_ref, wv_ref, out_ref):
    rows = self_ref.shape[0]
    block = block_of(True, False)
    term = project(block, 1, (self_ref, a2v_ref), (ws_ref, wa_ref), gain_ref)
    out_ref[0:rows, :] = (term + extra_ref[0:rows, :].astype(F32)).astype(BF16)
    term = project_audio(block, audio_ref, wv_ref)
    out_ref[rows:, :] = (term + extra_ref[rows:, :].astype(F32)).astype(BF16)


def finish_kernel(video_ref, audio_ref, gain_ref, own_ref, core_ref, low_ref, high_ref, video_out, audio_out):
    rows = video_ref.shape[0]
    cut = video_ref.shape[1] // 2
    near = own_ref[...] + core_ref[...].astype(F32)
    for half, ref in enumerate((low_ref, high_ref)):
        at = slice(half * cut, (half + 1) * cut)
        term = near[half * rows : (half + 1) * rows] + ref[0:rows, :].astype(F32)
        video_out[:, at] = (video_ref[:, at].astype(F32) + term).astype(BF16)
    term = near[2 * rows :] + high_ref[rows:, :].astype(F32)
    audio_out[...] = (audio_ref[...].astype(F32) + gain_ref[...] * term).astype(BF16)


def on_device_heads(
    video_in,
    audio_in,
    q_self,
    k_self,
    v_self,
    q_a2v,
    k_a2v,
    v_a2v,
    q_v2a,
    k_v2a,
    v_v2a,
    wo_self,
    wo_a2v,
    wo_v2a,
    video_gates,
    audio_gates,
    video_steps,
    audio_steps,
    audio_len,
    *,
    n,
):
    hops = [0] + OUT_ORDER
    rows, cols = q_self.shape
    rows_audio, cross = q_v2a.shape
    width = cols // n

    def trade(x, axis, hop, size):
        return lax.ppermute(x, axis, [(i, i ^ hop) for i in range(size)])

    video, audio = 3 * rows, cross // width * rows_audio

    def pack(some):
        ends = [1 if hop == FORWARDED else 3 for hop in some]
        return call(
            functools.partial(pack_kernel, some, width),
            [shape(video + end * audio, width) for end in ends],
            (q_self, k_self, v_self, q_v2a, k_a2v, v_a2v),
            [HBM] * 6,
            scratch=[pltpu.SemaphoreType.DMA((3 * len(some) + sum(ends) * audio // rows_audio,))],
        )

    packed = pack(hops[1:2])
    rest = pack(hops[:1] + hops[2:])
    packed = [rest[0], *packed, *rest[1:]]
    blocks = dict(zip(hops, packed))
    for hop in hops[1:]:
        blocks[hop] = trade(blocks[hop], "seq", hop, n)

    late = (k_v2a, v_v2a, q_a2v, wo_self, wo_a2v, wo_v2a, video_in, audio_in)
    steps = (video_steps.reshape(1, rows), audio_steps.reshape(1, rows_audio))
    gain, audio_gain, k_own, v_own, q_own, ws, wa, wv, video_own, audio_own = call(
        fetch_kernel,
        [shape(rows, 2 * video_gates.shape[2]), shape(*audio_in.shape, F32)]
        + [shape(*x.shape) for x in late],
        (audio_len, video_gates.reshape(NT, -1), *steps, audio_gates, *late),
        [SMEM, VMEM] + [HBM] * (3 + len(late)),
        scratch=[pltpu.VMEM(x.shape, x.dtype) for x in (*steps, audio_gates)]
        + [pltpu.SemaphoreType.DMA((3 + len(late),))],
    )
    back = rows + cross // 128 * rows_audio + LSE_ROWS
    result = call(
        functools.partial(attend_kernel, hops, DHC),
        [shape(back + 2 * audio if hop == 1 else back, width) for hop in hops[1:]]
        + [shape(rows, width), shape(rows_audio, cross, F32), shape(cross // DHC, 128, F32)],
        (k_own, v_own, *blocks.values()),
        flops=4 * n * n * rows * rows * width,
        scratch=[pltpu.VMEM((width, n * rows), BF16), pltpu.VMEM((cross, rows), BF16)]
        + [pltpu.VMEM((n * n * rows * width // DHV + cross // DHC * rows, 128), kind) for kind in (F32, BF16)],
    )
    sends, (own, own_v2a, own_lse) = result[: n - 1], result[n - 1 :]
    got = [trade(x, "seq", hop, n) for x, hop in zip(sends, hops[1:])]
    near = [hop for hop in hops if hop != FORWARDED]
    a2v_part, a2v_stats = call(
        functools.partial(attend_audio_kernel, near, rows_audio, DHC),
        [shape(cross, rows, F32), shape(cross // 64, 128 // DHC * rows, F32)],
        (audio_len, q_own, *(blocks[hop] for hop in near)),
        [SMEM] + [VMEM] * n,
        flops=8 * n * rows * rows_audio * cross,
    )

    half = video_in.shape[1] // 2
    flops = 2 * rows * (cols + cross) * half
    self_att, a2v_att, first = call(
        functools.partial(first_kernel, hops, rows_audio, DHC),
        [shape(rows, cols), shape(rows, cross), shape(rows, half)],
        (audio_len, q_own, a2v_part, a2v_stats, own, ws, wa, gain, *got),
        [SMEM] + [VMEM] * (n + 6),
        flops=flops,
    )
    first = trade(first, "sub", 1, 2)
    second, v2a_att, own_low = call(
        functools.partial(second_kernel, DHC),
        [shape(rows + rows_audio, half), shape(rows_audio, cross), shape(rows, half, F32)],
        (self_att, a2v_att, ws, wa, wv, gain, own_v2a, own_lse, *got),
        flops=2 * flops,
    )
    second = trade(second, "sub", 1, 2)
    (low,) = call(far_low_kernel, [shape(rows, half)], (own_low, first))
    low = trade(low, "mp", 1, 2)
    (high,) = call(
        far_high_kernel,
        [shape(rows + rows_audio, half)],
        (self_att, a2v_att, ws, wa, gain, second, v2a_att, wv),
        flops=flops,
    )
    high = trade(high, "mp", 1, 2)
    near, own_sum = call(
        near_kernel,
        [shape(2 * rows + rows_audio, half), shape(2 * rows + rows_audio, half, F32)],
        (self_att, a2v_att, v2a_att, ws, wa, wv, gain),
        flops=4 * flops,
    )
    near = trade(near, "sub", 1, 2)
    return call(
        finish_kernel,
        [shape(*video_in.shape), shape(*audio_in.shape)],
        (video_own, audio_own, audio_gain, own_sum, near, low, high),
    )


def on_device(n, mp, sub, *arrays):
    cols, cross = arrays[2].shape[1], arrays[5].shape[1]
    width = cols // n
    fits = (
        n == SEQ
        and (mp, sub) == (2, 2)
        and width % DHV == 0
        and cross % width == 0
        and 3 * (cross // DHC) <= LSE_ROWS
        and n * arrays[8].shape[0] == arrays[2].shape[0] == 128
        and arrays[0].shape[1] == 2 * arrays[1].shape[1]
    )
    if fits:
        return on_device_heads(*arrays, n=n)
    return on_device_gather(*arrays)


def solution(mesh):
    in_specs = (
        P(("groups", "seq"), ("mp", "sub")),
        P(("groups", "seq"), ("mp", "sub")),
        P(("groups", "seq"), ("mp", "sub")),
        P(("groups", "seq"), ("mp", "sub")),
        P(("groups", "seq"), ("mp", "sub")),
        P(("groups", "seq"), ("mp", "sub")),
        P(("groups", "seq"), ("mp", "sub")),
        P(("groups", "seq"), ("mp", "sub")),
        P(("groups", "seq"), ("mp", "sub")),
        P(("groups", "seq"), ("mp", "sub")),
        P(("groups", "seq"), ("mp", "sub")),
        P(("mp", "sub"), None),
        P(("mp", "sub"), None),
        P(("mp", "sub"), None),
        P(),
        P(),
        P(("groups", "seq")),
        P(("groups", "seq")),
        P("groups"),
    )
    out_specs = (P(("groups", "seq"), ("mp", "sub")), P(("groups", "seq"), ("mp", "sub")))
    return jax.shard_map(
        functools.partial(on_device, *(mesh.shape[a] for a in ("seq", "mp", "sub"))), mesh=mesh, in_specs=in_specs, out_specs=out_specs, check_vma=False
    )
```

```python
import functools
import math

import jax
import jax.numpy as jnp
from jax import lax
from jax.experimental import pallas as pl
from jax.experimental.pallas import tpu as pltpu
from jax.sharding import PartitionSpec as P


DHV = 128
DHC = 64
NT = 16


def start_state(rows, heads, width):
    return (
        jnp.full((rows, heads), -1e30, jnp.float32),
        jnp.zeros((rows, heads), jnp.float32),
        jnp.zeros((rows, heads, width), jnp.float32),
    )


def update_block(state, queries, keys, values, heads, width, allowed):
    rows = queries.shape[0]
    count = keys.shape[0]
    q_heads = queries.reshape(rows, heads, width)
    k_heads = keys.reshape(count, heads, width)
    v_heads = values.reshape(count, heads, width)
    scores = jnp.einsum(
        "qhd,khd->qhk", q_heads, k_heads, preferred_element_type=jnp.float32
    ) / math.sqrt(width)
    if allowed is not None:
        scores = jnp.where(allowed[None, None, :], scores, -jnp.inf)
    peak_old, total_old, summed_old = state
    peak = jnp.maximum(peak_old, jnp.max(scores, axis=2))
    weights = jnp.exp(scores - peak[:, :, None])
    factor = jnp.exp(peak_old - peak)
    total = total_old * factor + jnp.sum(weights, axis=2)
    summed = summed_old * factor[:, :, None] + jnp.einsum(
        "qhk,khd->qhd", weights.astype(jnp.bfloat16), v_heads, preferred_element_type=jnp.float32
    )
    return (peak, total, summed)


def update_state(state, queries, keys, values, heads, width, start, limit):
    count = keys.shape[0]
    block = 1024 if count > 1024 and count % 1024 == 0 else count
    if block == count:
        allowed = None
        if limit is not None:
            allowed = jnp.arange(count, dtype=jnp.int32) < limit
        return update_block(state, queries, keys, values, heads, width, allowed)
    steps = count // block
    key_blocks = keys.reshape(steps, block, keys.shape[1])
    value_blocks = values.reshape(steps, block, values.shape[1])
    offsets = jnp.arange(steps, dtype=jnp.int32) * block

    def one_block(carry, items):
        key_rows, value_rows, offset = items
        allowed = None
        if limit is not None:
            allowed = start + offset + jnp.arange(block, dtype=jnp.int32) < limit
        return (update_block(carry, queries, key_rows, value_rows, heads, width, allowed), None)

    result, _ = lax.scan(one_block, state, (key_blocks, value_blocks, offsets))
    return result


def finish(state, heads, width):
    _, total, summed = state
    rows = summed.shape[0]
    return (summed / total[:, :, None]).reshape(rows, heads * width).astype(jnp.bfloat16)


def on_device_gather(
    video_in,
    audio_in,
    q_self,
    k_self,
    v_self,
    q_a2v,
    k_a2v,
    v_a2v,
    q_v2a,
    k_v2a,
    v_v2a,
    wo_self,
    wo_a2v,
    wo_v2a,
    video_gates,
    audio_gates,
    video_steps,
    audio_steps,
    audio_len,
):
    heads_self = q_self.shape[1] // DHV
    heads_cross = q_a2v.shape[1] // DHC
    rows_video = q_self.shape[0]
    rows_audio = q_v2a.shape[0]
    limit = audio_len[0]
    piece = (
        lax.all_gather(k_a2v, "seq", axis=0, tiled=True),
        lax.all_gather(v_a2v, "seq", axis=0, tiled=True),
    )
    a2v_state = update_state(
        start_state(rows_video, heads_cross, DHC),
        q_a2v,
        piece[0],
        piece[1],
        heads_cross,
        DHC,
        jnp.int32(0),
        limit,
    )
    a2v_att = finish(a2v_state, heads_cross, DHC)
    piece = (
        lax.all_gather(k_self, "seq", axis=0, tiled=True),
        lax.all_gather(v_self, "seq", axis=0, tiled=True),
    )
    self_state = update_state(
        start_state(rows_video, heads_self, DHV),
        q_self,
        piece[0],
        piece[1],
        heads_self,
        DHV,
        jnp.int32(0),
        None,
    )
    piece = (
        lax.all_gather(k_v2a, "seq", axis=0, tiled=True),
        lax.all_gather(v_v2a, "seq", axis=0, tiled=True),
    )
    v2a_state = update_state(
        start_state(rows_audio, heads_cross, DHC),
        q_v2a,
        piece[0],
        piece[1],
        heads_cross,
        DHC,
        jnp.int32(0),
        None,
    )
    self_att = finish(self_state, heads_self, DHV)
    v2a_att = finish(v2a_state, heads_cross, DHC)
    levels = jnp.arange(NT, dtype=jnp.int32)
    video_hot = (video_steps[:, None] == levels[None, :]).astype(jnp.bfloat16)
    video_gain = jnp.dot(video_hot, video_gates.reshape(NT, -1), preferred_element_type=jnp.float32)
    width_video = video_gates.shape[2]
    video_term = video_gain[:, :width_video] * jnp.dot(
        self_att, wo_self, preferred_element_type=jnp.float32
    )
    video_term = video_term + video_gain[:, width_video:] * jnp.dot(
        a2v_att, wo_a2v, preferred_element_type=jnp.float32
    )
    audio_hot = (audio_steps[:, None] == levels[None, :]).astype(jnp.bfloat16)
    audio_gain = jnp.dot(audio_hot, audio_gates, preferred_element_type=jnp.float32)
    positions = lax.axis_index("seq") * rows_audio + jnp.arange(rows_audio, dtype=jnp.int32)
    present = (positions < limit).astype(jnp.float32)
    audio_term = (
        present[:, None] * audio_gain * jnp.dot(v2a_att, wo_v2a, preferred_element_type=jnp.float32)
    )
    video_sum, audio_sum = (
        lax.psum_scatter(
            video_term.astype(jnp.bfloat16), ("mp", "sub"), scatter_dimension=1, tiled=True
        ).astype(jnp.float32),
        lax.psum_scatter(
            audio_term.astype(jnp.bfloat16), ("mp", "sub"), scatter_dimension=1, tiled=True
        ).astype(jnp.float32),
    )
    video_out = (video_in.astype(jnp.float32) + video_sum).astype(jnp.bfloat16)
    audio_out = (audio_in.astype(jnp.float32) + audio_sum).astype(jnp.bfloat16)
    return (video_out, audio_out)


LOG2E = 1.4426950408889634
VMEM = pl.BlockSpec(memory_space=pltpu.VMEM)
SMEM = pl.BlockSpec(memory_space=pltpu.SMEM)
HBM = pl.BlockSpec(memory_space=pltpu.HBM)
BF16, F32 = jnp.bfloat16, jnp.float32
LSE_ROWS = 16
LEAST = float(jnp.finfo(jnp.float32).min)
SEQ, FORWARDED, OUT_ORDER = 4, 3, [3, 2, 1]


def call(kernel, outs, operands, specs=None, flops=0, scratch=(), limit=8 * 2**20):
    size = sum(math.prod(x.shape) * x.dtype.itemsize for x in (*operands, *outs))
    if specs:
        operands = [
            pltpu.with_memory_space_constraint(x, pltpu.HBM) if spec is HBM else x for x, spec in zip(operands, specs)
        ]
    return pl.pallas_call(
        kernel,
        out_shape=tuple(outs),
        in_specs=specs or [VMEM] * len(operands),
        out_specs=tuple(VMEM for _ in outs),
        scratch_shapes=list(scratch),
        compiler_params=pltpu.CompilerParams(vmem_limit_bytes=limit),
        cost_estimate=pl.CostEstimate(flops=flops, bytes_accessed=size, transcendentals=0),
    )(*operands)


def shape(rows, cols, kind=BF16):
    return jax.ShapeDtypeStruct((rows, cols), kind)


def dot_t(a, b):
    return lax.dot_general(a, b, (((1,), (1,)), ((), ())), preferred_element_type=F32)


def dot(a, b):
    return jnp.dot(a, b, preferred_element_type=F32)


def index_of(axis):
    return lax.axis_index(axis).astype(jnp.int32)


def columns(index, width):
    return pl.ds(pl.multiple_of(index * width, width), width)


def copy_all(pairs, sems):
    copies = [pltpu.make_async_copy(src, dst, sems.at[i]) for i, (src, dst) in enumerate(pairs)]
    for copy in copies:
        copy.start()
    for copy in copies:
        copy.wait()


def pack_kernel(hops, width, q_ref, k_ref, v_ref, qa_ref, ka_ref, va_ref, *rest):
    outs, sems = rest[:-1], rest[-1]
    rows = q_ref.shape[0]
    rows_audio, cols_audio = qa_ref.shape
    me = index_of("seq")
    pairs = []
    for hop, out in zip(hops, outs):
        for i, ref in enumerate((q_ref, k_ref, v_ref)):
            pairs.append((ref.at[:, columns(me ^ hop, width)], out.at[pl.ds(i * rows, rows), :]))
        at = 3 * rows
        for ref in (qa_ref,) if hop == FORWARDED else (qa_ref, ka_ref, va_ref):
            for i in range(cols_audio // width):
                pairs.append((ref.at[:, pl.ds(i * width, width)], out.at[pl.ds(at, rows_audio), :]))
                at += rows_audio
    copy_all(pairs, sems)


def audio_block(ref, end, rows, cols, block):
    at, column = divmod(block * 128, ref.shape[1])
    top = ref.shape[0] - end * (cols // ref.shape[1]) * rows + at * rows
    return ref[top : top + rows, column : column + 128]


def one_hot_t(steps_ref):
    levels = lax.broadcasted_iota(jnp.int32, (NT, steps_ref.shape[1]), 0)
    return (levels == steps_ref[...]).astype(BF16)


def pick(hot_t, table):
    return lax.dot_general(hot_t, table, (((0,), (0,)), ((), ())), preferred_element_type=F32)


def fetch_kernel(limit_ref, vg_ref, *rest):
    count = (len(rest) - 9) // 2
    loads, gain_ref, audio_ref = rest[: count + 3], rest[count + 3], rest[count + 4]
    fetched, (vs_ref, as_ref, ag_ref, sems) = rest[count + 5 : -4], rest[-4:]
    copies = [
        pltpu.make_async_copy(src, dst, sems.at[i])
        for i, (src, dst) in enumerate(zip(loads, (vs_ref, as_ref, ag_ref, *fetched)))
    ]
    for copy in copies:
        copy.start()
    for copy in copies[:3]:
        copy.wait()
    hot_t = one_hot_t(vs_ref)
    piece = min(vg_ref.shape[1], 2048)
    for at in range(0, vg_ref.shape[1], piece):
        gain_ref[:, at : at + piece] = pick(hot_t, vg_ref[:, at : at + piece]).astype(BF16)
    rows_audio, narrow = audio_ref.shape
    part = index_of("mp") * 2 + index_of("sub")
    gain = pick(one_hot_t(as_ref), ag_ref[:, columns(part, narrow)])
    at = index_of("seq") * rows_audio + lax.broadcasted_iota(jnp.int32, (rows_audio, 1), 0)
    audio_ref[...] = jnp.where(at < limit_ref[0], gain, 0.0)
    for copy in copies[3:]:
        copy.wait()


def softmax_t(scores, scale, allowed=None):
    if allowed is not None:
        scores = [jnp.where(ok, x, LEAST) for ok, x in zip(allowed, scores)]
    peak = functools.reduce(jnp.maximum, [jnp.max(x, axis=0, keepdims=True) for x in scores])
    weights = [jnp.exp2((x - peak) * (scale * LOG2E)) for x in scores]
    total = functools.reduce(jnp.add, [jnp.sum(x, axis=0, keepdims=True) for x in weights])
    return peak, [x.astype(BF16) for x in weights], total


def turn(x):
    return x.astype(F32).T.astype(BF16)


def pair_rows(x, head):
    lane = lax.broadcasted_iota(jnp.int32, (1, 128), 1) // head
    return jnp.concatenate([jnp.where(lane == i, x, 0).astype(BF16) for i in range(128 // head)], axis=0)


def pair_columns(x, head):
    pair = 128 // head
    rows = x.shape[1] // pair
    return jnp.concatenate([x[i * head : (i + 1) * head, i * rows : (i + 1) * rows] for i in range(pair)], axis=0)


def attend_kernel(hops, head, kv_ref, vv_ref, *rest):
    n = len(hops)
    blocks, sends, (own_ref, own_v2a_ref, own_lse_ref) = rest[:n], rest[n : 2 * n - 1], rest[2 * n - 1 : 2 * n + 2]
    vt_ref, vvt_ref, s_ref, p_ref = rest[2 * n + 2 :]
    rows, cols = kv_ref.shape
    width = blocks[0].shape[1]
    rows_audio = own_v2a_ref.shape[0]
    ends = [1 if hop == FORWARDED else 3 for hop in hops]
    for h in range(width // DHV):
        cut = slice(h * DHV, (h + 1) * DHV)
        for i, ref in enumerate(blocks):
            vt_ref[cut, i * rows : (i + 1) * rows] = turn(ref[2 * rows : 3 * rows, cut])
    for block in range(cols // 128):
        cut = slice(block * 128, (block + 1) * 128)
        vvt_ref[cut, :] = turn(vv_ref[:, cut])
    pair, row = 128 // head, 0
    parts = []
    for block in range(cols // 128):
        cut = slice(block * 128, (block + 1) * 128)
        q = [audio_block(ref, end, rows_audio, cols, block) for ref, end in zip(blocks, ends)]
        q = pair_rows(jnp.concatenate(q, axis=0), head)
        scores = dot_t(kv_ref[:, cut], q)
        for i in range(pair):
            at = slice(i * n * rows_audio, (i + 1) * n * rows_audio)
            s_ref[row + i * rows : row + (i + 1) * rows, :] = scores[:, at]
            parts.append((row + i * rows, rows, jnp.max(scores[:, at], axis=0, keepdims=True), 1.0 / math.sqrt(head)))
        row += pair * rows
    for ref in blocks:
        for h in range(width // DHV):
            cut = slice(h * DHV, (h + 1) * DHV)
            peak = None
            for i, other in enumerate(blocks):
                scores = dot_t(other[rows : 2 * rows, cut], ref[0:rows, cut])
                s_ref[row + i * rows : row + (i + 1) * rows, :] = scores
                top = jnp.max(scores, axis=0, keepdims=True)
                peak = top if i == 0 else jnp.maximum(peak, top)
            parts.append((row, n * rows, peak, 1.0 / math.sqrt(DHV)))
            row += n * rows

    def weigh(part):
        start, count, peak, scale = part
        total = None
        for at in range(start, start + count, 128):
            p = jnp.exp2((s_ref[at : at + 128, :] - peak) * (scale * LOG2E))
            p_ref[at : at + 128, :] = p.astype(BF16)
            summed = jnp.sum(p, axis=0, keepdims=True)
            total = summed if at == start else total + summed
        return total

    lses, at = [], 0
    for block in range(cols // 128):
        both = []
        for i in range(pair):
            start, count, peak, scale = parts[at]
            total = weigh(parts[at])
            lses.append(peak * (scale * LOG2E) + jnp.log2(total))
            column = block * 128 + i * head
            o = dot(vvt_ref[column : column + head, :], p_ref[start : start + count, :])
            both.append(o * (1.0 / total))
            at += 1
        v2a = jnp.concatenate(both, axis=0).T
        own_v2a_ref[:, block * 128 : (block + 1) * 128] = v2a[0:rows_audio]
        for j, dst in enumerate(sends):
            top = rows + block * rows_audio
            dst[top : top + rows_audio, 0:128] = v2a[(j + 1) * rows_audio : (j + 2) * rows_audio].astype(BF16)
    for j in range(n):
        for h in range(width // DHV):
            cut = slice(h * DHV, (h + 1) * DHV)
            start, count, _, _ = parts[at]
            total = weigh(parts[at])
            o = dot(vt_ref[cut, :], p_ref[start : start + count, :]) * (1.0 / total)
            dst = own_ref if j == 0 else sends[j - 1].at[0:rows, :]
            dst[:, cut] = o.T.astype(BF16)
            at += 1
    relayed = 2 * cols // width * rows_audio
    dst, src = sends[hops.index(1) - 1], blocks[hops.index(FORWARDED ^ 1)]
    dst[dst.shape[0] - relayed :, :] = src[src.shape[0] - relayed :, :]
    heads = len(lses)
    lse = jnp.concatenate(lses, axis=0)
    own_lse_ref[...] = lse
    pieces, left = [], lse
    for _ in range(3):
        pieces.append(left.astype(BF16).astype(F32))
        left = left - pieces[-1]
    packed = jnp.concatenate(pieces + [jnp.zeros((LSE_ROWS - 3 * heads, lse.shape[1]), F32)], axis=0)
    for j, dst in enumerate(sends):
        top = rows + cols // 128 * rows_audio
        dst[top : top + LSE_ROWS, 0:128] = pltpu.roll(packed, 128 - (j + 1) * rows_audio, 1).astype(BF16)


def audio_allowed(hop, rows_audio, limit):
    row = lax.broadcasted_iota(jnp.int32, (rows_audio, 1), 0)
    return (index_of("seq") ^ hop) * rows_audio + row < limit


def spread(x, head):
    pair = 128 // head
    rows = x.shape[1] // pair
    parts = [jnp.broadcast_to(x[:, i * rows : (i + 1) * rows], (head, rows)) for i in range(pair)]
    return jnp.concatenate(parts, axis=0)


def attend_audio_kernel(hops, rows_audio, head, limit_ref, q_ref, *rest):
    blocks, part_ref, stats_ref = rest[:-2], rest[-2], rest[-1]
    cols = q_ref.shape[1]
    allowed = [audio_allowed(hop, rows_audio, limit_ref[0]) for hop in hops]
    scale = 1.0 / math.sqrt(head)
    for block in range(cols // 128):
        cut = slice(block * 128, (block + 1) * 128)
        q = pair_rows(q_ref[:, cut], head)
        scores = [dot_t(audio_block(ref, 2, rows_audio, cols, block), q) for ref in blocks]
        peak, p, total = softmax_t(scores, scale, allowed)
        vt = turn(jnp.concatenate([audio_block(ref, 1, rows_audio, cols, block) for ref in blocks], axis=0))
        part_ref[cut, :] = pair_columns(dot(vt, jnp.concatenate(p, axis=0)), head)
        stats_ref[2 * block : 2 * block + 1, :] = peak
        stats_ref[2 * block + 1 : 2 * block + 2, :] = total


def finish_audio(head, limit, q_ref, part_ref, stats_ref, last_ref, rows_audio, out_ref):
    cols = q_ref.shape[1]
    scale = 1.0 / math.sqrt(head)
    allowed = audio_allowed(FORWARDED, rows_audio, limit)
    for block in range(cols // 128):
        cut = slice(block * 128, (block + 1) * 128)
        q = pair_rows(q_ref[:, cut], head)
        scores = jnp.where(allowed, dot_t(audio_block(last_ref, 2, rows_audio, cols, block), q), LEAST)
        before, summed = stats_ref[2 * block : 2 * block + 1, :], stats_ref[2 * block + 1 : 2 * block + 2, :]
        peak = jnp.maximum(before, jnp.max(scores, axis=0, keepdims=True))
        factor = jnp.exp2((before - peak) * (scale * LOG2E))
        p = jnp.exp2((scores - peak) * (scale * LOG2E))
        inverse = 1.0 / (summed * factor + jnp.sum(p, axis=0, keepdims=True))
        vt = turn(audio_block(last_ref, 1, rows_audio, cols, block))
        last = pair_columns(dot(vt, p.astype(BF16)), head)
        both = part_ref[cut, :] * spread(factor, head) + last
        out_ref[:, cut] = (both * spread(inverse, head)).T.astype(BF16)


def merge_audio(head, top, v2a_ref, lse_ref, got, out_ref):
    rows_audio, cols = v2a_ref.shape
    heads = cols // head
    lses = [lse_ref[...]]
    for ref in got:
        at = top + cols // 128 * rows_audio
        packed = ref[at : at + LSE_ROWS, 0:128].astype(F32)
        lses.append(packed[0:heads] + packed[heads : 2 * heads] + packed[2 * heads : 3 * heads])
    peak = functools.reduce(jnp.maximum, lses)
    parts = [jnp.exp2(x - peak) for x in lses]
    total = functools.reduce(jnp.add, parts)
    inverse = 1.0 / total
    parts = [x * inverse for x in parts]
    parts.append(jnp.zeros((128 - len(parts) * heads, 128), F32))
    shares = jnp.concatenate(parts, axis=0).T[0:rows_audio]
    pair = 128 // head
    lane = lax.broadcasted_iota(jnp.int32, (1, 128), 1) // head
    for block in range(cols // 128):
        cut = slice(block * 128, (block + 1) * 128)
        at = top + block * rows_audio
        summed = jnp.zeros((rows_audio, 128), F32)
        for j in range(len(lses)):
            o = v2a_ref[:, cut] if j == 0 else got[j - 1][at : at + rows_audio, 0:128].astype(F32)
            share = jnp.zeros((rows_audio, 128), F32)
            for i in range(pair):
                column = j * heads + block * pair + i
                share = jnp.where(lane == i, shares[:, column : column + 1], share)
            summed = summed + share * o
        out_ref[:, cut] = summed.astype(BF16)


def block_of(far, other):
    mp, sub = index_of("mp"), index_of("sub")
    return (1 - mp if far else mp) * 2 + (1 - sub if other else sub)


def project_self(block, half, att_ref, ws_ref, gain_ref):
    cut = ws_ref.shape[1] // 8
    at = columns(block * 2 + half, cut)
    return gain_ref[:, at].astype(F32) * dot(att_ref[...], ws_ref[:, at])


def project_a2v(block, half, a2v_ref, wa_ref, gain_ref):
    cut = wa_ref.shape[1] // 8
    gain = gain_ref[:, columns(block * 2 + half + 8, cut)].astype(F32)
    return gain * dot(a2v_ref[...], wa_ref[:, columns(block * 2 + half, cut)])


def project(block, half, heads, weights, gain_ref):
    term = project_self(block, half, heads[0], weights[0], gain_ref)
    return term + project_a2v(block, half, heads[1], weights[1], gain_ref)


def project_audio(block, v2a_ref, wv_ref):
    return dot(v2a_ref[...], wv_ref[:, columns(block, wv_ref.shape[1] // 4)])


def first_kernel(hops, rows_audio, head, limit_ref, q_ref, part_ref, stats_ref, own_ref, ws_ref, wa_ref, gain_ref, *rest):
    got, (self_ref, a2v_ref, out_ref, term_ref) = rest[: len(hops) - 1], rest[len(hops) - 1 :]
    rows, width = own_ref.shape
    last_ref = got[hops.index(1) - 1]
    self_ref[:, columns(index_of("seq"), width)] = own_ref[...]
    for hop, ref in zip(hops[1:], got):
        self_ref[:, columns(index_of("seq") ^ hop, width)] = ref[0:rows, :]
    block = block_of(True, True)
    term_ref[...] = project_self(block, 0, self_ref, ws_ref, gain_ref)
    finish_audio(head, limit_ref[0], q_ref, part_ref, stats_ref, last_ref, rows_audio, a2v_ref)
    out_ref[...] = (term_ref[...] + project_a2v(block, 0, a2v_ref, wa_ref, gain_ref)).astype(BF16)


def second_kernel(head, self_ref, a2v_ref, ws_ref, wa_ref, wv_ref, gain_ref, v2a_ref, lse_ref, *rest):
    got, (out_ref, audio_ref, low_ref) = rest[:-3], rest[-3:]
    rows = self_ref.shape[0]
    block = block_of(True, True)
    out_ref[0:rows, :] = project(block, 1, (self_ref, a2v_ref), (ws_ref, wa_ref), gain_ref).astype(BF16)
    merge_audio(head, rows, v2a_ref, lse_ref, got, audio_ref)
    out_ref[rows:, :] = project_audio(block, audio_ref, wv_ref).astype(BF16)
    low_ref[...] = project(block_of(True, False), 0, (self_ref, a2v_ref), (ws_ref, wa_ref), gain_ref)


def far_low_kernel(low_ref, extra_ref, out_ref):
    out_ref[...] = (low_ref[...] + extra_ref[...].astype(F32)).astype(BF16)


def near_kernel(self_ref, a2v_ref, audio_ref, ws_ref, wa_ref, wv_ref, gain_ref, send_ref, own_ref):
    rows = self_ref.shape[0]
    for out, other in ((send_ref, True), (own_ref, False)):
        block = block_of(False, other)
        for half in range(2):
            term = project(block, half, (self_ref, a2v_ref), (ws_ref, wa_ref), gain_ref)
            out[half * rows : (half + 1) * rows, :] = term.astype(out.dtype)
        out[2 * rows :, :] = project_audio(block, audio_ref, wv_ref).astype(out.dtype)


def far_high_kernel(self_ref, a2v_ref, ws_ref, wa_ref, gain_ref, extra_ref, audio_ref, wv_ref, out_ref):
    rows = self_ref.shape[0]
    block = block_of(True, False)
    term = project(block, 1, (self_ref, a2v_ref), (ws_ref, wa_ref), gain_ref)
    out_ref[0:rows, :] = (term + extra_ref[0:rows, :].astype(F32)).astype(BF16)
    term = project_audio(block, audio_ref, wv_ref)
    out_ref[rows:, :] = (term + extra_ref[rows:, :].astype(F32)).astype(BF16)


def finish_kernel(video_ref, audio_ref, gain_ref, own_ref, core_ref, low_ref, high_ref, video_out, audio_out):
    rows = video_ref.shape[0]
    cut = video_ref.shape[1] // 2
    near = own_ref[...] + core_ref[...].astype(F32)
    for half, ref in enumerate((low_ref, high_ref)):
        at = slice(half * cut, (half + 1) * cut)
        term = near[half * rows : (half + 1) * rows] + ref[0:rows, :].astype(F32)
        video_out[:, at] = (video_ref[:, at].astype(F32) + term).astype(BF16)
    term = near[2 * rows :] + high_ref[rows:, :].astype(F32)
    audio_out[...] = (audio_ref[...].astype(F32) + gain_ref[...] * term).astype(BF16)


def on_device_heads(
    video_in,
    audio_in,
    q_self,
    k_self,
    v_self,
    q_a2v,
    k_a2v,
    v_a2v,
    q_v2a,
    k_v2a,
    v_v2a,
    wo_self,
    wo_a2v,
    wo_v2a,
    video_gates,
    audio_gates,
    video_steps,
    audio_steps,
    audio_len,
    *,
    n,
):
    hops = [0] + OUT_ORDER
    rows, cols = q_self.shape
    rows_audio, cross = q_v2a.shape
    width = cols // n

    def trade(x, axis, hop, size):
        return lax.ppermute(x, axis, [(i, i ^ hop) for i in range(size)])

    video, audio = 3 * rows, cross // width * rows_audio

    def pack(some):
        ends = [1 if hop == FORWARDED else 3 for hop in some]
        return call(
            functools.partial(pack_kernel, some, width),
            [shape(video + end * audio, width) for end in ends],
            (q_self, k_self, v_self, q_v2a, k_a2v, v_a2v),
            [HBM] * 6,
            scratch=[pltpu.SemaphoreType.DMA((3 * len(some) + sum(ends) * audio // rows_audio,))],
        )

    packed = pack(hops[1:2])
    rest = pack(hops[:1] + hops[2:])
    packed = [rest[0], *packed, *rest[1:]]
    blocks = dict(zip(hops, packed))
    for hop in hops[1:]:
        blocks[hop] = trade(blocks[hop], "seq", hop, n)

    late = (k_v2a, v_v2a, q_a2v, wo_self, wo_a2v, wo_v2a, video_in, audio_in)
    steps = (video_steps.reshape(1, rows), audio_steps.reshape(1, rows_audio))
    gain, audio_gain, k_own, v_own, q_own, ws, wa, wv, video_own, audio_own = call(
        fetch_kernel,
        [shape(rows, 2 * video_gates.shape[2]), shape(*audio_in.shape, F32)]
        + [shape(*x.shape) for x in late],
        (audio_len, video_gates.reshape(NT, -1), *steps, audio_gates, *late),
        [SMEM, VMEM] + [HBM] * (3 + len(late)),
        scratch=[pltpu.VMEM(x.shape, x.dtype) for x in (*steps, audio_gates)]
        + [pltpu.SemaphoreType.DMA((3 + len(late),))],
    )
    back = rows + cross // 128 * rows_audio + LSE_ROWS
    result = call(
        functools.partial(attend_kernel, hops, DHC),
        [shape(back + 2 * audio if hop == 1 else back, width) for hop in hops[1:]]
        + [shape(rows, width), shape(rows_audio, cross, F32), shape(cross // DHC, 128, F32)],
        (k_own, v_own, *blocks.values()),
        flops=4 * n * n * rows * rows * width,
        scratch=[pltpu.VMEM((width, n * rows), BF16), pltpu.VMEM((cross, rows), BF16)]
        + [pltpu.VMEM((n * n * rows * width // DHV + cross // DHC * rows, 128), kind) for kind in (F32, BF16)],
    )
    sends, (own, own_v2a, own_lse) = result[: n - 1], result[n - 1 :]
    got = [trade(x, "seq", hop, n) for x, hop in zip(sends, hops[1:])]
    near = [hop for hop in hops if hop != FORWARDED]
    a2v_part, a2v_stats = call(
        functools.partial(attend_audio_kernel, near, rows_audio, DHC),
        [shape(cross, rows, F32), shape(cross // 64, 128 // DHC * rows, F32)],
        (audio_len, q_own, *(blocks[hop] for hop in near)),
        [SMEM] + [VMEM] * n,
        flops=8 * n * rows * rows_audio * cross,
    )

    half = video_in.shape[1] // 2
    flops = 2 * rows * (cols + cross) * half
    self_att, a2v_att, first = call(
        functools.partial(first_kernel, hops, rows_audio, DHC),
        [shape(rows, cols), shape(rows, cross), shape(rows, half)],
        (audio_len, q_own, a2v_part, a2v_stats, own, ws, wa, gain, *got),
        [SMEM] + [VMEM] * (n + 6),
        flops=flops,
        scratch=[pltpu.VMEM((rows, half), F32)],
    )
    first = trade(first, "sub", 1, 2)
    second, v2a_att, own_low = call(
        functools.partial(second_kernel, DHC),
        [shape(rows + rows_audio, half), shape(rows_audio, cross), shape(rows, half, F32)],
        (self_att, a2v_att, ws, wa, wv, gain, own_v2a, own_lse, *got),
        flops=2 * flops,
    )
    second = trade(second, "sub", 1, 2)
    (low,) = call(far_low_kernel, [shape(rows, half)], (own_low, first))
    low = trade(low, "mp", 1, 2)
    (high,) = call(
        far_high_kernel,
        [shape(rows + rows_audio, half)],
        (self_att, a2v_att, ws, wa, gain, second, v2a_att, wv),
        flops=flops,
    )
    high = trade(high, "mp", 1, 2)
    near, own_sum = call(
        near_kernel,
        [shape(2 * rows + rows_audio, half), shape(2 * rows + rows_audio, half, F32)],
        (self_att, a2v_att, v2a_att, ws, wa, wv, gain),
        flops=4 * flops,
    )
    near = trade(near, "sub", 1, 2)
    return call(
        finish_kernel,
        [shape(*video_in.shape), shape(*audio_in.shape)],
        (video_own, audio_own, audio_gain, own_sum, near, low, high),
    )


def on_device(n, mp, sub, *arrays):
    cols, cross = arrays[2].shape[1], arrays[5].shape[1]
    width = cols // n
    fits = (
        n == SEQ
        and (mp, sub) == (2, 2)
        and width % DHV == 0
        and cross % width == 0
        and 3 * (cross // DHC) <= LSE_ROWS
        and n * arrays[8].shape[0] == arrays[2].shape[0] == 128
        and arrays[0].shape[1] == 2 * arrays[1].shape[1]
    )
    if fits:
        return on_device_heads(*arrays, n=n)
    return on_device_gather(*arrays)


def solution(mesh):
    in_specs = (
        P(("groups", "seq"), ("mp", "sub")),
        P(("groups", "seq"), ("mp", "sub")),
        P(("groups", "seq"), ("mp", "sub")),
        P(("groups", "seq"), ("mp", "sub")),
        P(("groups", "seq"), ("mp", "sub")),
        P(("groups", "seq"), ("mp", "sub")),
        P(("groups", "seq"), ("mp", "sub")),
        P(("groups", "seq"), ("mp", "sub")),
        P(("groups", "seq"), ("mp", "sub")),
        P(("groups", "seq"), ("mp", "sub")),
        P(("groups", "seq"), ("mp", "sub")),
        P(("mp", "sub"), None),
        P(("mp", "sub"), None),
        P(("mp", "sub"), None),
        P(),
        P(),
        P(("groups", "seq")),
        P(("groups", "seq")),
        P("groups"),
    )
    out_specs = (P(("groups", "seq"), ("mp", "sub")), P(("groups", "seq"), ("mp", "sub")))
    return jax.shard_map(
        functools.partial(on_device, *(mesh.shape[a] for a in ("seq", "mp", "sub"))), mesh=mesh, in_specs=in_specs, out_specs=out_specs, check_vma=False
    )
```

```python
import functools
import math

import jax
import jax.numpy as jnp
from jax import lax
from jax.experimental import pallas as pl
from jax.experimental.pallas import tpu as pltpu
from jax.sharding import PartitionSpec as P


DHV = 128
DHC = 64
NT = 16


def start_state(rows, heads, width):
    return (
        jnp.full((rows, heads), -1e30, jnp.float32),
        jnp.zeros((rows, heads), jnp.float32),
        jnp.zeros((rows, heads, width), jnp.float32),
    )


def update_block(state, queries, keys, values, heads, width, allowed):
    rows = queries.shape[0]
    count = keys.shape[0]
    q_heads = queries.reshape(rows, heads, width)
    k_heads = keys.reshape(count, heads, width)
    v_heads = values.reshape(count, heads, width)
    scores = jnp.einsum(
        "qhd,khd->qhk", q_heads, k_heads, preferred_element_type=jnp.float32
    ) / math.sqrt(width)
    if allowed is not None:
        scores = jnp.where(allowed[None, None, :], scores, -jnp.inf)
    peak_old, total_old, summed_old = state
    peak = jnp.maximum(peak_old, jnp.max(scores, axis=2))
    weights = jnp.exp(scores - peak[:, :, None])
    factor = jnp.exp(peak_old - peak)
    total = total_old * factor + jnp.sum(weights, axis=2)
    summed = summed_old * factor[:, :, None] + jnp.einsum(
        "qhk,khd->qhd", weights.astype(jnp.bfloat16), v_heads, preferred_element_type=jnp.float32
    )
    return (peak, total, summed)


def update_state(state, queries, keys, values, heads, width, start, limit):
    count = keys.shape[0]
    block = 1024 if count > 1024 and count % 1024 == 0 else count
    if block == count:
        allowed = None
        if limit is not None:
            allowed = jnp.arange(count, dtype=jnp.int32) < limit
        return update_block(state, queries, keys, values, heads, width, allowed)
    steps = count // block
    key_blocks = keys.reshape(steps, block, keys.shape[1])
    value_blocks = values.reshape(steps, block, values.shape[1])
    offsets = jnp.arange(steps, dtype=jnp.int32) * block

    def one_block(carry, items):
        key_rows, value_rows, offset = items
        allowed = None
        if limit is not None:
            allowed = start + offset + jnp.arange(block, dtype=jnp.int32) < limit
        return (update_block(carry, queries, key_rows, value_rows, heads, width, allowed), None)

    result, _ = lax.scan(one_block, state, (key_blocks, value_blocks, offsets))
    return result


def finish(state, heads, width):
    _, total, summed = state
    rows = summed.shape[0]
    return (summed / total[:, :, None]).reshape(rows, heads * width).astype(jnp.bfloat16)


def on_device_gather(
    video_in,
    audio_in,
    q_self,
    k_self,
    v_self,
    q_a2v,
    k_a2v,
    v_a2v,
    q_v2a,
    k_v2a,
    v_v2a,
    wo_self,
    wo_a2v,
    wo_v2a,
    video_gates,
    audio_gates,
    video_steps,
    audio_steps,
    audio_len,
):
    heads_self = q_self.shape[1] // DHV
    heads_cross = q_a2v.shape[1] // DHC
    rows_video = q_self.shape[0]
    rows_audio = q_v2a.shape[0]
    limit = audio_len[0]
    piece = (
        lax.all_gather(k_a2v, "seq", axis=0, tiled=True),
        lax.all_gather(v_a2v, "seq", axis=0, tiled=True),
    )
    a2v_state = update_state(
        start_state(rows_video, heads_cross, DHC),
        q_a2v,
        piece[0],
        piece[1],
        heads_cross,
        DHC,
        jnp.int32(0),
        limit,
    )
    a2v_att = finish(a2v_state, heads_cross, DHC)
    piece = (
        lax.all_gather(k_self, "seq", axis=0, tiled=True),
        lax.all_gather(v_self, "seq", axis=0, tiled=True),
    )
    self_state = update_state(
        start_state(rows_video, heads_self, DHV),
        q_self,
        piece[0],
        piece[1],
        heads_self,
        DHV,
        jnp.int32(0),
        None,
    )
    piece = (
        lax.all_gather(k_v2a, "seq", axis=0, tiled=True),
        lax.all_gather(v_v2a, "seq", axis=0, tiled=True),
    )
    v2a_state = update_state(
        start_state(rows_audio, heads_cross, DHC),
        q_v2a,
        piece[0],
        piece[1],
        heads_cross,
        DHC,
        jnp.int32(0),
        None,
    )
    self_att = finish(self_state, heads_self, DHV)
    v2a_att = finish(v2a_state, heads_cross, DHC)
    levels = jnp.arange(NT, dtype=jnp.int32)
    video_hot = (video_steps[:, None] == levels[None, :]).astype(jnp.bfloat16)
    video_gain = jnp.dot(video_hot, video_gates.reshape(NT, -1), preferred_element_type=jnp.float32)
    width_video = video_gates.shape[2]
    video_term = video_gain[:, :width_video] * jnp.dot(
        self_att, wo_self, preferred_element_type=jnp.float32
    )
    video_term = video_term + video_gain[:, width_video:] * jnp.dot(
        a2v_att, wo_a2v, preferred_element_type=jnp.float32
    )
    audio_hot = (audio_steps[:, None] == levels[None, :]).astype(jnp.bfloat16)
    audio_gain = jnp.dot(audio_hot, audio_gates, preferred_element_type=jnp.float32)
    positions = lax.axis_index("seq") * rows_audio + jnp.arange(rows_audio, dtype=jnp.int32)
    present = (positions < limit).astype(jnp.float32)
    audio_term = (
        present[:, None] * audio_gain * jnp.dot(v2a_att, wo_v2a, preferred_element_type=jnp.float32)
    )
    video_sum, audio_sum = (
        lax.psum_scatter(
            video_term.astype(jnp.bfloat16), ("mp", "sub"), scatter_dimension=1, tiled=True
        ).astype(jnp.float32),
        lax.psum_scatter(
            audio_term.astype(jnp.bfloat16), ("mp", "sub"), scatter_dimension=1, tiled=True
        ).astype(jnp.float32),
    )
    video_out = (video_in.astype(jnp.float32) + video_sum).astype(jnp.bfloat16)
    audio_out = (audio_in.astype(jnp.float32) + audio_sum).astype(jnp.bfloat16)
    return (video_out, audio_out)


LOG2E = 1.4426950408889634
VMEM = pl.BlockSpec(memory_space=pltpu.VMEM)
SMEM = pl.BlockSpec(memory_space=pltpu.SMEM)
HBM = pl.BlockSpec(memory_space=pltpu.HBM)
BF16, F32 = jnp.bfloat16, jnp.float32
LSE_ROWS = 16
LEAST = float(jnp.finfo(jnp.float32).min)
SEQ, FORWARDED, OUT_ORDER, LAST = 4, 3, [3, 2, 1], 2


def call(kernel, outs, operands, specs=None, flops=0, scratch=(), limit=8 * 2**20):
    size = sum(math.prod(x.shape) * x.dtype.itemsize for x in (*operands, *outs))
    if specs:
        operands = [
            pltpu.with_memory_space_constraint(x, pltpu.HBM) if spec is HBM else x for x, spec in zip(operands, specs)
        ]
    return pl.pallas_call(
        kernel,
        out_shape=tuple(outs),
        in_specs=specs or [VMEM] * len(operands),
        out_specs=tuple(VMEM for _ in outs),
        scratch_shapes=list(scratch),
        compiler_params=pltpu.CompilerParams(vmem_limit_bytes=limit),
        cost_estimate=pl.CostEstimate(flops=flops, bytes_accessed=size, transcendentals=0),
    )(*operands)


def shape(rows, cols, kind=BF16):
    return jax.ShapeDtypeStruct((rows, cols), kind)


def dot_t(a, b):
    return lax.dot_general(a, b, (((1,), (1,)), ((), ())), preferred_element_type=F32)


def dot(a, b):
    return jnp.dot(a, b, preferred_element_type=F32)


def index_of(axis):
    return lax.axis_index(axis).astype(jnp.int32)


def columns(index, width):
    return pl.ds(pl.multiple_of(index * width, width), width)


def copy_all(pairs, sems):
    copies = [pltpu.make_async_copy(src, dst, sems.at[i]) for i, (src, dst) in enumerate(pairs)]
    for copy in copies:
        copy.start()
    for copy in copies:
        copy.wait()


def pack_kernel(hops, width, q_ref, k_ref, v_ref, qa_ref, ka_ref, va_ref, *rest):
    outs, sems = rest[:-1], rest[-1]
    rows = q_ref.shape[0]
    rows_audio, cols_audio = qa_ref.shape
    me = index_of("seq")
    pairs = []
    for hop, out in zip(hops, outs):
        for i, ref in enumerate((q_ref, k_ref, v_ref)):
            pairs.append((ref.at[:, columns(me ^ hop, width)], out.at[pl.ds(i * rows, rows), :]))
        at = 3 * rows
        for ref in (qa_ref,) if hop == FORWARDED else (qa_ref, ka_ref, va_ref):
            for i in range(cols_audio // width):
                pairs.append((ref.at[:, pl.ds(i * width, width)], out.at[pl.ds(at, rows_audio), :]))
                at += rows_audio
    copy_all(pairs, sems)


def audio_block(ref, end, rows, cols, block):
    at, column = divmod(block * 128, ref.shape[1])
    top = ref.shape[0] - end * (cols // ref.shape[1]) * rows + at * rows
    return ref[top : top + rows, column : column + 128]


def one_hot_t(steps_ref):
    levels = lax.broadcasted_iota(jnp.int32, (NT, steps_ref.shape[1]), 0)
    return (levels == steps_ref[...]).astype(BF16)


def pick(hot_t, table):
    return lax.dot_general(hot_t, table, (((0,), (0,)), ((), ())), preferred_element_type=F32)


def fetch_kernel(limit_ref, vg_ref, *rest):
    count = (len(rest) - 9) // 2
    loads, gain_ref, audio_ref = rest[: count + 3], rest[count + 3], rest[count + 4]
    fetched, (vs_ref, as_ref, ag_ref, sems) = rest[count + 5 : -4], rest[-4:]
    copies = [
        pltpu.make_async_copy(src, dst, sems.at[i])
        for i, (src, dst) in enumerate(zip(loads, (vs_ref, as_ref, ag_ref, *fetched)))
    ]
    for copy in copies:
        copy.start()
    for copy in copies[:3]:
        copy.wait()
    hot_t = one_hot_t(vs_ref)
    piece = min(vg_ref.shape[1], 2048)
    for at in range(0, vg_ref.shape[1], piece):
        gain_ref[:, at : at + piece] = pick(hot_t, vg_ref[:, at : at + piece]).astype(BF16)
    rows_audio, narrow = audio_ref.shape
    part = index_of("mp") * 2 + index_of("sub")
    gain = pick(one_hot_t(as_ref), ag_ref[:, columns(part, narrow)])
    at = index_of("seq") * rows_audio + lax.broadcasted_iota(jnp.int32, (rows_audio, 1), 0)
    audio_ref[...] = jnp.where(at < limit_ref[0], gain, 0.0)
    for copy in copies[3:]:
        copy.wait()


def softmax_t(scores, scale, allowed=None):
    if allowed is not None:
        scores = [jnp.where(ok, x, LEAST) for ok, x in zip(allowed, scores)]
    peak = functools.reduce(jnp.maximum, [jnp.max(x, axis=0, keepdims=True) for x in scores])
    weights = [jnp.exp2((x - peak) * (scale * LOG2E)) for x in scores]
    total = functools.reduce(jnp.add, [jnp.sum(x, axis=0, keepdims=True) for x in weights])
    return peak, [x.astype(BF16) for x in weights], total


def turn(x):
    return x.astype(F32).T.astype(BF16)


def pair_rows(x, head):
    lane = lax.broadcasted_iota(jnp.int32, (1, 128), 1) // head
    return jnp.concatenate([jnp.where(lane == i, x, 0).astype(BF16) for i in range(128 // head)], axis=0)


def pair_columns(x, head):
    pair = 128 // head
    rows = x.shape[1] // pair
    return jnp.concatenate([x[i * head : (i + 1) * head, i * rows : (i + 1) * rows] for i in range(pair)], axis=0)


def audio_part(q, keys, values_t, head):
    pair, rows = 128 // head, q.shape[0]
    scale = 1.0 / math.sqrt(head)
    both = pair_rows(q, head)
    both = jnp.concatenate([both] * (128 // both.shape[0]), axis=0)
    peak, p, total = softmax_t([dot_t(keys, both)], scale)
    o = dot(values_t, p[0]) * (1.0 / total)
    lse = peak * (scale * LOG2E) + jnp.log2(total)
    o = [o[i * head : (i + 1) * head] for i in range(pair)]
    o = [x if i == 0 else pltpu.roll(x, 128 - i * rows, 1) for i, x in enumerate(o)]
    lses = [lse if i == 0 else pltpu.roll(lse, 128 - i * rows, 1) for i in range(pair)]
    return jnp.concatenate(o, axis=0).T[0:rows], lses


def audio_parts(ref, end, kv_ref, vvt_ref, rows_audio, head):
    cols = kv_ref.shape[1]
    outs, lses = [], []
    for block in range(cols // 128):
        cut = slice(block * 128, (block + 1) * 128)
        q = audio_block(ref, end, rows_audio, cols, block)
        o, lse = audio_part(q, kv_ref[:, cut], vvt_ref[cut, :], head)
        outs.append(o)
        lses += lse
    return outs, jnp.concatenate(lses, axis=0)


def store_tail(dst, top, outs, lse):
    rows_audio = outs[0].shape[0]
    for i, o in enumerate(outs):
        dst[top + i * rows_audio : top + (i + 1) * rows_audio, 0:128] = o.astype(BF16)
    pieces, left = [], lse
    for _ in range(3):
        pieces.append(left.astype(BF16).astype(F32))
        left = left - pieces[-1]
    pieces.append(jnp.zeros((LSE_ROWS - 3 * lse.shape[0], 128), F32))
    top += len(outs) * rows_audio
    dst[top : top + LSE_ROWS, 0:128] = jnp.concatenate(pieces, axis=0).astype(BF16)


def early_kernel(early, head, kv_ref, vv_ref, *rest):
    count = len(early)
    blocks, (part_ref, stats_ref, vt_ref, vvt_ref, own_v2a_ref, own_lse_ref) = rest[:count], rest[count : count + 6]
    tails, (s_ref,) = rest[count + 6 : -1], rest[-1:]
    rows, cols = kv_ref.shape
    rows_audio = own_v2a_ref.shape[0]
    for i, ref in enumerate(blocks):
        vt_ref[:, i * rows : (i + 1) * rows] = turn(ref[2 * rows : 3 * rows, :])
    for block in range(cols // 128):
        cut = slice(block * 128, (block + 1) * 128)
        vvt_ref[cut, :] = turn(vv_ref[:, cut])
    scale = 1.0 / math.sqrt(DHV)
    peaks = []
    for j, ref in enumerate(blocks):
        peak = None
        for i, other in enumerate(blocks):
            scores = dot_t(other[rows : 2 * rows, :], ref[0:rows, :])
            s_ref[(j * count + i) * rows : (j * count + i + 1) * rows, :] = scores
            top = jnp.max(scores, axis=0, keepdims=True)
            peak = top if i == 0 else jnp.maximum(peak, top)
        peaks.append(peak)
    for j, peak in enumerate(peaks):
        total, p = None, []
        for i in range(count):
            x = jnp.exp2((s_ref[(j * count + i) * rows : (j * count + i + 1) * rows, :] - peak) * (scale * LOG2E))
            summed = jnp.sum(x, axis=0, keepdims=True)
            total = summed if i == 0 else total + summed
            p.append(x.astype(BF16))
        part_ref[j * DHV : (j + 1) * DHV, :] = dot(vt_ref[...], jnp.concatenate(p, axis=0))
        stats_ref[2 * j : 2 * j + 1, :] = peak
        stats_ref[2 * j + 1 : 2 * j + 2, :] = total
    for j, (hop, ref) in enumerate(zip(early, blocks)):
        outs, lse = audio_parts(ref, 1 if hop == FORWARDED else 3, kv_ref, vvt_ref, rows_audio, head)
        if j > 0:
            store_tail(tails[j - 1], 0, outs, lse)
            continue
        own_lse_ref[...] = lse
        for block, o in enumerate(outs):
            own_v2a_ref[:, block * 128 : (block + 1) * 128] = o


def late_kernel(early, hops, rows_audio, head, kv_ref, vvt_ref, part_ref, stats_ref, vt_ref, last_ref, *rest):
    count, n = len(early), len(hops)
    blocks, tails, outs, s_ref = rest[:count], rest[count : 2 * count - 1], rest[2 * count - 1 : -1], rest[-1]
    by_hop = dict(zip(hops, outs))
    rows = kv_ref.shape[0]
    last = next(hop for hop in hops if hop not in early)
    scale = 1.0 / math.sqrt(DHV)
    keys = last_ref[rows : 2 * rows, :]
    peaks = []
    for j, ref in enumerate((*blocks, last_ref)):
        scores = dot_t(keys, ref[0:rows, :])
        s_ref[j * rows : (j + 1) * rows, :] = scores
        top = jnp.max(scores, axis=0, keepdims=True)
        peaks.append(jnp.maximum(top, stats_ref[2 * j : 2 * j + 1, :]) if j < count else top)
    for i, other in enumerate(blocks):
        scores = dot_t(other[rows : 2 * rows, :], last_ref[0:rows, :])
        s_ref[(n + i) * rows : (n + i + 1) * rows, :] = scores
        peaks[-1] = jnp.maximum(peaks[-1], jnp.max(scores, axis=0, keepdims=True))
    values_t = turn(last_ref[2 * rows : 3 * rows, :])

    def weigh(at, peak):
        x = jnp.exp2((s_ref[at * rows : (at + 1) * rows, :] - peak) * (scale * LOG2E))
        return x.astype(BF16), jnp.sum(x, axis=0, keepdims=True)

    audio = audio_parts(last_ref, 3, kv_ref, vvt_ref, rows_audio, head)
    total, p = None, []
    for i in range(count):
        x, summed = weigh(n + i, peaks[-1])
        total = summed if i == 0 else total + summed
        p.append(x)
    x, summed = weigh(count, peaks[-1])
    o = dot(vt_ref[...], jnp.concatenate(p, axis=0)) + dot(values_t, x)
    by_hop[last][0:rows, :] = (o * (1.0 / (total + summed))).T.astype(BF16)
    for j, hop in enumerate(early):
        x, summed = weigh(j, peaks[j])
        factor = jnp.exp2((stats_ref[2 * j : 2 * j + 1, :] - peaks[j]) * (scale * LOG2E))
        total = stats_ref[2 * j + 1 : 2 * j + 2, :] * factor + summed
        o = part_ref[j * DHV : (j + 1) * DHV, :] * factor + dot(values_t, x)
        by_hop[hop][0:rows, :] = (o * (1.0 / total)).T.astype(BF16)
    store_tail(by_hop[last], rows, *audio)
    for hop, tail in zip(early[1:], tails):
        by_hop[hop][rows : rows + tail.shape[0], :] = tail[...]
    dst = by_hop[FORWARDED]
    top = rows + tails[0].shape[0]
    dst[top:, :] = blocks[0][blocks[0].shape[0] - (dst.shape[0] - top) :, :]


def audio_allowed(hop, rows_audio, limit):
    row = lax.broadcasted_iota(jnp.int32, (rows_audio, 1), 0)
    return (index_of("seq") ^ hop) * rows_audio + row < limit


def spread(x, head):
    pair = 128 // head
    rows = x.shape[1] // pair
    parts = [jnp.broadcast_to(x[:, i * rows : (i + 1) * rows], (head, rows)) for i in range(pair)]
    return jnp.concatenate(parts, axis=0)


def attend_audio_kernel(hops, rows_audio, head, limit_ref, q_ref, *rest):
    blocks, part_ref, stats_ref = rest[:-2], rest[-2], rest[-1]
    cols = q_ref.shape[1]
    allowed = [audio_allowed(hop, rows_audio, limit_ref[0]) for hop in hops]
    scale = 1.0 / math.sqrt(head)
    for block in range(cols // 128):
        cut = slice(block * 128, (block + 1) * 128)
        q = pair_rows(q_ref[:, cut], head)
        scores = [dot_t(audio_block(ref, 2, rows_audio, cols, block), q) for ref in blocks]
        peak, p, total = softmax_t(scores, scale, allowed)
        vt = turn(jnp.concatenate([audio_block(ref, 1, rows_audio, cols, block) for ref in blocks], axis=0))
        part_ref[cut, :] = pair_columns(dot(vt, jnp.concatenate(p, axis=0)), head)
        stats_ref[2 * block : 2 * block + 1, :] = peak
        stats_ref[2 * block + 1 : 2 * block + 2, :] = total


def finish_audio(head, limit, q_ref, part_ref, stats_ref, last_ref, rows_audio, out_ref):
    cols = q_ref.shape[1]
    scale = 1.0 / math.sqrt(head)
    allowed = audio_allowed(FORWARDED, rows_audio, limit)
    for block in range(cols // 128):
        cut = slice(block * 128, (block + 1) * 128)
        q = pair_rows(q_ref[:, cut], head)
        scores = jnp.where(allowed, dot_t(audio_block(last_ref, 2, rows_audio, cols, block), q), LEAST)
        before, summed = stats_ref[2 * block : 2 * block + 1, :], stats_ref[2 * block + 1 : 2 * block + 2, :]
        peak = jnp.maximum(before, jnp.max(scores, axis=0, keepdims=True))
        factor = jnp.exp2((before - peak) * (scale * LOG2E))
        p = jnp.exp2((scores - peak) * (scale * LOG2E))
        inverse = 1.0 / (summed * factor + jnp.sum(p, axis=0, keepdims=True))
        vt = turn(audio_block(last_ref, 1, rows_audio, cols, block))
        last = pair_columns(dot(vt, p.astype(BF16)), head)
        both = part_ref[cut, :] * spread(factor, head) + last
        out_ref[:, cut] = (both * spread(inverse, head)).T.astype(BF16)


def merge_audio(head, top, v2a_ref, lse_ref, got, out_ref):
    rows_audio, cols = v2a_ref.shape
    heads = cols // head
    lses = [lse_ref[...]]
    for ref in got:
        at = top + cols // 128 * rows_audio
        packed = ref[at : at + LSE_ROWS, 0:128].astype(F32)
        lses.append(packed[0:heads] + packed[heads : 2 * heads] + packed[2 * heads : 3 * heads])
    peak = functools.reduce(jnp.maximum, lses)
    parts = [jnp.exp2(x - peak) for x in lses]
    total = functools.reduce(jnp.add, parts)
    inverse = 1.0 / total
    parts = [x * inverse for x in parts]
    parts.append(jnp.zeros((128 - len(parts) * heads, 128), F32))
    shares = jnp.concatenate(parts, axis=0).T[0:rows_audio]
    pair = 128 // head
    lane = lax.broadcasted_iota(jnp.int32, (1, 128), 1) // head
    for block in range(cols // 128):
        cut = slice(block * 128, (block + 1) * 128)
        at = top + block * rows_audio
        summed = jnp.zeros((rows_audio, 128), F32)
        for j in range(len(lses)):
            o = v2a_ref[:, cut] if j == 0 else got[j - 1][at : at + rows_audio, 0:128].astype(F32)
            share = jnp.zeros((rows_audio, 128), F32)
            for i in range(pair):
                column = j * heads + block * pair + i
                share = jnp.where(lane == i, shares[:, column : column + 1], share)
            summed = summed + share * o
        out_ref[:, cut] = summed.astype(BF16)


def block_of(far, other):
    mp, sub = index_of("mp"), index_of("sub")
    return (1 - mp if far else mp) * 2 + (1 - sub if other else sub)


def project_self(block, half, att_ref, ws_ref, gain_ref):
    cut = ws_ref.shape[1] // 8
    at = columns(block * 2 + half, cut)
    return gain_ref[:, at].astype(F32) * dot(att_ref[...], ws_ref[:, at])


def project_a2v(block, half, a2v_ref, wa_ref, gain_ref):
    cut = wa_ref.shape[1] // 8
    gain = gain_ref[:, columns(block * 2 + half + 8, cut)].astype(F32)
    return gain * dot(a2v_ref[...], wa_ref[:, columns(block * 2 + half, cut)])


def project(block, half, heads, weights, gain_ref):
    term = project_self(block, half, heads[0], weights[0], gain_ref)
    return term + project_a2v(block, half, heads[1], weights[1], gain_ref)


def project_audio(block, v2a_ref, wv_ref):
    return dot(v2a_ref[...], wv_ref[:, columns(block, wv_ref.shape[1] // 4)])


def first_kernel(hops, rows_audio, head, limit_ref, q_ref, part_ref, stats_ref, own_ref, ws_ref, wa_ref, gain_ref, *rest):
    got, (self_ref, a2v_ref, out_ref, term_ref) = rest[: len(hops) - 1], rest[len(hops) - 1 :]
    rows, width = own_ref.shape
    last_ref = got[hops.index(FORWARDED) - 1]
    self_ref[:, columns(index_of("seq"), width)] = own_ref[...]
    for hop, ref in zip(hops[1:], got):
        self_ref[:, columns(index_of("seq") ^ hop, width)] = ref[0:rows, :]
    block = block_of(True, True)
    term_ref[...] = project_self(block, 0, self_ref, ws_ref, gain_ref)
    finish_audio(head, limit_ref[0], q_ref, part_ref, stats_ref, last_ref, rows_audio, a2v_ref)
    out_ref[...] = (term_ref[...] + project_a2v(block, 0, a2v_ref, wa_ref, gain_ref)).astype(BF16)


def second_kernel(head, self_ref, a2v_ref, ws_ref, wa_ref, wv_ref, gain_ref, v2a_ref, lse_ref, *rest):
    got, (out_ref, audio_ref, low_ref) = rest[:-3], rest[-3:]
    rows = self_ref.shape[0]
    block = block_of(True, True)
    out_ref[0:rows, :] = project(block, 1, (self_ref, a2v_ref), (ws_ref, wa_ref), gain_ref).astype(BF16)
    merge_audio(head, rows, v2a_ref, lse_ref, got, audio_ref)
    out_ref[rows:, :] = project_audio(block, audio_ref, wv_ref).astype(BF16)
    low_ref[...] = project(block_of(True, False), 0, (self_ref, a2v_ref), (ws_ref, wa_ref), gain_ref)


def far_low_kernel(low_ref, extra_ref, out_ref):
    out_ref[...] = (low_ref[...] + extra_ref[...].astype(F32)).astype(BF16)


def near_kernel(self_ref, a2v_ref, audio_ref, ws_ref, wa_ref, wv_ref, gain_ref, send_ref, own_ref):
    rows = self_ref.shape[0]
    for out, other in ((send_ref, True), (own_ref, False)):
        block = block_of(False, other)
        for half in range(2):
            term = project(block, half, (self_ref, a2v_ref), (ws_ref, wa_ref), gain_ref)
            out[half * rows : (half + 1) * rows, :] = term.astype(out.dtype)
        out[2 * rows :, :] = project_audio(block, audio_ref, wv_ref).astype(out.dtype)


def far_high_kernel(self_ref, a2v_ref, ws_ref, wa_ref, gain_ref, extra_ref, audio_ref, wv_ref, out_ref):
    rows = self_ref.shape[0]
    block = block_of(True, False)
    term = project(block, 1, (self_ref, a2v_ref), (ws_ref, wa_ref), gain_ref)
    out_ref[0:rows, :] = (term + extra_ref[0:rows, :].astype(F32)).astype(BF16)
    term = project_audio(block, audio_ref, wv_ref)
    out_ref[rows:, :] = (term + extra_ref[rows:, :].astype(F32)).astype(BF16)


def finish_kernel(video_ref, audio_ref, gain_ref, own_ref, core_ref, low_ref, high_ref, video_out, audio_out):
    rows = video_ref.shape[0]
    cut = video_ref.shape[1] // 2
    near = own_ref[...] + core_ref[...].astype(F32)
    for half, ref in enumerate((low_ref, high_ref)):
        at = slice(half * cut, (half + 1) * cut)
        term = near[half * rows : (half + 1) * rows] + ref[0:rows, :].astype(F32)
        video_out[:, at] = (video_ref[:, at].astype(F32) + term).astype(BF16)
    term = near[2 * rows :] + high_ref[rows:, :].astype(F32)
    audio_out[...] = (audio_ref[...].astype(F32) + gain_ref[...] * term).astype(BF16)


def on_device_heads(
    video_in,
    audio_in,
    q_self,
    k_self,
    v_self,
    q_a2v,
    k_a2v,
    v_a2v,
    q_v2a,
    k_v2a,
    v_v2a,
    wo_self,
    wo_a2v,
    wo_v2a,
    video_gates,
    audio_gates,
    video_steps,
    audio_steps,
    audio_len,
    *,
    n,
):
    hops = [0] + OUT_ORDER
    rows, cols = q_self.shape
    rows_audio, cross = q_v2a.shape
    width = cols // n

    def trade(x, axis, hop, size):
        return lax.ppermute(x, axis, [(i, i ^ hop) for i in range(size)])

    video, audio = 3 * rows, cross // width * rows_audio

    def pack(some):
        ends = [1 if hop == FORWARDED else 3 for hop in some]
        return call(
            functools.partial(pack_kernel, some, width),
            [shape(video + end * audio, width) for end in ends],
            (q_self, k_self, v_self, q_v2a, k_a2v, v_a2v),
            [HBM] * 6,
            scratch=[pltpu.SemaphoreType.DMA((3 * len(some) + sum(ends) * audio // rows_audio,))],
        )

    packed = pack(hops[1:2])
    rest = pack(hops[:1] + hops[2:])
    packed = [rest[0], *packed, *rest[1:]]
    blocks = dict(zip(hops, packed))
    for hop in hops[1:]:
        blocks[hop] = trade(blocks[hop], "seq", hop, n)

    late = (k_v2a, v_v2a, q_a2v, wo_self, wo_a2v, wo_v2a, video_in, audio_in)
    steps = (video_steps.reshape(1, rows), audio_steps.reshape(1, rows_audio))
    gain, audio_gain, k_own, v_own, q_own, ws, wa, wv, video_own, audio_own = call(
        fetch_kernel,
        [shape(rows, 2 * video_gates.shape[2]), shape(*audio_in.shape, F32)]
        + [shape(*x.shape) for x in late],
        (audio_len, video_gates.reshape(NT, -1), *steps, audio_gates, *late),
        [SMEM, VMEM] + [HBM] * (3 + len(late)),
        scratch=[pltpu.VMEM(x.shape, x.dtype) for x in (*steps, audio_gates)]
        + [pltpu.SemaphoreType.DMA((3 + len(late),))],
    )
    tail = cross // 128 * rows_audio + LSE_ROWS
    early = [hop for hop in hops if hop != LAST]
    count = len(early)
    part, stats, vt, vvt, own_v2a, own_lse, *tails = call(
        functools.partial(early_kernel, early, DHC),
        [
            shape(count * width, rows, F32),
            shape(2 * count, rows, F32),
            shape(width, count * rows),
            shape(cross, rows),
            shape(rows_audio, cross, F32),
            shape(cross // DHC, 128, F32),
        ]
        + [shape(tail, width)] * (count - 1),
        (k_own, v_own, *(blocks[hop] for hop in early)),
        flops=4 * count * count * rows * rows * width,
        scratch=[pltpu.VMEM((count * count * rows, rows), F32)],
    )
    own, *sends = call(
        functools.partial(late_kernel, early, hops, rows_audio, DHC),
        [shape(rows, width)]
        + [shape(rows + tail + (2 * audio if hop == FORWARDED else 0), width) for hop in hops[1:]],
        (k_own, vvt, part, stats, vt, blocks[LAST], *(blocks[hop] for hop in early), *tails),
        flops=4 * (2 * n - 1) * rows * rows * width,
        scratch=[pltpu.VMEM(((2 * n - 1) * rows, rows), F32)],
    )
    got = [trade(x, "seq", hop, n) for x, hop in zip(sends, hops[1:])]
    near = [hop for hop in hops if hop != FORWARDED]
    a2v_part, a2v_stats = call(
        functools.partial(attend_audio_kernel, near, rows_audio, DHC),
        [shape(cross, rows, F32), shape(cross // 64, 128 // DHC * rows, F32)],
        (audio_len, q_own, *(blocks[hop] for hop in near)),
        [SMEM] + [VMEM] * n,
        flops=8 * n * rows * rows_audio * cross,
    )

    half = video_in.shape[1] // 2
    flops = 2 * rows * (cols + cross) * half
    self_att, a2v_att, first = call(
        functools.partial(first_kernel, hops, rows_audio, DHC),
        [shape(rows, cols), shape(rows, cross), shape(rows, half)],
        (audio_len, q_own, a2v_part, a2v_stats, own, ws, wa, gain, *got),
        [SMEM] + [VMEM] * (n + 6),
        flops=flops,
        scratch=[pltpu.VMEM((rows, half), F32)],
    )
    first = trade(first, "sub", 1, 2)
    second, v2a_att, own_low = call(
        functools.partial(second_kernel, DHC),
        [shape(rows + rows_audio, half), shape(rows_audio, cross), shape(rows, half, F32)],
        (self_att, a2v_att, ws, wa, wv, gain, own_v2a, own_lse, *got),
        flops=2 * flops,
    )
    second = trade(second, "sub", 1, 2)
    (low,) = call(far_low_kernel, [shape(rows, half)], (own_low, first))
    low = trade(low, "mp", 1, 2)
    (high,) = call(
        far_high_kernel,
        [shape(rows + rows_audio, half)],
        (self_att, a2v_att, ws, wa, gain, second, v2a_att, wv),
        flops=flops,
    )
    high = trade(high, "mp", 1, 2)
    near, own_sum = call(
        near_kernel,
        [shape(2 * rows + rows_audio, half), shape(2 * rows + rows_audio, half, F32)],
        (self_att, a2v_att, v2a_att, ws, wa, wv, gain),
        flops=4 * flops,
    )
    near = trade(near, "sub", 1, 2)
    return call(
        finish_kernel,
        [shape(*video_in.shape), shape(*audio_in.shape)],
        (video_own, audio_own, audio_gain, own_sum, near, low, high),
    )


def on_device(n, mp, sub, *arrays):
    cols, cross = arrays[2].shape[1], arrays[5].shape[1]
    width = cols // n
    fits = (
        n == SEQ
        and (mp, sub) == (2, 2)
        and width == DHV == 128
        and cross % width == 0
        and 3 * (cross // DHC) <= LSE_ROWS
        and n * arrays[8].shape[0] == arrays[2].shape[0] == 128
        and arrays[0].shape[1] == 2 * arrays[1].shape[1]
    )
    if fits:
        return on_device_heads(*arrays, n=n)
    return on_device_gather(*arrays)


def solution(mesh):
    in_specs = (
        P(("groups", "seq"), ("mp", "sub")),
        P(("groups", "seq"), ("mp", "sub")),
        P(("groups", "seq"), ("mp", "sub")),
        P(("groups", "seq"), ("mp", "sub")),
        P(("groups", "seq"), ("mp", "sub")),
        P(("groups", "seq"), ("mp", "sub")),
        P(("groups", "seq"), ("mp", "sub")),
        P(("groups", "seq"), ("mp", "sub")),
        P(("groups", "seq"), ("mp", "sub")),
        P(("groups", "seq"), ("mp", "sub")),
        P(("groups", "seq"), ("mp", "sub")),
        P(("mp", "sub"), None),
        P(("mp", "sub"), None),
        P(("mp", "sub"), None),
        P(),
        P(),
        P(("groups", "seq")),
        P(("groups", "seq")),
        P("groups"),
    )
    out_specs = (P(("groups", "seq"), ("mp", "sub")), P(("groups", "seq"), ("mp", "sub")))
    return jax.shard_map(
        functools.partial(on_device, *(mesh.shape[a] for a in ("seq", "mp", "sub"))), mesh=mesh, in_specs=in_specs, out_specs=out_specs, check_vma=False
    )
```

```python
import functools
import math

import jax
import jax.numpy as jnp
from jax import lax
from jax.experimental import pallas as pl
from jax.experimental.pallas import tpu as pltpu
from jax.sharding import PartitionSpec as P


DHV = 128
DHC = 64
NT = 16


def start_state(rows, heads, width):
    return (
        jnp.full((rows, heads), -1e30, jnp.float32),
        jnp.zeros((rows, heads), jnp.float32),
        jnp.zeros((rows, heads, width), jnp.float32),
    )


def update_block(state, queries, keys, values, heads, width, allowed):
    rows = queries.shape[0]
    count = keys.shape[0]
    q_heads = queries.reshape(rows, heads, width)
    k_heads = keys.reshape(count, heads, width)
    v_heads = values.reshape(count, heads, width)
    scores = jnp.einsum(
        "qhd,khd->qhk", q_heads, k_heads, preferred_element_type=jnp.float32
    ) / math.sqrt(width)
    if allowed is not None:
        scores = jnp.where(allowed[None, None, :], scores, -jnp.inf)
    peak_old, total_old, summed_old = state
    peak = jnp.maximum(peak_old, jnp.max(scores, axis=2))
    weights = jnp.exp(scores - peak[:, :, None])
    factor = jnp.exp(peak_old - peak)
    total = total_old * factor + jnp.sum(weights, axis=2)
    summed = summed_old * factor[:, :, None] + jnp.einsum(
        "qhk,khd->qhd", weights.astype(jnp.bfloat16), v_heads, preferred_element_type=jnp.float32
    )
    return (peak, total, summed)


def update_state(state, queries, keys, values, heads, width, start, limit):
    count = keys.shape[0]
    block = 1024 if count > 1024 and count % 1024 == 0 else count
    if block == count:
        allowed = None
        if limit is not None:
            allowed = jnp.arange(count, dtype=jnp.int32) < limit
        return update_block(state, queries, keys, values, heads, width, allowed)
    steps = count // block
    key_blocks = keys.reshape(steps, block, keys.shape[1])
    value_blocks = values.reshape(steps, block, values.shape[1])
    offsets = jnp.arange(steps, dtype=jnp.int32) * block

    def one_block(carry, items):
        key_rows, value_rows, offset = items
        allowed = None
        if limit is not None:
            allowed = start + offset + jnp.arange(block, dtype=jnp.int32) < limit
        return (update_block(carry, queries, key_rows, value_rows, heads, width, allowed), None)

    result, _ = lax.scan(one_block, state, (key_blocks, value_blocks, offsets))
    return result


def finish(state, heads, width):
    _, total, summed = state
    rows = summed.shape[0]
    return (summed / total[:, :, None]).reshape(rows, heads * width).astype(jnp.bfloat16)


def on_device_gather(
    video_in,
    audio_in,
    q_self,
    k_self,
    v_self,
    q_a2v,
    k_a2v,
    v_a2v,
    q_v2a,
    k_v2a,
    v_v2a,
    wo_self,
    wo_a2v,
    wo_v2a,
    video_gates,
    audio_gates,
    video_steps,
    audio_steps,
    audio_len,
):
    heads_self = q_self.shape[1] // DHV
    heads_cross = q_a2v.shape[1] // DHC
    rows_video = q_self.shape[0]
    rows_audio = q_v2a.shape[0]
    limit = audio_len[0]
    piece = (
        lax.all_gather(k_a2v, "seq", axis=0, tiled=True),
        lax.all_gather(v_a2v, "seq", axis=0, tiled=True),
    )
    a2v_state = update_state(
        start_state(rows_video, heads_cross, DHC),
        q_a2v,
        piece[0],
        piece[1],
        heads_cross,
        DHC,
        jnp.int32(0),
        limit,
    )
    a2v_att = finish(a2v_state, heads_cross, DHC)
    piece = (
        lax.all_gather(k_self, "seq", axis=0, tiled=True),
        lax.all_gather(v_self, "seq", axis=0, tiled=True),
    )
    self_state = update_state(
        start_state(rows_video, heads_self, DHV),
        q_self,
        piece[0],
        piece[1],
        heads_self,
        DHV,
        jnp.int32(0),
        None,
    )
    piece = (
        lax.all_gather(k_v2a, "seq", axis=0, tiled=True),
        lax.all_gather(v_v2a, "seq", axis=0, tiled=True),
    )
    v2a_state = update_state(
        start_state(rows_audio, heads_cross, DHC),
        q_v2a,
        piece[0],
        piece[1],
        heads_cross,
        DHC,
        jnp.int32(0),
        None,
    )
    self_att = finish(self_state, heads_self, DHV)
    v2a_att = finish(v2a_state, heads_cross, DHC)
    levels = jnp.arange(NT, dtype=jnp.int32)
    video_hot = (video_steps[:, None] == levels[None, :]).astype(jnp.bfloat16)
    video_gain = jnp.dot(video_hot, video_gates.reshape(NT, -1), preferred_element_type=jnp.float32)
    width_video = video_gates.shape[2]
    video_term = video_gain[:, :width_video] * jnp.dot(
        self_att, wo_self, preferred_element_type=jnp.float32
    )
    video_term = video_term + video_gain[:, width_video:] * jnp.dot(
        a2v_att, wo_a2v, preferred_element_type=jnp.float32
    )
    audio_hot = (audio_steps[:, None] == levels[None, :]).astype(jnp.bfloat16)
    audio_gain = jnp.dot(audio_hot, audio_gates, preferred_element_type=jnp.float32)
    positions = lax.axis_index("seq") * rows_audio + jnp.arange(rows_audio, dtype=jnp.int32)
    present = (positions < limit).astype(jnp.float32)
    audio_term = (
        present[:, None] * audio_gain * jnp.dot(v2a_att, wo_v2a, preferred_element_type=jnp.float32)
    )
    video_sum, audio_sum = (
        lax.psum_scatter(
            video_term.astype(jnp.bfloat16), ("mp", "sub"), scatter_dimension=1, tiled=True
        ).astype(jnp.float32),
        lax.psum_scatter(
            audio_term.astype(jnp.bfloat16), ("mp", "sub"), scatter_dimension=1, tiled=True
        ).astype(jnp.float32),
    )
    video_out = (video_in.astype(jnp.float32) + video_sum).astype(jnp.bfloat16)
    audio_out = (audio_in.astype(jnp.float32) + audio_sum).astype(jnp.bfloat16)
    return (video_out, audio_out)


LOG2E = 1.4426950408889634
VMEM = pl.BlockSpec(memory_space=pltpu.VMEM)
SMEM = pl.BlockSpec(memory_space=pltpu.SMEM)
HBM = pl.BlockSpec(memory_space=pltpu.HBM)
BF16, F32 = jnp.bfloat16, jnp.float32
LSE_ROWS = 16
LEAST = float(jnp.finfo(jnp.float32).min)
SEQ, FORWARDED, OUT_ORDER, LAST = 4, 3, [3, 2, 1], 2


def call(kernel, outs, operands, specs=None, flops=0, scratch=(), limit=8 * 2**20):
    size = sum(math.prod(x.shape) * x.dtype.itemsize for x in (*operands, *outs))
    if specs:
        operands = [
            pltpu.with_memory_space_constraint(x, pltpu.HBM) if spec is HBM else x for x, spec in zip(operands, specs)
        ]
    return pl.pallas_call(
        kernel,
        out_shape=tuple(outs),
        in_specs=specs or [VMEM] * len(operands),
        out_specs=tuple(VMEM for _ in outs),
        scratch_shapes=list(scratch),
        compiler_params=pltpu.CompilerParams(vmem_limit_bytes=limit),
        cost_estimate=pl.CostEstimate(flops=flops, bytes_accessed=size, transcendentals=0),
    )(*operands)


def shape(rows, cols, kind=BF16):
    return jax.ShapeDtypeStruct((rows, cols), kind)


def dot_t(a, b):
    return lax.dot_general(a, b, (((1,), (1,)), ((), ())), preferred_element_type=F32)


def dot(a, b):
    return jnp.dot(a, b, preferred_element_type=F32)


def index_of(axis):
    return lax.axis_index(axis).astype(jnp.int32)


def columns(index, width):
    return pl.ds(pl.multiple_of(index * width, width), width)


def copy_all(pairs, sems):
    copies = [pltpu.make_async_copy(src, dst, sems.at[i]) for i, (src, dst) in enumerate(pairs)]
    for copy in copies:
        copy.start()
    for copy in copies:
        copy.wait()


def pack_kernel(hops, width, q_ref, k_ref, v_ref, qa_ref, ka_ref, va_ref, *rest):
    outs, sems = rest[:-1], rest[-1]
    rows = q_ref.shape[0]
    rows_audio, cols_audio = qa_ref.shape
    me = index_of("seq")
    pairs = []
    for hop, out in zip(hops, outs):
        for i, ref in enumerate((q_ref, k_ref, v_ref)):
            pairs.append((ref.at[:, columns(me ^ hop, width)], out.at[pl.ds(i * rows, rows), :]))
        at = 3 * rows
        for ref in (qa_ref,) if hop == FORWARDED else (qa_ref, ka_ref, va_ref):
            for i in range(cols_audio // width):
                pairs.append((ref.at[:, pl.ds(i * width, width)], out.at[pl.ds(at, rows_audio), :]))
                at += rows_audio
    copy_all(pairs, sems)


def audio_block(ref, end, rows, cols, block):
    at, column = divmod(block * 128, ref.shape[1])
    top = ref.shape[0] - end * (cols // ref.shape[1]) * rows + at * rows
    return ref[top : top + rows, column : column + 128]


def one_hot_t(steps_ref):
    levels = lax.broadcasted_iota(jnp.int32, (NT, steps_ref.shape[1]), 0)
    return (levels == steps_ref[...]).astype(BF16)


def pick(hot_t, table):
    return lax.dot_general(hot_t, table, (((0,), (0,)), ((), ())), preferred_element_type=F32)


def fetch_kernel(limit_ref, vg_ref, *rest):
    count = (len(rest) - 9) // 2
    loads, gain_ref, audio_ref = rest[: count + 3], rest[count + 3], rest[count + 4]
    fetched, (vs_ref, as_ref, ag_ref, sems) = rest[count + 5 : -4], rest[-4:]
    copies = [
        pltpu.make_async_copy(src, dst, sems.at[i])
        for i, (src, dst) in enumerate(zip(loads, (vs_ref, as_ref, ag_ref, *fetched)))
    ]
    for copy in copies:
        copy.start()
    for copy in copies[:3]:
        copy.wait()
    hot_t = one_hot_t(vs_ref)
    piece = min(vg_ref.shape[1], 2048)
    for at in range(0, vg_ref.shape[1], piece):
        gain_ref[:, at : at + piece] = pick(hot_t, vg_ref[:, at : at + piece]).astype(BF16)
    rows_audio, narrow = audio_ref.shape
    part = index_of("mp") * 2 + index_of("sub")
    gain = pick(one_hot_t(as_ref), ag_ref[:, columns(part, narrow)])
    at = index_of("seq") * rows_audio + lax.broadcasted_iota(jnp.int32, (rows_audio, 1), 0)
    audio_ref[...] = jnp.where(at < limit_ref[0], gain, 0.0)
    for copy in copies[3:]:
        copy.wait()


def softmax_t(scores, scale, allowed=None):
    if allowed is not None:
        scores = [jnp.where(ok, x, LEAST) for ok, x in zip(allowed, scores)]
    peak = functools.reduce(jnp.maximum, [jnp.max(x, axis=0, keepdims=True) for x in scores])
    weights = [jnp.exp2((x - peak) * (scale * LOG2E)) for x in scores]
    total = functools.reduce(jnp.add, [jnp.sum(x, axis=0, keepdims=True) for x in weights])
    return peak, [x.astype(BF16) for x in weights], total


def turn(x):
    return x.astype(F32).T.astype(BF16)


def pair_rows(x, head):
    lane = lax.broadcasted_iota(jnp.int32, (1, 128), 1) // head
    return jnp.concatenate([jnp.where(lane == i, x, 0).astype(BF16) for i in range(128 // head)], axis=0)


def pair_columns(x, head):
    pair = 128 // head
    rows = x.shape[1] // pair
    return jnp.concatenate([x[i * head : (i + 1) * head, i * rows : (i + 1) * rows] for i in range(pair)], axis=0)


def audio_part(q, keys, values_t, head):
    pair, rows = 128 // head, q.shape[0]
    scale = 1.0 / math.sqrt(head)
    both = pair_rows(q, head)
    both = jnp.concatenate([both] * (128 // both.shape[0]), axis=0)
    peak, p, total = softmax_t([dot_t(keys, both)], scale)
    o = dot(values_t, p[0]) * (1.0 / total)
    lse = peak * (scale * LOG2E) + jnp.log2(total)
    o = [o[i * head : (i + 1) * head] for i in range(pair)]
    o = [x if i == 0 else pltpu.roll(x, 128 - i * rows, 1) for i, x in enumerate(o)]
    lses = [lse if i == 0 else pltpu.roll(lse, 128 - i * rows, 1) for i in range(pair)]
    return jnp.concatenate(o, axis=0).T[0:rows], lses


def audio_parts(ref, end, kv_ref, vvt_ref, rows_audio, head):
    cols = kv_ref.shape[1]
    outs, lses = [], []
    for block in range(cols // 128):
        cut = slice(block * 128, (block + 1) * 128)
        q = audio_block(ref, end, rows_audio, cols, block)
        o, lse = audio_part(q, kv_ref[:, cut], vvt_ref[cut, :], head)
        outs.append(o)
        lses += lse
    return outs, jnp.concatenate(lses, axis=0)


def store_tail(dst, top, outs, lse):
    rows_audio = outs[0].shape[0]
    for i, o in enumerate(outs):
        dst[top + i * rows_audio : top + (i + 1) * rows_audio, 0:128] = o.astype(BF16)
    pieces, left = [], lse
    for _ in range(3):
        pieces.append(left.astype(BF16).astype(F32))
        left = left - pieces[-1]
    pieces.append(jnp.zeros((LSE_ROWS - 3 * lse.shape[0], 128), F32))
    top += len(outs) * rows_audio
    dst[top : top + LSE_ROWS, 0:128] = jnp.concatenate(pieces, axis=0).astype(BF16)


def early_kernel(early, head, kv_ref, vv_ref, *rest):
    count = len(early)
    blocks, (part_ref, stats_ref, vt_ref, vvt_ref, own_v2a_ref, own_lse_ref) = rest[:count], rest[count : count + 6]
    tails, (s_ref,) = rest[count + 6 : -1], rest[-1:]
    rows, cols = kv_ref.shape
    rows_audio = own_v2a_ref.shape[0]
    for i, ref in enumerate(blocks):
        vt_ref[:, i * rows : (i + 1) * rows] = turn(ref[2 * rows : 3 * rows, :])
    for block in range(cols // 128):
        cut = slice(block * 128, (block + 1) * 128)
        vvt_ref[cut, :] = turn(vv_ref[:, cut])
    tops = []
    for block in range(cols // 128):
        ends = [1 if hop == FORWARDED else 3 for hop in early]
        q = [audio_block(ref, end, rows_audio, cols, block) for ref, end in zip(blocks, ends)]
        q = jnp.concatenate(q + [q[0]] * (128 // rows_audio - count), axis=0)
        scores = dot_t(kv_ref[:, block * 128 : (block + 1) * 128], pair_rows(q, head))
        for i in range(128 // head):
            row = (count * count + block * (128 // head) + i) * rows
            s_ref[row : row + rows, :] = scores[:, i * 128 : (i + 1) * 128]
        tops.append(jnp.max(scores, axis=0, keepdims=True))
    scale = 1.0 / math.sqrt(DHV)
    peaks = []
    for j, ref in enumerate(blocks):
        peak = None
        for i, other in enumerate(blocks):
            scores = dot_t(other[rows : 2 * rows, :], ref[0:rows, :])
            s_ref[(j * count + i) * rows : (j * count + i + 1) * rows, :] = scores
            top = jnp.max(scores, axis=0, keepdims=True)
            peak = top if i == 0 else jnp.maximum(peak, top)
        peaks.append(peak)
    for j, peak in enumerate(peaks):
        total, p = None, []
        for i in range(count):
            x = jnp.exp2((s_ref[(j * count + i) * rows : (j * count + i + 1) * rows, :] - peak) * (scale * LOG2E))
            summed = jnp.sum(x, axis=0, keepdims=True)
            total = summed if i == 0 else total + summed
            p.append(x.astype(BF16))
        part_ref[j * DHV : (j + 1) * DHV, :] = dot(vt_ref[...], jnp.concatenate(p, axis=0))
        stats_ref[2 * j : 2 * j + 1, :] = peak
        stats_ref[2 * j + 1 : 2 * j + 2, :] = total
    pair, scale = 128 // head, 1.0 / math.sqrt(head)
    outs, lses = [], []
    for block in range(cols // 128):
        cut = slice(block * 128, (block + 1) * 128)
        peak = tops[block]
        both = []
        for i in range(pair):
            at = slice(i * 128, (i + 1) * 128)
            row = (count * count + block * pair + i) * rows
            p = jnp.exp2((s_ref[row : row + rows, :] - peak[:, at]) * (scale * LOG2E))
            total = jnp.sum(p, axis=0, keepdims=True)
            lses.append(peak[:, at] * (scale * LOG2E) + jnp.log2(total))
            column = block * 128 + i * head
            both.append(dot(vvt_ref[column : column + head, :], p.astype(BF16)) * (1.0 / total))
        outs.append(jnp.concatenate(both, axis=0).T)
    lse = jnp.concatenate(lses, axis=0)
    own_lse_ref[...] = lse
    for block, o in enumerate(outs):
        own_v2a_ref[:, block * 128 : (block + 1) * 128] = o[0:rows_audio]
    for j in range(1, count):
        mine = [o[j * rows_audio : (j + 1) * rows_audio] for o in outs]
        store_tail(tails[j - 1], 0, mine, pltpu.roll(lse, 128 - j * rows_audio, 1))


def late_kernel(early, hops, rows_audio, head, kv_ref, vvt_ref, part_ref, stats_ref, vt_ref, last_ref, *rest):
    count, n = len(early), len(hops)
    blocks, tails, outs, s_ref = rest[:count], rest[count : 2 * count - 1], rest[2 * count - 1 : -1], rest[-1]
    by_hop = dict(zip(hops, outs))
    rows = kv_ref.shape[0]
    last = next(hop for hop in hops if hop not in early)
    scale = 1.0 / math.sqrt(DHV)
    keys = last_ref[rows : 2 * rows, :]
    peaks = []
    for j, ref in enumerate((*blocks, last_ref)):
        scores = dot_t(keys, ref[0:rows, :])
        s_ref[j * rows : (j + 1) * rows, :] = scores
        top = jnp.max(scores, axis=0, keepdims=True)
        peaks.append(jnp.maximum(top, stats_ref[2 * j : 2 * j + 1, :]) if j < count else top)
    for i, other in enumerate(blocks):
        scores = dot_t(other[rows : 2 * rows, :], last_ref[0:rows, :])
        s_ref[(n + i) * rows : (n + i + 1) * rows, :] = scores
        peaks[-1] = jnp.maximum(peaks[-1], jnp.max(scores, axis=0, keepdims=True))
    values_t = turn(last_ref[2 * rows : 3 * rows, :])

    def weigh(at, peak):
        x = jnp.exp2((s_ref[at * rows : (at + 1) * rows, :] - peak) * (scale * LOG2E))
        return x.astype(BF16), jnp.sum(x, axis=0, keepdims=True)

    audio = audio_parts(last_ref, 3, kv_ref, vvt_ref, rows_audio, head)
    total, p = None, []
    for i in range(count):
        x, summed = weigh(n + i, peaks[-1])
        total = summed if i == 0 else total + summed
        p.append(x)
    x, summed = weigh(count, peaks[-1])
    o = dot(vt_ref[...], jnp.concatenate(p, axis=0)) + dot(values_t, x)
    by_hop[last][0:rows, :] = (o * (1.0 / (total + summed))).T.astype(BF16)
    for j, hop in enumerate(early):
        x, summed = weigh(j, peaks[j])
        factor = jnp.exp2((stats_ref[2 * j : 2 * j + 1, :] - peaks[j]) * (scale * LOG2E))
        total = stats_ref[2 * j + 1 : 2 * j + 2, :] * factor + summed
        o = part_ref[j * DHV : (j + 1) * DHV, :] * factor + dot(values_t, x)
        by_hop[hop][0:rows, :] = (o * (1.0 / total)).T.astype(BF16)
    store_tail(by_hop[last], rows, *audio)
    for hop, tail in zip(early[1:], tails):
        by_hop[hop][rows : rows + tail.shape[0], :] = tail[...]
    dst = by_hop[FORWARDED]
    top = rows + tails[0].shape[0]
    dst[top:, :] = blocks[0][blocks[0].shape[0] - (dst.shape[0] - top) :, :]


def audio_allowed(hop, rows_audio, limit):
    row = lax.broadcasted_iota(jnp.int32, (rows_audio, 1), 0)
    return (index_of("seq") ^ hop) * rows_audio + row < limit


def spread(x, head):
    pair = 128 // head
    rows = x.shape[1] // pair
    parts = [jnp.broadcast_to(x[:, i * rows : (i + 1) * rows], (head, rows)) for i in range(pair)]
    return jnp.concatenate(parts, axis=0)


def attend_audio_kernel(hops, rows_audio, head, limit_ref, q_ref, *rest):
    blocks, part_ref, stats_ref = rest[:-2], rest[-2], rest[-1]
    cols = q_ref.shape[1]
    allowed = [audio_allowed(hop, rows_audio, limit_ref[0]) for hop in hops]
    scale = 1.0 / math.sqrt(head)
    for block in range(cols // 128):
        cut = slice(block * 128, (block + 1) * 128)
        q = pair_rows(q_ref[:, cut], head)
        scores = [dot_t(audio_block(ref, 2, rows_audio, cols, block), q) for ref in blocks]
        peak, p, total = softmax_t(scores, scale, allowed)
        vt = turn(jnp.concatenate([audio_block(ref, 1, rows_audio, cols, block) for ref in blocks], axis=0))
        part_ref[cut, :] = pair_columns(dot(vt, jnp.concatenate(p, axis=0)), head)
        stats_ref[2 * block : 2 * block + 1, :] = peak
        stats_ref[2 * block + 1 : 2 * block + 2, :] = total


def finish_audio(head, limit, q_ref, part_ref, stats_ref, last_ref, rows_audio, out_ref):
    cols = q_ref.shape[1]
    scale = 1.0 / math.sqrt(head)
    allowed = audio_allowed(FORWARDED, rows_audio, limit)
    for block in range(cols // 128):
        cut = slice(block * 128, (block + 1) * 128)
        q = pair_rows(q_ref[:, cut], head)
        scores = jnp.where(allowed, dot_t(audio_block(last_ref, 2, rows_audio, cols, block), q), LEAST)
        before, summed = stats_ref[2 * block : 2 * block + 1, :], stats_ref[2 * block + 1 : 2 * block + 2, :]
        peak = jnp.maximum(before, jnp.max(scores, axis=0, keepdims=True))
        factor = jnp.exp2((before - peak) * (scale * LOG2E))
        p = jnp.exp2((scores - peak) * (scale * LOG2E))
        inverse = 1.0 / (summed * factor + jnp.sum(p, axis=0, keepdims=True))
        vt = turn(audio_block(last_ref, 1, rows_audio, cols, block))
        last = pair_columns(dot(vt, p.astype(BF16)), head)
        both = part_ref[cut, :] * spread(factor, head) + last
        out_ref[:, cut] = (both * spread(inverse, head)).T.astype(BF16)


def merge_audio(head, top, v2a_ref, lse_ref, got, out_ref):
    rows_audio, cols = v2a_ref.shape
    heads = cols // head
    lses = [lse_ref[...]]
    for ref in got:
        at = top + cols // 128 * rows_audio
        packed = ref[at : at + LSE_ROWS, 0:128].astype(F32)
        lses.append(packed[0:heads] + packed[heads : 2 * heads] + packed[2 * heads : 3 * heads])
    peak = functools.reduce(jnp.maximum, lses)
    parts = [jnp.exp2(x - peak) for x in lses]
    total = functools.reduce(jnp.add, parts)
    inverse = 1.0 / total
    parts = [x * inverse for x in parts]
    parts.append(jnp.zeros((128 - len(parts) * heads, 128), F32))
    shares = jnp.concatenate(parts, axis=0).T[0:rows_audio]
    pair = 128 // head
    lane = lax.broadcasted_iota(jnp.int32, (1, 128), 1) // head
    for block in range(cols // 128):
        cut = slice(block * 128, (block + 1) * 128)
        at = top + block * rows_audio
        summed = jnp.zeros((rows_audio, 128), F32)
        for j in range(len(lses)):
            o = v2a_ref[:, cut] if j == 0 else got[j - 1][at : at + rows_audio, 0:128].astype(F32)
            share = jnp.zeros((rows_audio, 128), F32)
            for i in range(pair):
                column = j * heads + block * pair + i
                share = jnp.where(lane == i, shares[:, column : column + 1], share)
            summed = summed + share * o
        out_ref[:, cut] = summed.astype(BF16)


def block_of(far, other):
    mp, sub = index_of("mp"), index_of("sub")
    return (1 - mp if far else mp) * 2 + (1 - sub if other else sub)


def project_self(block, half, att_ref, ws_ref, gain_ref):
    cut = ws_ref.shape[1] // 8
    at = columns(block * 2 + half, cut)
    return gain_ref[:, at].astype(F32) * dot(att_ref[...], ws_ref[:, at])


def project_a2v(block, half, a2v_ref, wa_ref, gain_ref):
    cut = wa_ref.shape[1] // 8
    gain = gain_ref[:, columns(block * 2 + half + 8, cut)].astype(F32)
    return gain * dot(a2v_ref[...], wa_ref[:, columns(block * 2 + half, cut)])


def project(block, half, heads, weights, gain_ref):
    term = project_self(block, half, heads[0], weights[0], gain_ref)
    return term + project_a2v(block, half, heads[1], weights[1], gain_ref)


def project_audio(block, v2a_ref, wv_ref):
    return dot(v2a_ref[...], wv_ref[:, columns(block, wv_ref.shape[1] // 4)])


def first_kernel(hops, rows_audio, head, limit_ref, q_ref, part_ref, stats_ref, own_ref, ws_ref, wa_ref, gain_ref, *rest):
    got, (self_ref, a2v_ref, out_ref, term_ref) = rest[: len(hops) - 1], rest[len(hops) - 1 :]
    rows, width = own_ref.shape
    last_ref = got[hops.index(FORWARDED) - 1]
    self_ref[:, columns(index_of("seq"), width)] = own_ref[...]
    for hop, ref in zip(hops[1:], got):
        self_ref[:, columns(index_of("seq") ^ hop, width)] = ref[0:rows, :]
    block = block_of(True, True)
    term_ref[...] = project_self(block, 0, self_ref, ws_ref, gain_ref)
    finish_audio(head, limit_ref[0], q_ref, part_ref, stats_ref, last_ref, rows_audio, a2v_ref)
    out_ref[...] = (term_ref[...] + project_a2v(block, 0, a2v_ref, wa_ref, gain_ref)).astype(BF16)


def second_kernel(head, self_ref, a2v_ref, ws_ref, wa_ref, wv_ref, gain_ref, v2a_ref, lse_ref, *rest):
    got, (out_ref, audio_ref, low_ref) = rest[:-3], rest[-3:]
    rows = self_ref.shape[0]
    block = block_of(True, True)
    out_ref[0:rows, :] = project(block, 1, (self_ref, a2v_ref), (ws_ref, wa_ref), gain_ref).astype(BF16)
    merge_audio(head, rows, v2a_ref, lse_ref, got, audio_ref)
    out_ref[rows:, :] = project_audio(block, audio_ref, wv_ref).astype(BF16)
    low_ref[...] = project(block_of(True, False), 0, (self_ref, a2v_ref), (ws_ref, wa_ref), gain_ref)


def far_low_kernel(low_ref, extra_ref, out_ref):
    out_ref[...] = (low_ref[...] + extra_ref[...].astype(F32)).astype(BF16)


def near_kernel(self_ref, a2v_ref, audio_ref, ws_ref, wa_ref, wv_ref, gain_ref, send_ref, own_ref):
    rows = self_ref.shape[0]
    for out, other in ((send_ref, True), (own_ref, False)):
        block = block_of(False, other)
        for half in range(2):
            term = project(block, half, (self_ref, a2v_ref), (ws_ref, wa_ref), gain_ref)
            out[half * rows : (half + 1) * rows, :] = term.astype(out.dtype)
        out[2 * rows :, :] = project_audio(block, audio_ref, wv_ref).astype(out.dtype)


def far_high_kernel(self_ref, a2v_ref, ws_ref, wa_ref, gain_ref, extra_ref, audio_ref, wv_ref, out_ref):
    rows = self_ref.shape[0]
    block = block_of(True, False)
    term = project(block, 1, (self_ref, a2v_ref), (ws_ref, wa_ref), gain_ref)
    out_ref[0:rows, :] = (term + extra_ref[0:rows, :].astype(F32)).astype(BF16)
    term = project_audio(block, audio_ref, wv_ref)
    out_ref[rows:, :] = (term + extra_ref[rows:, :].astype(F32)).astype(BF16)


def finish_kernel(video_ref, audio_ref, gain_ref, own_ref, core_ref, low_ref, high_ref, video_out, audio_out):
    rows = video_ref.shape[0]
    cut = video_ref.shape[1] // 2
    near = own_ref[...] + core_ref[...].astype(F32)
    for half, ref in enumerate((low_ref, high_ref)):
        at = slice(half * cut, (half + 1) * cut)
        term = near[half * rows : (half + 1) * rows] + ref[0:rows, :].astype(F32)
        video_out[:, at] = (video_ref[:, at].astype(F32) + term).astype(BF16)
    term = near[2 * rows :] + high_ref[rows:, :].astype(F32)
    audio_out[...] = (audio_ref[...].astype(F32) + gain_ref[...] * term).astype(BF16)


def on_device_heads(
    video_in,
    audio_in,
    q_self,
    k_self,
    v_self,
    q_a2v,
    k_a2v,
    v_a2v,
    q_v2a,
    k_v2a,
    v_v2a,
    wo_self,
    wo_a2v,
    wo_v2a,
    video_gates,
    audio_gates,
    video_steps,
    audio_steps,
    audio_len,
    *,
    n,
):
    hops = [0] + OUT_ORDER
    rows, cols = q_self.shape
    rows_audio, cross = q_v2a.shape
    width = cols // n

    def trade(x, axis, hop, size):
        return lax.ppermute(x, axis, [(i, i ^ hop) for i in range(size)])

    video, audio = 3 * rows, cross // width * rows_audio

    def pack(some):
        ends = [1 if hop == FORWARDED else 3 for hop in some]
        return call(
            functools.partial(pack_kernel, some, width),
            [shape(video + end * audio, width) for end in ends],
            (q_self, k_self, v_self, q_v2a, k_a2v, v_a2v),
            [HBM] * 6,
            scratch=[pltpu.SemaphoreType.DMA((3 * len(some) + sum(ends) * audio // rows_audio,))],
        )

    packed = pack(hops[1:2])
    rest = pack(hops[:1] + hops[2:])
    packed = [rest[0], *packed, *rest[1:]]
    blocks = dict(zip(hops, packed))
    for hop in hops[1:]:
        blocks[hop] = trade(blocks[hop], "seq", hop, n)

    late = (k_v2a, v_v2a, q_a2v, wo_self, wo_a2v, wo_v2a, video_in, audio_in)
    steps = (video_steps.reshape(1, rows), audio_steps.reshape(1, rows_audio))
    gain, audio_gain, k_own, v_own, q_own, ws, wa, wv, video_own, audio_own = call(
        fetch_kernel,
        [shape(rows, 2 * video_gates.shape[2]), shape(*audio_in.shape, F32)]
        + [shape(*x.shape) for x in late],
        (audio_len, video_gates.reshape(NT, -1), *steps, audio_gates, *late),
        [SMEM, VMEM] + [HBM] * (3 + len(late)),
        scratch=[pltpu.VMEM(x.shape, x.dtype) for x in (*steps, audio_gates)]
        + [pltpu.SemaphoreType.DMA((3 + len(late),))],
    )
    tail = cross // 128 * rows_audio + LSE_ROWS
    early = [hop for hop in hops if hop != LAST]
    count = len(early)
    part, stats, vt, vvt, own_v2a, own_lse, *tails = call(
        functools.partial(early_kernel, early, DHC),
        [
            shape(count * width, rows, F32),
            shape(2 * count, rows, F32),
            shape(width, count * rows),
            shape(cross, rows),
            shape(rows_audio, cross, F32),
            shape(cross // DHC, 128, F32),
        ]
        + [shape(tail, width)] * (count - 1),
        (k_own, v_own, *(blocks[hop] for hop in early)),
        flops=4 * count * count * rows * rows * width,
        scratch=[pltpu.VMEM(((count * count + cross // DHC) * rows, rows), F32)],
    )
    own, *sends = call(
        functools.partial(late_kernel, early, hops, rows_audio, DHC),
        [shape(rows, width)]
        + [shape(rows + tail + (2 * audio if hop == FORWARDED else 0), width) for hop in hops[1:]],
        (k_own, vvt, part, stats, vt, blocks[LAST], *(blocks[hop] for hop in early), *tails),
        flops=4 * (2 * n - 1) * rows * rows * width,
        scratch=[pltpu.VMEM(((2 * n - 1) * rows, rows), F32)],
    )
    got = [trade(x, "seq", hop, n) for x, hop in zip(sends, hops[1:])]
    near = [hop for hop in hops if hop != FORWARDED]
    a2v_part, a2v_stats = call(
        functools.partial(attend_audio_kernel, near, rows_audio, DHC),
        [shape(cross, rows, F32), shape(cross // 64, 128 // DHC * rows, F32)],
        (audio_len, q_own, *(blocks[hop] for hop in near)),
        [SMEM] + [VMEM] * n,
        flops=8 * n * rows * rows_audio * cross,
    )

    half = video_in.shape[1] // 2
    flops = 2 * rows * (cols + cross) * half
    self_att, a2v_att, first = call(
        functools.partial(first_kernel, hops, rows_audio, DHC),
        [shape(rows, cols), shape(rows, cross), shape(rows, half)],
        (audio_len, q_own, a2v_part, a2v_stats, own, ws, wa, gain, *got),
        [SMEM] + [VMEM] * (n + 6),
        flops=flops,
        scratch=[pltpu.VMEM((rows, half), F32)],
    )
    first = trade(first, "sub", 1, 2)
    second, v2a_att, own_low = call(
        functools.partial(second_kernel, DHC),
        [shape(rows + rows_audio, half), shape(rows_audio, cross), shape(rows, half, F32)],
        (self_att, a2v_att, ws, wa, wv, gain, own_v2a, own_lse, *got),
        flops=2 * flops,
    )
    second = trade(second, "sub", 1, 2)
    (low,) = call(far_low_kernel, [shape(rows, half)], (own_low, first))
    low = trade(low, "mp", 1, 2)
    (high,) = call(
        far_high_kernel,
        [shape(rows + rows_audio, half)],
        (self_att, a2v_att, ws, wa, gain, second, v2a_att, wv),
        flops=flops,
    )
    high = trade(high, "mp", 1, 2)
    near, own_sum = call(
        near_kernel,
        [shape(2 * rows + rows_audio, half), shape(2 * rows + rows_audio, half, F32)],
        (self_att, a2v_att, v2a_att, ws, wa, wv, gain),
        flops=4 * flops,
    )
    near = trade(near, "sub", 1, 2)
    return call(
        finish_kernel,
        [shape(*video_in.shape), shape(*audio_in.shape)],
        (video_own, audio_own, audio_gain, own_sum, near, low, high),
    )


def on_device(n, mp, sub, *arrays):
    cols, cross = arrays[2].shape[1], arrays[5].shape[1]
    width = cols // n
    fits = (
        n == SEQ
        and (mp, sub) == (2, 2)
        and width == DHV == 128
        and cross % width == 0
        and 3 * (cross // DHC) <= LSE_ROWS
        and n * arrays[8].shape[0] == arrays[2].shape[0] == 128
        and arrays[0].shape[1] == 2 * arrays[1].shape[1]
    )
    if fits:
        return on_device_heads(*arrays, n=n)
    return on_device_gather(*arrays)


def solution(mesh):
    in_specs = (
        P(("groups", "seq"), ("mp", "sub")),
        P(("groups", "seq"), ("mp", "sub")),
        P(("groups", "seq"), ("mp", "sub")),
        P(("groups", "seq"), ("mp", "sub")),
        P(("groups", "seq"), ("mp", "sub")),
        P(("groups", "seq"), ("mp", "sub")),
        P(("groups", "seq"), ("mp", "sub")),
        P(("groups", "seq"), ("mp", "sub")),
        P(("groups", "seq"), ("mp", "sub")),
        P(("groups", "seq"), ("mp", "sub")),
        P(("groups", "seq"), ("mp", "sub")),
        P(("mp", "sub"), None),
        P(("mp", "sub"), None),
        P(("mp", "sub"), None),
        P(),
        P(),
        P(("groups", "seq")),
        P(("groups", "seq")),
        P("groups"),
    )
    out_specs = (P(("groups", "seq"), ("mp", "sub")), P(("groups", "seq"), ("mp", "sub")))
    return jax.shard_map(
        functools.partial(on_device, *(mesh.shape[a] for a in ("seq", "mp", "sub"))), mesh=mesh, in_specs=in_specs, out_specs=out_specs, check_vma=False
    )
```

```python
import functools
import math

import jax
import jax.numpy as jnp
from jax import lax
from jax.experimental import pallas as pl
from jax.experimental.pallas import tpu as pltpu
from jax.sharding import PartitionSpec as P


DHV = 128
DHC = 64
NT = 16


def start_state(rows, heads, width):
    return (
        jnp.full((rows, heads), -1e30, jnp.float32),
        jnp.zeros((rows, heads), jnp.float32),
        jnp.zeros((rows, heads, width), jnp.float32),
    )


def update_block(state, queries, keys, values, heads, width, allowed):
    rows = queries.shape[0]
    count = keys.shape[0]
    q_heads = queries.reshape(rows, heads, width)
    k_heads = keys.reshape(count, heads, width)
    v_heads = values.reshape(count, heads, width)
    scores = jnp.einsum(
        "qhd,khd->qhk", q_heads, k_heads, preferred_element_type=jnp.float32
    ) / math.sqrt(width)
    if allowed is not None:
        scores = jnp.where(allowed[None, None, :], scores, -jnp.inf)
    peak_old, total_old, summed_old = state
    peak = jnp.maximum(peak_old, jnp.max(scores, axis=2))
    weights = jnp.exp(scores - peak[:, :, None])
    factor = jnp.exp(peak_old - peak)
    total = total_old * factor + jnp.sum(weights, axis=2)
    summed = summed_old * factor[:, :, None] + jnp.einsum(
        "qhk,khd->qhd", weights.astype(jnp.bfloat16), v_heads, preferred_element_type=jnp.float32
    )
    return (peak, total, summed)


def update_state(state, queries, keys, values, heads, width, start, limit):
    count = keys.shape[0]
    block = 1024 if count > 1024 and count % 1024 == 0 else count
    if block == count:
        allowed = None
        if limit is not None:
            allowed = jnp.arange(count, dtype=jnp.int32) < limit
        return update_block(state, queries, keys, values, heads, width, allowed)
    steps = count // block
    key_blocks = keys.reshape(steps, block, keys.shape[1])
    value_blocks = values.reshape(steps, block, values.shape[1])
    offsets = jnp.arange(steps, dtype=jnp.int32) * block

    def one_block(carry, items):
        key_rows, value_rows, offset = items
        allowed = None
        if limit is not None:
            allowed = start + offset + jnp.arange(block, dtype=jnp.int32) < limit
        return (update_block(carry, queries, key_rows, value_rows, heads, width, allowed), None)

    result, _ = lax.scan(one_block, state, (key_blocks, value_blocks, offsets))
    return result


def finish(state, heads, width):
    _, total, summed = state
    rows = summed.shape[0]
    return (summed / total[:, :, None]).reshape(rows, heads * width).astype(jnp.bfloat16)


def on_device_gather(
    video_in,
    audio_in,
    q_self,
    k_self,
    v_self,
    q_a2v,
    k_a2v,
    v_a2v,
    q_v2a,
    k_v2a,
    v_v2a,
    wo_self,
    wo_a2v,
    wo_v2a,
    video_gates,
    audio_gates,
    video_steps,
    audio_steps,
    audio_len,
):
    heads_self = q_self.shape[1] // DHV
    heads_cross = q_a2v.shape[1] // DHC
    rows_video = q_self.shape[0]
    rows_audio = q_v2a.shape[0]
    limit = audio_len[0]
    piece = (
        lax.all_gather(k_a2v, "seq", axis=0, tiled=True),
        lax.all_gather(v_a2v, "seq", axis=0, tiled=True),
    )
    a2v_state = update_state(
        start_state(rows_video, heads_cross, DHC),
        q_a2v,
        piece[0],
        piece[1],
        heads_cross,
        DHC,
        jnp.int32(0),
        limit,
    )
    a2v_att = finish(a2v_state, heads_cross, DHC)
    piece = (
        lax.all_gather(k_self, "seq", axis=0, tiled=True),
        lax.all_gather(v_self, "seq", axis=0, tiled=True),
    )
    self_state = update_state(
        start_state(rows_video, heads_self, DHV),
        q_self,
        piece[0],
        piece[1],
        heads_self,
        DHV,
        jnp.int32(0),
        None,
    )
    piece = (
        lax.all_gather(k_v2a, "seq", axis=0, tiled=True),
        lax.all_gather(v_v2a, "seq", axis=0, tiled=True),
    )
    v2a_state = update_state(
        start_state(rows_audio, heads_cross, DHC),
        q_v2a,
        piece[0],
        piece[1],
        heads_cross,
        DHC,
        jnp.int32(0),
        None,
    )
    self_att = finish(self_state, heads_self, DHV)
    v2a_att = finish(v2a_state, heads_cross, DHC)
    levels = jnp.arange(NT, dtype=jnp.int32)
    video_hot = (video_steps[:, None] == levels[None, :]).astype(jnp.bfloat16)
    video_gain = jnp.dot(video_hot, video_gates.reshape(NT, -1), preferred_element_type=jnp.float32)
    width_video = video_gates.shape[2]
    video_term = video_gain[:, :width_video] * jnp.dot(
        self_att, wo_self, preferred_element_type=jnp.float32
    )
    video_term = video_term + video_gain[:, width_video:] * jnp.dot(
        a2v_att, wo_a2v, preferred_element_type=jnp.float32
    )
    audio_hot = (audio_steps[:, None] == levels[None, :]).astype(jnp.bfloat16)
    audio_gain = jnp.dot(audio_hot, audio_gates, preferred_element_type=jnp.float32)
    positions = lax.axis_index("seq") * rows_audio + jnp.arange(rows_audio, dtype=jnp.int32)
    present = (positions < limit).astype(jnp.float32)
    audio_term = (
        present[:, None] * audio_gain * jnp.dot(v2a_att, wo_v2a, preferred_element_type=jnp.float32)
    )
    video_sum, audio_sum = (
        lax.psum_scatter(
            video_term.astype(jnp.bfloat16), ("mp", "sub"), scatter_dimension=1, tiled=True
        ).astype(jnp.float32),
        lax.psum_scatter(
            audio_term.astype(jnp.bfloat16), ("mp", "sub"), scatter_dimension=1, tiled=True
        ).astype(jnp.float32),
    )
    video_out = (video_in.astype(jnp.float32) + video_sum).astype(jnp.bfloat16)
    audio_out = (audio_in.astype(jnp.float32) + audio_sum).astype(jnp.bfloat16)
    return (video_out, audio_out)


LOG2E = 1.4426950408889634
VMEM = pl.BlockSpec(memory_space=pltpu.VMEM)
SMEM = pl.BlockSpec(memory_space=pltpu.SMEM)
HBM = pl.BlockSpec(memory_space=pltpu.HBM)
BF16, F32 = jnp.bfloat16, jnp.float32
LSE_ROWS, PARTS = 16, 4
LEAST = float(jnp.finfo(jnp.float32).min)
SEQ, FORWARDED, OUT_ORDER, LAST = 4, 3, [3, 2, 1], 2


def call(kernel, outs, operands, specs=None, flops=0, scratch=(), limit=8 * 2**20):
    size = sum(math.prod(x.shape) * x.dtype.itemsize for x in (*operands, *outs))
    if specs:
        operands = [
            pltpu.with_memory_space_constraint(x, pltpu.HBM) if spec is HBM else x for x, spec in zip(operands, specs)
        ]
    return pl.pallas_call(
        kernel,
        out_shape=tuple(outs),
        in_specs=specs or [VMEM] * len(operands),
        out_specs=tuple(VMEM for _ in outs),
        scratch_shapes=list(scratch),
        compiler_params=pltpu.CompilerParams(vmem_limit_bytes=limit),
        cost_estimate=pl.CostEstimate(flops=flops, bytes_accessed=size, transcendentals=0),
    )(*operands)


def shape(rows, cols, kind=BF16):
    return jax.ShapeDtypeStruct((rows, cols), kind)


def dot_t(a, b):
    return lax.dot_general(a, b, (((1,), (1,)), ((), ())), preferred_element_type=F32)


def dot(a, b):
    return jnp.dot(a, b, preferred_element_type=F32)


def index_of(axis):
    return lax.axis_index(axis).astype(jnp.int32)


def columns(index, width):
    return pl.ds(pl.multiple_of(index * width, width), width)


def copy_all(pairs, sems):
    copies = [pltpu.make_async_copy(src, dst, sems.at[i]) for i, (src, dst) in enumerate(pairs)]
    for copy in copies:
        copy.start()
    for copy in copies:
        copy.wait()


def pack_kernel(hops, width, q_ref, k_ref, v_ref, qa_ref, ka_ref, va_ref, *rest):
    outs, sems = rest[:-1], rest[-1]
    rows = q_ref.shape[0]
    rows_audio, cols_audio = qa_ref.shape
    me = index_of("seq")
    pairs = []
    for hop, out in zip(hops, outs):
        for i, ref in enumerate((q_ref, k_ref, v_ref)):
            pairs.append((ref.at[:, columns(me ^ hop, width)], out.at[pl.ds(i * rows, rows), :]))
        at = 3 * rows
        for ref in (qa_ref,) if hop == FORWARDED else (qa_ref, ka_ref, va_ref):
            for i in range(cols_audio // width):
                pairs.append((ref.at[:, pl.ds(i * width, width)], out.at[pl.ds(at, rows_audio), :]))
                at += rows_audio
    copy_all(pairs, sems)


def audio_block(ref, end, rows, cols, block):
    at, column = divmod(block * 128, ref.shape[1])
    top = ref.shape[0] - end * (cols // ref.shape[1]) * rows + at * rows
    return ref[top : top + rows, column : column + 128]


def one_hot_t(steps_ref):
    levels = lax.broadcasted_iota(jnp.int32, (NT, steps_ref.shape[1]), 0)
    return (levels == steps_ref[...]).astype(BF16)


def pick(hot_t, table):
    return lax.dot_general(hot_t, table, (((0,), (0,)), ((), ())), preferred_element_type=F32)


def fetch_kernel(limit_ref, vg_ref, *rest):
    count = (len(rest) - 9) // 2
    loads, gain_ref, audio_ref = rest[: count + 3], rest[count + 3], rest[count + 4]
    fetched, (vs_ref, as_ref, ag_ref, sems) = rest[count + 5 : -4], rest[-4:]
    copies = [
        pltpu.make_async_copy(src, dst, sems.at[i])
        for i, (src, dst) in enumerate(zip(loads, (vs_ref, as_ref, ag_ref, *fetched)))
    ]
    for copy in copies:
        copy.start()
    for copy in copies[:3]:
        copy.wait()
    hot_t = one_hot_t(vs_ref)
    piece = min(vg_ref.shape[1], 2048)
    for at in range(0, vg_ref.shape[1], piece):
        gain_ref[:, at : at + piece] = pick(hot_t, vg_ref[:, at : at + piece]).astype(BF16)
    rows_audio, narrow = audio_ref.shape
    part = index_of("mp") * 2 + index_of("sub")
    gain = pick(one_hot_t(as_ref), ag_ref[:, columns(part, narrow)])
    at = index_of("seq") * rows_audio + lax.broadcasted_iota(jnp.int32, (rows_audio, 1), 0)
    audio_ref[...] = jnp.where(at < limit_ref[0], gain, 0.0)
    for copy in copies[3:]:
        copy.wait()


def softmax_t(scores, scale, allowed=None):
    if allowed is not None:
        scores = [jnp.where(ok, x, LEAST) for ok, x in zip(allowed, scores)]
    peak = functools.reduce(jnp.maximum, [jnp.max(x, axis=0, keepdims=True) for x in scores])
    weights = [jnp.exp2((x - peak) * (scale * LOG2E)) for x in scores]
    total = functools.reduce(jnp.add, [jnp.sum(x, axis=0, keepdims=True) for x in weights])
    return peak, [x.astype(BF16) for x in weights], total


def turn(x):
    return x.astype(F32).T.astype(BF16)


def pair_rows(x, head):
    lane = lax.broadcasted_iota(jnp.int32, (1, 128), 1) // head
    return jnp.concatenate([jnp.where(lane == i, x, 0).astype(BF16) for i in range(128 // head)], axis=0)


def pair_columns(x, head):
    pair = 128 // head
    rows = x.shape[1] // pair
    return jnp.concatenate([x[i * head : (i + 1) * head, i * rows : (i + 1) * rows] for i in range(pair)], axis=0)


def audio_part(q, keys, values_t, head):
    pair, rows = 128 // head, q.shape[0]
    scale = 1.0 / math.sqrt(head)
    both = pair_rows(q, head)
    both = jnp.concatenate([both] * (128 // both.shape[0]), axis=0)
    peak, p, total = softmax_t([dot_t(keys, both)], scale)
    o = dot(values_t, p[0]) * (1.0 / total)
    lse = peak * (scale * LOG2E) + jnp.log2(total)
    o = [o[i * head : (i + 1) * head] for i in range(pair)]
    o = [x if i == 0 else pltpu.roll(x, 128 - i * rows, 1) for i, x in enumerate(o)]
    lses = [lse if i == 0 else pltpu.roll(lse, 128 - i * rows, 1) for i in range(pair)]
    return jnp.concatenate(o, axis=0).T[0:rows], lses


def audio_parts(ref, end, kv_ref, vvt_ref, rows_audio, head):
    cols = kv_ref.shape[1]
    outs, lses = [], []
    for block in range(cols // 128):
        cut = slice(block * 128, (block + 1) * 128)
        q = audio_block(ref, end, rows_audio, cols, block)
        o, lse = audio_part(q, kv_ref[:, cut], vvt_ref[cut, :], head)
        outs.append(o)
        lses += lse
    return outs, jnp.concatenate(lses, axis=0)


def store_tail(dst, top, outs, lse):
    rows_audio = outs[0].shape[0]
    for i, o in enumerate(outs):
        dst[top + i * rows_audio : top + (i + 1) * rows_audio, 0:128] = o.astype(BF16)
    pieces, left = [], lse
    for _ in range(3):
        pieces.append(left.astype(BF16).astype(F32))
        left = left - pieces[-1]
    pieces.append(jnp.zeros((LSE_ROWS - 3 * lse.shape[0], 128), F32))
    top += len(outs) * rows_audio
    dst[top : top + LSE_ROWS, 0:128] = jnp.concatenate(pieces, axis=0).astype(BF16)


def early_kernel(early, head, kv_ref, vv_ref, *rest):
    count = len(early)
    blocks, (part_ref, stats_ref, vt_ref, vvt_ref, own_v2a_ref, own_lse_ref) = rest[:count], rest[count : count + 6]
    tails, (s_ref,) = rest[count + 6 : -1], rest[-1:]
    rows, cols = kv_ref.shape
    rows_audio = own_v2a_ref.shape[0]
    for i, ref in enumerate(blocks):
        vt_ref[:, i * rows : (i + 1) * rows] = turn(ref[2 * rows : 3 * rows, :])
    for block in range(cols // 128):
        cut = slice(block * 128, (block + 1) * 128)
        vvt_ref[cut, :] = turn(vv_ref[:, cut])
    tops = []
    for block in range(cols // 128):
        ends = [1 if hop == FORWARDED else 3 for hop in early]
        q = [audio_block(ref, end, rows_audio, cols, block) for ref, end in zip(blocks, ends)]
        q = jnp.concatenate(q + [q[0]] * (128 // rows_audio - count), axis=0)
        scores = dot_t(kv_ref[:, block * 128 : (block + 1) * 128], pair_rows(q, head))
        for i in range(128 // head):
            row = (count * count + block * (128 // head) + i) * rows
            s_ref[row : row + rows, :] = scores[:, i * 128 : (i + 1) * 128]
        tops.append(jnp.max(scores, axis=0, keepdims=True))
    scale = 1.0 / math.sqrt(DHV)
    peaks = []
    for j, ref in enumerate(blocks):
        peak = None
        for i, other in enumerate(blocks):
            scores = dot_t(other[rows : 2 * rows, :], ref[0:rows, :])
            s_ref[(j * count + i) * rows : (j * count + i + 1) * rows, :] = scores
            top = jnp.max(scores, axis=0, keepdims=True)
            peak = top if i == 0 else jnp.maximum(peak, top)
        peaks.append(peak)
    for j, peak in enumerate(peaks):
        total, p = None, []
        for i in range(count):
            x = jnp.exp2((s_ref[(j * count + i) * rows : (j * count + i + 1) * rows, :] - peak) * (scale * LOG2E))
            summed = jnp.sum(x, axis=0, keepdims=True)
            total = summed if i == 0 else total + summed
            p.append(x.astype(BF16))
        part_ref[j * DHV : (j + 1) * DHV, :] = dot(vt_ref[...], jnp.concatenate(p, axis=0))
        stats_ref[2 * j : 2 * j + 1, :] = peak
        stats_ref[2 * j + 1 : 2 * j + 2, :] = total
    pair, scale = 128 // head, 1.0 / math.sqrt(head)
    outs, lses = [], []
    for block in range(cols // 128):
        cut = slice(block * 128, (block + 1) * 128)
        peak = tops[block]
        both = []
        for i in range(pair):
            at = slice(i * 128, (i + 1) * 128)
            row = (count * count + block * pair + i) * rows
            p = jnp.exp2((s_ref[row : row + rows, :] - peak[:, at]) * (scale * LOG2E))
            total = jnp.sum(p, axis=0, keepdims=True)
            lses.append(peak[:, at] * (scale * LOG2E) + jnp.log2(total))
            column = block * 128 + i * head
            both.append(dot(vvt_ref[column : column + head, :], p.astype(BF16)) * (1.0 / total))
        outs.append(jnp.concatenate(both, axis=0).T)
    lse = jnp.concatenate(lses, axis=0)
    own_lse_ref[...] = lse
    for block, o in enumerate(outs):
        own_v2a_ref[:, block * 128 : (block + 1) * 128] = o[0:rows_audio]
    for j in range(1, count):
        mine = [o[j * rows_audio : (j + 1) * rows_audio] for o in outs]
        store_tail(tails[j - 1], 0, mine, pltpu.roll(lse, 128 - j * rows_audio, 1))


def late_kernel(early, hops, rows_audio, head, kv_ref, vvt_ref, part_ref, stats_ref, vt_ref, last_ref, *rest):
    count, n = len(early), len(hops)
    blocks, tails, outs, s_ref = rest[:count], rest[count : 2 * count - 1], rest[2 * count - 1 : -1], rest[-1]
    by_hop = dict(zip(hops, outs))
    rows = kv_ref.shape[0]
    last = next(hop for hop in hops if hop not in early)
    scale = 1.0 / math.sqrt(DHV)
    keys = last_ref[rows : 2 * rows, :]
    peaks = []
    for j, ref in enumerate((*blocks, last_ref)):
        scores = dot_t(keys, ref[0:rows, :])
        s_ref[j * rows : (j + 1) * rows, :] = scores
        top = jnp.max(scores, axis=0, keepdims=True)
        peaks.append(jnp.maximum(top, stats_ref[2 * j : 2 * j + 1, :]) if j < count else top)
    for i, other in enumerate(blocks):
        scores = dot_t(other[rows : 2 * rows, :], last_ref[0:rows, :])
        s_ref[(n + i) * rows : (n + i + 1) * rows, :] = scores
        peaks[-1] = jnp.maximum(peaks[-1], jnp.max(scores, axis=0, keepdims=True))
    values_t = turn(last_ref[2 * rows : 3 * rows, :])

    def weigh(at, peak):
        x = jnp.exp2((s_ref[at * rows : (at + 1) * rows, :] - peak) * (scale * LOG2E))
        return x.astype(BF16), jnp.sum(x, axis=0, keepdims=True)

    audio = audio_parts(last_ref, 3, kv_ref, vvt_ref, rows_audio, head)
    total, p = None, []
    for i in range(count):
        x, summed = weigh(n + i, peaks[-1])
        total = summed if i == 0 else total + summed
        p.append(x)
    x, summed = weigh(count, peaks[-1])
    o = dot(vt_ref[...], jnp.concatenate(p, axis=0)) + dot(values_t, x)
    by_hop[last][0:rows, :] = (o * (1.0 / (total + summed))).T.astype(BF16)
    for j, hop in enumerate(early):
        x, summed = weigh(j, peaks[j])
        factor = jnp.exp2((stats_ref[2 * j : 2 * j + 1, :] - peaks[j]) * (scale * LOG2E))
        total = stats_ref[2 * j + 1 : 2 * j + 2, :] * factor + summed
        o = part_ref[j * DHV : (j + 1) * DHV, :] * factor + dot(values_t, x)
        by_hop[hop][0:rows, :] = (o * (1.0 / total)).T.astype(BF16)
    store_tail(by_hop[last], rows, *audio)
    for hop, tail in zip(early[1:], tails):
        by_hop[hop][rows : rows + tail.shape[0], :] = tail[...]
    top = rows + tails[0].shape[0]
    extra = by_hop[FORWARDED].shape[0] - top
    by_hop[FORWARDED][top:, :] = blocks[0][blocks[0].shape[0] - extra :, :]
    by_hop[1][top:, :] = last_ref[last_ref.shape[0] - 2 * extra : last_ref.shape[0] - extra, :]


def audio_allowed(hop, rows_audio, limit):
    row = lax.broadcasted_iota(jnp.int32, (rows_audio, 1), 0)
    return (index_of("seq") ^ hop) * rows_audio + row < limit


def spread(x, head):
    pair = 128 // head
    rows = x.shape[1] // pair
    parts = [jnp.broadcast_to(x[:, i * rows : (i + 1) * rows], (head, rows)) for i in range(pair)]
    return jnp.concatenate(parts, axis=0)


def attend_audio_kernel(hops, rows_audio, head, limit_ref, q_ref, *rest):
    blocks, part_ref, stats_ref = rest[:-2], rest[-2], rest[-1]
    cols = q_ref.shape[1]
    allowed = [audio_allowed(hop, rows_audio, limit_ref[0]) for hop in hops]
    scale = 1.0 / math.sqrt(head)
    for block in range(cols // 128):
        cut = slice(block * 128, (block + 1) * 128)
        q = pair_rows(q_ref[:, cut], head)
        scores = [dot_t(audio_block(ref, 2, rows_audio, cols, block), q) for ref in blocks]
        peak, p, total = softmax_t(scores, scale, allowed)
        vt = turn(jnp.concatenate([audio_block(ref, 1, rows_audio, cols, block) for ref in blocks], axis=0))
        part_ref[cut, :] = pair_columns(dot(vt, jnp.concatenate(p, axis=0)), head)
        stats_ref[2 * block : 2 * block + 1, :] = peak
        stats_ref[2 * block + 1 : 2 * block + 2, :] = total


def finish_audio(head, limit, q_ref, part_ref, stats_ref, keys_ref, values_ref, rows_audio, out_ref):
    cols = q_ref.shape[1]
    scale = 1.0 / math.sqrt(head)
    allowed = audio_allowed(FORWARDED, rows_audio, limit)
    for block in range(cols // 128):
        cut = slice(block * 128, (block + 1) * 128)
        q = pair_rows(q_ref[:, cut], head)
        scores = jnp.where(allowed, dot_t(audio_block(keys_ref, 1, rows_audio, cols, block), q), LEAST)
        before, summed = stats_ref[2 * block : 2 * block + 1, :], stats_ref[2 * block + 1 : 2 * block + 2, :]
        peak = jnp.maximum(before, jnp.max(scores, axis=0, keepdims=True))
        factor = jnp.exp2((before - peak) * (scale * LOG2E))
        p = jnp.exp2((scores - peak) * (scale * LOG2E))
        inverse = 1.0 / (summed * factor + jnp.sum(p, axis=0, keepdims=True))
        vt = turn(audio_block(values_ref, 1, rows_audio, cols, block))
        last = pair_columns(dot(vt, p.astype(BF16)), head)
        both = part_ref[cut, :] * spread(factor, head) + last
        out_ref[:, cut] = (both * spread(inverse, head)).T.astype(BF16)


def merge_audio(head, top, v2a_ref, lse_ref, got, out_ref):
    rows_audio, cols = v2a_ref.shape
    heads = cols // head
    lses = [lse_ref[...]]
    for ref in got:
        at = top + cols // 128 * rows_audio
        packed = ref[at : at + LSE_ROWS, 0:128].astype(F32)
        lses.append(packed[0:heads] + packed[heads : 2 * heads] + packed[2 * heads : 3 * heads])
    peak = functools.reduce(jnp.maximum, lses)
    parts = [jnp.exp2(x - peak) for x in lses]
    total = functools.reduce(jnp.add, parts)
    inverse = 1.0 / total
    parts = [x * inverse for x in parts]
    parts.append(jnp.zeros((128 - len(parts) * heads, 128), F32))
    shares = jnp.concatenate(parts, axis=0).T[0:rows_audio]
    pair = 128 // head
    lane = lax.broadcasted_iota(jnp.int32, (1, 128), 1) // head
    for block in range(cols // 128):
        cut = slice(block * 128, (block + 1) * 128)
        at = top + block * rows_audio
        summed = jnp.zeros((rows_audio, 128), F32)
        for j in range(len(lses)):
            o = v2a_ref[:, cut] if j == 0 else got[j - 1][at : at + rows_audio, 0:128].astype(F32)
            share = jnp.zeros((rows_audio, 128), F32)
            for i in range(pair):
                column = j * heads + block * pair + i
                share = jnp.where(lane == i, shares[:, column : column + 1], share)
            summed = summed + share * o
        out_ref[:, cut] = summed.astype(BF16)


def block_of(far, other):
    mp, sub = index_of("mp"), index_of("sub")
    return (1 - mp if far else mp) * 2 + (1 - sub if other else sub)


def project_self(block, part, att_ref, ws_ref, gain_ref):
    cut = ws_ref.shape[1] // (4 * PARTS)
    at = columns(block * PARTS + part, cut)
    return gain_ref[:, at].astype(F32) * dot(att_ref[...], ws_ref[:, at])


def project_a2v(block, part, a2v_ref, wa_ref, gain_ref):
    cut = wa_ref.shape[1] // (4 * PARTS)
    gain = gain_ref[:, columns((block + 4) * PARTS + part, cut)].astype(F32)
    return gain * dot(a2v_ref[...], wa_ref[:, columns(block * PARTS + part, cut)])


def project_audio(block, v2a_ref, wv_ref):
    return dot(v2a_ref[...], wv_ref[:, columns(block, wv_ref.shape[1] // 4)])


def project(block, parts, heads, weights, out, extra=None):
    (self_ref, a2v_ref, audio_ref), (ws_ref, wa_ref, wv_ref, gain_ref) = heads, weights
    rows, cut = self_ref.shape[0], out.shape[1]

    def store(at, term):
        if extra is not None:
            term = term + extra[at : at + term.shape[0], :].astype(F32)
        out[at : at + term.shape[0], :] = term.astype(out.dtype)

    for i, part in enumerate(parts):
        term = project_self(block, part, self_ref, ws_ref, gain_ref)
        store(i * rows, term + project_a2v(block, part, a2v_ref, wa_ref, gain_ref))
    term, rows_audio = project_audio(block, audio_ref, wv_ref), audio_ref.shape[0]
    for i in range(term.shape[1] // cut):
        store(len(parts) * rows + i * rows_audio, term[:, i * cut : (i + 1) * cut])


def first_kernel(hops, rows_audio, head, limit_ref, q_ref, part_ref, stats_ref, own_ref, ws_ref, wa_ref, gain_ref, *rest):
    got, (self_ref, a2v_ref, out_ref, term_ref) = rest[: len(hops) - 1], rest[len(hops) - 1 :]
    rows, width = own_ref.shape
    keys_ref, values_ref = got[hops.index(1) - 1], got[hops.index(FORWARDED) - 1]
    self_ref[:, columns(index_of("seq"), width)] = own_ref[...]
    for hop, ref in zip(hops[1:], got):
        self_ref[:, columns(index_of("seq") ^ hop, width)] = ref[0:rows, :]
    block = block_of(True, True)
    term_ref[...] = project_self(block, 0, self_ref, ws_ref, gain_ref)
    finish_audio(head, limit_ref[0], q_ref, part_ref, stats_ref, keys_ref, values_ref, rows_audio, a2v_ref)
    out_ref[...] = (term_ref[...] + project_a2v(block, 0, a2v_ref, wa_ref, gain_ref)).astype(BF16)


def second_kernel(head, self_ref, a2v_ref, ws_ref, wa_ref, wv_ref, gain_ref, v2a_ref, lse_ref, *rest):
    got, (out_ref, audio_ref, low_ref) = rest[:-3], rest[-3:]
    merge_audio(head, self_ref.shape[0], v2a_ref, lse_ref, got, audio_ref)
    heads, weights = (self_ref, a2v_ref, audio_ref), (ws_ref, wa_ref, wv_ref, gain_ref)
    project(block_of(True, True), range(1, PARTS), heads, weights, out_ref)
    block = block_of(True, False)
    term = project_self(block, 0, self_ref, ws_ref, gain_ref)
    low_ref[...] = term + project_a2v(block, 0, a2v_ref, wa_ref, gain_ref)


def far_low_kernel(low_ref, extra_ref, out_ref):
    out_ref[...] = (low_ref[...] + extra_ref[...].astype(F32)).astype(BF16)


def near_kernel(*refs):
    heads, weights, (send_ref, own_ref) = refs[:3], refs[3:7], refs[7:]
    project(block_of(False, True), range(PARTS), heads, weights, send_ref)
    project(block_of(False, False), range(PARTS), heads, weights, own_ref)


def far_high_kernel(*refs):
    heads, weights, (extra_ref, out_ref) = refs[:3], refs[3:7], refs[7:]
    project(block_of(True, False), range(1, PARTS), heads, weights, out_ref, extra_ref)


def finish_kernel(video_ref, audio_ref, gain_ref, own_ref, core_ref, low_ref, high_ref, video_out, audio_out):
    rows, cut = low_ref.shape
    rows_audio = audio_ref.shape[0]
    for part in range(PARTS):
        at = slice(part * cut, (part + 1) * cut)
        here = slice(part * rows, (part + 1) * rows)
        far = low_ref[...] if part == 0 else high_ref[(part - 1) * rows : part * rows, :]
        term = own_ref[here, :] + core_ref[here, :].astype(F32) + far.astype(F32)
        video_out[:, at] = (video_ref[:, at].astype(F32) + term).astype(BF16)
    for i in range(audio_ref.shape[1] // cut):
        at = slice(i * cut, (i + 1) * cut)
        top = PARTS * rows + i * rows_audio
        here, there = slice(top, top + rows_audio), slice(top - rows, top - rows + rows_audio)
        term = own_ref[here, :] + core_ref[here, :].astype(F32) + high_ref[there, :].astype(F32)
        audio_out[:, at] = (audio_ref[:, at].astype(F32) + gain_ref[:, at] * term).astype(BF16)


def on_device_heads(
    video_in,
    audio_in,
    q_self,
    k_self,
    v_self,
    q_a2v,
    k_a2v,
    v_a2v,
    q_v2a,
    k_v2a,
    v_v2a,
    wo_self,
    wo_a2v,
    wo_v2a,
    video_gates,
    audio_gates,
    video_steps,
    audio_steps,
    audio_len,
    *,
    n,
):
    hops = [0] + OUT_ORDER
    rows, cols = q_self.shape
    rows_audio, cross = q_v2a.shape
    width = cols // n

    def trade(x, axis, hop, size):
        return lax.ppermute(x, axis, [(i, i ^ hop) for i in range(size)])

    video, audio = 3 * rows, cross // width * rows_audio

    def pack(some):
        ends = [1 if hop == FORWARDED else 3 for hop in some]
        return call(
            functools.partial(pack_kernel, some, width),
            [shape(video + end * audio, width) for end in ends],
            (q_self, k_self, v_self, q_v2a, k_a2v, v_a2v),
            [HBM] * 6,
            scratch=[pltpu.SemaphoreType.DMA((3 * len(some) + sum(ends) * audio // rows_audio,))],
        )

    packed = pack(hops[1:2])
    rest = pack(hops[:1] + hops[2:])
    packed = [rest[0], *packed, *rest[1:]]
    blocks = dict(zip(hops, packed))
    for hop in hops[1:]:
        blocks[hop] = trade(blocks[hop], "seq", hop, n)

    late = (k_v2a, v_v2a, q_a2v, wo_self, wo_a2v, wo_v2a, video_in, audio_in)
    steps = (video_steps.reshape(1, rows), audio_steps.reshape(1, rows_audio))
    gain, audio_gain, k_own, v_own, q_own, ws, wa, wv, video_own, audio_own = call(
        fetch_kernel,
        [shape(rows, 2 * video_gates.shape[2]), shape(*audio_in.shape, F32)]
        + [shape(*x.shape) for x in late],
        (audio_len, video_gates.reshape(NT, -1), *steps, audio_gates, *late),
        [SMEM, VMEM] + [HBM] * (3 + len(late)),
        scratch=[pltpu.VMEM(x.shape, x.dtype) for x in (*steps, audio_gates)]
        + [pltpu.SemaphoreType.DMA((3 + len(late),))],
    )
    tail = cross // 128 * rows_audio + LSE_ROWS
    early = [hop for hop in hops if hop != LAST]
    count = len(early)
    part, stats, vt, vvt, own_v2a, own_lse, *tails = call(
        functools.partial(early_kernel, early, DHC),
        [
            shape(count * width, rows, F32),
            shape(2 * count, rows, F32),
            shape(width, count * rows),
            shape(cross, rows),
            shape(rows_audio, cross, F32),
            shape(cross // DHC, 128, F32),
        ]
        + [shape(tail, width)] * (count - 1),
        (k_own, v_own, *(blocks[hop] for hop in early)),
        flops=4 * count * count * rows * rows * width,
        scratch=[pltpu.VMEM(((count * count + cross // DHC) * rows, rows), F32)],
    )
    own, *sends = call(
        functools.partial(late_kernel, early, hops, rows_audio, DHC),
        [shape(rows, width)]
        + [shape(rows + tail + (0 if hop == LAST else audio), width) for hop in hops[1:]],
        (k_own, vvt, part, stats, vt, blocks[LAST], *(blocks[hop] for hop in early), *tails),
        flops=4 * (2 * n - 1) * rows * rows * width,
        scratch=[pltpu.VMEM(((2 * n - 1) * rows, rows), F32)],
    )
    got = [trade(x, "seq", hop, n) for x, hop in zip(sends, hops[1:])]
    near = [hop for hop in hops if hop != FORWARDED]
    a2v_part, a2v_stats = call(
        functools.partial(attend_audio_kernel, near, rows_audio, DHC),
        [shape(cross, rows, F32), shape(cross // 64, 128 // DHC * rows, F32)],
        (audio_len, q_own, *(blocks[hop] for hop in near)),
        [SMEM] + [VMEM] * n,
        flops=8 * n * rows * rows_audio * cross,
    )

    cut = video_in.shape[1] // PARTS
    below = rows_audio * audio_in.shape[1] // cut
    flops = 2 * rows * (cols + cross) * cut
    self_att, a2v_att, first = call(
        functools.partial(first_kernel, hops, rows_audio, DHC),
        [shape(rows, cols), shape(rows, cross), shape(rows, cut)],
        (audio_len, q_own, a2v_part, a2v_stats, own, ws, wa, gain, *got),
        [SMEM] + [VMEM] * (n + 6),
        flops=flops,
        scratch=[pltpu.VMEM((rows, cut), F32)],
    )
    first = trade(first, "sub", 1, 2)
    high_rows = (PARTS - 1) * rows + below
    second, v2a_att, own_low = call(
        functools.partial(second_kernel, DHC),
        [shape(high_rows, cut), shape(rows_audio, cross), shape(rows, cut, F32)],
        (self_att, a2v_att, ws, wa, wv, gain, own_v2a, own_lse, *got),
        flops=PARTS * flops,
    )
    second = trade(second, "sub", 1, 2)
    operands = (self_att, a2v_att, v2a_att, ws, wa, wv, gain)
    (low,) = call(far_low_kernel, [shape(rows, cut)], (own_low, first))
    low = trade(low, "mp", 1, 2)
    (high,) = call(far_high_kernel, [shape(high_rows, cut)], (*operands, second), flops=3 * flops)
    high = trade(high, "mp", 1, 2)
    near, own_sum = call(
        near_kernel,
        [shape(rows + high_rows, cut), shape(rows + high_rows, cut, F32)],
        operands,
        flops=2 * PARTS * flops,
    )
    near = trade(near, "sub", 1, 2)
    return call(
        finish_kernel,
        [shape(*video_in.shape), shape(*audio_in.shape)],
        (video_own, audio_own, audio_gain, own_sum, near, low, high),
    )


def on_device(n, mp, sub, *arrays):
    cols, cross = arrays[2].shape[1], arrays[5].shape[1]
    width = cols // n
    fits = (
        n == SEQ
        and (mp, sub) == (2, 2)
        and width == DHV == 128
        and cross % width == 0
        and 3 * (cross // DHC) <= LSE_ROWS
        and n * arrays[8].shape[0] == arrays[2].shape[0] == 128
        and arrays[0].shape[1] == 2 * arrays[1].shape[1]
        and arrays[0].shape[1] % (PARTS * 128) == 0
    )
    if fits:
        return on_device_heads(*arrays, n=n)
    return on_device_gather(*arrays)


def solution(mesh):
    in_specs = (
        P(("groups", "seq"), ("mp", "sub")),
        P(("groups", "seq"), ("mp", "sub")),
        P(("groups", "seq"), ("mp", "sub")),
        P(("groups", "seq"), ("mp", "sub")),
        P(("groups", "seq"), ("mp", "sub")),
        P(("groups", "seq"), ("mp", "sub")),
        P(("groups", "seq"), ("mp", "sub")),
        P(("groups", "seq"), ("mp", "sub")),
        P(("groups", "seq"), ("mp", "sub")),
        P(("groups", "seq"), ("mp", "sub")),
        P(("groups", "seq"), ("mp", "sub")),
        P(("mp", "sub"), None),
        P(("mp", "sub"), None),
        P(("mp", "sub"), None),
        P(),
        P(),
        P(("groups", "seq")),
        P(("groups", "seq")),
        P("groups"),
    )
    out_specs = (P(("groups", "seq"), ("mp", "sub")), P(("groups", "seq"), ("mp", "sub")))
    return jax.shard_map(
        functools.partial(on_device, *(mesh.shape[a] for a in ("seq", "mp", "sub"))), mesh=mesh, in_specs=in_specs, out_specs=out_specs, check_vma=False
    )
```

```python
import functools
import math

import jax
import jax.numpy as jnp
from jax import lax
from jax.experimental import pallas as pl
from jax.experimental.pallas import tpu as pltpu
from jax.sharding import PartitionSpec as P


DHV = 128
DHC = 64
NT = 16


def start_state(rows, heads, width):
    return (
        jnp.full((rows, heads), -1e30, jnp.float32),
        jnp.zeros((rows, heads), jnp.float32),
        jnp.zeros((rows, heads, width), jnp.float32),
    )


def update_block(state, queries, keys, values, heads, width, allowed):
    rows = queries.shape[0]
    count = keys.shape[0]
    q_heads = queries.reshape(rows, heads, width)
    k_heads = keys.reshape(count, heads, width)
    v_heads = values.reshape(count, heads, width)
    scores = jnp.einsum(
        "qhd,khd->qhk", q_heads, k_heads, preferred_element_type=jnp.float32
    ) / math.sqrt(width)
    if allowed is not None:
        scores = jnp.where(allowed[None, None, :], scores, -jnp.inf)
    peak_old, total_old, summed_old = state
    peak = jnp.maximum(peak_old, jnp.max(scores, axis=2))
    weights = jnp.exp(scores - peak[:, :, None])
    factor = jnp.exp(peak_old - peak)
    total = total_old * factor + jnp.sum(weights, axis=2)
    summed = summed_old * factor[:, :, None] + jnp.einsum(
        "qhk,khd->qhd", weights.astype(jnp.bfloat16), v_heads, preferred_element_type=jnp.float32
    )
    return (peak, total, summed)


def update_state(state, queries, keys, values, heads, width, start, limit):
    count = keys.shape[0]
    block = 1024 if count > 1024 and count % 1024 == 0 else count
    if block == count:
        allowed = None
        if limit is not None:
            allowed = jnp.arange(count, dtype=jnp.int32) < limit
        return update_block(state, queries, keys, values, heads, width, allowed)
    steps = count // block
    key_blocks = keys.reshape(steps, block, keys.shape[1])
    value_blocks = values.reshape(steps, block, values.shape[1])
    offsets = jnp.arange(steps, dtype=jnp.int32) * block

    def one_block(carry, items):
        key_rows, value_rows, offset = items
        allowed = None
        if limit is not None:
            allowed = start + offset + jnp.arange(block, dtype=jnp.int32) < limit
        return (update_block(carry, queries, key_rows, value_rows, heads, width, allowed), None)

    result, _ = lax.scan(one_block, state, (key_blocks, value_blocks, offsets))
    return result


def finish(state, heads, width):
    _, total, summed = state
    rows = summed.shape[0]
    return (summed / total[:, :, None]).reshape(rows, heads * width).astype(jnp.bfloat16)


def on_device_gather(
    video_in,
    audio_in,
    q_self,
    k_self,
    v_self,
    q_a2v,
    k_a2v,
    v_a2v,
    q_v2a,
    k_v2a,
    v_v2a,
    wo_self,
    wo_a2v,
    wo_v2a,
    video_gates,
    audio_gates,
    video_steps,
    audio_steps,
    audio_len,
):
    heads_self = q_self.shape[1] // DHV
    heads_cross = q_a2v.shape[1] // DHC
    rows_video = q_self.shape[0]
    rows_audio = q_v2a.shape[0]
    limit = audio_len[0]
    piece = (
        lax.all_gather(k_a2v, "seq", axis=0, tiled=True),
        lax.all_gather(v_a2v, "seq", axis=0, tiled=True),
    )
    a2v_state = update_state(
        start_state(rows_video, heads_cross, DHC),
        q_a2v,
        piece[0],
        piece[1],
        heads_cross,
        DHC,
        jnp.int32(0),
        limit,
    )
    a2v_att = finish(a2v_state, heads_cross, DHC)
    piece = (
        lax.all_gather(k_self, "seq", axis=0, tiled=True),
        lax.all_gather(v_self, "seq", axis=0, tiled=True),
    )
    self_state = update_state(
        start_state(rows_video, heads_self, DHV),
        q_self,
        piece[0],
        piece[1],
        heads_self,
        DHV,
        jnp.int32(0),
        None,
    )
    piece = (
        lax.all_gather(k_v2a, "seq", axis=0, tiled=True),
        lax.all_gather(v_v2a, "seq", axis=0, tiled=True),
    )
    v2a_state = update_state(
        start_state(rows_audio, heads_cross, DHC),
        q_v2a,
        piece[0],
        piece[1],
        heads_cross,
        DHC,
        jnp.int32(0),
        None,
    )
    self_att = finish(self_state, heads_self, DHV)
    v2a_att = finish(v2a_state, heads_cross, DHC)
    levels = jnp.arange(NT, dtype=jnp.int32)
    video_hot = (video_steps[:, None] == levels[None, :]).astype(jnp.bfloat16)
    video_gain = jnp.dot(video_hot, video_gates.reshape(NT, -1), preferred_element_type=jnp.float32)
    width_video = video_gates.shape[2]
    video_term = video_gain[:, :width_video] * jnp.dot(
        self_att, wo_self, preferred_element_type=jnp.float32
    )
    video_term = video_term + video_gain[:, width_video:] * jnp.dot(
        a2v_att, wo_a2v, preferred_element_type=jnp.float32
    )
    audio_hot = (audio_steps[:, None] == levels[None, :]).astype(jnp.bfloat16)
    audio_gain = jnp.dot(audio_hot, audio_gates, preferred_element_type=jnp.float32)
    positions = lax.axis_index("seq") * rows_audio + jnp.arange(rows_audio, dtype=jnp.int32)
    present = (positions < limit).astype(jnp.float32)
    audio_term = (
        present[:, None] * audio_gain * jnp.dot(v2a_att, wo_v2a, preferred_element_type=jnp.float32)
    )
    video_sum, audio_sum = (
        lax.psum_scatter(
            video_term.astype(jnp.bfloat16), ("mp", "sub"), scatter_dimension=1, tiled=True
        ).astype(jnp.float32),
        lax.psum_scatter(
            audio_term.astype(jnp.bfloat16), ("mp", "sub"), scatter_dimension=1, tiled=True
        ).astype(jnp.float32),
    )
    video_out = (video_in.astype(jnp.float32) + video_sum).astype(jnp.bfloat16)
    audio_out = (audio_in.astype(jnp.float32) + audio_sum).astype(jnp.bfloat16)
    return (video_out, audio_out)


LOG2E = 1.4426950408889634
VMEM = pl.BlockSpec(memory_space=pltpu.VMEM)
SMEM = pl.BlockSpec(memory_space=pltpu.SMEM)
HBM = pl.BlockSpec(memory_space=pltpu.HBM)
BF16, F32 = jnp.bfloat16, jnp.float32
LSE_ROWS, PARTS = 16, 4
LEAST = float(jnp.finfo(jnp.float32).min)
SEQ, FORWARDED, OUT_ORDER, LAST = 4, 3, [3, 2, 1], 2


def call(kernel, outs, operands, specs=None, flops=0, scratch=(), limit=8 * 2**20):
    size = sum(math.prod(x.shape) * x.dtype.itemsize for x in (*operands, *outs))
    if specs:
        operands = [
            pltpu.with_memory_space_constraint(x, pltpu.HBM) if spec is HBM else x for x, spec in zip(operands, specs)
        ]
    return pl.pallas_call(
        kernel,
        out_shape=tuple(outs),
        in_specs=specs or [VMEM] * len(operands),
        out_specs=tuple(VMEM for _ in outs),
        scratch_shapes=list(scratch),
        compiler_params=pltpu.CompilerParams(vmem_limit_bytes=limit),
        cost_estimate=pl.CostEstimate(flops=flops, bytes_accessed=size, transcendentals=0),
    )(*operands)


def shape(rows, cols, kind=BF16):
    return jax.ShapeDtypeStruct((rows, cols), kind)


def dot_t(a, b):
    return lax.dot_general(a, b, (((1,), (1,)), ((), ())), preferred_element_type=F32)


def dot(a, b):
    return jnp.dot(a, b, preferred_element_type=F32)


def index_of(axis):
    return lax.axis_index(axis).astype(jnp.int32)


def columns(index, width):
    return pl.ds(pl.multiple_of(index * width, width), width)


def copy_all(pairs, sems):
    copies = [pltpu.make_async_copy(src, dst, sems.at[i]) for i, (src, dst) in enumerate(pairs)]
    for copy in copies:
        copy.start()
    for copy in copies:
        copy.wait()


def pack_kernel(hops, width, q_ref, k_ref, v_ref, qa_ref, ka_ref, va_ref, *rest):
    outs, sems = rest[:-1], rest[-1]
    rows = q_ref.shape[0]
    rows_audio, cols_audio = qa_ref.shape
    me = index_of("seq")
    pairs = []
    for hop, out in zip(hops, outs):
        for i, ref in enumerate((q_ref, k_ref, v_ref)):
            pairs.append((ref.at[:, columns(me ^ hop, width)], out.at[pl.ds(i * rows, rows), :]))
        at = 3 * rows
        for ref in (qa_ref,) if hop == FORWARDED else (qa_ref, ka_ref, va_ref):
            for i in range(cols_audio // width):
                pairs.append((ref.at[:, pl.ds(i * width, width)], out.at[pl.ds(at, rows_audio), :]))
                at += rows_audio
    copy_all(pairs, sems)


def audio_block(ref, end, rows, cols, block):
    at, column = divmod(block * 128, ref.shape[1])
    top = ref.shape[0] - end * (cols // ref.shape[1]) * rows + at * rows
    return ref[top : top + rows, column : column + 128]


def one_hot_t(steps_ref):
    levels = lax.broadcasted_iota(jnp.int32, (NT, steps_ref.shape[1]), 0)
    return (levels == steps_ref[...]).astype(BF16)


def pick(hot_t, table):
    return lax.dot_general(hot_t, table, (((0,), (0,)), ((), ())), preferred_element_type=F32)


def fetch_kernel(limit_ref, vg_ref, *rest):
    count = (len(rest) - 9) // 2
    loads, gain_ref, audio_ref = rest[: count + 3], rest[count + 3], rest[count + 4]
    fetched, (vs_ref, as_ref, ag_ref, sems) = rest[count + 5 : -4], rest[-4:]
    copies = [
        pltpu.make_async_copy(src, dst, sems.at[i])
        for i, (src, dst) in enumerate(zip(loads, (vs_ref, as_ref, ag_ref, *fetched)))
    ]
    for copy in copies:
        copy.start()
    for copy in copies[:3]:
        copy.wait()
    hot_t = one_hot_t(vs_ref)
    piece = min(vg_ref.shape[1], 2048)
    for at in range(0, vg_ref.shape[1], piece):
        gain_ref[:, at : at + piece] = pick(hot_t, vg_ref[:, at : at + piece]).astype(BF16)
    rows_audio, narrow = audio_ref.shape
    part = index_of("mp") * 2 + index_of("sub")
    gain = pick(one_hot_t(as_ref), ag_ref[:, columns(part, narrow)])
    at = index_of("seq") * rows_audio + lax.broadcasted_iota(jnp.int32, (rows_audio, 1), 0)
    audio_ref[...] = jnp.where(at < limit_ref[0], gain, 0.0)
    for copy in copies[3:]:
        copy.wait()


def softmax_t(scores, scale, allowed=None):
    if allowed is not None:
        scores = [jnp.where(ok, x, LEAST) for ok, x in zip(allowed, scores)]
    peak = functools.reduce(jnp.maximum, [jnp.max(x, axis=0, keepdims=True) for x in scores])
    weights = [jnp.exp2((x - peak) * (scale * LOG2E)) for x in scores]
    total = functools.reduce(jnp.add, [jnp.sum(x, axis=0, keepdims=True) for x in weights])
    return peak, [x.astype(BF16) for x in weights], total


def turn(x):
    return x.astype(F32).T.astype(BF16)


def pair_rows(x, head):
    lane = lax.broadcasted_iota(jnp.int32, (1, 128), 1) // head
    return jnp.concatenate([jnp.where(lane == i, x, 0).astype(BF16) for i in range(128 // head)], axis=0)


def pair_columns(x, head):
    pair = 128 // head
    rows = x.shape[1] // pair
    return jnp.concatenate([x[i * head : (i + 1) * head, i * rows : (i + 1) * rows] for i in range(pair)], axis=0)


def audio_part(q, keys, values_t, head):
    pair, rows = 128 // head, q.shape[0]
    scale = 1.0 / math.sqrt(head)
    both = pair_rows(q, head)
    both = jnp.concatenate([both] * (128 // both.shape[0]), axis=0)
    peak, p, total = softmax_t([dot_t(keys, both)], scale)
    o = dot(values_t, p[0]) * (1.0 / total)
    lse = peak * (scale * LOG2E) + jnp.log2(total)
    o = [o[i * head : (i + 1) * head] for i in range(pair)]
    o = [x if i == 0 else pltpu.roll(x, 128 - i * rows, 1) for i, x in enumerate(o)]
    lses = [lse if i == 0 else pltpu.roll(lse, 128 - i * rows, 1) for i in range(pair)]
    return jnp.concatenate(o, axis=0).T[0:rows], lses


def audio_parts(ref, end, kv_ref, vvt_ref, rows_audio, head):
    cols = kv_ref.shape[1]
    outs, lses = [], []
    for block in range(cols // 128):
        cut = slice(block * 128, (block + 1) * 128)
        q = audio_block(ref, end, rows_audio, cols, block)
        o, lse = audio_part(q, kv_ref[:, cut], vvt_ref[cut, :], head)
        outs.append(o)
        lses += lse
    return outs, jnp.concatenate(lses, axis=0)


def store_tail(dst, top, outs, lse):
    rows_audio = outs[0].shape[0]
    for i, o in enumerate(outs):
        dst[top + i * rows_audio : top + (i + 1) * rows_audio, 0:128] = o.astype(BF16)
    pieces, left = [], lse
    for _ in range(3):
        pieces.append(left.astype(BF16).astype(F32))
        left = left - pieces[-1]
    pieces.append(jnp.zeros((LSE_ROWS - 3 * lse.shape[0], 128), F32))
    top += len(outs) * rows_audio
    dst[top : top + LSE_ROWS, 0:128] = jnp.concatenate(pieces, axis=0).astype(BF16)


def early_kernel(early, head, kv_ref, vv_ref, *rest):
    count = len(early)
    blocks, (part_ref, stats_ref, vt_ref, vvt_ref, own_v2a_ref, own_lse_ref) = rest[:count], rest[count : count + 6]
    tails, (s_ref,) = rest[count + 6 : -1], rest[-1:]
    rows, cols = kv_ref.shape
    rows_audio = own_v2a_ref.shape[0]
    for i, ref in enumerate(blocks):
        vt_ref[:, i * rows : (i + 1) * rows] = turn(ref[2 * rows : 3 * rows, :])
    for block in range(cols // 128):
        cut = slice(block * 128, (block + 1) * 128)
        vvt_ref[cut, :] = turn(vv_ref[:, cut])
    tops = []
    for block in range(cols // 128):
        ends = [1 if hop == FORWARDED else 3 for hop in early]
        q = [audio_block(ref, end, rows_audio, cols, block) for ref, end in zip(blocks, ends)]
        q = jnp.concatenate(q + [q[0]] * (128 // rows_audio - count), axis=0)
        scores = dot_t(kv_ref[:, block * 128 : (block + 1) * 128], pair_rows(q, head))
        for i in range(128 // head):
            row = (count * count + block * (128 // head) + i) * rows
            s_ref[row : row + rows, :] = scores[:, i * 128 : (i + 1) * 128]
        tops.append(jnp.max(scores, axis=0, keepdims=True))
    scale = 1.0 / math.sqrt(DHV)
    peaks = []
    for j, ref in enumerate(blocks):
        peak = None
        for i, other in enumerate(blocks):
            scores = dot_t(other[rows : 2 * rows, :], ref[0:rows, :])
            s_ref[(j * count + i) * rows : (j * count + i + 1) * rows, :] = scores
            top = jnp.max(scores, axis=0, keepdims=True)
            peak = top if i == 0 else jnp.maximum(peak, top)
        peaks.append(peak)
    for j, peak in enumerate(peaks):
        total, p = None, []
        for i in range(count):
            x = jnp.exp2((s_ref[(j * count + i) * rows : (j * count + i + 1) * rows, :] - peak) * (scale * LOG2E))
            summed = jnp.sum(x, axis=0, keepdims=True)
            total = summed if i == 0 else total + summed
            p.append(x.astype(BF16))
        part_ref[j * DHV : (j + 1) * DHV, :] = dot(vt_ref[...], jnp.concatenate(p, axis=0))
        stats_ref[2 * j : 2 * j + 1, :] = peak
        stats_ref[2 * j + 1 : 2 * j + 2, :] = total
    pair, scale = 128 // head, 1.0 / math.sqrt(head)
    outs, lses = [], []
    for block in range(cols // 128):
        cut = slice(block * 128, (block + 1) * 128)
        peak = tops[block]
        both = []
        for i in range(pair):
            at = slice(i * 128, (i + 1) * 128)
            row = (count * count + block * pair + i) * rows
            p = jnp.exp2((s_ref[row : row + rows, :] - peak[:, at]) * (scale * LOG2E))
            total = jnp.sum(p, axis=0, keepdims=True)
            lses.append(peak[:, at] * (scale * LOG2E) + jnp.log2(total))
            column = block * 128 + i * head
            both.append(dot(vvt_ref[column : column + head, :], p.astype(BF16)) * (1.0 / total))
        outs.append(jnp.concatenate(both, axis=0).T)
    lse = jnp.concatenate(lses, axis=0)
    own_lse_ref[...] = lse
    for block, o in enumerate(outs):
        own_v2a_ref[:, block * 128 : (block + 1) * 128] = o[0:rows_audio]
    for j in range(1, count):
        mine = [o[j * rows_audio : (j + 1) * rows_audio] for o in outs]
        store_tail(tails[j - 1], 0, mine, pltpu.roll(lse, 128 - j * rows_audio, 1))


def late_kernel(early, hops, rows_audio, head, kv_ref, vvt_ref, part_ref, stats_ref, vt_ref, last_ref, *rest):
    count, n = len(early), len(hops)
    blocks, tails, outs, (relay_ref, s_ref) = rest[:count], rest[count : 2 * count - 1], rest[2 * count - 1 : -2], rest[-2:]
    by_hop = dict(zip(hops, outs))
    rows = kv_ref.shape[0]
    last = next(hop for hop in hops if hop not in early)
    scale = 1.0 / math.sqrt(DHV)
    keys = last_ref[rows : 2 * rows, :]
    peaks = []
    for j, ref in enumerate((*blocks, last_ref)):
        scores = dot_t(keys, ref[0:rows, :])
        s_ref[j * rows : (j + 1) * rows, :] = scores
        top = jnp.max(scores, axis=0, keepdims=True)
        peaks.append(jnp.maximum(top, stats_ref[2 * j : 2 * j + 1, :]) if j < count else top)
    for i, other in enumerate(blocks):
        scores = dot_t(other[rows : 2 * rows, :], last_ref[0:rows, :])
        s_ref[(n + i) * rows : (n + i + 1) * rows, :] = scores
        peaks[-1] = jnp.maximum(peaks[-1], jnp.max(scores, axis=0, keepdims=True))
    values_t = turn(last_ref[2 * rows : 3 * rows, :])

    def weigh(at, peak):
        x = jnp.exp2((s_ref[at * rows : (at + 1) * rows, :] - peak) * (scale * LOG2E))
        return x.astype(BF16), jnp.sum(x, axis=0, keepdims=True)

    audio = audio_parts(last_ref, 3, kv_ref, vvt_ref, rows_audio, head)
    total, p = None, []
    for i in range(count):
        x, summed = weigh(n + i, peaks[-1])
        total = summed if i == 0 else total + summed
        p.append(x)
    x, summed = weigh(count, peaks[-1])
    o = dot(vt_ref[...], jnp.concatenate(p, axis=0)) + dot(values_t, x)
    by_hop[last][0:rows, :] = (o * (1.0 / (total + summed))).T.astype(BF16)
    for j, hop in enumerate(early):
        x, summed = weigh(j, peaks[j])
        factor = jnp.exp2((stats_ref[2 * j : 2 * j + 1, :] - peaks[j]) * (scale * LOG2E))
        total = stats_ref[2 * j + 1 : 2 * j + 2, :] * factor + summed
        o = part_ref[j * DHV : (j + 1) * DHV, :] * factor + dot(values_t, x)
        by_hop[hop][0:rows, :] = (o * (1.0 / total)).T.astype(BF16)
    store_tail(by_hop[last], rows, *audio)
    for hop, tail in zip(early[1:], tails):
        by_hop[hop][rows : rows + tail.shape[0], :] = tail[...]
    relay_ref[...] = last_ref[last_ref.shape[0] - relay_ref.shape[0] :, :]


def audio_allowed(hop, rows_audio, limit):
    row = lax.broadcasted_iota(jnp.int32, (rows_audio, 1), 0)
    return (index_of("seq") ^ hop) * rows_audio + row < limit


def spread(x, head):
    pair = 128 // head
    rows = x.shape[1] // pair
    parts = [jnp.broadcast_to(x[:, i * rows : (i + 1) * rows], (head, rows)) for i in range(pair)]
    return jnp.concatenate(parts, axis=0)


def attend_audio_kernel(hops, rows_audio, head, limit_ref, q_ref, *rest):
    blocks, part_ref, stats_ref = rest[:-2], rest[-2], rest[-1]
    cols = q_ref.shape[1]
    allowed = [audio_allowed(hop, rows_audio, limit_ref[0]) for hop in hops]
    scale = 1.0 / math.sqrt(head)
    for block in range(cols // 128):
        cut = slice(block * 128, (block + 1) * 128)
        q = pair_rows(q_ref[:, cut], head)
        scores = [dot_t(audio_block(ref, 2, rows_audio, cols, block), q) for ref in blocks]
        peak, p, total = softmax_t(scores, scale, allowed)
        vt = turn(jnp.concatenate([audio_block(ref, 1, rows_audio, cols, block) for ref in blocks], axis=0))
        part_ref[cut, :] = pair_columns(dot(vt, jnp.concatenate(p, axis=0)), head)
        stats_ref[2 * block : 2 * block + 1, :] = peak
        stats_ref[2 * block + 1 : 2 * block + 2, :] = total


def join_kernel(head, rows_audio, limit_ref, q_ref, part_ref, stats_ref, last_ref, out_ref):
    cols = q_ref.shape[1]
    scale = 1.0 / math.sqrt(head)
    allowed = audio_allowed(FORWARDED, rows_audio, limit_ref[0])
    for block in range(cols // 128):
        cut = slice(block * 128, (block + 1) * 128)
        q = pair_rows(q_ref[:, cut], head)
        scores = jnp.where(allowed, dot_t(audio_block(last_ref, 2, rows_audio, cols, block), q), LEAST)
        before, summed = stats_ref[2 * block : 2 * block + 1, :], stats_ref[2 * block + 1 : 2 * block + 2, :]
        peak = jnp.maximum(before, jnp.max(scores, axis=0, keepdims=True))
        factor = jnp.exp2((before - peak) * (scale * LOG2E))
        p = jnp.exp2((scores - peak) * (scale * LOG2E))
        inverse = 1.0 / (summed * factor + jnp.sum(p, axis=0, keepdims=True))
        vt = turn(audio_block(last_ref, 1, rows_audio, cols, block))
        last = pair_columns(dot(vt, p.astype(BF16)), head)
        both = part_ref[cut, :] * spread(factor, head) + last
        out_ref[:, cut] = (both * spread(inverse, head)).T.astype(BF16)


def merge_audio(head, top, v2a_ref, lse_ref, got, out_ref):
    rows_audio, cols = v2a_ref.shape
    heads = cols // head
    lses = [lse_ref[...]]
    for ref in got:
        at = top + cols // 128 * rows_audio
        packed = ref[at : at + LSE_ROWS, 0:128].astype(F32)
        lses.append(packed[0:heads] + packed[heads : 2 * heads] + packed[2 * heads : 3 * heads])
    peak = functools.reduce(jnp.maximum, lses)
    parts = [jnp.exp2(x - peak) for x in lses]
    total = functools.reduce(jnp.add, parts)
    inverse = 1.0 / total
    parts = [x * inverse for x in parts]
    parts.append(jnp.zeros((128 - len(parts) * heads, 128), F32))
    shares = jnp.concatenate(parts, axis=0).T[0:rows_audio]
    pair = 128 // head
    lane = lax.broadcasted_iota(jnp.int32, (1, 128), 1) // head
    for block in range(cols // 128):
        cut = slice(block * 128, (block + 1) * 128)
        at = top + block * rows_audio
        summed = jnp.zeros((rows_audio, 128), F32)
        for j in range(len(lses)):
            o = v2a_ref[:, cut] if j == 0 else got[j - 1][at : at + rows_audio, 0:128].astype(F32)
            share = jnp.zeros((rows_audio, 128), F32)
            for i in range(pair):
                column = j * heads + block * pair + i
                share = jnp.where(lane == i, shares[:, column : column + 1], share)
            summed = summed + share * o
        out_ref[:, cut] = summed.astype(BF16)


def block_of(far, other):
    mp, sub = index_of("mp"), index_of("sub")
    return (1 - mp if far else mp) * 2 + (1 - sub if other else sub)


def project_self(block, part, att_ref, ws_ref, gain_ref):
    cut = ws_ref.shape[1] // (4 * PARTS)
    at = columns(block * PARTS + part, cut)
    return gain_ref[:, at].astype(F32) * dot(att_ref[...], ws_ref[:, at])


def project_a2v(block, part, a2v_ref, wa_ref, gain_ref):
    cut = wa_ref.shape[1] // (4 * PARTS)
    gain = gain_ref[:, columns((block + 4) * PARTS + part, cut)].astype(F32)
    return gain * dot(a2v_ref[...], wa_ref[:, columns(block * PARTS + part, cut)])


def project_audio(block, v2a_ref, wv_ref):
    return dot(v2a_ref[...], wv_ref[:, columns(block, wv_ref.shape[1] // 4)])


def project(block, parts, heads, weights, out, extra=None):
    (self_ref, a2v_ref, audio_ref), (ws_ref, wa_ref, wv_ref, gain_ref) = heads, weights
    rows, cut = self_ref.shape[0], out.shape[1]

    def store(at, term):
        if extra is not None:
            term = term + extra[at : at + term.shape[0], :].astype(F32)
        out[at : at + term.shape[0], :] = term.astype(out.dtype)

    for i, part in enumerate(parts):
        term = project_self(block, part, self_ref, ws_ref, gain_ref)
        store(i * rows, term + project_a2v(block, part, a2v_ref, wa_ref, gain_ref))
    term, rows_audio = project_audio(block, audio_ref, wv_ref), audio_ref.shape[0]
    for i in range(term.shape[1] // cut):
        store(len(parts) * rows + i * rows_audio, term[:, i * cut : (i + 1) * cut])


def first_kernel(hops, own_ref, a2v_ref, ws_ref, wa_ref, gain_ref, *rest):
    got, (self_ref, out_ref) = rest[: len(hops) - 1], rest[len(hops) - 1 :]
    rows, width = own_ref.shape
    block, me = block_of(True, True), index_of("seq")
    term = project_a2v(block, 0, a2v_ref, wa_ref, gain_ref)
    self_ref[:, columns(me, width)] = own_ref[...]
    for hop, ref in zip(hops[1:], got):
        self_ref[:, columns(me ^ hop, width)] = ref[0:rows, :]
    out_ref[...] = (project_self(block, 0, self_ref, ws_ref, gain_ref) + term).astype(BF16)


def second_kernel(head, self_ref, a2v_ref, ws_ref, wa_ref, wv_ref, gain_ref, v2a_ref, lse_ref, *rest):
    got, (out_ref, audio_ref, low_ref) = rest[:-3], rest[-3:]
    merge_audio(head, self_ref.shape[0], v2a_ref, lse_ref, got, audio_ref)
    heads, weights = (self_ref, a2v_ref, audio_ref), (ws_ref, wa_ref, wv_ref, gain_ref)
    project(block_of(True, True), range(1, PARTS), heads, weights, out_ref)
    block = block_of(True, False)
    term = project_self(block, 0, self_ref, ws_ref, gain_ref)
    low_ref[...] = term + project_a2v(block, 0, a2v_ref, wa_ref, gain_ref)


def far_low_kernel(low_ref, extra_ref, out_ref):
    out_ref[...] = (low_ref[...] + extra_ref[...].astype(F32)).astype(BF16)


def near_kernel(*refs):
    heads, weights, (send_ref, own_ref) = refs[:3], refs[3:7], refs[7:]
    project(block_of(False, True), range(PARTS), heads, weights, send_ref)
    project(block_of(False, False), range(PARTS), heads, weights, own_ref)


def far_high_kernel(*refs):
    heads, weights, (extra_ref, out_ref) = refs[:3], refs[3:7], refs[7:]
    project(block_of(True, False), range(1, PARTS), heads, weights, out_ref, extra_ref)


def finish_kernel(video_ref, audio_ref, gain_ref, own_ref, core_ref, low_ref, high_ref, video_out, audio_out):
    rows, cut = low_ref.shape
    rows_audio = audio_ref.shape[0]
    for part in range(PARTS):
        at = slice(part * cut, (part + 1) * cut)
        here = slice(part * rows, (part + 1) * rows)
        far = low_ref[...] if part == 0 else high_ref[(part - 1) * rows : part * rows, :]
        term = own_ref[here, :] + core_ref[here, :].astype(F32) + far.astype(F32)
        video_out[:, at] = (video_ref[:, at].astype(F32) + term).astype(BF16)
    for i in range(audio_ref.shape[1] // cut):
        at = slice(i * cut, (i + 1) * cut)
        top = PARTS * rows + i * rows_audio
        here, there = slice(top, top + rows_audio), slice(top - rows, top - rows + rows_audio)
        term = own_ref[here, :] + core_ref[here, :].astype(F32) + high_ref[there, :].astype(F32)
        audio_out[:, at] = (audio_ref[:, at].astype(F32) + gain_ref[:, at] * term).astype(BF16)


def on_device_heads(
    video_in,
    audio_in,
    q_self,
    k_self,
    v_self,
    q_a2v,
    k_a2v,
    v_a2v,
    q_v2a,
    k_v2a,
    v_v2a,
    wo_self,
    wo_a2v,
    wo_v2a,
    video_gates,
    audio_gates,
    video_steps,
    audio_steps,
    audio_len,
    *,
    n,
):
    hops = [0] + OUT_ORDER
    rows, cols = q_self.shape
    rows_audio, cross = q_v2a.shape
    width = cols // n

    def trade(x, axis, hop, size):
        return lax.ppermute(x, axis, [(i, i ^ hop) for i in range(size)])

    video, audio = 3 * rows, cross // width * rows_audio

    def pack(some):
        ends = [1 if hop == FORWARDED else 3 for hop in some]
        return call(
            functools.partial(pack_kernel, some, width),
            [shape(video + end * audio, width) for end in ends],
            (q_self, k_self, v_self, q_v2a, k_a2v, v_a2v),
            [HBM] * 6,
            scratch=[pltpu.SemaphoreType.DMA((3 * len(some) + sum(ends) * audio // rows_audio,))],
        )

    packed = pack(hops[1:2])
    rest = pack(hops[:1] + hops[2:])
    packed = [rest[0], *packed, *rest[1:]]
    blocks = dict(zip(hops, packed))
    for hop in hops[1:]:
        blocks[hop] = trade(blocks[hop], "seq", hop, n)

    late = (k_v2a, v_v2a, q_a2v, wo_self, wo_a2v, wo_v2a, video_in, audio_in)
    steps = (video_steps.reshape(1, rows), audio_steps.reshape(1, rows_audio))
    gain, audio_gain, k_own, v_own, q_own, ws, wa, wv, video_own, audio_own = call(
        fetch_kernel,
        [shape(rows, 2 * video_gates.shape[2]), shape(*audio_in.shape, F32)]
        + [shape(*x.shape) for x in late],
        (audio_len, video_gates.reshape(NT, -1), *steps, audio_gates, *late),
        [SMEM, VMEM] + [HBM] * (3 + len(late)),
        scratch=[pltpu.VMEM(x.shape, x.dtype) for x in (*steps, audio_gates)]
        + [pltpu.SemaphoreType.DMA((3 + len(late),))],
    )
    tail = cross // 128 * rows_audio + LSE_ROWS
    early = [hop for hop in hops if hop != LAST]
    count = len(early)
    part, stats, vt, vvt, own_v2a, own_lse, *tails = call(
        functools.partial(early_kernel, early, DHC),
        [
            shape(count * width, rows, F32),
            shape(2 * count, rows, F32),
            shape(width, count * rows),
            shape(cross, rows),
            shape(rows_audio, cross, F32),
            shape(cross // DHC, 128, F32),
        ]
        + [shape(tail, width)] * (count - 1),
        (k_own, v_own, *(blocks[hop] for hop in early)),
        flops=4 * count * count * rows * rows * width,
        scratch=[pltpu.VMEM(((count * count + cross // DHC) * rows, rows), F32)],
    )
    own, *sends, relay = call(
        functools.partial(late_kernel, early, hops, rows_audio, DHC),
        [shape(rows, width)]
        + [shape(rows + tail, width)] * (n - 1)
        + [shape(2 * audio, width)],
        (k_own, vvt, part, stats, vt, blocks[LAST], *(blocks[hop] for hop in early), *tails),
        flops=4 * (2 * n - 1) * rows * rows * width,
        scratch=[pltpu.VMEM(((2 * n - 1) * rows, rows), F32)],
    )
    got = [trade(x, "seq", hop, n) for x, hop in zip(sends, hops[1:])]
    forwarded = trade(relay, "seq", FORWARDED ^ LAST, n)
    near = [hop for hop in hops if hop != FORWARDED]
    a2v_part, a2v_stats = call(
        functools.partial(attend_audio_kernel, near, rows_audio, DHC),
        [shape(cross, rows, F32), shape(cross // 64, 128 // DHC * rows, F32)],
        (audio_len, q_own, *(blocks[hop] for hop in near)),
        [SMEM] + [VMEM] * n,
        flops=8 * n * rows * rows_audio * cross,
    )

    (a2v_att,) = call(
        functools.partial(join_kernel, DHC, rows_audio),
        [shape(rows, cross)],
        (audio_len, q_own, a2v_part, a2v_stats, forwarded),
        [SMEM] + [VMEM] * 4,
        flops=4 * rows * rows_audio * cross,
    )

    cut = video_in.shape[1] // PARTS
    below = rows_audio * audio_in.shape[1] // cut
    flops = 2 * rows * (cols + cross) * cut
    self_att, first = call(
        functools.partial(first_kernel, hops),
        [shape(rows, cols), shape(rows, cut)],
        (own, a2v_att, ws, wa, gain, *got),
        flops=flops,
    )
    first = trade(first, "sub", 1, 2)
    high_rows = (PARTS - 1) * rows + below
    second, v2a_att, own_low = call(
        functools.partial(second_kernel, DHC),
        [shape(high_rows, cut), shape(rows_audio, cross), shape(rows, cut, F32)],
        (self_att, a2v_att, ws, wa, wv, gain, own_v2a, own_lse, *got),
        flops=PARTS * flops,
    )
    second = trade(second, "sub", 1, 2)
    operands = (self_att, a2v_att, v2a_att, ws, wa, wv, gain)
    (low,) = call(far_low_kernel, [shape(rows, cut)], (own_low, first))
    low = trade(low, "mp", 1, 2)
    (high,) = call(far_high_kernel, [shape(high_rows, cut)], (*operands, second), flops=3 * flops)
    high = trade(high, "mp", 1, 2)
    near, own_sum = call(
        near_kernel,
        [shape(rows + high_rows, cut), shape(rows + high_rows, cut, F32)],
        operands,
        flops=2 * PARTS * flops,
    )
    near = trade(near, "sub", 1, 2)
    return call(
        finish_kernel,
        [shape(*video_in.shape), shape(*audio_in.shape)],
        (video_own, audio_own, audio_gain, own_sum, near, low, high),
    )


def on_device(n, mp, sub, *arrays):
    cols, cross = arrays[2].shape[1], arrays[5].shape[1]
    width = cols // n
    fits = (
        n == SEQ
        and (mp, sub) == (2, 2)
        and width == DHV == 128
        and cross % width == 0
        and 3 * (cross // DHC) <= LSE_ROWS
        and n * arrays[8].shape[0] == arrays[2].shape[0] == 128
        and arrays[0].shape[1] == 2 * arrays[1].shape[1]
        and arrays[0].shape[1] % (PARTS * 128) == 0
    )
    if fits:
        return on_device_heads(*arrays, n=n)
    return on_device_gather(*arrays)


def solution(mesh):
    in_specs = (
        P(("groups", "seq"), ("mp", "sub")),
        P(("groups", "seq"), ("mp", "sub")),
        P(("groups", "seq"), ("mp", "sub")),
        P(("groups", "seq"), ("mp", "sub")),
        P(("groups", "seq"), ("mp", "sub")),
        P(("groups", "seq"), ("mp", "sub")),
        P(("groups", "seq"), ("mp", "sub")),
        P(("groups", "seq"), ("mp", "sub")),
        P(("groups", "seq"), ("mp", "sub")),
        P(("groups", "seq"), ("mp", "sub")),
        P(("groups", "seq"), ("mp", "sub")),
        P(("mp", "sub"), None),
        P(("mp", "sub"), None),
        P(("mp", "sub"), None),
        P(),
        P(),
        P(("groups", "seq")),
        P(("groups", "seq")),
        P("groups"),
    )
    out_specs = (P(("groups", "seq"), ("mp", "sub")), P(("groups", "seq"), ("mp", "sub")))
    return jax.shard_map(
        functools.partial(on_device, *(mesh.shape[a] for a in ("seq", "mp", "sub"))), mesh=mesh, in_specs=in_specs, out_specs=out_specs, check_vma=False
    )
```

```python
import functools
import math

import jax
import jax.numpy as jnp
from jax import lax
from jax.experimental import pallas as pl
from jax.experimental.pallas import tpu as pltpu
from jax.sharding import PartitionSpec as P


DHV = 128
DHC = 64
NT = 16


def start_state(rows, heads, width):
    return (
        jnp.full((rows, heads), -1e30, jnp.float32),
        jnp.zeros((rows, heads), jnp.float32),
        jnp.zeros((rows, heads, width), jnp.float32),
    )


def update_block(state, queries, keys, values, heads, width, allowed):
    rows = queries.shape[0]
    count = keys.shape[0]
    q_heads = queries.reshape(rows, heads, width)
    k_heads = keys.reshape(count, heads, width)
    v_heads = values.reshape(count, heads, width)
    scores = jnp.einsum(
        "qhd,khd->qhk", q_heads, k_heads, preferred_element_type=jnp.float32
    ) / math.sqrt(width)
    if allowed is not None:
        scores = jnp.where(allowed[None, None, :], scores, -jnp.inf)
    peak_old, total_old, summed_old = state
    peak = jnp.maximum(peak_old, jnp.max(scores, axis=2))
    weights = jnp.exp(scores - peak[:, :, None])
    factor = jnp.exp(peak_old - peak)
    total = total_old * factor + jnp.sum(weights, axis=2)
    summed = summed_old * factor[:, :, None] + jnp.einsum(
        "qhk,khd->qhd", weights.astype(jnp.bfloat16), v_heads, preferred_element_type=jnp.float32
    )
    return (peak, total, summed)


def update_state(state, queries, keys, values, heads, width, start, limit):
    count = keys.shape[0]
    block = 1024 if count > 1024 and count % 1024 == 0 else count
    if block == count:
        allowed = None
        if limit is not None:
            allowed = jnp.arange(count, dtype=jnp.int32) < limit
        return update_block(state, queries, keys, values, heads, width, allowed)
    steps = count // block
    key_blocks = keys.reshape(steps, block, keys.shape[1])
    value_blocks = values.reshape(steps, block, values.shape[1])
    offsets = jnp.arange(steps, dtype=jnp.int32) * block

    def one_block(carry, items):
        key_rows, value_rows, offset = items
        allowed = None
        if limit is not None:
            allowed = start + offset + jnp.arange(block, dtype=jnp.int32) < limit
        return (update_block(carry, queries, key_rows, value_rows, heads, width, allowed), None)

    result, _ = lax.scan(one_block, state, (key_blocks, value_blocks, offsets))
    return result


def finish(state, heads, width):
    _, total, summed = state
    rows = summed.shape[0]
    return (summed / total[:, :, None]).reshape(rows, heads * width).astype(jnp.bfloat16)


def on_device_gather(
    video_in,
    audio_in,
    q_self,
    k_self,
    v_self,
    q_a2v,
    k_a2v,
    v_a2v,
    q_v2a,
    k_v2a,
    v_v2a,
    wo_self,
    wo_a2v,
    wo_v2a,
    video_gates,
    audio_gates,
    video_steps,
    audio_steps,
    audio_len,
):
    heads_self = q_self.shape[1] // DHV
    heads_cross = q_a2v.shape[1] // DHC
    rows_video = q_self.shape[0]
    rows_audio = q_v2a.shape[0]
    limit = audio_len[0]
    piece = (
        lax.all_gather(k_a2v, "seq", axis=0, tiled=True),
        lax.all_gather(v_a2v, "seq", axis=0, tiled=True),
    )
    a2v_state = update_state(
        start_state(rows_video, heads_cross, DHC),
        q_a2v,
        piece[0],
        piece[1],
        heads_cross,
        DHC,
        jnp.int32(0),
        limit,
    )
    a2v_att = finish(a2v_state, heads_cross, DHC)
    piece = (
        lax.all_gather(k_self, "seq", axis=0, tiled=True),
        lax.all_gather(v_self, "seq", axis=0, tiled=True),
    )
    self_state = update_state(
        start_state(rows_video, heads_self, DHV),
        q_self,
        piece[0],
        piece[1],
        heads_self,
        DHV,
        jnp.int32(0),
        None,
    )
    piece = (
        lax.all_gather(k_v2a, "seq", axis=0, tiled=True),
        lax.all_gather(v_v2a, "seq", axis=0, tiled=True),
    )
    v2a_state = update_state(
        start_state(rows_audio, heads_cross, DHC),
        q_v2a,
        piece[0],
        piece[1],
        heads_cross,
        DHC,
        jnp.int32(0),
        None,
    )
    self_att = finish(self_state, heads_self, DHV)
    v2a_att = finish(v2a_state, heads_cross, DHC)
    levels = jnp.arange(NT, dtype=jnp.int32)
    video_hot = (video_steps[:, None] == levels[None, :]).astype(jnp.bfloat16)
    video_gain = jnp.dot(video_hot, video_gates.reshape(NT, -1), preferred_element_type=jnp.float32)
    width_video = video_gates.shape[2]
    video_term = video_gain[:, :width_video] * jnp.dot(
        self_att, wo_self, preferred_element_type=jnp.float32
    )
    video_term = video_term + video_gain[:, width_video:] * jnp.dot(
        a2v_att, wo_a2v, preferred_element_type=jnp.float32
    )
    audio_hot = (audio_steps[:, None] == levels[None, :]).astype(jnp.bfloat16)
    audio_gain = jnp.dot(audio_hot, audio_gates, preferred_element_type=jnp.float32)
    positions = lax.axis_index("seq") * rows_audio + jnp.arange(rows_audio, dtype=jnp.int32)
    present = (positions < limit).astype(jnp.float32)
    audio_term = (
        present[:, None] * audio_gain * jnp.dot(v2a_att, wo_v2a, preferred_element_type=jnp.float32)
    )
    video_sum, audio_sum = (
        lax.psum_scatter(
            video_term.astype(jnp.bfloat16), ("mp", "sub"), scatter_dimension=1, tiled=True
        ).astype(jnp.float32),
        lax.psum_scatter(
            audio_term.astype(jnp.bfloat16), ("mp", "sub"), scatter_dimension=1, tiled=True
        ).astype(jnp.float32),
    )
    video_out = (video_in.astype(jnp.float32) + video_sum).astype(jnp.bfloat16)
    audio_out = (audio_in.astype(jnp.float32) + audio_sum).astype(jnp.bfloat16)
    return (video_out, audio_out)


LOG2E = 1.4426950408889634
VMEM = pl.BlockSpec(memory_space=pltpu.VMEM)
SMEM = pl.BlockSpec(memory_space=pltpu.SMEM)
HBM = pl.BlockSpec(memory_space=pltpu.HBM)
BF16, F32 = jnp.bfloat16, jnp.float32
LSE_ROWS, PARTS = 16, 4
LEAST = float(jnp.finfo(jnp.float32).min)
SEQ, FORWARDED, OUT_ORDER, LAST = 4, 3, [3, 2, 1], 2


def call(kernel, outs, operands, specs=None, flops=0, scratch=(), limit=8 * 2**20):
    size = sum(math.prod(x.shape) * x.dtype.itemsize for x in (*operands, *outs))
    if specs:
        operands = [
            pltpu.with_memory_space_constraint(x, pltpu.HBM) if spec is HBM else x for x, spec in zip(operands, specs)
        ]
    return pl.pallas_call(
        kernel,
        out_shape=tuple(outs),
        in_specs=specs or [VMEM] * len(operands),
        out_specs=tuple(VMEM for _ in outs),
        scratch_shapes=list(scratch),
        compiler_params=pltpu.CompilerParams(vmem_limit_bytes=limit),
        cost_estimate=pl.CostEstimate(flops=flops, bytes_accessed=size, transcendentals=0),
    )(*operands)


def shape(rows, cols, kind=BF16):
    return jax.ShapeDtypeStruct((rows, cols), kind)


def dot_t(a, b):
    return lax.dot_general(a, b, (((1,), (1,)), ((), ())), preferred_element_type=F32)


def dot(a, b):
    return jnp.dot(a, b, preferred_element_type=F32)


def index_of(axis):
    return lax.axis_index(axis).astype(jnp.int32)


def columns(index, width):
    return pl.ds(pl.multiple_of(index * width, width), width)


def copy_all(pairs, sems):
    copies = [pltpu.make_async_copy(src, dst, sems.at[i]) for i, (src, dst) in enumerate(pairs)]
    for copy in copies:
        copy.start()
    for copy in copies:
        copy.wait()


def pack_kernel(hops, width, q_ref, k_ref, v_ref, qa_ref, ka_ref, va_ref, *rest):
    outs, sems = rest[:-1], rest[-1]
    rows = q_ref.shape[0]
    rows_audio, cols_audio = qa_ref.shape
    me = index_of("seq")
    pairs = []
    for hop, out in zip(hops, outs):
        for i, ref in enumerate((q_ref, k_ref, v_ref)):
            pairs.append((ref.at[:, columns(me ^ hop, width)], out.at[pl.ds(i * rows, rows), :]))
        at = 3 * rows
        for ref in (qa_ref,) if hop == FORWARDED else (qa_ref, ka_ref, va_ref):
            for i in range(cols_audio // width):
                pairs.append((ref.at[:, pl.ds(i * width, width)], out.at[pl.ds(at, rows_audio), :]))
                at += rows_audio
    copy_all(pairs, sems)


def audio_block(ref, end, rows, cols, block):
    at, column = divmod(block * 128, ref.shape[1])
    top = ref.shape[0] - end * (cols // ref.shape[1]) * rows + at * rows
    return ref[top : top + rows, column : column + 128]


def one_hot_t(steps_ref):
    levels = lax.broadcasted_iota(jnp.int32, (NT, steps_ref.shape[1]), 0)
    return (levels == steps_ref[...]).astype(BF16)


def pick(hot_t, table):
    return lax.dot_general(hot_t, table, (((0,), (0,)), ((), ())), preferred_element_type=F32)


def fetch_kernel(limit_ref, vg_ref, *rest):
    count = (len(rest) - 9) // 2
    loads, gain_ref, audio_ref = rest[: count + 3], rest[count + 3], rest[count + 4]
    fetched, (vs_ref, as_ref, ag_ref, sems) = rest[count + 5 : -4], rest[-4:]
    copies = [
        pltpu.make_async_copy(src, dst, sems.at[i])
        for i, (src, dst) in enumerate(zip(loads, (vs_ref, as_ref, ag_ref, *fetched)))
    ]
    for copy in copies:
        copy.start()
    for copy in copies[:3]:
        copy.wait()
    hot_t = one_hot_t(vs_ref)
    piece = min(vg_ref.shape[1], 2048)
    for at in range(0, vg_ref.shape[1], piece):
        gain_ref[:, at : at + piece] = pick(hot_t, vg_ref[:, at : at + piece]).astype(BF16)
    rows_audio, narrow = audio_ref.shape
    part = index_of("mp") * 2 + index_of("sub")
    gain = pick(one_hot_t(as_ref), ag_ref[:, columns(part, narrow)])
    at = index_of("seq") * rows_audio + lax.broadcasted_iota(jnp.int32, (rows_audio, 1), 0)
    audio_ref[...] = jnp.where(at < limit_ref[0], gain, 0.0)
    for copy in copies[3:]:
        copy.wait()


def softmax_t(scores, scale, allowed=None):
    if allowed is not None:
        scores = [jnp.where(ok, x, LEAST) for ok, x in zip(allowed, scores)]
    peak = functools.reduce(jnp.maximum, [jnp.max(x, axis=0, keepdims=True) for x in scores])
    weights = [jnp.exp2((x - peak) * (scale * LOG2E)) for x in scores]
    total = functools.reduce(jnp.add, [jnp.sum(x, axis=0, keepdims=True) for x in weights])
    return peak, [x.astype(BF16) for x in weights], total


def turn(x):
    return x.astype(F32).T.astype(BF16)


def pair_rows(x, head):
    lane = lax.broadcasted_iota(jnp.int32, (1, 128), 1) // head
    return jnp.concatenate([jnp.where(lane == i, x, 0).astype(BF16) for i in range(128 // head)], axis=0)


def pair_columns(x, head):
    pair = 128 // head
    rows = x.shape[1] // pair
    return jnp.concatenate([x[i * head : (i + 1) * head, i * rows : (i + 1) * rows] for i in range(pair)], axis=0)


def audio_part(q, keys, values_t, head):
    pair, rows = 128 // head, q.shape[0]
    scale = 1.0 / math.sqrt(head)
    both = pair_rows(q, head)
    both = jnp.concatenate([both] * (128 // both.shape[0]), axis=0)
    peak, p, total = softmax_t([dot_t(keys, both)], scale)
    o = dot(values_t, p[0]) * (1.0 / total)
    lse = peak * (scale * LOG2E) + jnp.log2(total)
    o = [o[i * head : (i + 1) * head] for i in range(pair)]
    o = [x if i == 0 else pltpu.roll(x, 128 - i * rows, 1) for i, x in enumerate(o)]
    lses = [lse if i == 0 else pltpu.roll(lse, 128 - i * rows, 1) for i in range(pair)]
    return jnp.concatenate(o, axis=0).T[0:rows], lses


def audio_parts(ref, end, kv_ref, vvt_ref, rows_audio, head):
    cols = kv_ref.shape[1]
    outs, lses = [], []
    for block in range(cols // 128):
        cut = slice(block * 128, (block + 1) * 128)
        q = audio_block(ref, end, rows_audio, cols, block)
        o, lse = audio_part(q, kv_ref[:, cut], vvt_ref[cut, :], head)
        outs.append(o)
        lses += lse
    return outs, jnp.concatenate(lses, axis=0)


def store_tail(dst, top, outs, lse):
    rows_audio = outs[0].shape[0]
    for i, o in enumerate(outs):
        dst[top + i * rows_audio : top + (i + 1) * rows_audio, 0:128] = o.astype(BF16)
    pieces, left = [], lse
    for _ in range(3):
        pieces.append(left.astype(BF16).astype(F32))
        left = left - pieces[-1]
    pieces.append(jnp.zeros((LSE_ROWS - 3 * lse.shape[0], 128), F32))
    top += len(outs) * rows_audio
    dst[top : top + LSE_ROWS, 0:128] = jnp.concatenate(pieces, axis=0).astype(BF16)


def early_kernel(early, head, kv_ref, vv_ref, *rest):
    count = len(early)
    blocks, (part_ref, stats_ref, vt_ref, vvt_ref, own_v2a_ref, own_lse_ref) = rest[:count], rest[count : count + 6]
    tails, (s_ref,) = rest[count + 6 : -1], rest[-1:]
    rows, cols = kv_ref.shape
    rows_audio = own_v2a_ref.shape[0]
    for i, ref in enumerate(blocks):
        vt_ref[:, i * rows : (i + 1) * rows] = turn(ref[2 * rows : 3 * rows, :])
    for block in range(cols // 128):
        cut = slice(block * 128, (block + 1) * 128)
        vvt_ref[cut, :] = turn(vv_ref[:, cut])
    tops = []
    for block in range(cols // 128):
        ends = [1 if hop == FORWARDED else 3 for hop in early]
        q = [audio_block(ref, end, rows_audio, cols, block) for ref, end in zip(blocks, ends)]
        q = jnp.concatenate(q + [q[0]] * (128 // rows_audio - count), axis=0)
        scores = dot_t(kv_ref[:, block * 128 : (block + 1) * 128], pair_rows(q, head))
        for i in range(128 // head):
            row = (count * count + block * (128 // head) + i) * rows
            s_ref[row : row + rows, :] = scores[:, i * 128 : (i + 1) * 128]
        tops.append(jnp.max(scores, axis=0, keepdims=True))
    scale = 1.0 / math.sqrt(DHV)
    peaks = []
    for j, ref in enumerate(blocks):
        peak = None
        for i, other in enumerate(blocks):
            scores = dot_t(other[rows : 2 * rows, :], ref[0:rows, :])
            s_ref[(j * count + i) * rows : (j * count + i + 1) * rows, :] = scores
            top = jnp.max(scores, axis=0, keepdims=True)
            peak = top if i == 0 else jnp.maximum(peak, top)
        peaks.append(peak)
    for j, peak in enumerate(peaks):
        total, p = None, []
        for i in range(count):
            x = jnp.exp2((s_ref[(j * count + i) * rows : (j * count + i + 1) * rows, :] - peak) * (scale * LOG2E))
            summed = jnp.sum(x, axis=0, keepdims=True)
            total = summed if i == 0 else total + summed
            p.append(x.astype(BF16))
        part_ref[j * DHV : (j + 1) * DHV, :] = dot(vt_ref[...], jnp.concatenate(p, axis=0))
        stats_ref[2 * j : 2 * j + 1, :] = peak
        stats_ref[2 * j + 1 : 2 * j + 2, :] = total
    pair, scale = 128 // head, 1.0 / math.sqrt(head)
    outs, lses = [], []
    for block in range(cols // 128):
        cut = slice(block * 128, (block + 1) * 128)
        peak = tops[block]
        both = []
        for i in range(pair):
            at = slice(i * 128, (i + 1) * 128)
            row = (count * count + block * pair + i) * rows
            p = jnp.exp2((s_ref[row : row + rows, :] - peak[:, at]) * (scale * LOG2E))
            total = jnp.sum(p, axis=0, keepdims=True)
            lses.append(peak[:, at] * (scale * LOG2E) + jnp.log2(total))
            column = block * 128 + i * head
            both.append(dot(vvt_ref[column : column + head, :], p.astype(BF16)) * (1.0 / total))
        outs.append(jnp.concatenate(both, axis=0).T)
    lse = jnp.concatenate(lses, axis=0)
    own_lse_ref[...] = lse
    for block, o in enumerate(outs):
        own_v2a_ref[:, block * 128 : (block + 1) * 128] = o[0:rows_audio]
    for j in range(1, count):
        mine = [o[j * rows_audio : (j + 1) * rows_audio] for o in outs]
        store_tail(tails[j - 1], 0, mine, pltpu.roll(lse, 128 - j * rows_audio, 1))


def late_kernel(early, hops, rows_audio, head, kv_ref, vvt_ref, part_ref, stats_ref, vt_ref, last_ref, *rest):
    count, n = len(early), len(hops)
    blocks, tails, outs, s_ref = rest[:count], rest[count : 2 * count - 1], rest[2 * count - 1 : -1], rest[-1]
    by_hop = dict(zip(hops, outs))
    rows = kv_ref.shape[0]
    last = next(hop for hop in hops if hop not in early)
    scale = 1.0 / math.sqrt(DHV)
    keys = last_ref[rows : 2 * rows, :]
    peaks = []
    for j, ref in enumerate((*blocks, last_ref)):
        scores = dot_t(keys, ref[0:rows, :])
        s_ref[j * rows : (j + 1) * rows, :] = scores
        top = jnp.max(scores, axis=0, keepdims=True)
        peaks.append(jnp.maximum(top, stats_ref[2 * j : 2 * j + 1, :]) if j < count else top)
    for i, other in enumerate(blocks):
        scores = dot_t(other[rows : 2 * rows, :], last_ref[0:rows, :])
        s_ref[(n + i) * rows : (n + i + 1) * rows, :] = scores
        peaks[-1] = jnp.maximum(peaks[-1], jnp.max(scores, axis=0, keepdims=True))
    values_t = turn(last_ref[2 * rows : 3 * rows, :])

    def weigh(at, peak):
        x = jnp.exp2((s_ref[at * rows : (at + 1) * rows, :] - peak) * (scale * LOG2E))
        return x.astype(BF16), jnp.sum(x, axis=0, keepdims=True)

    audio = audio_parts(last_ref, 3, kv_ref, vvt_ref, rows_audio, head)
    total, p = None, []
    for i in range(count):
        x, summed = weigh(n + i, peaks[-1])
        total = summed if i == 0 else total + summed
        p.append(x)
    x, summed = weigh(count, peaks[-1])
    o = dot(vt_ref[...], jnp.concatenate(p, axis=0)) + dot(values_t, x)
    by_hop[last][0:rows, :] = (o * (1.0 / (total + summed))).T.astype(BF16)
    for j, hop in enumerate(early):
        x, summed = weigh(j, peaks[j])
        factor = jnp.exp2((stats_ref[2 * j : 2 * j + 1, :] - peaks[j]) * (scale * LOG2E))
        total = stats_ref[2 * j + 1 : 2 * j + 2, :] * factor + summed
        o = part_ref[j * DHV : (j + 1) * DHV, :] * factor + dot(values_t, x)
        by_hop[hop][0:rows, :] = (o * (1.0 / total)).T.astype(BF16)
    store_tail(by_hop[last], rows, *audio)
    for hop, tail in zip(early[1:], tails):
        by_hop[hop][rows : rows + tail.shape[0], :] = tail[...]
    dst, src = by_hop[last], blocks[early.index(FORWARDED ^ last)]
    extra = dst.shape[0] - rows - tails[0].shape[0]
    dst[dst.shape[0] - extra :, :] = src[src.shape[0] - extra :, :]


def audio_allowed(hop, rows_audio, limit):
    row = lax.broadcasted_iota(jnp.int32, (rows_audio, 1), 0)
    return (index_of("seq") ^ hop) * rows_audio + row < limit


def spread(x, head):
    pair = 128 // head
    rows = x.shape[1] // pair
    parts = [jnp.broadcast_to(x[:, i * rows : (i + 1) * rows], (head, rows)) for i in range(pair)]
    return jnp.concatenate(parts, axis=0)


def attend_audio_kernel(hops, rows_audio, head, limit_ref, q_ref, *rest):
    blocks, part_ref, stats_ref = rest[:-2], rest[-2], rest[-1]
    cols = q_ref.shape[1]
    allowed = [audio_allowed(hop, rows_audio, limit_ref[0]) for hop in hops]
    scale = 1.0 / math.sqrt(head)
    for block in range(cols // 128):
        cut = slice(block * 128, (block + 1) * 128)
        q = pair_rows(q_ref[:, cut], head)
        scores = [dot_t(audio_block(ref, 2, rows_audio, cols, block), q) for ref in blocks]
        peak, p, total = softmax_t(scores, scale, allowed)
        vt = turn(jnp.concatenate([audio_block(ref, 1, rows_audio, cols, block) for ref in blocks], axis=0))
        part_ref[cut, :] = pair_columns(dot(vt, jnp.concatenate(p, axis=0)), head)
        stats_ref[2 * block : 2 * block + 1, :] = peak
        stats_ref[2 * block + 1 : 2 * block + 2, :] = total


def join_kernel(head, rows_audio, limit_ref, q_ref, part_ref, stats_ref, last_ref, out_ref):
    cols = q_ref.shape[1]
    scale = 1.0 / math.sqrt(head)
    allowed = audio_allowed(FORWARDED, rows_audio, limit_ref[0])
    for block in range(cols // 128):
        cut = slice(block * 128, (block + 1) * 128)
        q = pair_rows(q_ref[:, cut], head)
        scores = jnp.where(allowed, dot_t(audio_block(last_ref, 2, rows_audio, cols, block), q), LEAST)
        before, summed = stats_ref[2 * block : 2 * block + 1, :], stats_ref[2 * block + 1 : 2 * block + 2, :]
        peak = jnp.maximum(before, jnp.max(scores, axis=0, keepdims=True))
        factor = jnp.exp2((before - peak) * (scale * LOG2E))
        p = jnp.exp2((scores - peak) * (scale * LOG2E))
        inverse = 1.0 / (summed * factor + jnp.sum(p, axis=0, keepdims=True))
        vt = turn(audio_block(last_ref, 1, rows_audio, cols, block))
        last = pair_columns(dot(vt, p.astype(BF16)), head)
        both = part_ref[cut, :] * spread(factor, head) + last
        out_ref[:, cut] = (both * spread(inverse, head)).T.astype(BF16)


def merge_audio(head, top, v2a_ref, lse_ref, got, out_ref):
    rows_audio, cols = v2a_ref.shape
    heads = cols // head
    lses = [lse_ref[...]]
    for ref in got:
        at = top + cols // 128 * rows_audio
        packed = ref[at : at + LSE_ROWS, 0:128].astype(F32)
        lses.append(packed[0:heads] + packed[heads : 2 * heads] + packed[2 * heads : 3 * heads])
    peak = functools.reduce(jnp.maximum, lses)
    parts = [jnp.exp2(x - peak) for x in lses]
    total = functools.reduce(jnp.add, parts)
    inverse = 1.0 / total
    parts = [x * inverse for x in parts]
    parts.append(jnp.zeros((128 - len(parts) * heads, 128), F32))
    shares = jnp.concatenate(parts, axis=0).T[0:rows_audio]
    pair = 128 // head
    lane = lax.broadcasted_iota(jnp.int32, (1, 128), 1) // head
    for block in range(cols // 128):
        cut = slice(block * 128, (block + 1) * 128)
        at = top + block * rows_audio
        summed = jnp.zeros((rows_audio, 128), F32)
        for j in range(len(lses)):
            o = v2a_ref[:, cut] if j == 0 else got[j - 1][at : at + rows_audio, 0:128].astype(F32)
            share = jnp.zeros((rows_audio, 128), F32)
            for i in range(pair):
                column = j * heads + block * pair + i
                share = jnp.where(lane == i, shares[:, column : column + 1], share)
            summed = summed + share * o
        out_ref[:, cut] = summed.astype(BF16)


def block_of(far, other):
    mp, sub = index_of("mp"), index_of("sub")
    return (1 - mp if far else mp) * 2 + (1 - sub if other else sub)


def project_self(block, part, att_ref, ws_ref, gain_ref):
    cut = ws_ref.shape[1] // (4 * PARTS)
    at = columns(block * PARTS + part, cut)
    return gain_ref[:, at].astype(F32) * dot(att_ref[...], ws_ref[:, at])


def project_a2v(block, part, a2v_ref, wa_ref, gain_ref):
    cut = wa_ref.shape[1] // (4 * PARTS)
    gain = gain_ref[:, columns((block + 4) * PARTS + part, cut)].astype(F32)
    return gain * dot(a2v_ref[...], wa_ref[:, columns(block * PARTS + part, cut)])


def project_audio(block, v2a_ref, wv_ref):
    return dot(v2a_ref[...], wv_ref[:, columns(block, wv_ref.shape[1] // 4)])


def project(block, parts, heads, weights, out, extra=None):
    (self_ref, a2v_ref, audio_ref), (ws_ref, wa_ref, wv_ref, gain_ref) = heads, weights
    rows, cut = self_ref.shape[0], out.shape[1]

    def store(at, term):
        if extra is not None:
            term = term + extra[at : at + term.shape[0], :].astype(F32)
        out[at : at + term.shape[0], :] = term.astype(out.dtype)

    for i, part in enumerate(parts):
        term = project_self(block, part, self_ref, ws_ref, gain_ref)
        store(i * rows, term + project_a2v(block, part, a2v_ref, wa_ref, gain_ref))
    term, rows_audio = project_audio(block, audio_ref, wv_ref), audio_ref.shape[0]
    for i in range(term.shape[1] // cut):
        store(len(parts) * rows + i * rows_audio, term[:, i * cut : (i + 1) * cut])


def first_kernel(hops, own_ref, a2v_ref, ws_ref, wa_ref, gain_ref, *rest):
    got, (self_ref, out_ref) = rest[: len(hops) - 1], rest[len(hops) - 1 :]
    rows, width = own_ref.shape
    block, me = block_of(True, True), index_of("seq")
    term = project_a2v(block, 0, a2v_ref, wa_ref, gain_ref)
    self_ref[:, columns(me, width)] = own_ref[...]
    for hop, ref in zip(hops[1:], got):
        self_ref[:, columns(me ^ hop, width)] = ref[0:rows, :]
    out_ref[...] = (project_self(block, 0, self_ref, ws_ref, gain_ref) + term).astype(BF16)


def second_kernel(head, self_ref, a2v_ref, ws_ref, wa_ref, wv_ref, gain_ref, v2a_ref, lse_ref, *rest):
    got, (out_ref, audio_ref, low_ref) = rest[:-3], rest[-3:]
    merge_audio(head, self_ref.shape[0], v2a_ref, lse_ref, got, audio_ref)
    heads, weights = (self_ref, a2v_ref, audio_ref), (ws_ref, wa_ref, wv_ref, gain_ref)
    project(block_of(True, True), range(1, PARTS), heads, weights, out_ref)
    block = block_of(True, False)
    term = project_self(block, 0, self_ref, ws_ref, gain_ref)
    low_ref[...] = term + project_a2v(block, 0, a2v_ref, wa_ref, gain_ref)


def far_low_kernel(low_ref, extra_ref, out_ref):
    out_ref[...] = (low_ref[...] + extra_ref[...].astype(F32)).astype(BF16)


def near_kernel(*refs):
    heads, weights, (send_ref, own_ref) = refs[:3], refs[3:7], refs[7:]
    project(block_of(False, True), range(PARTS), heads, weights, send_ref)
    project(block_of(False, False), range(PARTS), heads, weights, own_ref)


def far_high_kernel(*refs):
    heads, weights, (extra_ref, out_ref) = refs[:3], refs[3:7], refs[7:]
    project(block_of(True, False), range(1, PARTS), heads, weights, out_ref, extra_ref)


def finish_kernel(video_ref, audio_ref, gain_ref, own_ref, core_ref, low_ref, high_ref, video_out, audio_out):
    rows, cut = low_ref.shape
    rows_audio = audio_ref.shape[0]
    for part in range(PARTS):
        at = slice(part * cut, (part + 1) * cut)
        here = slice(part * rows, (part + 1) * rows)
        far = low_ref[...] if part == 0 else high_ref[(part - 1) * rows : part * rows, :]
        term = own_ref[here, :] + core_ref[here, :].astype(F32) + far.astype(F32)
        video_out[:, at] = (video_ref[:, at].astype(F32) + term).astype(BF16)
    for i in range(audio_ref.shape[1] // cut):
        at = slice(i * cut, (i + 1) * cut)
        top = PARTS * rows + i * rows_audio
        here, there = slice(top, top + rows_audio), slice(top - rows, top - rows + rows_audio)
        term = own_ref[here, :] + core_ref[here, :].astype(F32) + high_ref[there, :].astype(F32)
        audio_out[:, at] = (audio_ref[:, at].astype(F32) + gain_ref[:, at] * term).astype(BF16)


def on_device_heads(
    video_in,
    audio_in,
    q_self,
    k_self,
    v_self,
    q_a2v,
    k_a2v,
    v_a2v,
    q_v2a,
    k_v2a,
    v_v2a,
    wo_self,
    wo_a2v,
    wo_v2a,
    video_gates,
    audio_gates,
    video_steps,
    audio_steps,
    audio_len,
    *,
    n,
):
    hops = [0] + OUT_ORDER
    rows, cols = q_self.shape
    rows_audio, cross = q_v2a.shape
    width = cols // n

    def trade(x, axis, hop, size):
        return lax.ppermute(x, axis, [(i, i ^ hop) for i in range(size)])

    video, audio = 3 * rows, cross // width * rows_audio

    def pack(some):
        ends = [1 if hop == FORWARDED else 3 for hop in some]
        return call(
            functools.partial(pack_kernel, some, width),
            [shape(video + end * audio, width) for end in ends],
            (q_self, k_self, v_self, q_v2a, k_a2v, v_a2v),
            [HBM] * 6,
            scratch=[pltpu.SemaphoreType.DMA((3 * len(some) + sum(ends) * audio // rows_audio,))],
        )

    packed = pack(hops[1:2])
    rest = pack(hops[:1] + hops[2:])
    packed = [rest[0], *packed, *rest[1:]]
    blocks = dict(zip(hops, packed))
    for hop in hops[1:]:
        blocks[hop] = trade(blocks[hop], "seq", hop, n)

    late = (k_v2a, v_v2a, q_a2v, wo_self, wo_a2v, wo_v2a, video_in, audio_in)
    steps = (video_steps.reshape(1, rows), audio_steps.reshape(1, rows_audio))
    gain, audio_gain, k_own, v_own, q_own, ws, wa, wv, video_own, audio_own = call(
        fetch_kernel,
        [shape(rows, 2 * video_gates.shape[2]), shape(*audio_in.shape, F32)]
        + [shape(*x.shape) for x in late],
        (audio_len, video_gates.reshape(NT, -1), *steps, audio_gates, *late),
        [SMEM, VMEM] + [HBM] * (3 + len(late)),
        scratch=[pltpu.VMEM(x.shape, x.dtype) for x in (*steps, audio_gates)]
        + [pltpu.SemaphoreType.DMA((3 + len(late),))],
    )
    tail = cross // 128 * rows_audio + LSE_ROWS
    early = [hop for hop in hops if hop != LAST]
    count = len(early)
    part, stats, vt, vvt, own_v2a, own_lse, *tails = call(
        functools.partial(early_kernel, early, DHC),
        [
            shape(count * width, rows, F32),
            shape(2 * count, rows, F32),
            shape(width, count * rows),
            shape(cross, rows),
            shape(rows_audio, cross, F32),
            shape(cross // DHC, 128, F32),
        ]
        + [shape(tail, width)] * (count - 1),
        (k_own, v_own, *(blocks[hop] for hop in early)),
        flops=4 * count * count * rows * rows * width,
        scratch=[pltpu.VMEM(((count * count + cross // DHC) * rows, rows), F32)],
    )
    own, *sends = call(
        functools.partial(late_kernel, early, hops, rows_audio, DHC),
        [shape(rows, width)]
        + [shape(rows + tail + (2 * audio if hop == LAST else 0), width) for hop in hops[1:]],
        (k_own, vvt, part, stats, vt, blocks[LAST], *(blocks[hop] for hop in early), *tails),
        flops=4 * (2 * n - 1) * rows * rows * width,
        scratch=[pltpu.VMEM(((2 * n - 1) * rows, rows), F32)],
    )
    got = [trade(x, "seq", hop, n) for x, hop in zip(sends, hops[1:])]
    near = [hop for hop in hops if hop != FORWARDED]
    a2v_part, a2v_stats = call(
        functools.partial(attend_audio_kernel, near, rows_audio, DHC),
        [shape(cross, rows, F32), shape(cross // 64, 128 // DHC * rows, F32)],
        (audio_len, q_own, *(blocks[hop] for hop in near)),
        [SMEM] + [VMEM] * n,
        flops=8 * n * rows * rows_audio * cross,
    )

    (a2v_att,) = call(
        functools.partial(join_kernel, DHC, rows_audio),
        [shape(rows, cross)],
        (audio_len, q_own, a2v_part, a2v_stats, got[hops.index(LAST) - 1]),
        [SMEM] + [VMEM] * 4,
        flops=4 * rows * rows_audio * cross,
    )

    cut = video_in.shape[1] // PARTS
    below = rows_audio * audio_in.shape[1] // cut
    flops = 2 * rows * (cols + cross) * cut
    self_att, first = call(
        functools.partial(first_kernel, hops),
        [shape(rows, cols), shape(rows, cut)],
        (own, a2v_att, ws, wa, gain, *got),
        flops=flops,
    )
    first = trade(first, "sub", 1, 2)
    high_rows = (PARTS - 1) * rows + below
    second, v2a_att, own_low = call(
        functools.partial(second_kernel, DHC),
        [shape(high_rows, cut), shape(rows_audio, cross), shape(rows, cut, F32)],
        (self_att, a2v_att, ws, wa, wv, gain, own_v2a, own_lse, *got),
        flops=PARTS * flops,
    )
    second = trade(second, "sub", 1, 2)
    operands = (self_att, a2v_att, v2a_att, ws, wa, wv, gain)
    (low,) = call(far_low_kernel, [shape(rows, cut)], (own_low, first))
    low = trade(low, "mp", 1, 2)
    (high,) = call(far_high_kernel, [shape(high_rows, cut)], (*operands, second), flops=3 * flops)
    high = trade(high, "mp", 1, 2)
    near, own_sum = call(
        near_kernel,
        [shape(rows + high_rows, cut), shape(rows + high_rows, cut, F32)],
        operands,
        flops=2 * PARTS * flops,
    )
    near = trade(near, "sub", 1, 2)
    return call(
        finish_kernel,
        [shape(*video_in.shape), shape(*audio_in.shape)],
        (video_own, audio_own, audio_gain, own_sum, near, low, high),
    )


def on_device(n, mp, sub, *arrays):
    cols, cross = arrays[2].shape[1], arrays[5].shape[1]
    width = cols // n
    fits = (
        n == SEQ
        and (mp, sub) == (2, 2)
        and width == DHV == 128
        and cross % width == 0
        and 3 * (cross // DHC) <= LSE_ROWS
        and n * arrays[8].shape[0] == arrays[2].shape[0] == 128
        and arrays[0].shape[1] == 2 * arrays[1].shape[1]
        and arrays[0].shape[1] % (PARTS * 128) == 0
    )
    if fits:
        return on_device_heads(*arrays, n=n)
    return on_device_gather(*arrays)


def solution(mesh):
    in_specs = (
        P(("groups", "seq"), ("mp", "sub")),
        P(("groups", "seq"), ("mp", "sub")),
        P(("groups", "seq"), ("mp", "sub")),
        P(("groups", "seq"), ("mp", "sub")),
        P(("groups", "seq"), ("mp", "sub")),
        P(("groups", "seq"), ("mp", "sub")),
        P(("groups", "seq"), ("mp", "sub")),
        P(("groups", "seq"), ("mp", "sub")),
        P(("groups", "seq"), ("mp", "sub")),
        P(("groups", "seq"), ("mp", "sub")),
        P(("groups", "seq"), ("mp", "sub")),
        P(("mp", "sub"), None),
        P(("mp", "sub"), None),
        P(("mp", "sub"), None),
        P(),
        P(),
        P(("groups", "seq")),
        P(("groups", "seq")),
        P("groups"),
    )
    out_specs = (P(("groups", "seq"), ("mp", "sub")), P(("groups", "seq"), ("mp", "sub")))
    return jax.shard_map(
        functools.partial(on_device, *(mesh.shape[a] for a in ("seq", "mp", "sub"))), mesh=mesh, in_specs=in_specs, out_specs=out_specs, check_vma=False
    )
```
